32 devices in a mesh: grp: 4 (over x, core), row: 8 (over z, y).
Axes of the slice: x: 2, y: 2, z: 4, core: 2. Of those that a mesh axis runs over, the one named last changes fastest.
Arguments:
- tokens: bfloat16 [4, 2048, 768], P('grp', 'row'), may hold values from -6 to 6
- cont_lengths: int32 [4, 8], P('grp'), may hold values from 1 to 256, 1024 in all within a row
- cotangent: bfloat16 [4, 2048, 768], P('grp', 'row'), may hold values from -6 to 6
- w_query: bfloat16 [768, 768], P(('grp', 'row')), may hold values from -0.21875 to 0.21875
- w_key: bfloat16 [768, 768], P(('grp', 'row')), may hold values from -0.21875 to 0.21875
- w_value: bfloat16 [768, 768], P(('grp', 'row')), may hold values from -0.21875 to 0.21875
- w_output: bfloat16 [768, 768], P(('grp', 'row')), may hold values from -2.5 to 2.5
- w_inner: bfloat16 [768, 3072], P(('grp', 'row')), may hold values from -0.21875 to 0.21875
- w_outer: bfloat16 [3072, 768], P(('grp', 'row')), may hold values from -0.109375 to 0.109375
- bias_query: bfloat16 [768], P(('grp', 'row')), may hold values from -3 to 3
- bias_value: bfloat16 [768], P(('grp', 'row')), may hold values from -0.59765625 to 0.59765625
- bias_output: bfloat16 [768], P(('grp', 'row')), may hold values from -1.1953125 to 1.1953125
- gain_first: bfloat16 [768], P(('grp', 'row')), may hold values from 0.5 to 1.5
- shift_first: bfloat16 [768], P(('grp', 'row')), may hold values from -1.1953125 to 1.1953125
- bias_inner: bfloat16 [3072], P(('grp', 'row')), may hold values from -1.1953125 to 1.1953125
- bias_outer: bfloat16 [768], P(('grp', 'row')), may hold values from -1.1953125 to 1.1953125
- gain_second: bfloat16 [768], P(('grp', 'row')), may hold values from 0.5 to 1.5
- shift_second: bfloat16 [768], P(('grp', 'row')), may hold values from -1.1953125 to 1.1953125
Outputs:
- layer_out: bfloat16 [4, 2048, 768], P('grp', 'row')
- grad_tokens: bfloat16 [4, 2048, 768], P('grp', 'row')
- grad_w_query: float32 [768, 768], P(('grp', 'row'))
- grad_w_key: float32 [768, 768], P(('grp', 'row'))
- grad_w_value: float32 [768, 768], P(('grp', 'row'))
- grad_w_output: float32 [768, 768], P(('grp', 'row'))
- grad_w_inner: float32 [768, 3072], P(('grp', 'row'))
- grad_w_outer: float32 [3072, 768], P(('grp', 'row'))
- grad_bias_query: float32 [768], P(('grp', 'row'))
- grad_bias_value: float32 [768], P(('grp', 'row'))
- grad_bias_output: float32 [768], P(('grp', 'row'))
- grad_gain_first: float32 [768], P(('grp', 'row'))
- grad_shift_first: float32 [768], P(('grp', 'row'))
- grad_bias_inner: float32 [3072], P(('grp', 'row'))
- grad_bias_outer: float32 [768], P(('grp', 'row'))
- grad_gain_second: float32 [768], P(('grp', 'row'))
- grad_shift_second: float32 [768], P(('grp', 'row'))
The draws below stay inside these ranges and needn't reach their ends.
Inputs may be any that keep to these rules, and one draw needn't show every extreme that they name: `cont_lengths`: each group's 8 lengths sum to 1024, and the longest of each group is 256.
All inputs are finite; a program needn't handle non-finite values.
Results may differ from the reference program's by a relative error of at most 0.017.
Values may be sent and summed in bfloat16 or wider, within the bound.
No kernel may reach another device: no remote copies, remote signals or barrier semaphores. Data moves between devices by JAX's collectives and lax.ppermute only.
A program may use at most 192 MiB of HBM per device.

```python
import math
import jax
import jax.numpy as jnp
import numpy as np
from jax import lax

D = 768
HEADS = 12
HDIM = 64
FF = 3072
PROMPT = 1024
NCONT = 8
CONT_TOK = 1024
CONT_MOST = 256
GTOK = 2048
GROUPS = 4


def spiked(array, own_key, source, target, parts, factor):
    owner, partner = [(jnp.arange(array.shape[position]) // (array.shape[position] // parts)).reshape([-1 if axis == position else 1 for axis in range(array.ndim)]) for position in (source, target)]
    chosen = jax.random.permutation(own_key, parts)[partner]
    strong = (owner == chosen) | (owner == (partner + parts // 2) % parts)
    return jnp.where(strong, factor * array, array)


def levels(rng, extent, split, least, high):
    def one(position, blocks):
        draws = jax.random.uniform(jax.random.fold_in(jax.random.fold_in(rng, 6), position), (blocks,), jnp.float32, least / len(split), high / len(split))
        return jnp.repeat(jnp.exp(draws), extent[position] // blocks).reshape((-1,) + (1,) * (len(extent) - position - 1))

    level = one(*split[0])
    for cut in split[1:]:
        level = level * one(*cut)
    return level


def length_profile(amount, total, bound, lean):
    portions = [(1 << 20) // math.isqrt(standing ** lean) + 1 for standing in range(2, amount + 1)]
    rest, holding = total - bound - (amount - 1), [1] * (amount - 1)
    while rest > 0:
        free = [i for i in range(amount - 1) if holding[i] < bound]
        pool, left = sum([portions[i] for i in free]), rest
        for i in free:
            more = min(bound - holding[i], max(1, left * portions[i] // pool), rest)
            holding[i] = holding[i] + more
            rest = rest - more
    return np.array([bound] + holding)


def ragged_sizes(key, number_of, total, most, slope):
    if number_of == 2:
        one = jax.random.randint(key, (), max(1, total - most), min(most, total - 1) + 1)
        return jnp.stack([one, total - one])
    tallies = jnp.asarray(length_profile(number_of, total, most, slope), jnp.int32)
    twos = (number_of - 1) // 2
    giver, receiver = tallies[1:1 + 2 * twos:2], tallies[2:2 + 2 * twos:2]
    room = jnp.minimum(giver - 1, most - receiver)
    moved = jax.random.randint(jax.random.fold_in(key, 1), (twos,), 0, 1 << 20) % (room + 1)
    tallies = tallies.at[1:1 + 2 * twos:2].set(giver - moved).at[2:2 + 2 * twos:2].set(receiver + moved)
    return tallies[jax.random.permutation(jax.random.fold_in(key, 2), number_of)]


def gaussian(own_key, extent, scale, reach, split=(), held_as=jnp.bfloat16):
    gain = levels(own_key, extent, split, -0.22, 0.18) if split else 1.0
    drawn = jax.random.normal(own_key, extent, jnp.float32) * scale * gain
    return jnp.minimum(jnp.maximum(drawn, -reach), reach).astype(held_as)


def heavy_noise(own_key, shape, deviation, limit, cuts, heavy, held_as=jnp.bfloat16):
    drawn = deviation * jax.random.normal(own_key, shape, jnp.float32)
    if cuts:
        drawn = drawn * levels(own_key, shape, cuts, -0.22, 0.18)
    return jnp.clip(spiked(drawn, jax.random.fold_in(own_key, 3), *heavy), -limit, limit).astype(held_as)


def setup_inputs(seed: int = 0) -> dict:
    keys = jax.random.split(jax.random.key(seed), 19)
    return {
        "tokens": gaussian(keys[0], (GROUPS, GTOK, D), 1.0, 6.0, ((0, 4), (1, 8))),
        "cont_lengths": jax.vmap(lambda own: ragged_sizes(own, NCONT, CONT_TOK, CONT_MOST, 2))(jax.random.split(keys[1], GROUPS)).reshape((GROUPS, NCONT)).astype(jnp.int32),
        "cotangent": heavy_noise(keys[2], (GROUPS, GTOK, D), 1.0, 6.0, ((0, 4), (1, 8)), (1, 2, 8, 2.0)),
        "w_query": gaussian(keys[3], (D, D), D ** -0.5, 0.21875, ((0, 32),)),
        "w_key": gaussian(keys[4], (D, D), D ** -0.5, 0.21875, ((0, 32),)),
        "w_value": gaussian(keys[5], (D, D), D ** -0.5, 0.21875, ((0, 32),)),
        "w_output": gaussian(keys[6], (D, D), (D // 128) ** -0.5, 2.5, ((0, 32),)),
        "w_inner": gaussian(keys[7], (D, FF), D ** -0.5, 0.21875, ((0, 32),)),
        "w_outer": gaussian(keys[8], (FF, D), FF ** -0.5, 0.109375, ((0, 32),)),
        "bias_query": gaussian(keys[9], (D,), 0.5, 3.0, ((0, 32),)),
        "bias_value": gaussian(keys[10], (D,), 0.1, 0.59765625, ((0, 32),)),
        "bias_output": gaussian(keys[11], (D,), 0.2, 1.1953125, ((0, 32),)),
        "gain_first": jnp.clip(1.0 + 0.1 * jax.random.normal(keys[12], (D,), jnp.float32), 0.5, 1.5).astype(jnp.bfloat16),
        "shift_first": gaussian(keys[13], (D,), 0.2, 1.1953125, ((0, 32),)),
        "bias_inner": gaussian(keys[14], (FF,), 0.2, 1.1953125, ((0, 32),)),
        "bias_outer": gaussian(keys[15], (D,), 0.2, 1.1953125, ((0, 32),)),
        "gain_second": jnp.clip(1.0 + 0.1 * jax.random.normal(keys[16], (D,), jnp.float32), 0.5, 1.5).astype(jnp.bfloat16),
        "shift_second": gaussian(keys[17], (D,), 0.2, 1.1953125, ((0, 32),)),
    }


NORM_EPS = 1e-12
MASK_FILL = -1000000000.0
HIGH = lax.Precision.HIGHEST

@jax.custom_vjp
def low(v):
    return lax.optimization_barrier(v.astype(jnp.bfloat16)).astype(jnp.float32)

@jax.custom_vjp
def low_back(v):
    return v

def low_keep(v):
    return (low(v), None)

def low_pass(kept, grad):
    return (grad,)

def back_keep(v):
    return (v, None)

def back_low(kept, grad):
    return (low(grad),)
low.defvjp(low_keep, low_pass)
low_back.defvjp(back_keep, back_low)

def product(left, right):
    return jnp.dot(left, right, precision=HIGH, preferred_element_type=jnp.float32)

def segment_ids(cont_lengths, prompt_len, group_len):
    ends = jnp.cumsum(cont_lengths, axis=-1).astype(jnp.int32)
    places = jnp.arange(group_len, dtype=jnp.int32)
    later = places - prompt_len
    passed = lax.optimization_barrier(jnp.sum((later[None, :, None] >= ends[:, None, :]).astype(jnp.int32), axis=-1))
    return jnp.where(places[None, :] < prompt_len, 0, 1 + passed).astype(jnp.int32)

def layer_norm(hidden, norm_gain, norm_shift):
    average = lax.optimization_barrier(jnp.mean(hidden, axis=-1, keepdims=True))
    centred = hidden - average
    spread = lax.optimization_barrier(jnp.mean(centred * centred, axis=-1, keepdims=True))
    return centred * lax.rsqrt(spread + NORM_EPS) * norm_gain + norm_shift

def group_forward(group_rows, group_segs, params):
    w_query, w_key, w_value, w_output, w_inner, w_outer, bias_query, bias_value, bias_output, gain_first, shift_first, bias_inner, bias_outer, gain_second, shift_second = params
    length = group_rows.shape[0]
    queries = low_back(low((product(group_rows, w_query) + bias_query) * HDIM ** (-0.5)))
    key_rows = low_back(low(product(group_rows, w_key)))
    value_rows = low_back(low(product(group_rows, w_value) + bias_value))
    heads_query = queries.reshape(length, HEADS, HDIM)
    heads_key = key_rows.reshape(length, HEADS, HDIM)
    heads_value = value_rows.reshape(length, HEADS, HDIM)
    scores = low_back(jnp.einsum('qhd,khd->hqk', heads_query, heads_key, precision=HIGH))
    allowed = (group_segs[None, :] == 0) | (group_segs[None, :] == group_segs[:, None])
    scores = jnp.where(allowed[None, :, :], scores, MASK_FILL)
    shares = low(jax.nn.softmax(scores, axis=-1))
    mixed = jnp.einsum('hqk,khd->qhd', shares, heads_value, precision=HIGH)
    context = low_back(low(mixed.reshape(length, HEADS * HDIM)))
    attn_out = low_back(product(context, w_output) + bias_output)
    first = layer_norm(group_rows + attn_out, gain_first, shift_first)
    pre_act = low_back(product(low(first), w_inner) + bias_inner)
    activation = low(jax.nn.gelu(pre_act, approximate=False))
    ffn_out = low_back(product(activation, w_outer) + bias_outer)
    return layer_norm(first + ffn_out, gain_second, shift_second)

def reference(tokens, cont_lengths, cotangent, w_query, w_key, w_value, w_output, w_inner, w_outer, bias_query, bias_value, bias_output, gain_first, shift_first, bias_inner, bias_outer, gain_second, shift_second):
    params = tuple((p.astype(jnp.float32) for p in (w_query, w_key, w_value, w_output, w_inner, w_outer, bias_query, bias_value, bias_output, gain_first, shift_first, bias_inner, bias_outer, gain_second, shift_second)))
    group_segs = segment_ids(cont_lengths, PROMPT, GTOK)

    def forward(inputs, weights):
        group_step = jax.checkpoint(lambda rows_in, segs_in: group_forward(rows_in, segs_in, weights))

        def scan_step(unused, pieces):
            return (unused, group_step(pieces[0], pieces[1]))
        _, outputs = lax.scan(scan_step, None, (inputs, group_segs))
        return outputs
    inputs = tokens.astype(jnp.float32)
    outputs, pullback = jax.vjp(forward, inputs, params)
    grad_inputs, grads = pullback(cotangent.astype(jnp.float32))
    g_query, g_key, g_value, g_output, g_inner, g_outer, g_bias_query, g_bias_value, g_bias_output, g_gain_first, g_shift_first, g_bias_inner, g_bias_outer, g_gain_second, g_shift_second = grads
    return (outputs.astype(jnp.bfloat16), grad_inputs.astype(jnp.bfloat16), g_query, g_key, g_value, g_output, g_inner, g_outer, g_bias_query, g_bias_value, g_bias_output, g_gain_first, g_shift_first, g_bias_inner, g_bias_outer, g_gain_second, g_shift_second)
```

```python
import jax
import jax.numpy as jnp
import numpy as np
from jax import lax
from jax.sharding import PartitionSpec as P

HEADS = 12
HDIM = 64
PROMPT = 1024
CONT_MOST = 256
BF = jnp.bfloat16
F32 = jnp.float32

NORM_EPS = 1e-12
MASK_FILL = -1000000000.0
SQRT_HALF = 0.7071067811865476
INV_ROOT_TAU = 0.3989422804014327
AXES = ("grp", "row")


def mm(left, right):
    return jnp.dot(left, right, preferred_element_type=F32)


def contract_last(left, right):
    return lax.dot_general(left, right, (((1,), (1,)), ((), ())), preferred_element_type=F32)


def contract_rows(left, right):
    return lax.dot_general(left, right, (((0,), (0,)), ((), ())), preferred_element_type=F32)


def segment_ids(lengths, group_len):
    ends = jnp.cumsum(lengths)
    places = jnp.arange(group_len, dtype=jnp.int32)
    passed = jnp.sum(((places - PROMPT)[:, None] >= ends[None, :]).astype(jnp.int32), axis=-1)
    return jnp.where(places < PROMPT, 0, 1 + passed)


def norm_forward(hidden, gain, shift):
    average = jnp.mean(hidden, axis=-1, keepdims=True)
    centred = hidden - average
    inverse = lax.rsqrt(jnp.mean(centred * centred, axis=-1, keepdims=True) + NORM_EPS)
    normed = centred * inverse
    return normed * gain + shift, normed, inverse


def norm_backward(grad_out, gain, normed, inverse):
    grad_norm = grad_out * gain
    one = jnp.mean(grad_norm, axis=-1, keepdims=True)
    two = jnp.mean(grad_norm * normed, axis=-1, keepdims=True)
    return inverse * (grad_norm - one - normed * two)


def gelu_slope(pre_act):
    cumulative = 0.5 * (1.0 + jax.scipy.special.erf(pre_act * SQRT_HALF))
    return cumulative + pre_act * jnp.exp(-0.5 * pre_act * pre_act) * INV_ROOT_TAU


def split_heads(rows_in):
    return rows_in.reshape(rows_in.shape[0], HEADS, HDIM)


class Plan:
    def __init__(self, grp, row):
        self.grp, self.row, self.count = grp, row, grp * row
        self.y = row // 4
        bits = lambda base, size: [base << i for i in range(size.bit_length() - 1)]
        ys, zs = bits(1, self.y), bits(self.y, 4)
        core, xs = bits(row, 2), bits(2 * row, grp // 2)
        self.orders = (tuple(zs + ys + xs + core), tuple(zs + xs + ys + core))

    def swap(self, value, mask):
        return lax.ppermute(value, AXES, [(i, i ^ mask) for i in range(self.count)])

    def send(self, value, moves):
        pairs = [(g * self.row + a, g * self.row + b) for g in range(self.grp) for a, b in moves]
        return lax.ppermute(value, AXES, pairs)

    def me(self):
        return lax.axis_index("grp") * self.row + lax.axis_index("row")

    def gather(self, value, order):
        held, masks = value[None], [0]
        for bit in order:
            held = jnp.concatenate([held, self.swap(held, bit)], 0)
            masks = masks + [m ^ bit for m in masks]
        slot = np.zeros(self.count, np.int32)
        for j, m in enumerate(masks):
            slot[m] = j
        places = jnp.asarray(slot)[self.me() ^ jnp.arange(self.count)]
        return jnp.take(held, places, axis=0, mode="clip")


def token_blocks(plan, own, rows):
    if plan.row != 8:
        every = lax.all_gather(own, "row", axis=0, tiled=True)
        start = jnp.maximum(lax.axis_index("row") * rows - CONT_MOST, 0)
        padded = jnp.concatenate([every, jnp.zeros((CONT_MOST, own.shape[1]), own.dtype)], 0)
        near = lax.dynamic_slice_in_dim(padded, start, rows + 2 * CONT_MOST, 0)
        return jnp.concatenate([every[:PROMPT], near], 0)
    row = lax.axis_index("row")
    across = plan.send(own, [(0, 4), (1, 5), (2, 6), (3, 7)])
    same = jnp.where(row < 4, own, across)
    beside = plan.swap(own, 1)
    diagonal = plan.send(own, [(5, 6), (6, 5)])
    other = plan.swap(same, 2)
    same_y = plan.swap(same, 1)
    other_y = plan.swap(other, 1)
    return jnp.concatenate([same, other, same_y, other_y, own, beside, diagonal], 0)


def near_segments(plan, segments, rows):
    row = lax.axis_index("row")
    if plan.row != 8:
        start = jnp.maximum(row * rows - CONT_MOST, 0)
        padded = jnp.concatenate([segments, jnp.full((CONT_MOST,), -1, jnp.int32)], 0)
        near = lax.dynamic_slice_in_dim(padded, start, rows + 2 * CONT_MOST, 0)
        return jnp.where((near == 0) | (row * rows < PROMPT), -1, near)
    pieces = []
    for block, valid in (
        (row, row >= 4),
        (row ^ 1, row >= 4),
        (11 - row, (row == 5) | (row == 6)),
    ):
        block = jnp.clip(block, 0, 7)
        ids = lax.dynamic_slice_in_dim(segments, block * rows, rows, 0)
        pieces.append(jnp.where(valid, ids, -1))
    return jnp.concatenate(pieces, 0)


def token_return(plan, parts, rows):
    if plan.row != 8:
        row = lax.axis_index("row")
        start = jnp.maximum(row * rows - CONT_MOST, 0)
        whole = jnp.zeros((plan.row * rows + CONT_MOST, parts.shape[1]), F32)
        whole = whole.at[:PROMPT].set(parts[:PROMPT])
        near = lax.dynamic_slice_in_dim(whole, start, rows + 2 * CONT_MOST, 0) + parts[PROMPT:]
        whole = lax.dynamic_update_slice_in_dim(whole, near, start, 0)
        return lax.psum_scatter(whole[: plan.row * rows], "row", scatter_dimension=0, tiled=True)
    row = lax.axis_index("row")
    same, other, same_y, other_y, own, beside, diagonal = [
        parts[i * rows : (i + 1) * rows] for i in range(7)
    ]
    low = lambda v: v.astype(BF)
    wide = lambda v: v.astype(F32)
    other = other + wide(plan.swap(low(other_y), 1))
    same = same + wide(plan.swap(low(same_y), 1))
    own = own + wide(plan.swap(low(beside), 1))
    own = own + wide(plan.send(low(diagonal), [(5, 6), (6, 5)]))
    same = same + wide(plan.swap(low(other), 2))
    back = plan.send(low(same), [(4, 0), (5, 1), (6, 2), (7, 3)])
    return jnp.where(row < 4, same + wide(back), own)


def attend(queries, keys, values, allowed):
    scores = jnp.einsum(
        "qhd,khd->hqk", split_heads(queries), split_heads(keys), preferred_element_type=F32
    )
    scores = jnp.where(allowed[None], scores, MASK_FILL)
    peak = jnp.max(scores, axis=-1, keepdims=True)
    grown = jnp.exp(scores - peak)
    total = jnp.sum(grown, axis=-1, keepdims=True)
    shares = (grown / total).astype(BF)
    mixed = jnp.einsum("hqk,khd->qhd", shares, split_heads(values), preferred_element_type=F32)
    return mixed.reshape(queries.shape).astype(BF), peak + jnp.log(total)


def attend_back(queries, keys, values, allowed, log_total, grad_context):
    hq, hk, hv, hg = [split_heads(v) for v in (queries, keys, values, grad_context)]
    scores = jnp.einsum("qhd,khd->hqk", hq, hk, preferred_element_type=F32)
    scores = jnp.where(allowed[None], scores, MASK_FILL)
    shares = jnp.exp(scores - log_total)
    grad_shares = jnp.einsum("qhd,khd->hqk", hg, hv, preferred_element_type=F32)
    inner = jnp.sum(shares * grad_shares, axis=-1, keepdims=True)
    grad_scores = (shares * (grad_shares - inner)).astype(BF)
    grad_queries = jnp.einsum("hqk,khd->qhd", grad_scores, hk, preferred_element_type=F32)
    grad_keys = jnp.einsum("hqk,qhd->khd", grad_scores, hq, preferred_element_type=F32)
    grad_values = jnp.einsum("hqk,qhd->khd", shares.astype(BF), hg, preferred_element_type=F32)
    return (
        grad_queries.reshape(queries.shape).astype(BF),
        grad_keys.reshape(keys.shape).astype(BF),
        grad_values.reshape(keys.shape).astype(BF),
    )


def solution(mesh):
    plan = Plan(mesh.shape["grp"], mesh.shape["row"])

    def per_device(
        tokens, cont_lengths, cotangent, w_query, w_key, w_value, w_output, w_inner, w_outer,
        bias_query, bias_value, bias_output, gain_first, shift_first, bias_inner, bias_outer,
        gain_second, shift_second,
    ):
        count = plan.count
        _, rows, width = tokens.shape
        step = w_query.shape[0]
        wide = w_inner.shape[1] // width
        row = lax.axis_index("row")
        scale = HDIM ** (-0.5)
        own = tokens[0]

        vectors = (
            bias_query, bias_value, bias_output, gain_first, shift_first, bias_outer, gain_second,
            shift_second, bias_inner,
        )
        line = jnp.concatenate(vectors)
        small = len(vectors) - 1
        line = jnp.pad(line, (0, width - line.shape[0]))[None]
        line = jnp.pad(line, ((0, 7), (0, 0)))
        pack_a = jnp.concatenate([w_query, line], 0)
        pack_b = jnp.concatenate([w_key, w_value], 0)
        got_a = plan.gather(pack_a, plan.orders[0])
        got_b = plan.gather(pack_b, plan.orders[1])
        blocks = token_blocks(plan, own, rows)

        inner_rows = w_inner.reshape(step, wide, width).transpose(1, 0, 2).reshape(-1, width)
        pack_c = jnp.concatenate([w_output, inner_rows, w_outer], 0)
        got_c = lax.all_gather(pack_c, AXES, axis=0, tiled=True).reshape(count, -1, width)

        full_query = got_a[:, :step].reshape(width, width)
        lines = got_a[:, step]
        table = lines[:, : small * step].reshape(count, small, step).transpose(1, 0, 2)
        table = table.reshape(small, width).astype(F32)
        v_bq, v_bv, v_bo, v_g1, v_s1, v_bout, v_g2, v_s2 = [table[i] for i in range(small)]
        v_bin = lines[:, small * step : (small + wide) * step].reshape(-1).astype(F32)
        full_key = got_b[:, :step].reshape(width, width)
        full_value = got_b[:, step : 2 * step].reshape(width, width)

        queries = ((mm(own, full_query) + v_bq) * scale).astype(BF)
        keys = mm(blocks, full_key).astype(BF)
        values = (mm(blocks, full_value) + v_bv).astype(BF)

        segments = segment_ids(cont_lengths[0], plan.row * rows)
        seg_own = lax.dynamic_slice_in_dim(segments, row * rows, rows, 0)
        near = near_segments(plan, segments, rows)
        allowed = jnp.concatenate(
            [
                jnp.ones((rows, PROMPT), jnp.bool_),
                near[None, :] == seg_own[:, None],
            ],
            1,
        )
        context, log_total = attend(queries, keys, values, allowed)

        full_output = got_c[:, :step].reshape(width, width)
        full_inner = got_c[:, step : step * (1 + wide)].reshape(count, wide, step, width)
        full_inner = full_inner.transpose(0, 2, 1, 3).reshape(width, wide * width)
        full_outer = got_c[:, step * (1 + wide) :].reshape(wide * width, width)

        attn_out = mm(context, full_output) + v_bo
        first, normed_one, inverse_one = norm_forward(own.astype(F32) + attn_out, v_g1, v_s1)
        first_low = first.astype(BF)
        pre_act = mm(first_low, full_inner) + v_bin
        activation = jax.nn.gelu(pre_act, approximate=False).astype(BF)
        ffn_out = mm(activation, full_outer) + v_bout
        second, normed_two, inverse_two = norm_forward(first + ffn_out, v_g2, v_s2)
        layer_out = second.astype(BF)

        grad_out = cotangent[0].astype(F32)
        d_gain_second = jnp.sum(grad_out * normed_two, axis=0)
        d_shift_second = jnp.sum(grad_out, axis=0)
        grad_h2 = norm_backward(grad_out, v_g2, normed_two, inverse_two)
        grad_ffn = grad_h2.astype(BF)
        d_bias_outer = jnp.sum(grad_ffn.astype(F32), axis=0)
        d_outer = contract_rows(activation, grad_ffn).astype(BF)
        grad_pre = (contract_last(grad_ffn, full_outer) * gelu_slope(pre_act)).astype(BF)
        d_bias_inner = jnp.sum(grad_pre.astype(F32), axis=0)
        d_inner = contract_rows(first_low, grad_pre).astype(BF)
        grad_first = grad_h2 + contract_last(grad_pre, full_inner)
        d_gain_first = jnp.sum(grad_first * normed_one, axis=0)
        d_shift_first = jnp.sum(grad_first, axis=0)
        grad_h1 = norm_backward(grad_first, v_g1, normed_one, inverse_one)
        grad_attn = grad_h1.astype(BF)
        d_bias_output = jnp.sum(grad_attn.astype(F32), axis=0)
        d_output = contract_rows(context, grad_attn).astype(BF)
        grad_context = contract_last(grad_attn, full_output).astype(BF)

        def scatter(pieces):
            whole = jnp.concatenate(pieces, 1)
            depth = whole.shape[1]
            flat = whole.reshape(count * depth, width)
            return lax.psum_scatter(flat, AXES, scatter_dimension=0, tiled=True).astype(F32)

        by_owner = lambda grad: grad.reshape(count, step, width)
        sums_c = scatter(
            [
                by_owner(d_output),
                d_inner.reshape(count, step, wide, width)
                .transpose(0, 2, 1, 3)
                .reshape(count, wide * step, width),
                d_outer.reshape(count, wide * step, width),
            ]
        )

        grad_queries, grad_keys, grad_values = attend_back(
            queries, keys, values, allowed, log_total, grad_context
        )
        d_query = (contract_rows(own, grad_queries) * scale).astype(BF)
        d_bias_query = jnp.sum(grad_queries.astype(F32), axis=0) * scale
        d_key = contract_rows(blocks, grad_keys).astype(BF)
        d_value = contract_rows(blocks, grad_values).astype(BF)
        d_bias_value = jnp.sum(grad_values.astype(F32), axis=0)
        shared = contract_last(grad_keys, full_key) + contract_last(grad_values, full_value)
        returned = token_return(plan, shared, rows)
        grad_tokens = grad_h1 + contract_last(grad_queries, full_query) * scale + returned

        d_table = jnp.stack(
            [d_bias_query, d_bias_value, d_bias_output, d_gain_first, d_shift_first, d_bias_outer,
             d_gain_second, d_shift_second]
        )
        d_lines = jnp.concatenate(
            [
                d_table.reshape(small, count, step).transpose(1, 0, 2).reshape(count, -1),
                d_bias_inner.reshape(count, wide * step),
            ],
            1,
        )
        d_lines = jnp.pad(d_lines, ((0, 0), (0, width - d_lines.shape[1]))).astype(BF)
        d_lines = jnp.pad(d_lines[:, None], ((0, 0), (0, 7), (0, 0)))
        sums_a = scatter([by_owner(d_query), by_owner(d_key), by_owner(d_value), d_lines])

        o_line = sums_a[3 * step]
        o_small = [o_line[i * step : (i + 1) * step] for i in range(small)]
        o_bin = o_line[small * step : (small + wide) * step]
        o_inner = sums_c[step : step * (1 + wide)].reshape(wide, step, width)
        o_inner = o_inner.transpose(1, 0, 2).reshape(step, wide * width)
        return (
            layer_out[None],
            grad_tokens.astype(BF)[None],
            sums_a[:step],
            sums_a[step : 2 * step],
            sums_a[2 * step : 3 * step],
            sums_c[:step],
            o_inner,
            sums_c[step * (1 + wide) :],
            o_small[0],
            o_small[1],
            o_small[2],
            o_small[3],
            o_small[4],
            o_bin,
            o_small[5],
            o_small[6],
            o_small[7],
        )

    split = P("grp", "row", None)
    owned2, owned1 = P(AXES, None), P(AXES)
    in_specs = (split, P("grp", None), split) + (owned2,) * 6 + (owned1,) * 9
    out_specs = (split, split) + (owned2,) * 6 + (owned1,) * 9
    return jax.shard_map(
        per_device, mesh=mesh, in_specs=in_specs, out_specs=out_specs, check_vma=False
    )
```

```python
import jax
import jax.numpy as jnp
import numpy as np
from jax import lax
from jax.sharding import PartitionSpec as P

HEADS = 12
HDIM = 64
PROMPT = 1024
CONT_MOST = 256
BF = jnp.bfloat16
F32 = jnp.float32

NORM_EPS = 1e-12
MASK_FILL = -1000000000.0
SQRT_HALF = 0.7071067811865476
INV_ROOT_TAU = 0.3989422804014327
AXES = ("grp", "row")


def mm(left, right):
    return jnp.dot(left, right, preferred_element_type=F32)


def contract_last(left, right):
    return lax.dot_general(left, right, (((1,), (1,)), ((), ())), preferred_element_type=F32)


def contract_rows(left, right):
    return lax.dot_general(left, right, (((0,), (0,)), ((), ())), preferred_element_type=F32)


def segment_ids(lengths, group_len):
    ends = jnp.cumsum(lengths)
    places = jnp.arange(group_len, dtype=jnp.int32)
    passed = jnp.sum(((places - PROMPT)[:, None] >= ends[None, :]).astype(jnp.int32), axis=-1)
    return jnp.where(places < PROMPT, 0, 1 + passed)


def norm_forward(hidden, gain, shift):
    average = jnp.mean(hidden, axis=-1, keepdims=True)
    centred = hidden - average
    inverse = lax.rsqrt(jnp.mean(centred * centred, axis=-1, keepdims=True) + NORM_EPS)
    normed = centred * inverse
    return normed * gain + shift, normed, inverse


def norm_backward(grad_out, gain, normed, inverse):
    grad_norm = grad_out * gain
    one = jnp.mean(grad_norm, axis=-1, keepdims=True)
    two = jnp.mean(grad_norm * normed, axis=-1, keepdims=True)
    return inverse * (grad_norm - one - normed * two)


def gelu_slope(pre_act):
    cumulative = 0.5 * (1.0 + jax.scipy.special.erf(pre_act * SQRT_HALF))
    return cumulative + pre_act * jnp.exp(-0.5 * pre_act * pre_act) * INV_ROOT_TAU


def split_heads(rows_in):
    return rows_in.reshape(rows_in.shape[0], HEADS, HDIM)


class Plan:
    def __init__(self, grp, row):
        self.grp, self.row, self.count = grp, row, grp * row
        self.y = row // 4
        bits = lambda base, size: [base << i for i in range(size.bit_length() - 1)]
        ys, zs = bits(1, self.y), bits(self.y, 4)
        core, xs = bits(row, 2), bits(2 * row, grp // 2)
        self.orders = (tuple(zs + ys + xs + core), tuple(zs + xs + ys + core))
        flat = [ys + xs] if len(ys + xs) == 2 else [ys, xs]
        self.scatter_stages = [core] + flat + [zs]
        self.bits = (grp * row).bit_length() - 1

    def swap(self, value, mask):
        return lax.ppermute(value, AXES, [(i, i ^ mask) for i in range(self.count)])

    def send(self, value, moves):
        pairs = [(g * self.row + a, g * self.row + b) for g in range(self.grp) for a, b in moves]
        return lax.ppermute(value, AXES, pairs)

    def me(self):
        return lax.axis_index("grp") * self.row + lax.axis_index("row")

    def gather(self, value, order):
        held, masks = value[None], [0]
        for bit in order:
            held = jnp.concatenate([held, self.swap(held, bit)], 0)
            masks = masks + [m ^ bit for m in masks]
        slot = np.zeros(self.count, np.int32)
        for j, m in enumerate(masks):
            slot[m] = j
        places = jnp.asarray(slot)[self.me() ^ jnp.arange(self.count)]
        return jnp.take(held, places, axis=0, mode="clip")


    def scatter(self, value):
        me = self.me()
        rest = value.shape[1:]
        left = [1 << i for i in reversed(range(self.bits))]
        value = value.astype(BF).reshape([2] * self.bits + list(rest))
        for stage in self.scatter_stages:

            def part(array, mask):
                for bit in stage:
                    axis = at.index(bit)
                    place = ((me ^ mask) // bit) & 1
                    array = lax.dynamic_slice_in_dim(array, place, 1, axis)
                return array

            at = left
            masks = [0]
            for bit in stage:
                masks = masks + [m ^ bit for m in masks]
            total = part(value, 0).astype(F32)
            for mask in masks[1:]:
                total = total + self.swap(part(value, mask), mask).astype(F32)
            left = [b for b in left if b not in stage]
            shape = [2] * len(left) + list(rest)
            value = total.reshape(shape)
            if left:
                value = value.astype(BF)
        return value


def token_blocks(plan, own, rows):
    if plan.row != 8:
        every = lax.all_gather(own, "row", axis=0, tiled=True)
        start = jnp.maximum(lax.axis_index("row") * rows - CONT_MOST, 0)
        padded = jnp.concatenate([every, jnp.zeros((CONT_MOST, own.shape[1]), own.dtype)], 0)
        near = lax.dynamic_slice_in_dim(padded, start, rows + 2 * CONT_MOST, 0)
        return jnp.concatenate([every[:PROMPT], near], 0)
    row = lax.axis_index("row")
    across = plan.send(own, [(0, 4), (1, 5), (2, 6), (3, 7)])
    same = jnp.where(row < 4, own, across)
    beside = plan.swap(own, 1)
    diagonal = plan.send(own, [(5, 6), (6, 5)])
    other = plan.swap(same, 2)
    same_y = plan.swap(same, 1)
    other_y = plan.swap(other, 1)
    return jnp.concatenate([same, other, same_y, other_y, own, beside, diagonal], 0)


def near_segments(plan, segments, rows):
    row = lax.axis_index("row")
    if plan.row != 8:
        start = jnp.maximum(row * rows - CONT_MOST, 0)
        padded = jnp.concatenate([segments, jnp.full((CONT_MOST,), -1, jnp.int32)], 0)
        near = lax.dynamic_slice_in_dim(padded, start, rows + 2 * CONT_MOST, 0)
        return jnp.where((near == 0) | (row * rows < PROMPT), -1, near)
    pieces = []
    for block, valid in (
        (row, row >= 4),
        (row ^ 1, row >= 4),
        (11 - row, (row == 5) | (row == 6)),
    ):
        block = jnp.clip(block, 0, 7)
        ids = lax.dynamic_slice_in_dim(segments, block * rows, rows, 0)
        pieces.append(jnp.where(valid, ids, -1))
    return jnp.concatenate(pieces, 0)


def token_return(plan, parts, rows):
    if plan.row != 8:
        row = lax.axis_index("row")
        start = jnp.maximum(row * rows - CONT_MOST, 0)
        whole = jnp.zeros((plan.row * rows + CONT_MOST, parts.shape[1]), F32)
        whole = whole.at[:PROMPT].set(parts[:PROMPT])
        near = lax.dynamic_slice_in_dim(whole, start, rows + 2 * CONT_MOST, 0) + parts[PROMPT:]
        whole = lax.dynamic_update_slice_in_dim(whole, near, start, 0)
        return lax.psum_scatter(whole[: plan.row * rows], "row", scatter_dimension=0, tiled=True)
    row = lax.axis_index("row")
    same, other, same_y, other_y, own, beside, diagonal = [
        parts[i * rows : (i + 1) * rows] for i in range(7)
    ]
    low = lambda v: v.astype(BF)
    wide = lambda v: v.astype(F32)
    other = other + wide(plan.swap(low(other_y), 1))
    same = same + wide(plan.swap(low(same_y), 1))
    own = own + wide(plan.swap(low(beside), 1))
    own = own + wide(plan.send(low(diagonal), [(5, 6), (6, 5)]))
    same = same + wide(plan.swap(low(other), 2))
    back = plan.send(low(same), [(4, 0), (5, 1), (6, 2), (7, 3)])
    return jnp.where(row < 4, same + wide(back), own)


def attend(queries, keys, values, allowed):
    scores = jnp.einsum(
        "qhd,khd->hqk", split_heads(queries), split_heads(keys), preferred_element_type=F32
    )
    scores = jnp.where(allowed[None], scores, MASK_FILL)
    peak = jnp.max(scores, axis=-1, keepdims=True)
    grown = jnp.exp(scores - peak)
    total = jnp.sum(grown, axis=-1, keepdims=True)
    shares = (grown / total).astype(BF)
    mixed = jnp.einsum("hqk,khd->qhd", shares, split_heads(values), preferred_element_type=F32)
    return mixed.reshape(queries.shape).astype(BF), peak + jnp.log(total)


def attend_back(queries, keys, values, allowed, log_total, grad_context):
    hq, hk, hv, hg = [split_heads(v) for v in (queries, keys, values, grad_context)]
    scores = jnp.einsum("qhd,khd->hqk", hq, hk, preferred_element_type=F32)
    scores = jnp.where(allowed[None], scores, MASK_FILL)
    shares = jnp.exp(scores - log_total)
    grad_shares = jnp.einsum("qhd,khd->hqk", hg, hv, preferred_element_type=F32)
    inner = jnp.sum(shares * grad_shares, axis=-1, keepdims=True)
    grad_scores = (shares * (grad_shares - inner)).astype(BF)
    grad_queries = jnp.einsum("hqk,khd->qhd", grad_scores, hk, preferred_element_type=F32)
    grad_keys = jnp.einsum("hqk,qhd->khd", grad_scores, hq, preferred_element_type=F32)
    grad_values = jnp.einsum("hqk,qhd->khd", shares.astype(BF), hg, preferred_element_type=F32)
    return (
        grad_queries.reshape(queries.shape).astype(BF),
        grad_keys.reshape(keys.shape).astype(BF),
        grad_values.reshape(keys.shape).astype(BF),
    )


def solution(mesh):
    plan = Plan(mesh.shape["grp"], mesh.shape["row"])

    def per_device(
        tokens, cont_lengths, cotangent, w_query, w_key, w_value, w_output, w_inner, w_outer,
        bias_query, bias_value, bias_output, gain_first, shift_first, bias_inner, bias_outer,
        gain_second, shift_second,
    ):
        count = plan.count
        _, rows, width = tokens.shape
        step = w_query.shape[0]
        wide = w_inner.shape[1] // width
        row = lax.axis_index("row")
        scale = HDIM ** (-0.5)
        own = tokens[0]

        vectors = (
            bias_query, bias_value, bias_output, gain_first, shift_first, bias_outer, gain_second,
            shift_second, bias_inner,
        )
        line = jnp.concatenate(vectors)
        small = len(vectors) - 1
        line = jnp.pad(line, (0, width - line.shape[0]))[None]
        line = jnp.pad(line, ((0, 7), (0, 0)))
        pack_a = jnp.concatenate([w_query, line], 0)
        pack_b = jnp.concatenate([w_key, w_value], 0)
        got_a = plan.gather(pack_a, plan.orders[0])
        got_b = plan.gather(pack_b, plan.orders[1])
        blocks = token_blocks(plan, own, rows)

        inner_rows = w_inner.reshape(step, wide, width).transpose(1, 0, 2).reshape(-1, width)
        pack_c = jnp.concatenate([w_output, inner_rows, w_outer], 0)
        got_c = lax.all_gather(pack_c, AXES, axis=0, tiled=True).reshape(count, -1, width)

        full_query = got_a[:, :step].reshape(width, width)
        lines = got_a[:, step]
        table = lines[:, : small * step].reshape(count, small, step).transpose(1, 0, 2)
        table = table.reshape(small, width).astype(F32)
        v_bq, v_bv, v_bo, v_g1, v_s1, v_bout, v_g2, v_s2 = [table[i] for i in range(small)]
        v_bin = lines[:, small * step : (small + wide) * step].reshape(-1).astype(F32)
        full_key = got_b[:, :step].reshape(width, width)
        full_value = got_b[:, step : 2 * step].reshape(width, width)

        queries = ((mm(own, full_query) + v_bq) * scale).astype(BF)
        keys = mm(blocks, full_key).astype(BF)
        values = (mm(blocks, full_value) + v_bv).astype(BF)

        segments = segment_ids(cont_lengths[0], plan.row * rows)
        seg_own = lax.dynamic_slice_in_dim(segments, row * rows, rows, 0)
        near = near_segments(plan, segments, rows)
        allowed = jnp.concatenate(
            [
                jnp.ones((rows, PROMPT), jnp.bool_),
                near[None, :] == seg_own[:, None],
            ],
            1,
        )
        context, log_total = attend(queries, keys, values, allowed)

        full_output = got_c[:, :step].reshape(width, width)
        full_inner = got_c[:, step : step * (1 + wide)].reshape(count, wide, step, width)
        full_inner = full_inner.transpose(0, 2, 1, 3).reshape(width, wide * width)
        full_outer = got_c[:, step * (1 + wide) :].reshape(wide * width, width)

        attn_out = mm(context, full_output) + v_bo
        first, normed_one, inverse_one = norm_forward(own.astype(F32) + attn_out, v_g1, v_s1)
        first_low = first.astype(BF)
        pre_act = mm(first_low, full_inner) + v_bin
        activation = jax.nn.gelu(pre_act, approximate=False).astype(BF)
        ffn_out = mm(activation, full_outer) + v_bout
        second, normed_two, inverse_two = norm_forward(first + ffn_out, v_g2, v_s2)
        layer_out = second.astype(BF)

        grad_out = cotangent[0].astype(F32)
        d_gain_second = jnp.sum(grad_out * normed_two, axis=0)
        d_shift_second = jnp.sum(grad_out, axis=0)
        grad_h2 = norm_backward(grad_out, v_g2, normed_two, inverse_two)
        grad_ffn = grad_h2.astype(BF)
        d_bias_outer = jnp.sum(grad_ffn.astype(F32), axis=0)
        d_outer = contract_rows(activation, grad_ffn).astype(BF)
        grad_pre = (contract_last(grad_ffn, full_outer) * gelu_slope(pre_act)).astype(BF)
        d_bias_inner = jnp.sum(grad_pre.astype(F32), axis=0)
        d_inner = contract_rows(first_low, grad_pre).astype(BF)
        grad_first = grad_h2 + contract_last(grad_pre, full_inner)
        d_gain_first = jnp.sum(grad_first * normed_one, axis=0)
        d_shift_first = jnp.sum(grad_first, axis=0)
        grad_h1 = norm_backward(grad_first, v_g1, normed_one, inverse_one)
        grad_attn = grad_h1.astype(BF)
        d_bias_output = jnp.sum(grad_attn.astype(F32), axis=0)
        d_output = contract_rows(context, grad_attn).astype(BF)
        grad_context = contract_last(grad_attn, full_output).astype(BF)

        by_owner = lambda grad: grad.reshape(count, step, -1)
        o_outer = plan.scatter(d_outer.reshape(count, wide * step, width))
        o_inner = plan.scatter(by_owner(d_inner))
        o_output = plan.scatter(by_owner(d_output))

        grad_queries, grad_keys, grad_values = attend_back(
            queries, keys, values, allowed, log_total, grad_context
        )
        d_query = (contract_rows(own, grad_queries) * scale).astype(BF)
        d_bias_query = jnp.sum(grad_queries.astype(F32), axis=0) * scale
        both = jnp.concatenate([grad_keys, grad_values], 1)
        d_both = contract_rows(blocks, both).astype(BF)
        d_bias_value = jnp.sum(grad_values.astype(F32), axis=0)
        shared = contract_last(grad_keys, full_key) + contract_last(grad_values, full_value)
        returned = token_return(plan, shared, rows)
        grad_tokens = grad_h1 + contract_last(grad_queries, full_query) * scale + returned

        d_table = jnp.stack(
            [d_bias_query, d_bias_value, d_bias_output, d_gain_first, d_shift_first, d_bias_outer,
             d_gain_second, d_shift_second]
        )
        d_lines = jnp.concatenate(
            [
                d_table.reshape(small, count, step).transpose(1, 0, 2).reshape(count, -1),
                d_bias_inner.reshape(count, wide * step),
            ],
            1,
        )
        d_lines = jnp.pad(d_lines, ((0, 0), (0, width - d_lines.shape[1]))).astype(BF)
        d_lines = jnp.pad(d_lines[:, None], ((0, 0), (0, 7), (0, 0)))
        o_query = plan.scatter(jnp.concatenate([by_owner(d_query), d_lines], 1))
        o_both = plan.scatter(by_owner(d_both))

        o_line = o_query[step]
        o_small = [o_line[i * step : (i + 1) * step] for i in range(small)]
        o_bin = o_line[small * step : (small + wide) * step]
        return (
            layer_out[None],
            grad_tokens.astype(BF)[None],
            o_query[:step],
            o_both[:, :width],
            o_both[:, width:],
            o_output,
            o_inner,
            o_outer,
            o_small[0],
            o_small[1],
            o_small[2],
            o_small[3],
            o_small[4],
            o_bin,
            o_small[5],
            o_small[6],
            o_small[7],
        )

    split = P("grp", "row", None)
    owned2, owned1 = P(AXES, None), P(AXES)
    in_specs = (split, P("grp", None), split) + (owned2,) * 6 + (owned1,) * 9
    out_specs = (split, split) + (owned2,) * 6 + (owned1,) * 9
    return jax.shard_map(
        per_device, mesh=mesh, in_specs=in_specs, out_specs=out_specs, check_vma=False
    )
```

```python
import functools

import jax
import jax.numpy as jnp
import numpy as np
from jax import lax
from jax.experimental import pallas as pl
from jax.experimental.pallas import tpu as pltpu
from jax.sharding import PartitionSpec as P

HEADS = 12
HDIM = 64
PROMPT = 1024
CONT_MOST = 256
BF = jnp.bfloat16
F32 = jnp.float32

NORM_EPS = 1e-12
MASK_FILL = -1000000000.0
SQRT_HALF = 0.7071067811865476
INV_ROOT_TAU = 0.3989422804014327
AXES = ("grp", "row")


def mm(left, right):
    return jnp.dot(left, right, preferred_element_type=F32)


def segment_ids(lengths, group_len):
    ends = jnp.cumsum(lengths)
    places = jnp.arange(group_len, dtype=jnp.int32)
    passed = jnp.sum(((places - PROMPT)[:, None] >= ends[None, :]).astype(jnp.int32), axis=-1)
    return jnp.where(places < PROMPT, 0, 1 + passed)


class Plan:
    def __init__(self, grp, row):
        self.grp, self.row, self.count = grp, row, grp * row
        self.y = row // 4
        bits = lambda base, size: [base << i for i in range(size.bit_length() - 1)]
        ys, zs = bits(1, self.y), bits(self.y, 4)
        core, xs = bits(row, 2), bits(2 * row, grp // 2)
        self.orders = (tuple(zs + ys + xs + core), tuple(zs + xs + ys + core))
        flat = [ys + xs] if len(ys + xs) == 2 else [ys, xs]
        self.scatter_stages = [core] + flat + [zs]
        self.bits = (grp * row).bit_length() - 1

    def swap(self, value, mask):
        return lax.ppermute(value, AXES, [(i, i ^ mask) for i in range(self.count)])

    def send(self, value, moves):
        pairs = [(g * self.row + a, g * self.row + b) for g in range(self.grp) for a, b in moves]
        return lax.ppermute(value, AXES, pairs)

    def me(self):
        return lax.axis_index("grp") * self.row + lax.axis_index("row")

    def gather(self, value, order):
        held, masks = value[None], [0]
        for bit in order:
            held = jnp.concatenate([held, self.swap(held, bit)], 0)
            masks = masks + [m ^ bit for m in masks]
        slot = np.zeros(self.count, np.int32)
        for j, m in enumerate(masks):
            slot[m] = j
        places = jnp.asarray(slot)[self.me() ^ jnp.arange(self.count)]
        return jnp.take(held, places, axis=0, mode="clip")


    def scatter(self, value, before=0):
        me = self.me()
        lead, rest = value.shape[:before], value.shape[before + 1 :]
        left = [1 << i for i in reversed(range(self.bits))]
        value = value.astype(BF).reshape(list(lead) + [2] * self.bits + list(rest))
        for stage in self.scatter_stages:

            def part(array, mask):
                for bit in stage:
                    axis = before + at.index(bit)
                    place = ((me ^ mask) // bit) & 1
                    array = lax.dynamic_slice_in_dim(array, place, 1, axis)
                return array

            at = left
            masks = [0]
            for bit in stage:
                masks = masks + [m ^ bit for m in masks]
            total = part(value, 0).astype(F32)
            for mask in masks[1:]:
                total = total + self.swap(part(value, mask), mask).astype(F32)
            left = [b for b in left if b not in stage]
            shape = list(lead) + [2] * len(left) + list(rest)
            value = total.reshape(shape)
            if left:
                value = value.astype(BF)
        return value


def token_blocks(plan, own, rows):
    row = lax.axis_index("row")
    if plan.row != 8:
        every = lax.all_gather(own, "row", axis=0, tiled=True)
        start = jnp.maximum(row * rows - CONT_MOST, 0)
        padded = jnp.concatenate([every, jnp.zeros((CONT_MOST, own.shape[1]), own.dtype)], 0)
        near = lax.dynamic_slice_in_dim(padded, start, rows + 2 * CONT_MOST, 0)
        every = jnp.concatenate([every[:PROMPT], near], 0)
        spots = [every[i : i + rows] for i in range(0, every.shape[0], rows)]
        return spots, jnp.where(row * rows < PROMPT, 0, near.shape[0] // rows)
    across = plan.send(own, [(0, 4), (1, 5), (2, 6), (3, 7)])
    same = jnp.where(row < 4, own, across)
    beside = plan.swap(own, 1)
    diagonal = plan.send(own, [(5, 6), (6, 5)])
    other = plan.swap(same, 2)
    same_y = plan.swap(same, 1)
    other_y = plan.swap(other, 1)
    near = jnp.where(row < 4, 0, jnp.where((row == 5) | (row == 6), 3, 2))
    return [same, other, same_y, other_y, own, beside, diagonal], near


def near_segments(plan, segments, rows):
    row = lax.axis_index("row")
    if plan.row != 8:
        start = jnp.maximum(row * rows - CONT_MOST, 0)
        padded = jnp.concatenate([segments, jnp.full((CONT_MOST,), -1, jnp.int32)], 0)
        near = lax.dynamic_slice_in_dim(padded, start, rows + 2 * CONT_MOST, 0)
        return jnp.where((near == 0) | (row * rows < PROMPT), -1, near)
    pieces = []
    for block, valid in (
        (row, row >= 4),
        (row ^ 1, row >= 4),
        (11 - row, (row == 5) | (row == 6)),
    ):
        block = jnp.clip(block, 0, 7)
        ids = lax.dynamic_slice_in_dim(segments, block * rows, rows, 0)
        pieces.append(jnp.where(valid, ids, -1))
    return jnp.concatenate(pieces, 0)


def token_return(plan, parts, rows):
    row = lax.axis_index("row")
    if plan.row != 8:
        parts = parts.reshape(-1, parts.shape[-1]).astype(F32)
        start = jnp.maximum(row * rows - CONT_MOST, 0)
        whole = jnp.zeros((plan.row * rows + CONT_MOST, parts.shape[1]), F32)
        whole = whole.at[:PROMPT].set(parts[:PROMPT])
        near = jnp.where(row * rows < PROMPT, 0, parts[PROMPT:])
        near = lax.dynamic_slice_in_dim(whole, start, rows + 2 * CONT_MOST, 0) + near
        whole = lax.dynamic_update_slice_in_dim(whole, near, start, 0)
        return lax.psum_scatter(whole[: plan.row * rows], "row", scatter_dimension=0, tiled=True)
    same, other, same_y, other_y, own, beside, diagonal = [parts[i] for i in range(7)]
    low = lambda v: v.astype(BF)
    wide = lambda v: v.astype(F32)
    other = wide(other) + wide(plan.swap(other_y, 1))
    same = wide(same) + wide(plan.swap(same_y, 1))
    own = wide(own) + wide(plan.swap(beside, 1))
    own = own + wide(plan.send(diagonal, [(5, 6), (6, 5)]))
    same = same + wide(plan.swap(low(other), 2))
    back = plan.send(low(same), [(4, 0), (5, 1), (6, 2), (7, 3)])
    return jnp.where(row < 4, same + wide(back), own)


def heads_mask(lanes, head):
    lane = lax.broadcasted_iota(jnp.int32, lanes, 1)
    return (lane >= head * HDIM) & (lane < (head + 1) * HDIM)


def nt(left, right):
    return lax.dot_general(left, right, (((1,), (1,)), ((), ())), preferred_element_type=F32)


def tn(left, right):
    return lax.dot_general(left, right, (((0,), (0,)), ((), ())), preferred_element_type=F32)


def attention_kernel(blocks, first, rows, *refs):
    spots = refs[:blocks]
    (near_ref, own_ref, wq_ref, wk_ref, wv_ref, bq_ref, bv_ref, segq_ref, segk_ref,
     q_ref, k_ref, v_ref, ctx_ref, lse_ref, x_ref, s_ref, sems) = refs[blocks:]
    near = near_ref[0]

    @pl.when(pl.program_id(0) == 0)
    def _():
        copies = [
            pltpu.make_async_copy(spot, x_ref.at[pl.ds(i * rows, rows)], sems.at[i])
            for i, spot in enumerate(spots)
        ]
        for copy in copies:
            copy.start()
        for copy in copies:
            copy.wait()

    queries = (mm(own_ref[...], wq_ref[...]) + bq_ref[...]) * (HDIM**-0.5)
    q_ref[...] = queries.astype(BF)

    @pl.loop(0, first + near)
    def _(b):
        here = pl.ds(pl.multiple_of(b * rows, rows), rows)
        x = x_ref[here, :]
        k_ref[here, :] = mm(x, wk_ref[...]).astype(BF)
        v_ref[here, :] = (mm(x, wv_ref[...]) + bv_ref[...]).astype(BF)

    width = q_ref.shape[1]
    heads = width // HDIM
    q = q_ref[...]
    parts = [jnp.where(heads_mask(q.shape, h), q, 0) for h in range(heads)]

    def scores(b, peaks, masked):
        here = pl.ds(pl.multiple_of(b * rows, rows), rows)
        k = k_ref[here, :]
        out = []
        for h in range(heads):
            s = nt(k, parts[h])
            if masked:
                side = pl.ds(pl.multiple_of((b - first) * rows, rows), rows)
                s = jnp.where(segk_ref[side, :] == segq_ref[...], s, MASK_FILL)
            s_ref[h, here, :] = s
            out.append(jnp.maximum(peaks[h], jnp.max(s, axis=0, keepdims=True)))
        return tuple(out)

    peaks = tuple(jnp.full((1, rows), MASK_FILL, F32) for _ in range(heads))
    peaks = lax.fori_loop(0, first, lambda b, c: scores(b, c, False), peaks)
    peaks = lax.fori_loop(first, first + near, lambda b, c: scores(b, c, True), peaks)

    def mix(b, carry):
        totals, mixed = carry
        here = pl.ds(pl.multiple_of(b * rows, rows), rows)
        vt = v_ref[here, :].T
        new_totals, new_mixed = [], []
        for h in range(heads):
            p = jnp.exp(s_ref[h, here, :] - peaks[h])
            new_totals.append(totals[h] + jnp.sum(p, axis=0, keepdims=True))
            new_mixed.append(mixed[h] + mm(vt[h * HDIM : (h + 1) * HDIM], p.astype(BF)))
        return tuple(new_totals), tuple(new_mixed)

    zero = (
        tuple(jnp.zeros((1, rows), F32) for _ in range(heads)),
        tuple(jnp.zeros((HDIM, rows), F32) for _ in range(heads)),
    )
    totals, mixed = lax.fori_loop(0, first + near, mix, zero)
    whole = jnp.concatenate([mixed[h] / totals[h] for h in range(heads)], 0)
    ctx_ref[...] = whole.T.astype(BF)
    for h in range(heads):
        lse_ref[0, h : h + 1, :] = peaks[h] + jnp.log(totals[h])


def attention_call(spots, first, near, own, wq, wk, wv, bq, bv, segq, segk):
    rows, width = own.shape
    blocks = len(spots)
    tall = blocks * rows
    part = 256
    steps = width // part
    heads = part // HDIM
    cols = lambda depth: pl.BlockSpec((depth, part), lambda g: (0, g))
    flops = 2 * tall * width * width * 2 + 4 * tall * rows * width * 4
    return pl.pallas_call(
        functools.partial(attention_kernel, blocks, first, rows),
        grid=(steps,),
        in_specs=[pl.BlockSpec(memory_space=pl.ANY)] * blocks
        + [
            pl.BlockSpec(memory_space=pltpu.SMEM),
            pl.BlockSpec((rows, width), lambda g: (0, 0)),
            cols(width), cols(width), cols(width), cols(1), cols(1),
            pl.BlockSpec((1, rows), lambda g: (0, 0)),
            pl.BlockSpec(segk.shape, lambda g: (0, 0)),
        ],
        out_specs=[
            cols(rows), cols(tall), cols(tall), cols(rows),
            pl.BlockSpec((1, 8, rows), lambda g: (g, 0, 0)),
        ],
        out_shape=[
            jax.ShapeDtypeStruct((rows, width), BF),
            jax.ShapeDtypeStruct((tall, width), BF),
            jax.ShapeDtypeStruct((tall, width), BF),
            jax.ShapeDtypeStruct((rows, width), BF),
            jax.ShapeDtypeStruct((steps, 8, rows), F32),
        ],
        scratch_shapes=[
            pltpu.VMEM((tall, width), BF),
            pltpu.VMEM((heads, tall, rows), F32),
            pltpu.SemaphoreType.DMA((blocks,)),
        ],
        compiler_params=pltpu.CompilerParams(vmem_limit_bytes=60 * 2**20),
        cost_estimate=pl.CostEstimate(
            flops=flops, bytes_accessed=12 * 2**20, transcendentals=tall * rows * 12
        ),
        name="attention",
    )(*spots, near, own, wq, wk, wv, bq, bv, segq, segk)


def middle_kernel(wide, ctx_ref, own_ref, cot_ref, wo_ref, wi_ref, wu_ref, vec_ref, bin_ref,
                  out_ref, h1_ref, gctx_ref, dwo_ref, dwi_ref, dwu_ref, sums_ref, sbin_ref,
                  first_ref, n1_ref, inv_ref, low_ref, pre_ref, cdf_ref, act_ref, acc_ref,
                  gffn_ref, glow_ref):
    step = pl.program_id(0)
    width = ctx_ref.shape[1]
    vec = lambda i: vec_ref[i : i + 1, :]
    mean = lambda v: jnp.sum(v, axis=-1, keepdims=True) * (1.0 / width)
    down = lambda v: jnp.sum(v, axis=0, keepdims=True)

    @pl.when(step == 0)
    def _():
        hidden = own_ref[...].astype(F32) + mm(ctx_ref[...], wo_ref[...]) + vec(0)
        centred = hidden - mean(hidden)
        inverse = lax.rsqrt(mean(centred * centred) + NORM_EPS)
        normed = centred * inverse
        n1_ref[...] = normed
        inv_ref[...] = inverse
        first = normed * vec(1) + vec(2)
        first_ref[...] = first
        low_ref[...] = first.astype(BF)

    @pl.when(step < wide)
    def _():
        chunk = pl.ds(pl.multiple_of(step * width, width), width)
        pre = mm(low_ref[...], wi_ref[0]) + bin_ref[pl.ds(step, 1), :]
        cdf = 0.5 * (1.0 + lax.erf(pre * SQRT_HALF))
        act = (pre * cdf).astype(BF)
        pre_ref[:, chunk] = pre
        cdf_ref[:, chunk] = cdf
        act_ref[:, chunk] = act
        more = mm(act, wu_ref[...])

        @pl.when(step == 0)
        def _():
            acc_ref[...] = more

        @pl.when(step > 0)
        def _():
            acc_ref[...] += more

    @pl.when(step == wide - 1)
    def _():
        hidden = first_ref[...] + acc_ref[...] + vec(3)
        centred = hidden - mean(hidden)
        inverse = lax.rsqrt(mean(centred * centred) + NORM_EPS)
        normed = centred * inverse
        out_ref[...] = (normed * vec(4) + vec(5)).astype(BF)
        grad = cot_ref[...].astype(F32)
        sums_ref[0:1, :] = down(grad * normed)
        sums_ref[1:2, :] = down(grad)
        e = grad * vec(4)
        back = inverse * (e - mean(e) - normed * mean(e * normed))
        gffn_ref[...] = back
        low = back.astype(BF)
        glow_ref[...] = low
        sums_ref[2:3, :] = down(low.astype(F32))

    @pl.when(step >= wide)
    def _():
        at = 2 * wide - 1 - step
        chunk = pl.ds(pl.multiple_of(at * width, width), width)
        pre = pre_ref[:, chunk]
        slope = cdf_ref[:, chunk] + pre * jnp.exp(-0.5 * pre * pre) * INV_ROOT_TAU
        low = glow_ref[...]
        grad = (nt(low, wu_ref[...]) * slope).astype(BF)
        sbin_ref[pl.ds(at, 1), :] = down(grad.astype(F32))
        dwu_ref[...] = tn(act_ref[:, chunk], low).astype(BF)
        dwi_ref[0] = tn(low_ref[...], grad).astype(BF)
        gffn_ref[...] += nt(grad, wi_ref[0])

    @pl.when(step == 2 * wide - 1)
    def _():
        grad = gffn_ref[...]
        normed = n1_ref[...]
        sums_ref[3:4, :] = down(grad * normed)
        sums_ref[4:5, :] = down(grad)
        e = grad * vec(1)
        back = inv_ref[...] * (e - mean(e) - normed * mean(e * normed))
        h1_ref[...] = back
        low = back.astype(BF)
        sums_ref[5:6, :] = down(low.astype(F32))
        sums_ref[6:8, :] = jnp.zeros((2, width), F32)
        dwo_ref[...] = tn(ctx_ref[...], low).astype(BF)
        gctx_ref[...] = nt(low, wo_ref[...]).astype(BF)


def middle_call(ctx, own, cot, wo, wi, wu, vec, b_inner):
    rows, width = own.shape
    wide = wi.shape[0]
    whole = lambda shape: pl.BlockSpec(shape, lambda s: (0,) * len(shape))
    at = lambda s: jnp.where(s < wide, s, 2 * wide - 1 - s)
    back = lambda s: jnp.where(s < wide, wide - 1, 2 * wide - 1 - s)
    shape = jax.ShapeDtypeStruct
    return pl.pallas_call(
        functools.partial(middle_kernel, wide),
        grid=(2 * wide,),
        in_specs=[
            whole((rows, width)), whole((rows, width)), whole((rows, width)), whole((width, width)),
            pl.BlockSpec((1, width, width), lambda s: (at(s), 0, 0)),
            pl.BlockSpec((width, width), lambda s: (at(s), 0)),
            whole((8, width)), whole((8, width)),
        ],
        out_specs=[
            whole((rows, width)), whole((rows, width)), whole((rows, width)), whole((width, width)),
            pl.BlockSpec((1, width, width), lambda s: (back(s), 0, 0)),
            pl.BlockSpec((width, width), lambda s: (back(s), 0)),
            whole((8, width)), whole((8, width)),
        ],
        out_shape=[
            shape((rows, width), BF), shape((rows, width), F32), shape((rows, width), BF),
            shape((width, width), BF), shape((wide, width, width), BF),
            shape((wide * width, width), BF), shape((8, width), F32), shape((8, width), F32),
        ],
        scratch_shapes=[
            pltpu.VMEM((rows, width), F32), pltpu.VMEM((rows, width), F32), pltpu.VMEM((rows, 1), F32),
            pltpu.VMEM((rows, width), BF), pltpu.VMEM((rows, wide * width), F32),
            pltpu.VMEM((rows, wide * width), F32), pltpu.VMEM((rows, wide * width), BF),
            pltpu.VMEM((rows, width), F32), pltpu.VMEM((rows, width), F32),
            pltpu.VMEM((rows, width), BF),
        ],
        compiler_params=pltpu.CompilerParams(vmem_limit_bytes=60 * 2**20),
        cost_estimate=pl.CostEstimate(
            flops=2 * rows * width * width * (6 * wide + 3), bytes_accessed=32 * 2**20,
            transcendentals=2 * rows * width * wide,
        ),
        name="middle",
    )(ctx, own, cot, wo, wi, wu, vec, b_inner)


def back_kernel(blocks, first, rows, *refs):
    spots = refs[:blocks]
    (near_ref, own_ref, gctx_ref, ctx_ref, q_ref, k_ref, v_ref, lse_ref, wq_ref, wk_ref, wv_ref,
     segq_ref, segk_ref, h1_ref, dw_ref, gx_ref, gown_ref, sums_ref,
     x_ref, dk_ref, dv_ref, acc_ref, keep_ref, sems) = refs[blocks:]
    near = near_ref[0]
    step = pl.program_id(0)

    @pl.when(step == 0)
    def _():
        copies = [
            pltpu.make_async_copy(spot, x_ref.at[pl.ds(i * rows, rows)], sems.at[i])
            for i, spot in enumerate(spots)
        ]
        for copy in copies:
            copy.start()
        for copy in copies:
            copy.wait()
        acc_ref[...] = jnp.zeros_like(acc_ref)
        keep_ref[...] = h1_ref[...]

    q, g = q_ref[...], gctx_ref[...]
    part = q.shape[1]
    heads = part // HDIM
    masks = [heads_mask(q.shape, h) for h in range(heads)]
    q_parts = [jnp.where(m, q, 0) for m in masks]
    g_parts = [jnp.where(m, g, 0) for m in masks]
    product = (g.astype(F32) * ctx_ref[...].astype(F32)).T
    inner = [
        jnp.sum(product[h * HDIM : (h + 1) * HDIM], axis=0, keepdims=True) for h in range(heads)
    ]

    def one(b, dq, masked):
        here = pl.ds(pl.multiple_of(b * rows, rows), rows)
        k, v = k_ref[here, :], v_ref[here, :]
        kt = k.T
        if masked:
            side = pl.ds(pl.multiple_of((b - first) * rows, rows), rows)
            allowed = segk_ref[side, :] == segq_ref[...]
        dk = jnp.zeros((rows, part), F32)
        dv = jnp.zeros((rows, part), F32)
        out = []
        for h in range(heads):
            s = nt(k, q_parts[h])
            if masked:
                s = jnp.where(allowed, s, MASK_FILL)
            p = jnp.exp(s - lse_ref[0, h : h + 1, :])
            dp = nt(v, g_parts[h])
            ds = (p * (dp - inner[h])).astype(BF)
            dv = dv + mm(p.astype(BF), g_parts[h])
            dk = dk + mm(ds, q_parts[h])
            out.append(dq[h] + mm(kt[h * HDIM : (h + 1) * HDIM], ds))
        dk_ref[here, :] = dk.astype(BF)
        dv_ref[here, :] = dv.astype(BF)
        return tuple(out)

    dq = tuple(jnp.zeros((HDIM, rows), F32) for _ in range(heads))
    dq = lax.fori_loop(0, first, lambda b, c: one(b, c, False), dq)
    dq = lax.fori_loop(first, first + near, lambda b, c: one(b, c, True), dq)
    dq_low = jnp.concatenate(dq, 0).T.astype(BF)
    scale = HDIM**-0.5
    keep_ref[...] += nt(dq_low, wq_ref[...]) * scale
    dw_ref[:, 0:part] = (tn(own_ref[...], dq_low) * scale).astype(BF)
    sums_ref[0:1, :] = jnp.sum(dq_low.astype(F32), axis=0, keepdims=True) * scale

    def products(b, carry):
        here = pl.ds(pl.multiple_of(b * rows, rows), rows)
        dk, dv, x = dk_ref[here, :], dv_ref[here, :], x_ref[here, :]
        acc_ref[here, :] += nt(dk, wk_ref[...]) + nt(dv, wv_ref[...])
        wk, wv, bv = carry
        bv = bv + jnp.sum(dv.astype(F32), axis=0, keepdims=True)
        return wk + tn(x, dk), wv + tn(x, dv), bv

    width = x_ref.shape[1]
    zero = jnp.zeros((width, part), F32)
    wk, wv, bv = lax.fori_loop(0, first + near, products, (zero, zero, jnp.zeros((1, part), F32)))
    dw_ref[:, part : 2 * part] = wk.astype(BF)
    dw_ref[:, 2 * part :] = wv.astype(BF)
    sums_ref[1:2, :] = bv
    sums_ref[2:8, :] = jnp.zeros((6, part), F32)

    @pl.when(step == pl.num_programs(0) - 1)
    def _():
        gown_ref[...] = keep_ref[...]
        for b in range(blocks):
            gx_ref[b] = acc_ref[b * rows : (b + 1) * rows, :].astype(BF)


def back_call(spots, first, near, own, gctx, ctx, q, k, v, lse, wq, wk, wv, segq, segk, h1):
    rows, width = own.shape
    blocks = len(spots)
    tall = blocks * rows
    part = 256
    steps = width // part
    cols = lambda depth: pl.BlockSpec((depth, part), lambda g: (0, g))
    whole = lambda shape: pl.BlockSpec(shape, lambda g: (0,) * len(shape))
    flops = 2 * tall * width * width * 4 + 10 * tall * rows * width * 4
    shape = jax.ShapeDtypeStruct
    return pl.pallas_call(
        functools.partial(back_kernel, blocks, first, rows),
        grid=(steps,),
        in_specs=[pl.BlockSpec(memory_space=pl.ANY)] * blocks
        + [
            pl.BlockSpec(memory_space=pltpu.SMEM),
            whole((rows, width)),
            cols(rows), cols(rows), cols(rows), cols(tall), cols(tall),
            pl.BlockSpec((1, 8, rows), lambda g: (g, 0, 0)),
            cols(width), cols(width), cols(width),
            whole((1, rows)), whole(segk.shape), whole((rows, width)),
        ],
        out_specs=[
            pl.BlockSpec((width, 3 * part), lambda g: (0, g)),
            whole((blocks, rows, width)), whole((rows, width)), cols(8),
        ],
        out_shape=[
            shape((width, 3 * width), BF), shape((blocks, rows, width), BF),
            shape((rows, width), F32), shape((8, width), F32),
        ],
        scratch_shapes=[
            pltpu.VMEM((tall, width), BF), pltpu.VMEM((tall, part), BF), pltpu.VMEM((tall, part), BF),
            pltpu.VMEM((tall, width), F32), pltpu.VMEM((rows, width), F32),
            pltpu.SemaphoreType.DMA((blocks,)),
        ],
        compiler_params=pltpu.CompilerParams(vmem_limit_bytes=60 * 2**20),
        cost_estimate=pl.CostEstimate(
            flops=flops, bytes_accessed=24 * 2**20, transcendentals=tall * rows * 12
        ),
        name="attention_back",
    )(*spots, near, own, gctx, ctx, q, k, v, lse, wq, wk, wv, segq, segk, h1)


def solution(mesh):
    plan = Plan(mesh.shape["grp"], mesh.shape["row"])

    def per_device(
        tokens, cont_lengths, cotangent, w_query, w_key, w_value, w_output, w_inner, w_outer,
        bias_query, bias_value, bias_output, gain_first, shift_first, bias_inner, bias_outer,
        gain_second, shift_second,
    ):
        count = plan.count
        _, rows, width = tokens.shape
        step = w_query.shape[0]
        wide = w_inner.shape[1] // width
        row = lax.axis_index("row")
        scale = HDIM ** (-0.5)
        own = tokens[0]

        vectors = (
            bias_query, bias_value, bias_output, gain_first, shift_first, bias_outer, gain_second,
            shift_second, bias_inner,
        )
        line = jnp.concatenate(vectors)
        small = len(vectors) - 1
        line = jnp.pad(line, (0, width - line.shape[0]))[None]
        line = jnp.pad(line, ((0, 7), (0, 0)))
        pack_a = jnp.concatenate([w_query, line], 0)
        pack_b = jnp.concatenate([w_key, w_value], 0)
        got_a = plan.gather(pack_a, plan.orders[0])
        got_b = plan.gather(pack_b, plan.orders[1])
        spots, near = token_blocks(plan, own, rows)
        first_near = PROMPT // rows

        inner_rows = w_inner.reshape(step, wide, width).transpose(1, 0, 2).reshape(-1, width)
        pack_c = jnp.concatenate([w_output, inner_rows, w_outer], 0)
        got_c = lax.all_gather(pack_c, AXES, axis=0, tiled=True).reshape(count, -1, width)

        full_query = got_a[:, :step].reshape(width, width)
        lines = got_a[:, step]
        table = lines[:, : small * step].reshape(count, small, step).transpose(1, 0, 2)
        table = table.reshape(small, width).astype(F32)
        v_bin = lines[:, small * step : (small + wide) * step].reshape(wide, width).astype(F32)
        v_bin = jnp.pad(v_bin, ((0, 8 - wide), (0, 0)))
        full_key = got_b[:, :step].reshape(width, width)
        full_value = got_b[:, step : 2 * step].reshape(width, width)

        segments = segment_ids(cont_lengths[0], plan.row * rows)
        seg_own = lax.dynamic_slice_in_dim(segments, row * rows, rows, 0)[None, :]
        seg_near = near_segments(plan, segments, rows)[:, None]
        near = near.astype(jnp.int32).reshape(1)

        queries, keys, values, context, log_total = attention_call(
            spots, first_near, near, own, full_query, full_key, full_value, table[0:1], table[1:2],
            seg_own, seg_near,
        )

        full_output = got_c[:, :step].reshape(width, width)
        full_inner = got_c[:, step : step * (1 + wide)].reshape(count, wide, step, width)
        full_inner = full_inner.transpose(1, 0, 2, 3).reshape(wide, width, width)
        full_outer = got_c[:, step * (1 + wide) :].reshape(wide * width, width)
        vec = jnp.concatenate([table[2:], jnp.zeros((2, width), F32)], 0)
        layer_out, grad_h1, grad_context, d_output, d_inner, d_outer, sums, sums_bin = middle_call(
            context, own, cotangent[0], full_output, full_inner, full_outer, vec, v_bin
        )
        by_owner = lambda grad: grad.reshape(count, step, -1)
        o_outer = plan.scatter(d_outer.reshape(count, wide * step, width))
        o_inner = plan.scatter(d_inner.reshape(wide, count, step, width), 1)
        o_output = plan.scatter(by_owner(d_output))

        d_qkv, shared, grad_own, sums_qkv = back_call(
            spots, first_near, near, own, grad_context, context, queries, keys, values, log_total,
            full_query, full_key, full_value, seg_own, seg_near, grad_h1,
        )
        grad_tokens = grad_own + token_return(plan, shared, rows)

        order = (5, 3, 4, 2, 0, 1)
        d_table = jnp.concatenate([sums_qkv[:2]] + [sums[i : i + 1] for i in order], 0)
        d_lines = jnp.concatenate(
            [
                d_table.reshape(small, count, step).transpose(1, 0, 2).reshape(count, -1),
                sums_bin[:wide].reshape(count, wide * step),
            ],
            1,
        )
        d_lines = jnp.pad(d_lines, ((0, 0), (0, width - d_lines.shape[1])))[:, None]
        o_line = plan.scatter(jnp.pad(d_lines, ((0, 0), (0, 7), (0, 0))))[0]
        parts = 3 * width // 768
        o_qkv = plan.scatter(by_owner(d_qkv)).reshape(step, parts, 3, width // parts)

        o_small = [o_line[i * step : (i + 1) * step] for i in range(small)]
        o_bin = o_line[small * step : (small + wide) * step]
        return (
            layer_out[None],
            grad_tokens.astype(BF)[None],
            o_qkv[:, :, 0].reshape(step, width),
            o_qkv[:, :, 1].reshape(step, width),
            o_qkv[:, :, 2].reshape(step, width),
            o_output,
            o_inner.transpose(1, 0, 2).reshape(step, wide * width),
            o_outer,
            o_small[0],
            o_small[1],
            o_small[2],
            o_small[3],
            o_small[4],
            o_bin,
            o_small[5],
            o_small[6],
            o_small[7],
        )

    split = P("grp", "row", None)
    owned2, owned1 = P(AXES, None), P(AXES)
    in_specs = (split, P("grp", None), split) + (owned2,) * 6 + (owned1,) * 9
    out_specs = (split, split) + (owned2,) * 6 + (owned1,) * 9
    return jax.shard_map(
        per_device, mesh=mesh, in_specs=in_specs, out_specs=out_specs, check_vma=False
    )
```

```python
import functools

import jax
import jax.numpy as jnp
import numpy as np
from jax import lax
from jax.experimental import pallas as pl
from jax.experimental.pallas import tpu as pltpu
from jax.sharding import PartitionSpec as P

HEADS = 12
HDIM = 64
PROMPT = 1024
CONT_MOST = 256
BF = jnp.bfloat16
F32 = jnp.float32

NORM_EPS = 1e-12
MASK_FILL = -1000000000.0
SQRT_HALF = 0.7071067811865476
INV_ROOT_TAU = 0.3989422804014327
AXES = ("grp", "row")


def mm(left, right):
    return jnp.dot(left, right, preferred_element_type=F32)


def segment_ids(lengths, group_len):
    ends = jnp.cumsum(lengths)
    places = jnp.arange(group_len, dtype=jnp.int32)
    passed = jnp.sum(((places - PROMPT)[:, None] >= ends[None, :]).astype(jnp.int32), axis=-1)
    return jnp.where(places < PROMPT, 0, 1 + passed)


class Plan:
    def __init__(self, grp, row):
        self.grp, self.row, self.count = grp, row, grp * row
        y = row // 4
        bits = lambda base, size: [base << i for i in range(size.bit_length() - 1)]
        self.y, self.z = bits(1, y), bits(y, 4)
        self.core, self.x = bits(row, 2), bits(2 * row, grp // 2)
        self.bits = self.count.bit_length() - 1

    def swap(self, value, mask):
        return lax.ppermute(value, AXES, [(i, i ^ mask) for i in range(self.count)])

    def send(self, value, moves):
        pairs = [(g * self.row + a, g * self.row + b) for g in range(self.grp) for a, b in moves]
        return lax.ppermute(value, AXES, pairs)

    def me(self):
        return lax.axis_index("grp") * self.row + lax.axis_index("row")


def combos(stage):
    masks = [0]
    for bit in stage:
        masks = masks + [m ^ bit for m in masks]
    return masks


class Gather:
    def __init__(self, plan, value):
        self.plan, self.held, self.masks = plan, value[None], [0]

    def stage(self, bits):
        masks = combos(bits)
        self.held = jnp.concatenate(
            [self.held] + [self.plan.swap(self.held, m) for m in masks[1:]], 0
        )
        self.masks = [m ^ k for k in masks for m in self.masks]

    def ordered(self):
        slot = np.zeros(self.plan.count, np.int32)
        for j, m in enumerate(self.masks):
            slot[m] = j
        places = jnp.asarray(slot)[self.plan.me() ^ jnp.arange(self.plan.count)]
        return jnp.take(self.held, places, axis=0, mode="clip")


class Reduce:
    def __init__(self, plan, value, before=0):
        self.plan, self.before = plan, before
        self.lead, self.rest = list(value.shape[:before]), list(value.shape[before + 1 :])
        self.left = [1 << i for i in reversed(range(plan.bits))]
        self.value = value.astype(BF).reshape(self.lead + [2] * plan.bits + self.rest)

    def stage(self, bits):
        me, value = self.plan.me(), self.value

        def part(mask):
            array = value
            for bit in bits:
                place = ((me ^ mask) // bit) & 1
                axis = self.before + self.left.index(bit)
                array = lax.dynamic_slice_in_dim(array, place, 1, axis)
            return array

        total = part(0).astype(F32)
        for mask in combos(bits)[1:]:
            total = total + self.plan.swap(part(mask), mask).astype(F32)
        self.left = [b for b in self.left if b not in bits]
        value = total.reshape(self.lead + [2] * len(self.left) + self.rest)
        self.value = value.astype(BF) if self.left else value


def tie(*values):
    return lax.optimization_barrier(values)


class Tokens:
    def __init__(self, plan, own):
        self.plan, self.own = plan, own
        self.rows = own.shape[0]
        self.ready = plan.row == 8

    def stage_one(self):
        if self.ready:
            plan, own = self.plan, self.own
            across = plan.send(own, [(0, 4), (1, 5), (2, 6), (3, 7)])
            self.same = jnp.where(lax.axis_index("row") < 4, own, across)
            self.beside = plan.swap(own, 1)
            return [self.same, self.beside]
        return []

    def stage_two(self):
        if self.ready:
            plan = self.plan
            self.other = plan.swap(self.same, 2)
            self.same_y = plan.swap(self.same, 1)
            self.diagonal = plan.send(self.own, [(5, 6), (6, 5)])
            return [self.other, self.same_y, self.diagonal]
        return []

    def stage_three(self):
        if self.ready:
            self.other_y = self.plan.swap(self.other, 1)

    def spots(self):
        row, rows, own = lax.axis_index("row"), self.rows, self.own
        if self.ready:
            near = jnp.where(row < 4, 0, jnp.where((row == 5) | (row == 6), 3, 2))
            return [
                self.same, self.other, self.same_y, self.other_y, own, self.beside, self.diagonal,
            ], near
        every = lax.all_gather(own, "row", axis=0, tiled=True)
        start = jnp.maximum(row * rows - CONT_MOST, 0)
        padded = jnp.concatenate([every, jnp.zeros((CONT_MOST, own.shape[1]), own.dtype)], 0)
        near = lax.dynamic_slice_in_dim(padded, start, rows + 2 * CONT_MOST, 0)
        every = jnp.concatenate([every[:PROMPT], near], 0)
        spots = [every[i : i + rows] for i in range(0, every.shape[0], rows)]
        return spots, jnp.where(row * rows < PROMPT, 0, near.shape[0] // rows)


def near_segments(plan, segments, rows):
    row = lax.axis_index("row")
    if plan.row != 8:
        start = jnp.maximum(row * rows - CONT_MOST, 0)
        padded = jnp.concatenate([segments, jnp.full((CONT_MOST,), -1, jnp.int32)], 0)
        near = lax.dynamic_slice_in_dim(padded, start, rows + 2 * CONT_MOST, 0)
        return jnp.where((near == 0) | (row * rows < PROMPT), -1, near)
    pieces = []
    for block, valid in (
        (row, row >= 4),
        (row ^ 1, row >= 4),
        (11 - row, (row == 5) | (row == 6)),
    ):
        block = jnp.clip(block, 0, 7)
        ids = lax.dynamic_slice_in_dim(segments, block * rows, rows, 0)
        pieces.append(jnp.where(valid, ids, -1))
    return jnp.concatenate(pieces, 0)


class Return:
    def __init__(self, plan, rows):
        self.plan, self.rows = plan, rows

    def prompt_one(self, parts):
        self.prompt = self.same = parts
        if self.plan.row == 8:
            same, other, same_y, other_y = [parts[i].astype(F32) for i in range(4)]
            self.other = (other + self.plan.swap(parts[3], 1).astype(F32)).astype(BF)
            self.same = same + self.plan.swap(parts[2], 1).astype(F32)

    def prompt_two(self):
        if self.plan.row == 8:
            self.same = self.same + self.plan.swap(self.other, 2).astype(F32)

    def prompt_three(self):
        if self.plan.row == 8:
            back = self.plan.send(self.same.astype(BF), [(4, 0), (5, 1), (6, 2), (7, 3)])
            self.same = self.same + back.astype(F32)

    def near(self, parts):
        self.around = parts
        if self.plan.row == 8:
            own = parts[0].astype(F32) + self.plan.swap(parts[1], 1).astype(F32)
            self.own = own + self.plan.send(parts[2], [(5, 6), (6, 5)]).astype(F32)

    def total(self):
        row, rows = lax.axis_index("row"), self.rows
        if self.plan.row == 8:
            return jnp.where(row < 4, self.same, self.own)
        around = self.around.reshape(-1, self.around.shape[-1]).astype(F32)
        start = jnp.maximum(row * rows - CONT_MOST, 0)
        whole = jnp.zeros((self.plan.row * rows + CONT_MOST, around.shape[1]), F32)
        whole = whole.at[:PROMPT].set(self.prompt.reshape(PROMPT, -1).astype(F32))
        near = jnp.where(row * rows < PROMPT, 0, around)
        near = lax.dynamic_slice_in_dim(whole, start, rows + 2 * CONT_MOST, 0) + near
        whole = lax.dynamic_update_slice_in_dim(whole, near, start, 0)
        return lax.psum_scatter(whole[: self.plan.row * rows], "row", scatter_dimension=0, tiled=True)


def heads_mask(lanes, head):
    lane = lax.broadcasted_iota(jnp.int32, lanes, 1)
    return (lane >= head * HDIM) & (lane < (head + 1) * HDIM)


def nt(left, right):
    return lax.dot_general(left, right, (((1,), (1,)), ((), ())), preferred_element_type=F32)


def tn(left, right):
    return lax.dot_general(left, right, (((0,), (0,)), ((), ())), preferred_element_type=F32)


def attention_kernel(blocks, first, rows, *refs):
    spots = refs[:blocks]
    (near_ref, own_ref, wq_ref, wk_ref, wv_ref, bq_ref, bv_ref, segq_ref, segk_ref,
     q_ref, kp_ref, vp_ref, kn_ref, vn_ref, ctx_ref, lse_ref, x_ref, s_ref, sems) = refs[blocks:]
    near = near_ref[0]
    at = lambda b: pl.ds(pl.multiple_of(b * rows, rows), rows)

    @pl.when(pl.program_id(0) == 0)
    def _():
        copies = [
            pltpu.make_async_copy(spot, x_ref.at[pl.ds(i * rows, rows)], sems.at[i])
            for i, spot in enumerate(spots)
        ]
        for copy in copies:
            copy.start()
        for copy in copies:
            copy.wait()

    queries = (mm(own_ref[...], wq_ref[...]) + bq_ref[...]) * (HDIM**-0.5)
    q_ref[...] = queries.astype(BF)

    def project(b, k_ref, v_ref, side):
        x = x_ref[at(b), :]
        k_ref[at(side), :] = mm(x, wk_ref[...]).astype(BF)
        v_ref[at(side), :] = (mm(x, wv_ref[...]) + bv_ref[...]).astype(BF)

    @pl.loop(0, first)
    def _(b):
        project(b, kp_ref, vp_ref, b)

    @pl.loop(0, near)
    def _(b):
        project(first + b, kn_ref, vn_ref, b)

    width = q_ref.shape[1]
    heads = width // HDIM
    q = q_ref[...]
    parts = [jnp.where(heads_mask(q.shape, h), q, 0) for h in range(heads)]

    def scores(b, peaks, k_ref, base):
        k = k_ref[at(b), :]
        out = []
        for h in range(heads):
            s = nt(k, parts[h])
            if base:
                s = jnp.where(segk_ref[at(b), :] == segq_ref[...], s, MASK_FILL)
            s_ref[h, at(base + b), :] = s
            out.append(jnp.maximum(peaks[h], jnp.max(s, axis=0, keepdims=True)))
        return tuple(out)

    peaks = tuple(jnp.full((1, rows), MASK_FILL, F32) for _ in range(heads))
    peaks = lax.fori_loop(0, first, lambda b, c: scores(b, c, kp_ref, 0), peaks)
    peaks = lax.fori_loop(0, near, lambda b, c: scores(b, c, kn_ref, first), peaks)

    def mix(b, carry, v_ref, base):
        totals, mixed = carry
        vt = v_ref[at(b), :].T
        new_totals, new_mixed = [], []
        for h in range(heads):
            p = jnp.exp(s_ref[h, at(base + b), :] - peaks[h])
            new_totals.append(totals[h] + jnp.sum(p, axis=0, keepdims=True))
            new_mixed.append(mixed[h] + mm(vt[h * HDIM : (h + 1) * HDIM], p.astype(BF)))
        return tuple(new_totals), tuple(new_mixed)

    zero = (
        tuple(jnp.zeros((1, rows), F32) for _ in range(heads)),
        tuple(jnp.zeros((HDIM, rows), F32) for _ in range(heads)),
    )
    carry = lax.fori_loop(0, first, lambda b, c: mix(b, c, vp_ref, 0), zero)
    totals, mixed = lax.fori_loop(0, near, lambda b, c: mix(b, c, vn_ref, first), carry)
    whole = jnp.concatenate([mixed[h] / totals[h] for h in range(heads)], 0)
    ctx_ref[...] = whole.T.astype(BF)
    for h in range(heads):
        lse_ref[0, h : h + 1, :] = peaks[h] + jnp.log(totals[h])


def attention_call(spots, first, near, own, wq, wk, wv, bq, bv, segq, segk):
    rows, width = own.shape
    blocks = len(spots)
    tall = blocks * rows
    part = 256
    steps = width // part
    heads = part // HDIM
    cols = lambda depth: pl.BlockSpec((depth, part), lambda g: (0, g))
    flops = 2 * tall * width * width * 2 + 4 * tall * rows * width * 4
    return pl.pallas_call(
        functools.partial(attention_kernel, blocks, first, rows),
        grid=(steps,),
        in_specs=[pl.BlockSpec(memory_space=pl.ANY)] * blocks
        + [
            pl.BlockSpec(memory_space=pltpu.SMEM),
            pl.BlockSpec((rows, width), lambda g: (0, 0)),
            cols(width), cols(width), cols(width), cols(1), cols(1),
            pl.BlockSpec((1, rows), lambda g: (0, 0)),
            pl.BlockSpec(segk.shape, lambda g: (0, 0)),
        ],
        out_specs=[
            cols(rows), cols(PROMPT), cols(PROMPT), cols(tall - PROMPT), cols(tall - PROMPT),
            cols(rows), pl.BlockSpec((1, 8, rows), lambda g: (g, 0, 0)),
        ],
        out_shape=[
            jax.ShapeDtypeStruct((rows, width), BF),
            jax.ShapeDtypeStruct((PROMPT, width), BF),
            jax.ShapeDtypeStruct((PROMPT, width), BF),
            jax.ShapeDtypeStruct((tall - PROMPT, width), BF),
            jax.ShapeDtypeStruct((tall - PROMPT, width), BF),
            jax.ShapeDtypeStruct((rows, width), BF),
            jax.ShapeDtypeStruct((steps, 8, rows), F32),
        ],
        scratch_shapes=[
            pltpu.VMEM((tall, width), BF),
            pltpu.VMEM((heads, tall, rows), F32),
            pltpu.SemaphoreType.DMA((blocks,)),
        ],
        compiler_params=pltpu.CompilerParams(vmem_limit_bytes=60 * 2**20),
        cost_estimate=pl.CostEstimate(
            flops=flops, bytes_accessed=12 * 2**20, transcendentals=tall * rows * 12
        ),
        name="attention",
    )(*spots, near, own, wq, wk, wv, bq, bv, segq, segk)


def middle_kernel(wide, ctx_ref, own_ref, cot_ref, wo_ref, wi_ref, wu_ref, vec_ref, bin_ref,
                  out_ref, h1_ref, gctx_ref, dwo_ref, dwi_ref, dwu_ref, sums_ref, sbin_ref,
                  first_ref, n1_ref, inv_ref, low_ref, pre_ref, cdf_ref, act_ref, acc_ref,
                  gffn_ref, glow_ref):
    step = pl.program_id(0)
    width = ctx_ref.shape[1]
    square = lambda ref: ref[...].reshape(width, width)
    vec = lambda i: vec_ref[i : i + 1, :]
    mean = lambda v: jnp.sum(v, axis=-1, keepdims=True) * (1.0 / width)
    down = lambda v: jnp.sum(v, axis=0, keepdims=True)

    @pl.when(step == 0)
    def _():
        hidden = own_ref[...].astype(F32) + mm(ctx_ref[...], square(wo_ref)) + vec(0)
        centred = hidden - mean(hidden)
        inverse = lax.rsqrt(mean(centred * centred) + NORM_EPS)
        normed = centred * inverse
        n1_ref[...] = normed
        inv_ref[...] = inverse
        first = normed * vec(1) + vec(2)
        first_ref[...] = first
        low_ref[...] = first.astype(BF)

    @pl.when(step < wide)
    def _():
        chunk = pl.ds(pl.multiple_of(step * width, width), width)
        pre = mm(low_ref[...], square(wi_ref)) + bin_ref[pl.ds(step, 1), :]
        cdf = 0.5 * (1.0 + lax.erf(pre * SQRT_HALF))
        act = (pre * cdf).astype(BF)
        pre_ref[:, chunk] = pre
        cdf_ref[:, chunk] = cdf
        act_ref[:, chunk] = act
        more = mm(act, square(wu_ref))

        @pl.when(step == 0)
        def _():
            acc_ref[...] = more

        @pl.when(step > 0)
        def _():
            acc_ref[...] += more

    @pl.when(step == wide - 1)
    def _():
        hidden = first_ref[...] + acc_ref[...] + vec(3)
        centred = hidden - mean(hidden)
        inverse = lax.rsqrt(mean(centred * centred) + NORM_EPS)
        normed = centred * inverse
        out_ref[...] = (normed * vec(4) + vec(5)).astype(BF)
        grad = cot_ref[...].astype(F32)
        sums_ref[0:1, :] = down(grad * normed)
        sums_ref[1:2, :] = down(grad)
        e = grad * vec(4)
        back = inverse * (e - mean(e) - normed * mean(e * normed))
        gffn_ref[...] = back
        low = back.astype(BF)
        glow_ref[...] = low
        sums_ref[2:3, :] = down(low.astype(F32))

    @pl.when(step >= wide)
    def _():
        at = 2 * wide - 1 - step
        chunk = pl.ds(pl.multiple_of(at * width, width), width)
        pre = pre_ref[:, chunk]
        slope = cdf_ref[:, chunk] + pre * jnp.exp(-0.5 * pre * pre) * INV_ROOT_TAU
        low = glow_ref[...]
        grad = (nt(low, square(wu_ref)) * slope).astype(BF)
        sbin_ref[pl.ds(at, 1), :] = down(grad.astype(F32))
        dwu_ref[...] = tn(act_ref[:, chunk], low).astype(BF)
        dwi_ref[0] = tn(low_ref[...], grad).astype(BF)
        gffn_ref[...] += nt(grad, square(wi_ref))

    @pl.when(step == 2 * wide - 1)
    def _():
        grad = gffn_ref[...]
        normed = n1_ref[...]
        sums_ref[3:4, :] = down(grad * normed)
        sums_ref[4:5, :] = down(grad)
        e = grad * vec(1)
        back = inv_ref[...] * (e - mean(e) - normed * mean(e * normed))
        h1_ref[...] = back
        low = back.astype(BF)
        sums_ref[5:6, :] = down(low.astype(F32))
        sums_ref[6:8, :] = jnp.zeros((2, width), F32)
        dwo_ref[...] = tn(ctx_ref[...], low).astype(BF)
        gctx_ref[...] = nt(low, square(wo_ref)).astype(BF)


def middle_call(ctx, own, cot, got, vec, b_inner):
    rows, width = own.shape
    owners = got.shape[0]
    each = width // owners
    wide = got.shape[1] // each // 2
    whole = lambda shape: pl.BlockSpec(shape, lambda s: (0,) * len(shape))
    at = lambda s: jnp.where(s < wide, s, 2 * wide - 1 - s)
    back = lambda s: jnp.where(s < wide, wide - 1, 2 * wide - 1 - s)
    shape = jax.ShapeDtypeStruct
    return pl.pallas_call(
        functools.partial(middle_kernel, wide),
        grid=(2 * wide,),
        in_specs=[
            whole((rows, width)), whole((rows, width)), whole((rows, width)),
            pl.BlockSpec((owners, each, width), lambda s: (0, wide, 0)),
            pl.BlockSpec((owners, each, width), lambda s: (0, wide + 1 + at(s), 0)),
            pl.BlockSpec((owners // wide, wide * each, width), lambda s: (at(s), 0, 0)),
            whole((8, width)), whole((8, width)),
        ],
        out_specs=[
            whole((rows, width)), whole((rows, width)), whole((rows, width)), whole((width, width)),
            pl.BlockSpec((1, width, width), lambda s: (back(s), 0, 0)),
            pl.BlockSpec((width, width), lambda s: (back(s), 0)),
            whole((8, width)), whole((8, width)),
        ],
        out_shape=[
            shape((rows, width), BF), shape((rows, width), F32), shape((rows, width), BF),
            shape((width, width), BF), shape((wide, width, width), BF),
            shape((wide * width, width), BF), shape((8, width), F32), shape((8, width), F32),
        ],
        scratch_shapes=[
            pltpu.VMEM((rows, width), F32), pltpu.VMEM((rows, width), F32), pltpu.VMEM((rows, 1), F32),
            pltpu.VMEM((rows, width), BF), pltpu.VMEM((rows, wide * width), F32),
            pltpu.VMEM((rows, wide * width), F32), pltpu.VMEM((rows, wide * width), BF),
            pltpu.VMEM((rows, width), F32), pltpu.VMEM((rows, width), F32),
            pltpu.VMEM((rows, width), BF),
        ],
        compiler_params=pltpu.CompilerParams(vmem_limit_bytes=60 * 2**20),
        cost_estimate=pl.CostEstimate(
            flops=2 * rows * width * width * (6 * wide + 3), bytes_accessed=32 * 2**20,
            transcendentals=2 * rows * width * wide,
        ),
        name="middle",
    )(ctx, own, cot, got, got, got, vec, b_inner)


def back_kernel(rows, bound, *refs):
    (near_ref, gctx_ref, ctx_ref, q_ref, k_ref, v_ref, lse_ref, segq_ref, segk_ref, dq0_ref,
     dk_ref, dv_ref, dq_ref) = refs
    q, g = q_ref[...], gctx_ref[...]
    part = q.shape[1]
    heads = part // HDIM
    masks = [heads_mask(q.shape, h) for h in range(heads)]
    q_parts = [jnp.where(m, q, 0) for m in masks]
    g_parts = [jnp.where(m, g, 0) for m in masks]
    product = (g.astype(F32) * ctx_ref[...].astype(F32)).T
    inner = [
        jnp.sum(product[h * HDIM : (h + 1) * HDIM], axis=0, keepdims=True) for h in range(heads)
    ]

    def one(b, dq):
        here = pl.ds(pl.multiple_of(b * rows, rows), rows)
        k, v = k_ref[here, :], v_ref[here, :]
        kt = k.T
        if bound is None:
            allowed = segk_ref[here, :] == segq_ref[...]
        dk = jnp.zeros((rows, part), F32)
        dv = jnp.zeros((rows, part), F32)
        out = []
        for h in range(heads):
            s = nt(k, q_parts[h])
            if bound is None:
                s = jnp.where(allowed, s, MASK_FILL)
            p = jnp.exp(s - lse_ref[0, h : h + 1, :])
            dp = nt(v, g_parts[h])
            ds = (p * (dp - inner[h])).astype(BF)
            dv = dv + mm(p.astype(BF), g_parts[h])
            dk = dk + mm(ds, q_parts[h])
            out.append(dq[h] + mm(kt[h * HDIM : (h + 1) * HDIM], ds))
        dk_ref[here, :] = dk.astype(BF)
        dv_ref[here, :] = dv.astype(BF)
        return tuple(out)

    dq = tuple(dq0_ref[h * HDIM : (h + 1) * HDIM, :] for h in range(heads))
    dq = lax.fori_loop(0, near_ref[0] if bound is None else bound, one, dq)
    dq_ref[...] = jnp.concatenate(dq, 0)


def back_call(start, steps, bound, near, gctx, ctx, q, k, v, lse, segq, segk, dq0):
    rows = q.shape[0]
    tall = k.shape[0]
    part = 256
    cols = lambda depth: pl.BlockSpec((depth, part), lambda g: (0, start + g))
    mine = lambda depth: pl.BlockSpec((depth, part), lambda g: (0, g))
    whole = lambda shape: pl.BlockSpec(shape, lambda g: (0,) * len(shape))
    shape = jax.ShapeDtypeStruct
    return pl.pallas_call(
        functools.partial(back_kernel, rows, bound),
        grid=(steps,),
        in_specs=[
            pl.BlockSpec(memory_space=pltpu.SMEM),
            cols(rows), cols(rows), cols(rows), cols(tall), cols(tall),
            pl.BlockSpec((1, 8, rows), lambda g: (start + g, 0, 0)),
            whole((1, rows)), whole(segk.shape),
            pl.BlockSpec((part, rows), lambda g: (g, 0)),
        ],
        out_specs=[mine(tall), mine(tall), pl.BlockSpec((part, rows), lambda g: (g, 0))],
        out_shape=[
            shape((tall, steps * part), BF), shape((tall, steps * part), BF),
            shape((steps * part, rows), F32),
        ],
        compiler_params=pltpu.CompilerParams(vmem_limit_bytes=60 * 2**20),
        cost_estimate=pl.CostEstimate(
            flops=2 * 10 * 2 * tall * rows * part * steps * 2,
            bytes_accessed=8 * tall * part * steps, transcendentals=tall * rows * 4 * steps,
        ),
        name="attention_back",
    )(near, gctx, ctx, q, k, v, lse, segq, segk, dq0)


def product_kernel(rows, bound, near_ref, dk_ref, dv_ref, wk_ref, wv_ref, gx_ref):
    @pl.when((pl.program_id(0) < near_ref[0]) | (bound is not None))
    def _():
        gx_ref[0] = (nt(dk_ref[...], wk_ref[...]) + nt(dv_ref[...], wv_ref[...])).astype(BF)


def product_call(bound, near, dk, dv, wk, wv, rows):
    tall, width = dk.shape
    whole = lambda shape: pl.BlockSpec(shape, lambda b: (0,) * len(shape))
    return pl.pallas_call(
        functools.partial(product_kernel, rows, bound),
        grid=(tall // rows,),
        in_specs=[
            pl.BlockSpec(memory_space=pltpu.SMEM),
            pl.BlockSpec((rows, width), lambda b: (b, 0)),
            pl.BlockSpec((rows, width), lambda b: (b, 0)),
            whole((width, width)), whole((width, width)),
        ],
        out_specs=pl.BlockSpec((1, rows, width), lambda b: (b, 0, 0)),
        out_shape=jax.ShapeDtypeStruct((tall // rows, rows, width), BF),
        compiler_params=pltpu.CompilerParams(vmem_limit_bytes=60 * 2**20),
        cost_estimate=pl.CostEstimate(
            flops=4 * tall * width * width, bytes_accessed=6 * tall * width, transcendentals=0
        ),
        name="token_product",
    )(near, dk, dv, wk, wv)


def weight_kernel(blocks, first, rows, *refs):
    spots = refs[:blocks]
    (near_ref, own_ref, dq_ref, wq_ref, h1_ref, dkp_ref, dvp_ref, dkn_ref, dvn_ref,
     dwq_ref, dwkv_ref, gown_ref, sums_ref, x_ref, sems) = refs[blocks:]
    at = lambda b: pl.ds(pl.multiple_of(b * rows, rows), rows)
    step = pl.program_id(0)

    @pl.when(step == 0)
    def _():
        copies = [
            pltpu.make_async_copy(spot, x_ref.at[pl.ds(i * rows, rows)], sems.at[i])
            for i, spot in enumerate(spots)
        ]
        for copy in copies:
            copy.start()
        for copy in copies:
            copy.wait()
        gown_ref[...] = h1_ref[...]

    scale = HDIM**-0.5
    dq = dq_ref[...].T.astype(BF)
    part = dq.shape[1]
    gown_ref[...] += nt(dq, wq_ref[...]) * scale
    dwq_ref[...] = (tn(own_ref[...], dq) * scale).astype(BF)
    sums_ref[0:1, :] = jnp.sum(dq.astype(F32), axis=0, keepdims=True) * scale

    def products(b, carry, dk_ref, dv_ref, base):
        dk, dv, x = dk_ref[at(b), :], dv_ref[at(b), :], x_ref[at(base + b), :]
        wk, wv, bv = carry
        bv = bv + jnp.sum(dv.astype(F32), axis=0, keepdims=True)
        return wk + tn(x, dk), wv + tn(x, dv), bv

    width = x_ref.shape[1]
    zero = jnp.zeros((width, part), F32)
    carry = (zero, zero, jnp.zeros((1, part), F32))
    carry = lax.fori_loop(0, first, lambda b, c: products(b, c, dkp_ref, dvp_ref, 0), carry)
    carry = lax.fori_loop(0, near_ref[0], lambda b, c: products(b, c, dkn_ref, dvn_ref, first), carry)
    wk, wv, bv = carry
    dwkv_ref[:, :part] = wk.astype(BF)
    dwkv_ref[:, part:] = wv.astype(BF)
    sums_ref[1:2, :] = bv
    sums_ref[2:8, :] = jnp.zeros((6, part), F32)


def weight_call(spots, first, near, own, dq, wq, h1, dkp, dvp, dkn, dvn):
    rows, width = own.shape
    blocks = len(spots)
    tall = blocks * rows
    part = 256
    steps = width // part
    cols = lambda depth, size=part: pl.BlockSpec((depth, size), lambda g: (0, g))
    whole = lambda shape: pl.BlockSpec(shape, lambda g: (0,) * len(shape))
    shape = jax.ShapeDtypeStruct
    return pl.pallas_call(
        functools.partial(weight_kernel, blocks, first, rows),
        grid=(steps,),
        in_specs=[pl.BlockSpec(memory_space=pl.ANY)] * blocks
        + [
            pl.BlockSpec(memory_space=pltpu.SMEM),
            whole((rows, width)), pl.BlockSpec((part, rows), lambda g: (g, 0)), cols(width),
            whole((rows, width)), cols(PROMPT), cols(PROMPT), cols(tall - PROMPT), cols(tall - PROMPT),
        ],
        out_specs=[cols(width), cols(width, 2 * part), whole((rows, width)), cols(8)],
        out_shape=[
            shape((width, width), BF), shape((width, 2 * width), BF), shape((rows, width), F32),
            shape((8, width), F32),
        ],
        scratch_shapes=[pltpu.VMEM((tall, width), BF), pltpu.SemaphoreType.DMA((blocks,))],
        compiler_params=pltpu.CompilerParams(vmem_limit_bytes=60 * 2**20),
        cost_estimate=pl.CostEstimate(
            flops=4 * tall * width * width, bytes_accessed=12 * tall * width, transcendentals=0
        ),
        name="weight_product",
    )(*spots, near, own, dq, wq, h1, dkp, dvp, dkn, dvn)


def solution(mesh):
    plan = Plan(mesh.shape["grp"], mesh.shape["row"])

    def per_device(
        tokens, cont_lengths, cotangent, w_query, w_key, w_value, w_output, w_inner, w_outer,
        bias_query, bias_value, bias_output, gain_first, shift_first, bias_inner, bias_outer,
        gain_second, shift_second,
    ):
        count = plan.count
        _, rows, width = tokens.shape
        step = w_query.shape[0]
        wide = w_inner.shape[1] // width
        row = lax.axis_index("row")
        scale = HDIM ** (-0.5)
        own = tokens[0]

        vectors = (
            bias_query, bias_value, bias_output, gain_first, shift_first, bias_outer, gain_second,
            shift_second, bias_inner,
        )
        line = jnp.concatenate(vectors)
        small = len(vectors) - 1
        line = jnp.pad(line, (0, width - line.shape[0]))[None]
        line = jnp.pad(line, ((0, 7), (0, 0)))
        inner_rows = w_inner.reshape(step, wide, width).transpose(1, 0, 2).reshape(-1, width)
        pack_c = jnp.concatenate([w_outer, w_output, inner_rows], 0)
        got_c = lax.all_gather(pack_c, AXES, axis=0, tiled=True).reshape(count, -1, width)

        gather = Gather(plan, jnp.concatenate([w_query, w_key, w_value, line], 0))
        exchange = Tokens(plan, own)
        gather.stage(plan.z)
        gather.held, *seen = tie(gather.held, *exchange.stage_one())
        if seen:
            exchange.same, exchange.beside = seen
        gather.stage(plan.y)
        gather.held, *seen = tie(gather.held, *exchange.stage_two())
        if seen:
            exchange.other, exchange.same_y, exchange.diagonal = seen
        gather.stage(plan.x)
        exchange.stage_three()
        gather.stage(plan.core)
        got_a = gather.ordered()
        spots, near = exchange.spots()
        first_near = PROMPT // rows

        full_query, full_key, full_value = [
            got_a[:, i * step : (i + 1) * step].reshape(width, width) for i in range(3)
        ]
        lines = got_a[:, 3 * step]
        table = lines[:, : small * step].reshape(count, small, step).transpose(1, 0, 2)
        table = table.reshape(small, width).astype(F32)
        v_bin = lines[:, small * step : (small + wide) * step].reshape(wide, width).astype(F32)
        v_bin = jnp.pad(v_bin, ((0, 8 - wide), (0, 0)))
        segments = segment_ids(cont_lengths[0], plan.row * rows)
        seg_own = lax.dynamic_slice_in_dim(segments, row * rows, rows, 0)[None, :]
        seg_near = near_segments(plan, segments, rows)[:, None]
        near = near.astype(jnp.int32).reshape(1)

        queries, keys_p, values_p, keys_n, values_n, context, log_total = attention_call(
            spots, first_near, near, own, full_query, full_key, full_value, table[0:1], table[1:2],
            seg_own, seg_near,
        )

        if step % 8:
            cuts = [wide * step, (wide + 1) * step]
            outer, output, inner = jnp.split(got_c, cuts, axis=1)
            inner = inner.reshape(count, wide, step, width).transpose(1, 0, 2, 3)
            inner = inner.reshape(wide, 32, width // 32, width).transpose(1, 0, 2, 3)
            got_c = jnp.concatenate(
                [v.reshape(32, -1, width) for v in (outer, output, inner)], 1
            )
        vec = jnp.concatenate([table[2:], jnp.zeros((2, width), F32)], 0)
        layer_out, grad_h1, grad_context, d_output, d_inner, d_outer, sums, sums_bin = middle_call(
            context, own, cotangent[0], got_c, vec, v_bin
        )
        by_owner = lambda grad: grad.reshape(count, step, -1)
        r_outer = Reduce(plan, d_outer.reshape(count, wide * step, width))
        r_inner = Reduce(plan, d_inner.reshape(wide, count, step, width), 1)
        r_output = Reduce(plan, by_owner(d_output))
        big = (r_outer, r_inner, r_output)

        def hold(*values):
            tied = tie(*[r.value for r in big], *values)
            for r, value in zip(big, tied):
                r.value = value
            return tied[len(big) :]

        part = 256
        none = jnp.zeros((part, rows), F32)
        back = lambda start, gctx: back_call(
            start, 1, first_near, near, gctx, context, queries, keys_p, values_p, log_total,
            seg_own, seg_near, none,
        )
        heads_p = [back(0, grad_context)]
        for r in big:
            r.stage(plan.core)
        (grad_context,) = hold(grad_context)
        r_outer.stage(plan.x)
        r_inner.stage(plan.y)
        r_output.stage(plan.x)
        heads_p += [back(i, grad_context) for i in range(1, width // part)]
        dkp, dvp, dqp = [
            jnp.concatenate([h[i] for h in heads_p], 1 if i < 2 else 0) for i in range(3)
        ]
        shared_p = product_call(first_near, near, dkp, dvp, full_key, full_value, rows)
        grad_context, dqp, shared_p = hold(grad_context, dqp, shared_p)
        returned = Return(plan, rows)
        returned.prompt_one(shared_p)
        r_outer.stage(plan.y)
        r_inner.stage(plan.x)
        r_output.stage(plan.y)
        dkn, dvn, dq = back_call(
            0, width // part, None, near, grad_context, context, queries, keys_n, values_n, log_total,
            seg_own, seg_near, dqp,
        )
        shared_n = product_call(None, near, dkn, dvn, full_key, full_value, rows)
        d_query, d_both, grad_own, sums_qkv = weight_call(
            spots, first_near, near, own, dq, full_query, grad_h1, dkp, dvp, dkn, dvn
        )
        returned.prompt_two()
        d_query, d_both, shared_n, returned.same = hold(d_query, d_both, shared_n, returned.same)
        returned.prompt_three()
        returned.near(shared_n)
        for r in big:
            r.stage(plan.z)
        o_outer, o_inner, o_output = [r.value.reshape(r.lead + r.rest) for r in big]
        grad_tokens = grad_own + returned.total()

        order = (5, 3, 4, 2, 0, 1)
        d_table = jnp.concatenate([sums_qkv[:2]] + [sums[i : i + 1] for i in order], 0)
        d_lines = jnp.concatenate(
            [
                d_table.reshape(small, count, step).transpose(1, 0, 2).reshape(count, -1),
                sums_bin[:wide].reshape(count, wide * step),
            ],
            1,
        )
        d_lines = jnp.pad(d_lines, ((0, 0), (0, width - d_lines.shape[1])))[:, None].astype(BF)
        d_lines = jnp.pad(d_lines, ((0, 0), (0, 7), (0, 0)))
        r_query = Reduce(plan, jnp.concatenate([by_owner(d_query), d_lines], 1))
        r_both = Reduce(plan, by_owner(d_both))
        for one, two in ((plan.core, plan.core), (plan.x, plan.y), (plan.y, plan.x), (plan.z, plan.z)):
            r_query.stage(one)
            r_both.stage(two)
        o_query = r_query.value
        o_line = o_query[step]
        o_both = r_both.value.reshape(step, width // part, 2, part)

        o_small = [o_line[i * step : (i + 1) * step] for i in range(small)]
        o_bin = o_line[small * step : (small + wide) * step]
        return (
            layer_out[None],
            grad_tokens.astype(BF)[None],
            o_query[:step],
            o_both[:, :, 0].reshape(step, width),
            o_both[:, :, 1].reshape(step, width),
            o_output,
            o_inner.transpose(1, 0, 2).reshape(step, wide * width),
            o_outer,
            o_small[0],
            o_small[1],
            o_small[2],
            o_small[3],
            o_small[4],
            o_bin,
            o_small[5],
            o_small[6],
            o_small[7],
        )

    split = P("grp", "row", None)
    owned2, owned1 = P(AXES, None), P(AXES)
    in_specs = (split, P("grp", None), split) + (owned2,) * 6 + (owned1,) * 9
    out_specs = (split, split) + (owned2,) * 6 + (owned1,) * 9
    return jax.shard_map(
        per_device, mesh=mesh, in_specs=in_specs, out_specs=out_specs, check_vma=False
    )
```

```python
import functools

import jax
import jax.numpy as jnp
import numpy as np
from jax import lax
from jax.experimental import pallas as pl
from jax.experimental.pallas import tpu as pltpu
from jax.sharding import PartitionSpec as P

HEADS = 12
HDIM = 64
PROMPT = 1024
CONT_MOST = 256
BF = jnp.bfloat16
F32 = jnp.float32

NORM_EPS = 1e-12
MASK_FILL = -1000000000.0
SQRT_HALF = 0.7071067811865476
INV_ROOT_TAU = 0.3989422804014327
AXES = ("grp", "row")
WIDE = 4
WO, WI, WQ, WK, WV = 4, 5, 9, 10, 11


def mm(left, right):
    return jnp.dot(left, right, preferred_element_type=F32)


def segment_ids(lengths, group_len):
    ends = jnp.cumsum(lengths)
    places = jnp.arange(group_len, dtype=jnp.int32)
    passed = jnp.sum(((places - PROMPT)[:, None] >= ends[None, :]).astype(jnp.int32), axis=-1)
    return jnp.where(places < PROMPT, 0, 1 + passed)


class Plan:
    def __init__(self, grp, row):
        self.grp, self.row, self.count = grp, row, grp * row
        y = row // 4
        bits = lambda base, size: [base << i for i in range(size.bit_length() - 1)]
        self.y, self.z = bits(1, y), bits(y, 4)
        self.core, self.x = bits(row, 2), bits(2 * row, grp // 2)
        self.bits = self.count.bit_length() - 1

    def swap(self, value, mask):
        return lax.ppermute(value, AXES, [(i, i ^ mask) for i in range(self.count)])

    def send(self, value, moves):
        pairs = [(g * self.row + a, g * self.row + b) for g in range(self.grp) for a, b in moves]
        return lax.ppermute(value, AXES, pairs)

    def me(self):
        return lax.axis_index("grp") * self.row + lax.axis_index("row")


class Reduce:
    def __init__(self, plan, terms, left=None):
        self.plan, self.terms = plan, list(terms)
        self.left = left or [1 << i for i in reversed(range(plan.bits))]

    def cut(self, term, bit, place):
        at = self.left.index(bit)
        high, low = 1 << at, 1 << (len(self.left) - at - 1)
        _, rows, width = term.shape
        term = term.reshape(high, 2, low * rows, width)
        return lax.dynamic_slice_in_dim(term, place, 1, 1).reshape(high * low, rows, width)

    def total(self, terms):
        return sum([t.astype(F32) for t in terms[1:]], terms[0].astype(F32))

    def stage(self, bit):
        place = (self.plan.me() // bit) & 1
        away = self.total([self.cut(t, bit, 1 - place) for t in self.terms]).astype(BF)
        here = [self.cut(t, bit, place) for t in self.terms]
        self.left = [b for b in self.left if b != bit]
        self.terms = here + [self.plan.swap(away, bit)]

    def result(self):
        return self.total(self.terms)[0]


def tie(*values):
    return lax.optimization_barrier(values)


class Tokens:
    def __init__(self, plan, own):
        self.plan, self.own = plan, own
        self.rows = own.shape[0]
        self.ready = plan.row == 8

    def stage_one(self):
        if self.ready:
            plan, own = self.plan, self.own
            across = plan.send(own, [(0, 4), (1, 5), (2, 6), (3, 7)])
            self.same = jnp.where(lax.axis_index("row") < 4, own, across)
            self.beside = plan.swap(own, 1)
            return [self.same, self.beside]
        return []

    def stage_two(self):
        if self.ready:
            plan = self.plan
            self.other = plan.swap(self.same, 2)
            self.same_y = plan.swap(self.same, 1)
            self.diagonal = plan.send(self.own, [(5, 6), (6, 5)])
            return [self.other, self.same_y, self.diagonal]
        return []

    def stage_three(self):
        if self.ready:
            self.other_y = self.plan.swap(self.other, 1)

    def spots(self):
        row, rows, own = lax.axis_index("row"), self.rows, self.own
        if self.ready:
            near = jnp.where(row < 4, 0, jnp.where((row == 5) | (row == 6), 3, 2))
            return [
                self.same, self.other, self.same_y, self.other_y, own, self.beside, self.diagonal,
            ], near
        every = lax.all_gather(own, "row", axis=0, tiled=True)
        start = jnp.maximum(row * rows - CONT_MOST, 0)
        padded = jnp.concatenate([every, jnp.zeros((CONT_MOST, own.shape[1]), own.dtype)], 0)
        near = lax.dynamic_slice_in_dim(padded, start, rows + 2 * CONT_MOST, 0)
        every = jnp.concatenate([every[:PROMPT], near], 0)
        spots = [every[i : i + rows] for i in range(0, every.shape[0], rows)]
        return spots, jnp.where(row * rows < PROMPT, 0, near.shape[0] // rows)


def near_segments(plan, segments, rows):
    row = lax.axis_index("row")
    if plan.row != 8:
        start = jnp.maximum(row * rows - CONT_MOST, 0)
        padded = jnp.concatenate([segments, jnp.full((CONT_MOST,), -1, jnp.int32)], 0)
        near = lax.dynamic_slice_in_dim(padded, start, rows + 2 * CONT_MOST, 0)
        return jnp.where((near == 0) | (row * rows < PROMPT), -1, near)
    pieces = []
    for block, valid in (
        (row, row >= 4),
        (row ^ 1, row >= 4),
        (11 - row, (row == 5) | (row == 6)),
    ):
        block = jnp.clip(block, 0, 7)
        ids = lax.dynamic_slice_in_dim(segments, block * rows, rows, 0)
        pieces.append(jnp.where(valid, ids, -1))
    return jnp.concatenate(pieces, 0)


class Return:
    def __init__(self, plan, rows):
        self.plan, self.rows = plan, rows

    def prompt_one(self, parts):
        self.prompt = self.same = parts
        if self.plan.row == 8:
            same, other, same_y, other_y = [parts[i].astype(F32) for i in range(4)]
            self.other = (other + self.plan.swap(parts[3], 1).astype(F32)).astype(BF)
            self.same = same + self.plan.swap(parts[2], 1).astype(F32)

    def prompt_two(self):
        if self.plan.row == 8:
            self.same = self.same + self.plan.swap(self.other, 2).astype(F32)

    def prompt_three(self):
        if self.plan.row == 8:
            back = self.plan.send(self.same.astype(BF), [(4, 0), (5, 1), (6, 2), (7, 3)])
            self.same = self.same + back.astype(F32)

    def near(self, parts):
        self.around = parts
        if self.plan.row == 8:
            own = parts[0].astype(F32) + self.plan.swap(parts[1], 1).astype(F32)
            self.own = own + self.plan.send(parts[2], [(5, 6), (6, 5)]).astype(F32)

    def total(self):
        row, rows = lax.axis_index("row"), self.rows
        if self.plan.row == 8:
            return jnp.where(row < 4, self.same, self.own)
        around = self.around.reshape(-1, self.around.shape[-1]).astype(F32)
        start = jnp.maximum(row * rows - CONT_MOST, 0)
        whole = jnp.zeros((self.plan.row * rows + CONT_MOST, around.shape[1]), F32)
        whole = whole.at[:PROMPT].set(self.prompt.reshape(PROMPT, -1).astype(F32))
        near = jnp.where(row * rows < PROMPT, 0, around)
        near = lax.dynamic_slice_in_dim(whole, start, rows + 2 * CONT_MOST, 0) + near
        whole = lax.dynamic_update_slice_in_dim(whole, near, start, 0)
        return lax.psum_scatter(whole[: self.plan.row * rows], "row", scatter_dimension=0, tiled=True)


def heads_mask(lanes, head):
    lane = lax.broadcasted_iota(jnp.int32, lanes, 1)
    return (lane >= head * HDIM) & (lane < (head + 1) * HDIM)


def nt(left, right):
    return lax.dot_general(left, right, (((1,), (1,)), ((), ())), preferred_element_type=F32)


def tn(left, right):
    return lax.dot_general(left, right, (((0,), (0,)), ((), ())), preferred_element_type=F32)


def attention_kernel(blocks, first, rows, *refs):
    spots = refs[:blocks]
    (near_ref, own_ref, wq_ref, wk_ref, wv_ref, bq_ref, bv_ref, segq_ref, segk_ref,
     q_ref, kp_ref, vp_ref, kn_ref, vn_ref, ctx_ref, lse_ref, x_ref, s_ref, sems) = refs[blocks:]
    near = near_ref[0]
    at = lambda b: pl.ds(pl.multiple_of(b * rows, rows), rows)
    depth = own_ref.shape[1]
    wq, wk, wv = [ref[...].reshape(depth, -1) for ref in (wq_ref, wk_ref, wv_ref)]

    @pl.when(pl.program_id(0) == 0)
    def _():
        copies = [
            pltpu.make_async_copy(spot, x_ref.at[pl.ds(i * rows, rows)], sems.at[i])
            for i, spot in enumerate(spots)
        ]
        for copy in copies:
            copy.start()
        for copy in copies:
            copy.wait()

    queries = (mm(own_ref[...], wq) + bq_ref[...]) * (HDIM**-0.5)
    q_ref[...] = queries.astype(BF)

    def project(b, k_ref, v_ref, side):
        x = x_ref[at(b), :]
        k_ref[at(side), :] = mm(x, wk).astype(BF)
        v_ref[at(side), :] = (mm(x, wv) + bv_ref[...]).astype(BF)

    @pl.loop(0, first)
    def _(b):
        project(b, kp_ref, vp_ref, b)

    @pl.loop(0, near)
    def _(b):
        project(first + b, kn_ref, vn_ref, b)

    width = q_ref.shape[1]
    heads = width // HDIM
    q = q_ref[...]
    parts = [jnp.where(heads_mask(q.shape, h), q, 0) for h in range(heads)]

    def scores(b, peaks, k_ref, base):
        k = k_ref[at(b), :]
        out = []
        for h in range(heads):
            s = nt(k, parts[h])
            if base:
                s = jnp.where(segk_ref[at(b), :] == segq_ref[...], s, MASK_FILL)
            s_ref[h, at(base + b), :] = s
            out.append(jnp.maximum(peaks[h], jnp.max(s, axis=0, keepdims=True)))
        return tuple(out)

    peaks = tuple(jnp.full((1, rows), MASK_FILL, F32) for _ in range(heads))
    peaks = lax.fori_loop(0, first, lambda b, c: scores(b, c, kp_ref, 0), peaks)
    peaks = lax.fori_loop(0, near, lambda b, c: scores(b, c, kn_ref, first), peaks)

    def mix(b, carry, v_ref, base):
        totals, mixed = carry
        vt = v_ref[at(b), :].T
        new_totals, new_mixed = [], []
        for h in range(heads):
            p = jnp.exp(s_ref[h, at(base + b), :] - peaks[h])
            new_totals.append(totals[h] + jnp.sum(p, axis=0, keepdims=True))
            new_mixed.append(mixed[h] + mm(vt[h * HDIM : (h + 1) * HDIM], p.astype(BF)))
        return tuple(new_totals), tuple(new_mixed)

    zero = (
        tuple(jnp.zeros((1, rows), F32) for _ in range(heads)),
        tuple(jnp.zeros((HDIM, rows), F32) for _ in range(heads)),
    )
    carry = lax.fori_loop(0, first, lambda b, c: mix(b, c, vp_ref, 0), zero)
    totals, mixed = lax.fori_loop(0, near, lambda b, c: mix(b, c, vn_ref, first), carry)
    whole = jnp.concatenate([mixed[h] / totals[h] for h in range(heads)], 0)
    ctx_ref[...] = whole.T.astype(BF)
    for h in range(heads):
        lse_ref[0, h : h + 1, :] = peaks[h] + jnp.log(totals[h])


def attention_call(spots, first, near, own, got, bq, bv, segq, segk):
    rows, width = own.shape
    blocks = len(spots)
    tall = blocks * rows
    part = 256
    steps = width // part
    heads = part // HDIM
    cols = lambda depth: pl.BlockSpec((depth, part), lambda g: (0, g))
    flops = 2 * tall * width * width * 2 + 4 * tall * rows * width * 4
    owners, each = got.shape[0], width // got.shape[0]
    weight = lambda place: pl.BlockSpec((owners, each, part), lambda g: (0, place, g))
    return pl.pallas_call(
        functools.partial(attention_kernel, blocks, first, rows),
        grid=(steps,),
        in_specs=[pl.BlockSpec(memory_space=pl.ANY)] * blocks
        + [
            pl.BlockSpec(memory_space=pltpu.SMEM),
            pl.BlockSpec((rows, width), lambda g: (0, 0)),
            weight(WQ), weight(WK), weight(WV), cols(1), cols(1),
            pl.BlockSpec((1, rows), lambda g: (0, 0)),
            pl.BlockSpec(segk.shape, lambda g: (0, 0)),
        ],
        out_specs=[
            cols(rows), cols(PROMPT), cols(PROMPT), cols(tall - PROMPT), cols(tall - PROMPT),
            cols(rows), pl.BlockSpec((1, 8, rows), lambda g: (g, 0, 0)),
        ],
        out_shape=[
            jax.ShapeDtypeStruct((rows, width), BF),
            jax.ShapeDtypeStruct((PROMPT, width), BF),
            jax.ShapeDtypeStruct((PROMPT, width), BF),
            jax.ShapeDtypeStruct((tall - PROMPT, width), BF),
            jax.ShapeDtypeStruct((tall - PROMPT, width), BF),
            jax.ShapeDtypeStruct((rows, width), BF),
            jax.ShapeDtypeStruct((steps, 8, rows), F32),
        ],
        scratch_shapes=[
            pltpu.VMEM((tall, width), BF),
            pltpu.VMEM((heads, tall, rows), F32),
            pltpu.SemaphoreType.DMA((blocks,)),
        ],
        compiler_params=pltpu.CompilerParams(vmem_limit_bytes=60 * 2**20),
        cost_estimate=pl.CostEstimate(
            flops=flops, bytes_accessed=12 * 2**20, transcendentals=tall * rows * 12
        ),
        name="attention",
    )(*spots, near, own, got, got, got, bq, bv, segq, segk)


def halves(value, runs, core):
    depth = value.shape[0] // runs
    pick = lambda first: jnp.concatenate(
        [value[i * depth : (i + 1) * depth] for i in range(first, runs, 2)], 0
    )
    even, odd = pick(0), pick(1)
    return jnp.where(core == 0, odd, even), jnp.where(core == 0, even, odd)


def middle_kernel(wide, runs, core_ref, ctx_ref, own_ref, cot_ref, wo_ref, wi_ref, wu_ref, vec_ref, bin_ref,
                  out_ref, h1_ref, gctx_ref, a_send, a_keep, b_send, b_keep, sums_ref, sbin_ref,
                  first_ref, n1_ref, inv_ref, low_ref, pre_ref, cdf_ref, act_ref, acc_ref,
                  gffn_ref, glow_ref, out_buf, wo_buf, sems):
    step = pl.program_id(0)
    width = ctx_ref.shape[1]
    square = lambda ref: ref[...].reshape(width, width)
    vec = lambda i: vec_ref[i : i + 1, :]
    mean = lambda v: jnp.sum(v, axis=-1, keepdims=True) * (1.0 / width)
    down = lambda v: jnp.sum(v, axis=0, keepdims=True)
    core = core_ref[0]
    owners = wi_ref.shape[0]
    each = width // owners
    run = owners // runs

    def put(source, runs_here, base, top, sem, act):
        size = source.shape[0] // runs_here
        for i in range(runs_here):
            number = base + i
            place = pl.ds(number // 2 * run, run)
            rows_here = source.shape[1]

            @pl.when(number % 2 == core)
            def _():
                act(pltpu.make_async_copy(
                    source.at[pl.ds(i * size, size)], a_keep.at[place, pl.ds(top, rows_here)], sem.at[i]
                ))

            @pl.when(number % 2 != core)
            def _():
                act(pltpu.make_async_copy(
                    source.at[pl.ds(i * size, size)], a_send.at[place, pl.ds(top, rows_here)], sem.at[i]
                ))

    @pl.when(step == 0)
    def _():
        hidden = own_ref[...].astype(F32) + mm(ctx_ref[...], square(wo_ref)) + vec(0)
        centred = hidden - mean(hidden)
        inverse = lax.rsqrt(mean(centred * centred) + NORM_EPS)
        normed = centred * inverse
        n1_ref[...] = normed
        inv_ref[...] = inverse
        first = normed * vec(1) + vec(2)
        first_ref[...] = first
        low_ref[...] = first.astype(BF)

    @pl.when(step < wide)
    def _():
        chunk = pl.ds(pl.multiple_of(step * width, width), width)
        pre = mm(low_ref[...], square(wi_ref)) + bin_ref[pl.ds(step, 1), :]
        cdf = 0.5 * (1.0 + lax.erf(pre * SQRT_HALF))
        act = (pre * cdf).astype(BF)
        pre_ref[:, chunk] = pre
        cdf_ref[:, chunk] = cdf
        act_ref[:, chunk] = act
        more = mm(act, square(wu_ref))

        @pl.when(step == 0)
        def _():
            acc_ref[...] = more

        @pl.when(step > 0)
        def _():
            acc_ref[...] += more

    @pl.when(step == wide - 1)
    def _():
        hidden = first_ref[...] + acc_ref[...] + vec(3)
        centred = hidden - mean(hidden)
        inverse = lax.rsqrt(mean(centred * centred) + NORM_EPS)
        normed = centred * inverse
        out_ref[...] = (normed * vec(4) + vec(5)).astype(BF)
        grad = cot_ref[...].astype(F32)
        sums_ref[0:1, :] = down(grad * normed)
        sums_ref[1:2, :] = down(grad)
        e = grad * vec(4)
        back = inverse * (e - mean(e) - normed * mean(e * normed))
        gffn_ref[...] = back
        low = back.astype(BF)
        glow_ref[...] = low
        sums_ref[2:3, :] = down(low.astype(F32))

    @pl.when(step >= wide)
    def _():
        at = 2 * wide - 1 - step
        chunk = pl.ds(pl.multiple_of(at * width, width), width)
        pre = pre_ref[:, chunk]
        slope = cdf_ref[:, chunk] + pre * jnp.exp(-0.5 * pre * pre) * INV_ROOT_TAU
        low = glow_ref[...]
        grad = (nt(low, square(wu_ref)) * slope).astype(BF)
        sbin_ref[pl.ds(at, 1), :] = down(grad.astype(F32))
        turn = step % 2
        chunk_runs = runs // wide
        outer = lambda which, at, act: put(
            out_buf.at[which], chunk_runs, at * chunk_runs, 0, sems.at[which], act
        )

        @pl.when(step >= wide + 2)
        def _():
            outer(turn, at + 2, lambda c: c.wait())

        d_outer = tn(act_ref[:, chunk], low).astype(BF)
        out_buf[turn] = d_outer.reshape(owners // wide, wide * each, width)
        outer(turn, at, lambda c: c.start())
        away, here = halves(tn(low_ref[...], grad).astype(BF), runs, core)
        b_send[...] = away.reshape(owners // 2, each, width)
        b_keep[...] = here.reshape(owners // 2, each, width)
        gffn_ref[...] += nt(grad, square(wi_ref))

    @pl.when(step == 2 * wide - 1)
    def _():
        grad = gffn_ref[...]
        normed = n1_ref[...]
        sums_ref[3:4, :] = down(grad * normed)
        sums_ref[4:5, :] = down(grad)
        e = grad * vec(1)
        back = inv_ref[...] * (e - mean(e) - normed * mean(e * normed))
        h1_ref[...] = back
        low = back.astype(BF)
        sums_ref[5:6, :] = down(low.astype(F32))
        wo_buf[...] = tn(ctx_ref[...], low).astype(BF).reshape(owners, each, width)
        put(wo_buf, runs, 0, wide * each, sems.at[2], lambda c: c.start())
        gctx = nt(low, square(wo_ref)).astype(BF)
        gctx_ref[...] = gctx
        sums_ref[6:7, :] = down(gctx.astype(F32))
        sums_ref[7:8, :] = jnp.zeros((1, width), F32)
        chunk_runs = runs // wide
        for at in (1, 0):
            put(out_buf.at[(2 * wide - 1 - at) % 2], chunk_runs, at * chunk_runs, 0,
                sems.at[(2 * wide - 1 - at) % 2], lambda c: c.wait())
        put(wo_buf, runs, 0, wide * each, sems.at[2], lambda c: c.wait())


def middle_call(ctx, own, cot, got, vec, b_inner, core, runs):
    rows, width = own.shape
    owners = got.shape[0]
    each = width // owners
    wide = WIDE
    half = owners // 2
    whole = lambda shape: pl.BlockSpec(shape, lambda s: (0,) * len(shape))
    at = lambda s: jnp.where(s < wide, s, 2 * wide - 1 - s)
    back = lambda s: jnp.where(s < wide, wide - 1, 2 * wide - 1 - s)
    shape = jax.ShapeDtypeStruct
    return pl.pallas_call(
        functools.partial(middle_kernel, wide, runs),
        grid=(2 * wide,),
        in_specs=[
            pl.BlockSpec(memory_space=pltpu.SMEM),
            whole((rows, width)), whole((rows, width)), whole((rows, width)),
            pl.BlockSpec((owners, each, width), lambda s: (0, WO, 0)),
            pl.BlockSpec((owners, each, width), lambda s: (0, WI + at(s), 0)),
            pl.BlockSpec((owners // wide, wide * each, width), lambda s: (at(s), 0, 0)),
            whole((8, width)), whole((8, width)),
        ],
        out_specs=[
            whole((rows, width)), whole((rows, width)), whole((rows, width)),
            pl.BlockSpec(memory_space=pl.ANY), pl.BlockSpec(memory_space=pl.ANY),
            pl.BlockSpec((half, each, width), lambda s: (0, back(s), 0)),
            pl.BlockSpec((half, each, width), lambda s: (0, back(s), 0)),
            whole((8, width)), whole((8, width)),
        ],
        out_shape=[
            shape((rows, width), BF), shape((rows, width), F32), shape((rows, width), BF),
            shape((half, (wide + 1) * each, width), BF), shape((half, (wide + 1) * each, width), BF),
            shape((half, wide * each, width), BF), shape((half, wide * each, width), BF),
            shape((8, width), F32), shape((8, width), F32),
        ],
        scratch_shapes=[
            pltpu.VMEM((rows, width), F32), pltpu.VMEM((rows, width), F32), pltpu.VMEM((rows, 1), F32),
            pltpu.VMEM((rows, width), BF), pltpu.VMEM((rows, wide * width), F32),
            pltpu.VMEM((rows, wide * width), F32), pltpu.VMEM((rows, wide * width), BF),
            pltpu.VMEM((rows, width), F32), pltpu.VMEM((rows, width), F32),
            pltpu.VMEM((rows, width), BF),
            pltpu.VMEM((2, owners // wide, wide * each, width), BF),
            pltpu.VMEM((owners, each, width), BF), pltpu.SemaphoreType.DMA((3, runs)),
        ],
        compiler_params=pltpu.CompilerParams(vmem_limit_bytes=60 * 2**20),
        cost_estimate=pl.CostEstimate(
            flops=2 * rows * width * width * (6 * wide + 3), bytes_accessed=32 * 2**20,
            transcendentals=2 * rows * width * wide,
        ),
        name="middle",
    )(core, ctx, own, cot, got, got, got, vec, b_inner)


def back_kernel(rows, bound, started, *refs):
    near_ref, gctx_ref, ctx_ref, q_ref, k_ref, v_ref, lse_ref, segq_ref, segk_ref = refs[:9]
    dk_ref, dv_ref, dq_ref = refs[-3:]
    q, g = q_ref[...], gctx_ref[...]
    part = q.shape[1]
    heads = part // HDIM
    masks = [heads_mask(q.shape, h) for h in range(heads)]
    q_parts = [jnp.where(m, q, 0) for m in masks]
    g_parts = [jnp.where(m, g, 0) for m in masks]
    product = (g.astype(F32) * ctx_ref[...].astype(F32)).T
    inner = [
        jnp.sum(product[h * HDIM : (h + 1) * HDIM], axis=0, keepdims=True) for h in range(heads)
    ]

    def one(b, dq):
        here = pl.ds(pl.multiple_of(b * rows, rows), rows)
        k, v = k_ref[here, :], v_ref[here, :]
        kt = k.T
        if bound is None:
            allowed = segk_ref[here, :] == segq_ref[...]
        dk = jnp.zeros((rows, part), F32)
        dv = jnp.zeros((rows, part), F32)
        out = []
        for h in range(heads):
            s = nt(k, q_parts[h])
            if bound is None:
                s = jnp.where(allowed, s, MASK_FILL)
            p = jnp.exp(s - lse_ref[0, h : h + 1, :])
            dp = nt(v, g_parts[h])
            ds = (p * (dp - inner[h])).astype(BF)
            dv = dv + mm(p.astype(BF), g_parts[h])
            dk = dk + mm(ds, q_parts[h])
            out.append(dq[h] + mm(kt[h * HDIM : (h + 1) * HDIM], ds))
        dk_ref[here, :] = dk.astype(BF)
        dv_ref[here, :] = dv.astype(BF)
        return tuple(out)

    if started:
        dq = tuple(refs[9][h * HDIM : (h + 1) * HDIM, :] for h in range(heads))
    else:
        dq = tuple(jnp.zeros((HDIM, rows), F32) for _ in range(heads))
    dq = lax.fori_loop(0, near_ref[0] if bound is None else bound, one, dq)
    dq_ref[...] = jnp.concatenate(dq, 0)


def back_call(start, steps, bound, near, gctx, ctx, q, k, v, lse, segq, segk, dq0=None, into=None):
    rows, width = q.shape
    tall = k.shape[0]
    part = 256
    cols = lambda depth: pl.BlockSpec((depth, part), lambda g: (0, start + g))
    whole = lambda shape: pl.BlockSpec(shape, lambda g: (0,) * len(shape))
    down = pl.BlockSpec((part, rows), lambda g: (start + g, 0))
    shape = jax.ShapeDtypeStruct
    extra = ([dq0] if dq0 is not None else []) + list(into or [])
    specs = ([down] if dq0 is not None else []) + [pl.BlockSpec(memory_space=pl.ANY)] * len(into or [])
    return pl.pallas_call(
        functools.partial(back_kernel, rows, bound, dq0 is not None),
        grid=(steps,),
        in_specs=[
            pl.BlockSpec(memory_space=pltpu.SMEM),
            cols(rows), cols(rows), cols(rows), cols(tall), cols(tall),
            pl.BlockSpec((1, 8, rows), lambda g: (start + g, 0, 0)),
            whole((1, rows)), whole(segk.shape),
        ] + specs,
        out_specs=[cols(tall), cols(tall), down],
        out_shape=[shape((tall, width), BF), shape((tall, width), BF), shape((width, rows), F32)],
        input_output_aliases={9 + i: i for i in range(3)} if into else {},
        compiler_params=pltpu.CompilerParams(vmem_limit_bytes=60 * 2**20),
        cost_estimate=pl.CostEstimate(
            flops=2 * 10 * 2 * tall * rows * part * steps * 2,
            bytes_accessed=8 * tall * part * steps, transcendentals=tall * rows * 4 * steps,
        ),
        name="attention_back",
    )(near, gctx, ctx, q, k, v, lse, segq, segk, *extra)


def product_kernel(rows, bound, near_ref, dk_ref, dv_ref, wk_ref, wv_ref, gx_ref):
    @pl.when((pl.program_id(0) < near_ref[0]) | (bound is not None))
    def _():
        width = dk_ref.shape[1]
        wk, wv = wk_ref[...].reshape(width, width), wv_ref[...].reshape(width, width)
        gx_ref[0] = (nt(dk_ref[...], wk) + nt(dv_ref[...], wv)).astype(BF)


def product_call(bound, near, dk, dv, got, rows):
    tall, width = dk.shape
    owners, each = got.shape[0], width // got.shape[0]
    weight = lambda place: pl.BlockSpec((owners, each, width), lambda b: (0, place, 0))
    return pl.pallas_call(
        functools.partial(product_kernel, rows, bound),
        grid=(tall // rows,),
        in_specs=[
            pl.BlockSpec(memory_space=pltpu.SMEM),
            pl.BlockSpec((rows, width), lambda b: (b, 0)),
            pl.BlockSpec((rows, width), lambda b: (b, 0)),
            weight(WK), weight(WV),
        ],
        out_specs=pl.BlockSpec((1, rows, width), lambda b: (b, 0, 0)),
        out_shape=jax.ShapeDtypeStruct((tall // rows, rows, width), BF),
        compiler_params=pltpu.CompilerParams(vmem_limit_bytes=60 * 2**20),
        cost_estimate=pl.CostEstimate(
            flops=4 * tall * width * width, bytes_accessed=6 * tall * width, transcendentals=0
        ),
        name="token_product",
    )(near, dk, dv, got, got)


def weight_kernel(blocks, first, rows, runs, *refs):
    spots = refs[:blocks]
    (near_ref, core_ref, own_ref, dq_ref, wq_ref, h1_ref, dkp_ref, dvp_ref, dkn_ref, dvn_ref,
     q_send, q_keep, kv_send, kv_keep, gown_ref, sums_ref, x_ref, sems) = refs[blocks:]
    core = core_ref[0]
    at = lambda b: pl.ds(pl.multiple_of(b * rows, rows), rows)
    step = pl.program_id(0)

    @pl.when(step == 0)
    def _():
        copies = [
            pltpu.make_async_copy(spot, x_ref.at[pl.ds(i * rows, rows)], sems.at[i])
            for i, spot in enumerate(spots)
        ]
        for copy in copies:
            copy.start()
        for copy in copies:
            copy.wait()
        gown_ref[...] = h1_ref[...]

    scale = HDIM**-0.5
    dq = dq_ref[...].T.astype(BF)
    part = dq.shape[1]
    width = x_ref.shape[1]
    gown_ref[...] += nt(dq, wq_ref[...].reshape(width, part)) * scale
    away, here = halves((tn(own_ref[...], dq) * scale).astype(BF), runs, core)
    q_send[...] = away.reshape(q_send.shape)
    q_keep[...] = here.reshape(q_send.shape)
    sums_ref[0:1, :] = jnp.sum(dq.astype(F32), axis=0, keepdims=True) * scale

    def products(b, carry, dk_ref, dv_ref, base):
        dk, dv, x = dk_ref[at(b), :], dv_ref[at(b), :], x_ref[at(base + b), :]
        wk, wv = carry
        return wk + tn(x, dk), wv + tn(x, dv)

    zero = jnp.zeros((width, part), F32)
    carry = (zero, zero)
    carry = lax.fori_loop(0, first, lambda b, c: products(b, c, dkp_ref, dvp_ref, 0), carry)
    carry = lax.fori_loop(0, near_ref[0], lambda b, c: products(b, c, dkn_ref, dvn_ref, first), carry)
    for i, grad in enumerate(carry):
        away, here = halves(grad.astype(BF), runs, core)
        shape = kv_send.shape[:2] + (part,)
        kv_send[:, :, i * part : (i + 1) * part] = away.reshape(shape)
        kv_keep[:, :, i * part : (i + 1) * part] = here.reshape(shape)
    sums_ref[1:8, :] = jnp.zeros((7, part), F32)


def weight_call(spots, first, near, own, dq, got, h1, dkp, dvp, dkn, dvn, core, runs):
    rows, width = own.shape
    blocks = len(spots)
    tall = blocks * rows
    part = 256
    steps = width // part
    cols = lambda depth, size=part: pl.BlockSpec((depth, size), lambda g: (0, g))
    whole = lambda shape: pl.BlockSpec(shape, lambda g: (0,) * len(shape))
    shape = jax.ShapeDtypeStruct
    owners, each = got.shape[0], width // got.shape[0]
    half = owners // 2
    slab = lambda size: pl.BlockSpec((half, each, size), lambda g: (0, 0, g))
    return pl.pallas_call(
        functools.partial(weight_kernel, blocks, first, rows, runs),
        grid=(steps,),
        in_specs=[pl.BlockSpec(memory_space=pl.ANY)] * blocks
        + [
            pl.BlockSpec(memory_space=pltpu.SMEM),
            pl.BlockSpec(memory_space=pltpu.SMEM),
            whole((rows, width)), pl.BlockSpec((part, rows), lambda g: (g, 0)),
            pl.BlockSpec((owners, each, part), lambda g: (0, WQ, g)),
            whole((rows, width)), cols(PROMPT), cols(PROMPT), cols(tall - PROMPT), cols(tall - PROMPT),
        ],
        out_specs=[
            slab(part), slab(part), slab(2 * part), slab(2 * part), whole((rows, width)), cols(8),
        ],
        out_shape=[
            shape((half, each, width), BF), shape((half, each, width), BF),
            shape((half, each, 2 * width), BF), shape((half, each, 2 * width), BF),
            shape((rows, width), F32), shape((8, width), F32),
        ],
        scratch_shapes=[pltpu.VMEM((tall, width), BF), pltpu.SemaphoreType.DMA((blocks,))],
        compiler_params=pltpu.CompilerParams(vmem_limit_bytes=60 * 2**20),
        cost_estimate=pl.CostEstimate(
            flops=4 * tall * width * width, bytes_accessed=12 * tall * width, transcendentals=0
        ),
        name="weight_product",
    )(*spots, near, core, own, dq, got, h1, dkp, dvp, dkn, dvn)


def real_owners(half, count, step, width):
    split = count // 32
    take = lambda v, n: v.reshape(16, n, split, step, width).transpose(0, 2, 1, 3, 4)
    outer, rest = half[:, : 4 * split * step], half[:, 4 * split * step :]
    if rest.shape[1]:
        pieces = [outer.reshape(16 * split, 4 * step, width), rest.reshape(16 * split, step, width)]
        return jnp.concatenate(pieces, 1)
    return take(outer, 4).reshape(16 * split, 4 * step, width)


def solution(mesh):
    plan = Plan(mesh.shape["grp"], mesh.shape["row"])

    def per_device(
        tokens, cont_lengths, cotangent, w_query, w_key, w_value, w_output, w_inner, w_outer,
        bias_query, bias_value, bias_output, gain_first, shift_first, bias_inner, bias_outer,
        gain_second, shift_second,
    ):
        count = plan.count
        _, rows, width = tokens.shape
        step = w_query.shape[0]
        wide = w_inner.shape[1] // width
        row = lax.axis_index("row")
        scale = HDIM ** (-0.5)
        own = tokens[0]

        vectors = (
            bias_query, bias_value, bias_output, gain_first, shift_first, bias_outer, gain_second,
            shift_second, bias_inner,
        )
        small = len(vectors) - 1
        line, place = 0, 0
        for vector in vectors:
            size = vector.shape[0]
            line = line + jnp.pad(vector, (place, width - place - size))
            place += size
        line = jnp.pad(line[None], ((0, 7), (0, 0)))
        inner_rows = [w_inner[:, i * width : (i + 1) * width] for i in range(wide)]
        pack = jnp.concatenate([w_outer, w_output, *inner_rows, w_query, w_key, w_value, line], 0)
        got = lax.all_gather(pack, AXES, axis=0, tiled=True).reshape(count, -1, width)
        lines = got[:, 12 * step]
        if step % 8:
            cuts = [wide * step, (wide + 1) * step, (2 * wide + 1) * step, 12 * step]
            outer, output, inner, rest, _ = jnp.split(got, cuts, axis=1)
            apart = lambda v, n: v.reshape(count, n, step, width).transpose(1, 0, 2, 3)
            inner, rest = [
                v.reshape(v.shape[0], 32, width // 32, width).transpose(1, 0, 2, 3)
                for v in (apart(inner, wide), apart(rest, 3))
            ]
            got = jnp.concatenate(
                [v.reshape(32, -1, width) for v in (outer, output, inner, rest)], 1
            )
        runs = plan.grp
        core = (lax.axis_index("grp") % 2).astype(jnp.int32).reshape(1)

        exchange = Tokens(plan, own)
        exchange.stage_one()
        exchange.stage_two()
        exchange.stage_three()
        spots, near = exchange.spots()
        first_near = PROMPT // rows

        table = lines[:, : small * step].reshape(count, small, step).transpose(1, 0, 2)
        table = table.reshape(small, width).astype(F32)
        v_bin = lines[:, small * step : (small + wide) * step].reshape(wide, width).astype(F32)
        v_bin = jnp.pad(v_bin, ((0, 8 - wide), (0, 0)))
        segments = segment_ids(cont_lengths[0], plan.row * rows)
        seg_own = lax.dynamic_slice_in_dim(segments, row * rows, rows, 0)[None, :]
        seg_near = near_segments(plan, segments, rows)[:, None]
        near = near.astype(jnp.int32).reshape(1)

        queries, keys_p, values_p, keys_n, values_n, context, log_total = attention_call(
            spots, first_near, near, own, got, table[0:1], table[1:2], seg_own, seg_near
        )
        vec = jnp.concatenate([table[2:], jnp.zeros((2, width), F32)], 0)
        layer_out, grad_h1, grad_context, a_send, a_keep, b_send, b_keep, sums, sums_bin = middle_call(
            context, own, cotangent[0], got, vec, v_bin, core, runs
        )
        if step % 8:
            a_send, a_keep, b_send, b_keep = [
                real_owners(v, count, step, width) for v in (a_send, a_keep, b_send, b_keep)
            ]
        core_bit = plan.core[0]
        left = [1 << i for i in reversed(range(plan.bits)) if 1 << i != core_bit]
        back = lambda start, gctx, into: back_call(
            start, 1, first_near, near, gctx, context, queries, keys_p, values_p, log_total,
            seg_own, seg_near, None, into,
        )
        parts = width // 256
        a_got, b_got = plan.swap(a_send, core_bit), plan.swap(b_send, core_bit)
        into = back(0, grad_context, None)
        a_keep, a_got, b_keep, b_got, grad_context = tie(a_keep, a_got, b_keep, b_got, grad_context)
        r_a, r_b = Reduce(plan, [a_keep, a_got], left), Reduce(plan, [b_keep, b_got], left)

        def stages(reduce, bits):
            for bit in bits:
                reduce.stage(bit)

        def hold(*values):
            n, m = len(r_a.terms), len(r_b.terms)
            tied = tie(*r_a.terms, *r_b.terms, *values)
            r_a.terms, r_b.terms = list(tied[:n]), list(tied[n : n + m])
            return tied[n + m :]

        stages(r_a, plan.x)
        stages(r_b, plan.y)
        for i in range(1, parts):
            into = back(i, grad_context, into)
        dkp, dvp, dqp = into
        shared_p = product_call(first_near, near, dkp, dvp, got, rows)
        returned = Return(plan, rows)
        returned.prompt_one(shared_p)
        dkn, dvn, dq = back_call(
            0, parts, None, near, grad_context, context, queries, keys_n, values_n, log_total,
            seg_own, seg_near, dqp,
        )
        dkn, dvn, dq = hold(dkn, dvn, dq)
        stages(r_a, plan.y)
        stages(r_b, plan.x)
        shared_n = product_call(None, near, dkn, dvn, got, rows)
        returned.near(shared_n)
        returned.prompt_two()
        q_send, q_keep, kv_send, kv_keep, grad_own, sums_qkv = weight_call(
            spots, first_near, near, own, dq, got, grad_h1, dkp, dvp, dkn, dvn, core, runs
        )
        q_send, q_keep, kv_send, kv_keep = hold(q_send, q_keep, kv_send, kv_keep)
        returned.prompt_three()
        stages(r_a, plan.z[::-1])
        stages(r_b, plan.z[::-1])
        o_a, o_b = r_a.result(), r_b.result()
        grad_tokens = grad_own + returned.total()

        order = (6, 5, 3, 4, 2, 0, 1)
        d_table = jnp.concatenate([sums_qkv[:1]] + [sums[i : i + 1] for i in order], 0)
        d_lines = jnp.concatenate(
            [
                d_table.reshape(small, count, step).transpose(1, 0, 2).reshape(count, -1),
                sums_bin[:wide].reshape(count, wide * step),
            ],
            1,
        )
        d_lines = jnp.pad(d_lines, ((0, 0), (0, width - d_lines.shape[1])))[:, None].astype(BF)
        d_lines = jnp.pad(d_lines, ((0, 0), (0, 7), (0, 0)))
        place = core[0]
        pick = Reduce(plan, [])
        if step % 8:
            q_send, q_keep, kv_send, kv_keep = [
                v.reshape(count // 2, step, -1) for v in (q_send, q_keep, kv_send, kv_keep)
            ]
        q_send = jnp.concatenate([q_send, pick.cut(d_lines, core_bit, 1 - place)], 1)
        q_keep = jnp.concatenate([q_keep, pick.cut(d_lines, core_bit, place)], 1)
        r_q = Reduce(plan, [q_keep, plan.swap(q_send, core_bit)], left)
        r_kv = Reduce(plan, [kv_keep, plan.swap(kv_send, core_bit)], left)
        stages(r_q, plan.x + plan.y + plan.z[::-1])
        stages(r_kv, plan.y + plan.x + plan.z[::-1])
        o_query = r_q.result()
        o_line = o_query[step]
        o_both = r_kv.result().reshape(step, parts, 2, width // parts)

        o_small = [o_line[i * step : (i + 1) * step] for i in range(small)]
        o_bin = o_line[small * step : (small + wide) * step]
        return (
            layer_out[None],
            grad_tokens.astype(BF)[None],
            o_query[:step],
            o_both[:, :, 0].reshape(step, width),
            o_both[:, :, 1].reshape(step, width),
            o_a[wide * step :],
            o_b.reshape(wide, step, width).transpose(1, 0, 2).reshape(step, wide * width),
            o_a[: wide * step],
            o_small[0],
            o_small[1],
            o_small[2],
            o_small[3],
            o_small[4],
            o_bin,
            o_small[5],
            o_small[6],
            o_small[7],
        )

    split = P("grp", "row", None)
    owned2, owned1 = P(AXES, None), P(AXES)
    in_specs = (split, P("grp", None), split) + (owned2,) * 6 + (owned1,) * 9
    out_specs = (split, split) + (owned2,) * 6 + (owned1,) * 9
    return jax.shard_map(
        per_device, mesh=mesh, in_specs=in_specs, out_specs=out_specs, check_vma=False
    )
```

```python
import functools

import jax
import jax.numpy as jnp
import numpy as np
from jax import lax
from jax.experimental import pallas as pl
from jax.experimental.pallas import tpu as pltpu
from jax.sharding import PartitionSpec as P

HEADS = 12
HDIM = 64
PROMPT = 1024
CONT_MOST = 256
BF = jnp.bfloat16
F32 = jnp.float32

NORM_EPS = 1e-12
MASK_FILL = -1000000000.0
SQRT_HALF = 0.7071067811865476
INV_ROOT_TAU = 0.3989422804014327
AXES = ("grp", "row")
WIDE = 4
WO, WI, WQ, WK, WV = 4, 5, 9, 10, 11


def mm(left, right):
    return jnp.dot(left, right, preferred_element_type=F32)


def segment_ids(lengths, group_len):
    ends = jnp.cumsum(lengths)
    places = jnp.arange(group_len, dtype=jnp.int32)
    passed = jnp.sum(((places - PROMPT)[:, None] >= ends[None, :]).astype(jnp.int32), axis=-1)
    return jnp.where(places < PROMPT, 0, 1 + passed)


class Plan:
    def __init__(self, grp, row):
        self.grp, self.row, self.count = grp, row, grp * row
        y = row // 4
        bits = lambda base, size: [base << i for i in range(size.bit_length() - 1)]
        self.y, self.z = bits(1, y), bits(y, 4)
        self.core, self.x = bits(row, 2), bits(2 * row, grp // 2)
        self.bits = self.count.bit_length() - 1

    def swap(self, value, mask):
        return lax.ppermute(value, AXES, [(i, i ^ mask) for i in range(self.count)])

    def send(self, value, moves):
        pairs = [(g * self.row + a, g * self.row + b) for g in range(self.grp) for a, b in moves]
        return lax.ppermute(value, AXES, pairs)

    def me(self):
        return lax.axis_index("grp") * self.row + lax.axis_index("row")


class Reduce:
    def __init__(self, plan, terms, left=None):
        self.plan, self.terms = plan, list(terms)
        self.left = left or [1 << i for i in reversed(range(plan.bits))]

    def cut(self, term, bit, place):
        at = self.left.index(bit)
        high, low = 1 << at, 1 << (len(self.left) - at - 1)
        _, rows, width = term.shape
        term = term.reshape(high, 2, low * rows, width)
        return lax.dynamic_slice_in_dim(term, place, 1, 1).reshape(high * low, rows, width)

    def total(self, terms):
        return sum([t.astype(F32) for t in terms[1:]], terms[0].astype(F32))

    def stage(self, bit):
        place = (self.plan.me() // bit) & 1
        away = self.total([self.cut(t, bit, 1 - place) for t in self.terms]).astype(BF)
        here = [self.cut(t, bit, place) for t in self.terms]
        self.left = [b for b in self.left if b != bit]
        self.terms = here + [self.plan.swap(away, bit)]

    def result(self):
        return self.total(self.terms)[0]


def tie(*values):
    return lax.optimization_barrier(values)


class Tokens:
    def __init__(self, plan, own):
        self.plan, self.own = plan, own
        self.rows = own.shape[0]
        self.ready = plan.row == 8

    def stage_one(self):
        if self.ready:
            plan, own = self.plan, self.own
            across = plan.send(own, [(0, 4), (1, 5), (2, 6), (3, 7)])
            self.same = jnp.where(lax.axis_index("row") < 4, own, across)
            self.beside = plan.swap(own, 1)
            return [self.same, self.beside]
        return []

    def stage_two(self):
        if self.ready:
            plan = self.plan
            self.other = plan.swap(self.same, 2)
            self.same_y = plan.swap(self.same, 1)
            self.diagonal = plan.send(self.own, [(5, 6), (6, 5)])
            return [self.other, self.same_y, self.diagonal]
        return []

    def stage_three(self):
        if self.ready:
            self.other_y = self.plan.swap(self.other, 1)

    def spots(self):
        row, rows, own = lax.axis_index("row"), self.rows, self.own
        if self.ready:
            near = jnp.where(row < 4, 0, jnp.where((row == 5) | (row == 6), 3, 2))
            return [
                self.same, self.other, self.same_y, self.other_y, own, self.beside, self.diagonal,
            ], near
        every = lax.all_gather(own, "row", axis=0, tiled=True)
        start = jnp.maximum(row * rows - CONT_MOST, 0)
        padded = jnp.concatenate([every, jnp.zeros((CONT_MOST, own.shape[1]), own.dtype)], 0)
        near = lax.dynamic_slice_in_dim(padded, start, rows + 2 * CONT_MOST, 0)
        every = jnp.concatenate([every[:PROMPT], near], 0)
        spots = [every[i : i + rows] for i in range(0, every.shape[0], rows)]
        return spots, jnp.where(row * rows < PROMPT, 0, near.shape[0] // rows)


def near_segments(plan, segments, rows):
    row = lax.axis_index("row")
    if plan.row != 8:
        start = jnp.maximum(row * rows - CONT_MOST, 0)
        padded = jnp.concatenate([segments, jnp.full((CONT_MOST,), -1, jnp.int32)], 0)
        near = lax.dynamic_slice_in_dim(padded, start, rows + 2 * CONT_MOST, 0)
        return jnp.where((near == 0) | (row * rows < PROMPT), -1, near)
    pieces = []
    for block, valid in (
        (row, row >= 4),
        (row ^ 1, row >= 4),
        (11 - row, (row == 5) | (row == 6)),
    ):
        block = jnp.clip(block, 0, 7)
        ids = lax.dynamic_slice_in_dim(segments, block * rows, rows, 0)
        pieces.append(jnp.where(valid, ids, -1))
    return jnp.concatenate(pieces, 0)


class Return:
    def __init__(self, plan, rows):
        self.plan, self.rows = plan, rows

    def prompt_one(self, parts):
        self.prompt = self.same = self.own = self.back = parts
        if self.plan.row == 8:
            same, other, same_y, other_y = [parts[i].astype(F32) for i in range(4)]
            self.other = (other + self.plan.swap(parts[3], 1).astype(F32)).astype(BF)
            self.same = same + self.plan.swap(parts[2], 1).astype(F32)

    def prompt_two(self):
        if self.plan.row == 8:
            self.same = self.same + self.plan.swap(self.other, 2).astype(F32)

    def prompt_three(self):
        if self.plan.row == 8:
            self.back = self.plan.send(self.same.astype(BF), [(4, 0), (5, 1), (6, 2), (7, 3)])

    def near(self, parts):
        self.around = parts
        if self.plan.row == 8:
            own = parts[0].astype(F32) + self.plan.swap(parts[1], 1).astype(F32)
            self.own = own + self.plan.send(parts[2], [(5, 6), (6, 5)]).astype(F32)

    def total(self):
        row, rows = lax.axis_index("row"), self.rows
        if self.plan.row == 8:
            return jnp.where(row < 4, self.same + self.back.astype(F32), self.own)
        around = self.around.reshape(-1, self.around.shape[-1]).astype(F32)
        start = jnp.maximum(row * rows - CONT_MOST, 0)
        whole = jnp.zeros((self.plan.row * rows + CONT_MOST, around.shape[1]), F32)
        whole = whole.at[:PROMPT].set(self.prompt.reshape(PROMPT, -1).astype(F32))
        near = jnp.where(row * rows < PROMPT, 0, around)
        near = lax.dynamic_slice_in_dim(whole, start, rows + 2 * CONT_MOST, 0) + near
        whole = lax.dynamic_update_slice_in_dim(whole, near, start, 0)
        return lax.psum_scatter(whole[: self.plan.row * rows], "row", scatter_dimension=0, tiled=True)


def heads_mask(lanes, head):
    lane = lax.broadcasted_iota(jnp.int32, lanes, 1)
    return (lane >= head * HDIM) & (lane < (head + 1) * HDIM)


def nt(left, right):
    return lax.dot_general(left, right, (((1,), (1,)), ((), ())), preferred_element_type=F32)


def tn(left, right):
    return lax.dot_general(left, right, (((0,), (0,)), ((), ())), preferred_element_type=F32)


def attention_kernel(blocks, first, rows, *refs):
    spots = refs[:blocks]
    (near_ref, own_ref, wq_ref, wk_ref, wv_ref, bq_ref, bv_ref, segq_ref, segk_ref,
     q_ref, kp_ref, vp_ref, kn_ref, vn_ref, ctx_ref, lse_ref, x_ref, s_ref, sems) = refs[blocks:]
    near = near_ref[0]
    at = lambda b: pl.ds(pl.multiple_of(b * rows, rows), rows)
    depth = own_ref.shape[1]
    wq, wk, wv = [ref[...].reshape(depth, -1) for ref in (wq_ref, wk_ref, wv_ref)]

    @pl.when(pl.program_id(0) == 0)
    def _():
        copies = [
            pltpu.make_async_copy(spot, x_ref.at[pl.ds(i * rows, rows)], sems.at[i])
            for i, spot in enumerate(spots)
        ]
        for copy in copies:
            copy.start()
        for copy in copies:
            copy.wait()

    queries = (mm(own_ref[...], wq) + bq_ref[...]) * (HDIM**-0.5)
    q_ref[...] = queries.astype(BF)

    def project(b, k_ref, v_ref, side):
        x = x_ref[at(b), :]
        k_ref[at(side), :] = mm(x, wk).astype(BF)
        v_ref[at(side), :] = (mm(x, wv) + bv_ref[...]).astype(BF)

    @pl.loop(0, first)
    def _(b):
        project(b, kp_ref, vp_ref, b)

    @pl.loop(0, near)
    def _(b):
        project(first + b, kn_ref, vn_ref, b)

    width = q_ref.shape[1]
    heads = width // HDIM
    q = q_ref[...]
    parts = [jnp.where(heads_mask(q.shape, h), q, 0) for h in range(heads)]

    def scores(b, peaks, k_ref, base):
        k = k_ref[at(b), :]
        out = []
        for h in range(heads):
            s = nt(k, parts[h])
            if base:
                s = jnp.where(segk_ref[at(b), :] == segq_ref[...], s, MASK_FILL)
            s_ref[h, at(base + b), :] = s
            out.append(jnp.maximum(peaks[h], jnp.max(s, axis=0, keepdims=True)))
        return tuple(out)

    peaks = tuple(jnp.full((1, rows), MASK_FILL, F32) for _ in range(heads))
    peaks = lax.fori_loop(0, first, lambda b, c: scores(b, c, kp_ref, 0), peaks)
    peaks = lax.fori_loop(0, near, lambda b, c: scores(b, c, kn_ref, first), peaks)

    def mix(b, carry, v_ref, base):
        totals, mixed = carry
        vt = v_ref[at(b), :].T
        new_totals, new_mixed = [], []
        for h in range(heads):
            p = jnp.exp(s_ref[h, at(base + b), :] - peaks[h])
            new_totals.append(totals[h] + jnp.sum(p, axis=0, keepdims=True))
            new_mixed.append(mixed[h] + mm(vt[h * HDIM : (h + 1) * HDIM], p.astype(BF)))
        return tuple(new_totals), tuple(new_mixed)

    zero = (
        tuple(jnp.zeros((1, rows), F32) for _ in range(heads)),
        tuple(jnp.zeros((HDIM, rows), F32) for _ in range(heads)),
    )
    carry = lax.fori_loop(0, first, lambda b, c: mix(b, c, vp_ref, 0), zero)
    totals, mixed = lax.fori_loop(0, near, lambda b, c: mix(b, c, vn_ref, first), carry)
    whole = jnp.concatenate([mixed[h] / totals[h] for h in range(heads)], 0)
    ctx_ref[...] = whole.T.astype(BF)
    for h in range(heads):
        lse_ref[0, h : h + 1, :] = peaks[h] + jnp.log(totals[h])


def attention_call(spots, first, near, own, got, bq, bv, segq, segk):
    rows, width = own.shape
    blocks = len(spots)
    tall = blocks * rows
    part = 256
    steps = width // part
    heads = part // HDIM
    cols = lambda depth: pl.BlockSpec((depth, part), lambda g: (0, g))
    flops = 2 * tall * width * width * 2 + 4 * tall * rows * width * 4
    owners, each = got.shape[0], width // got.shape[0]
    weight = lambda place: pl.BlockSpec((owners, each, part), lambda g: (0, place, g))
    return pl.pallas_call(
        functools.partial(attention_kernel, blocks, first, rows),
        grid=(steps,),
        in_specs=[pl.BlockSpec(memory_space=pl.ANY)] * blocks
        + [
            pl.BlockSpec(memory_space=pltpu.SMEM),
            pl.BlockSpec((rows, width), lambda g: (0, 0)),
            weight(WQ), weight(WK), weight(WV), cols(1), cols(1),
            pl.BlockSpec((1, rows), lambda g: (0, 0)),
            pl.BlockSpec(segk.shape, lambda g: (0, 0)),
        ],
        out_specs=[
            cols(rows), cols(PROMPT), cols(PROMPT), cols(tall - PROMPT), cols(tall - PROMPT),
            cols(rows), pl.BlockSpec((1, 8, rows), lambda g: (g, 0, 0)),
        ],
        out_shape=[
            jax.ShapeDtypeStruct((rows, width), BF),
            jax.ShapeDtypeStruct((PROMPT, width), BF),
            jax.ShapeDtypeStruct((PROMPT, width), BF),
            jax.ShapeDtypeStruct((tall - PROMPT, width), BF),
            jax.ShapeDtypeStruct((tall - PROMPT, width), BF),
            jax.ShapeDtypeStruct((rows, width), BF),
            jax.ShapeDtypeStruct((steps, 8, rows), F32),
        ],
        scratch_shapes=[
            pltpu.VMEM((tall, width), BF),
            pltpu.VMEM((heads, tall, rows), F32),
            pltpu.SemaphoreType.DMA((blocks,)),
        ],
        compiler_params=pltpu.CompilerParams(vmem_limit_bytes=60 * 2**20),
        cost_estimate=pl.CostEstimate(
            flops=flops, bytes_accessed=12 * 2**20, transcendentals=tall * rows * 12
        ),
        name="attention",
    )(*spots, near, own, got, got, got, bq, bv, segq, segk)


def halves(value, runs, core):
    depth = value.shape[0] // runs
    pick = lambda first: jnp.concatenate(
        [value[i * depth : (i + 1) * depth] for i in range(first, runs, 2)], 0
    )
    even, odd = pick(0), pick(1)
    return jnp.where(core == 0, odd, even), jnp.where(core == 0, even, odd)


def middle_kernel(wide, ctx_ref, own_ref, cot_ref, wo_ref, wi_ref, wu_ref, vec_ref, bin_ref,
                  out_ref, h1_ref, gctx_ref, grads, sums_ref, sbin_ref,
                  first_ref, n1_ref, inv_ref, low_ref, pre_ref, cdf_ref, act_ref, acc_ref,
                  gffn_ref, glow_ref, out_buf, in_buf, wo_buf, sems):
    step = pl.program_id(0)
    width = ctx_ref.shape[1]
    square = lambda ref: ref[...].reshape(width, width)
    vec = lambda i: vec_ref[i : i + 1, :]
    mean = lambda v: jnp.sum(v, axis=-1, keepdims=True) * (1.0 / width)
    down = lambda v: jnp.sum(v, axis=0, keepdims=True)
    owners = wi_ref.shape[0]
    each = width // owners
    some = owners // wide

    def outer(at):
        turn = (2 * wide - 1 - at) % 2
        place = grads.at[pl.ds(at * some, some), pl.ds(0, wide * each)]
        return pltpu.make_async_copy(out_buf.at[turn], place, sems.at[turn])

    def inner(at):
        turn = (2 * wide - 1 - at) % 2
        place = grads.at[:, pl.ds((wide + 1 + at) * each, each)]
        return pltpu.make_async_copy(in_buf.at[turn], place, sems.at[2 + turn])

    def output():
        return pltpu.make_async_copy(wo_buf, grads.at[:, pl.ds(wide * each, each)], sems.at[4])

    @pl.when(step == 0)
    def _():
        hidden = own_ref[...].astype(F32) + mm(ctx_ref[...], square(wo_ref)) + vec(0)
        centred = hidden - mean(hidden)
        inverse = lax.rsqrt(mean(centred * centred) + NORM_EPS)
        normed = centred * inverse
        n1_ref[...] = normed
        inv_ref[...] = inverse
        first = normed * vec(1) + vec(2)
        first_ref[...] = first
        low_ref[...] = first.astype(BF)

    @pl.when(step < wide)
    def _():
        chunk = pl.ds(pl.multiple_of(step * width, width), width)
        pre = mm(low_ref[...], square(wi_ref)) + bin_ref[pl.ds(step, 1), :]
        cdf = 0.5 * (1.0 + lax.erf(pre * SQRT_HALF))
        act = (pre * cdf).astype(BF)
        pre_ref[:, chunk] = pre
        cdf_ref[:, chunk] = cdf
        act_ref[:, chunk] = act
        more = mm(act, square(wu_ref))

        @pl.when(step == 0)
        def _():
            acc_ref[...] = more

        @pl.when(step > 0)
        def _():
            acc_ref[...] += more

    @pl.when(step == wide - 1)
    def _():
        hidden = first_ref[...] + acc_ref[...] + vec(3)
        centred = hidden - mean(hidden)
        inverse = lax.rsqrt(mean(centred * centred) + NORM_EPS)
        normed = centred * inverse
        out_ref[...] = (normed * vec(4) + vec(5)).astype(BF)
        grad = cot_ref[...].astype(F32)
        sums_ref[0:1, :] = down(grad * normed)
        sums_ref[1:2, :] = down(grad)
        e = grad * vec(4)
        back = inverse * (e - mean(e) - normed * mean(e * normed))
        gffn_ref[...] = back
        low = back.astype(BF)
        glow_ref[...] = low
        sums_ref[2:3, :] = down(low.astype(F32))

    @pl.when(step >= wide)
    def _():
        at = 2 * wide - 1 - step
        chunk = pl.ds(pl.multiple_of(at * width, width), width)
        pre = pre_ref[:, chunk]
        slope = cdf_ref[:, chunk] + pre * jnp.exp(-0.5 * pre * pre) * INV_ROOT_TAU
        low = glow_ref[...]
        grad = (nt(low, square(wu_ref)) * slope).astype(BF)
        sbin_ref[pl.ds(at, 1), :] = down(grad.astype(F32))
        turn = step % 2

        @pl.when(step >= wide + 2)
        def _():
            outer(at + 2).wait()
            inner(at + 2).wait()

        out_buf[turn] = tn(act_ref[:, chunk], low).astype(BF).reshape(some, wide * each, width)
        outer(at).start()
        in_buf[turn] = tn(low_ref[...], grad).astype(BF).reshape(owners, each, width)
        inner(at).start()
        gffn_ref[...] += nt(grad, square(wi_ref))

    @pl.when(step == 2 * wide - 1)
    def _():
        grad = gffn_ref[...]
        normed = n1_ref[...]
        sums_ref[3:4, :] = down(grad * normed)
        sums_ref[4:5, :] = down(grad)
        e = grad * vec(1)
        back = inv_ref[...] * (e - mean(e) - normed * mean(e * normed))
        h1_ref[...] = back
        low = back.astype(BF)
        sums_ref[5:6, :] = down(low.astype(F32))
        wo_buf[...] = tn(ctx_ref[...], low).astype(BF).reshape(owners, each, width)
        output().start()
        gctx = nt(low, square(wo_ref)).astype(BF)
        gctx_ref[...] = gctx
        sums_ref[6:7, :] = down(gctx.astype(F32))
        sums_ref[7:8, :] = jnp.zeros((1, width), F32)
        for at in (1, 0):
            outer(at).wait()
            inner(at).wait()
        output().wait()


def middle_call(ctx, own, cot, got, vec, b_inner):
    rows, width = own.shape
    owners = got.shape[0]
    each = width // owners
    wide = WIDE
    whole = lambda shape: pl.BlockSpec(shape, lambda s: (0,) * len(shape))
    at = lambda s: jnp.where(s < wide, s, 2 * wide - 1 - s)
    shape = jax.ShapeDtypeStruct
    return pl.pallas_call(
        functools.partial(middle_kernel, wide),
        grid=(2 * wide,),
        in_specs=[
            whole((rows, width)), whole((rows, width)), whole((rows, width)),
            pl.BlockSpec((owners, each, width), lambda s: (0, WO, 0)),
            pl.BlockSpec((owners, each, width), lambda s: (0, WI + at(s), 0)),
            pl.BlockSpec((owners // wide, wide * each, width), lambda s: (at(s), 0, 0)),
            whole((8, width)), whole((8, width)),
        ],
        out_specs=[
            whole((rows, width)), whole((rows, width)), whole((rows, width)),
            pl.BlockSpec(memory_space=pl.ANY),
            whole((8, width)), whole((8, width)),
        ],
        out_shape=[
            shape((rows, width), BF), shape((rows, width), F32), shape((rows, width), BF),
            shape((owners, (2 * wide + 1) * each, width), BF),
            shape((8, width), F32), shape((8, width), F32),
        ],
        scratch_shapes=[
            pltpu.VMEM((rows, width), F32), pltpu.VMEM((rows, width), F32), pltpu.VMEM((rows, 1), F32),
            pltpu.VMEM((rows, width), BF), pltpu.VMEM((rows, wide * width), F32),
            pltpu.VMEM((rows, wide * width), F32), pltpu.VMEM((rows, wide * width), BF),
            pltpu.VMEM((rows, width), F32), pltpu.VMEM((rows, width), F32),
            pltpu.VMEM((rows, width), BF),
            pltpu.VMEM((2, owners // wide, wide * each, width), BF),
            pltpu.VMEM((2, owners, each, width), BF),
            pltpu.VMEM((owners, each, width), BF), pltpu.SemaphoreType.DMA((5,)),
        ],
        compiler_params=pltpu.CompilerParams(vmem_limit_bytes=60 * 2**20),
        cost_estimate=pl.CostEstimate(
            flops=2 * rows * width * width * (6 * wide + 3), bytes_accessed=32 * 2**20,
            transcendentals=2 * rows * width * wide,
        ),
        name="middle",
    )(ctx, own, cot, got, got, got, vec, b_inner)


def back_kernel(rows, bound, started, *refs):
    near_ref, gctx_ref, ctx_ref, q_ref, k_ref, v_ref, lse_ref, segq_ref, segk_ref = refs[:9]
    dk_ref, dv_ref, dq_ref = refs[-3:]
    q, g = q_ref[...], gctx_ref[...]
    part = q.shape[1]
    heads = part // HDIM
    masks = [heads_mask(q.shape, h) for h in range(heads)]
    q_parts = [jnp.where(m, q, 0) for m in masks]
    g_parts = [jnp.where(m, g, 0) for m in masks]
    product = (g.astype(F32) * ctx_ref[...].astype(F32)).T
    inner = [
        jnp.sum(product[h * HDIM : (h + 1) * HDIM], axis=0, keepdims=True) for h in range(heads)
    ]

    def one(b, dq):
        here = pl.ds(pl.multiple_of(b * rows, rows), rows)
        k, v = k_ref[here, :], v_ref[here, :]
        kt = k.T
        if bound is None:
            allowed = segk_ref[here, :] == segq_ref[...]
        dk = jnp.zeros((rows, part), F32)
        dv = jnp.zeros((rows, part), F32)
        out = []
        for h in range(heads):
            s = nt(k, q_parts[h])
            if bound is None:
                s = jnp.where(allowed, s, MASK_FILL)
            p = jnp.exp(s - lse_ref[0, h : h + 1, :])
            dp = nt(v, g_parts[h])
            ds = (p * (dp - inner[h])).astype(BF)
            dv = dv + mm(p.astype(BF), g_parts[h])
            dk = dk + mm(ds, q_parts[h])
            out.append(dq[h] + mm(kt[h * HDIM : (h + 1) * HDIM], ds))
        dk_ref[here, :] = dk.astype(BF)
        dv_ref[here, :] = dv.astype(BF)
        return tuple(out)

    if started:
        dq = tuple(refs[9][h * HDIM : (h + 1) * HDIM, :] for h in range(heads))
    else:
        dq = tuple(jnp.zeros((HDIM, rows), F32) for _ in range(heads))
    dq = lax.fori_loop(0, near_ref[0] if bound is None else bound, one, dq)
    dq_ref[...] = jnp.concatenate(dq, 0)


def back_call(start, steps, bound, near, gctx, ctx, q, k, v, lse, segq, segk, dq0=None, into=None):
    rows, width = q.shape
    tall = k.shape[0]
    part = 256
    cols = lambda depth: pl.BlockSpec((depth, part), lambda g: (0, start + g))
    whole = lambda shape: pl.BlockSpec(shape, lambda g: (0,) * len(shape))
    down = pl.BlockSpec((part, rows), lambda g: (start + g, 0))
    shape = jax.ShapeDtypeStruct
    extra = ([dq0] if dq0 is not None else []) + list(into or [])
    specs = ([down] if dq0 is not None else []) + [pl.BlockSpec(memory_space=pl.ANY)] * len(into or [])
    return pl.pallas_call(
        functools.partial(back_kernel, rows, bound, dq0 is not None),
        grid=(steps,),
        in_specs=[
            pl.BlockSpec(memory_space=pltpu.SMEM),
            cols(rows), cols(rows), cols(rows), cols(tall), cols(tall),
            pl.BlockSpec((1, 8, rows), lambda g: (start + g, 0, 0)),
            whole((1, rows)), whole(segk.shape),
        ] + specs,
        out_specs=[cols(tall), cols(tall), down],
        out_shape=[shape((tall, width), BF), shape((tall, width), BF), shape((width, rows), F32)],
        input_output_aliases={9 + i: i for i in range(3)} if into else {},
        compiler_params=pltpu.CompilerParams(vmem_limit_bytes=60 * 2**20),
        cost_estimate=pl.CostEstimate(
            flops=2 * 10 * 2 * tall * rows * part * steps * 2,
            bytes_accessed=8 * tall * part * steps, transcendentals=tall * rows * 4 * steps,
        ),
        name="attention_back",
    )(near, gctx, ctx, q, k, v, lse, segq, segk, *extra)


def product_kernel(rows, bound, near_ref, dk_ref, dv_ref, wk_ref, wv_ref, gx_ref):
    @pl.when((pl.program_id(0) < near_ref[0]) | (bound is not None))
    def _():
        width = dk_ref.shape[1]
        wk, wv = wk_ref[...].reshape(width, width), wv_ref[...].reshape(width, width)
        gx_ref[0] = (nt(dk_ref[...], wk) + nt(dv_ref[...], wv)).astype(BF)


def product_call(bound, near, dk, dv, got, rows):
    tall, width = dk.shape
    owners, each = got.shape[0], width // got.shape[0]
    weight = lambda place: pl.BlockSpec((owners, each, width), lambda b: (0, place, 0))
    return pl.pallas_call(
        functools.partial(product_kernel, rows, bound),
        grid=(tall // rows,),
        in_specs=[
            pl.BlockSpec(memory_space=pltpu.SMEM),
            pl.BlockSpec((rows, width), lambda b: (b, 0)),
            pl.BlockSpec((rows, width), lambda b: (b, 0)),
            weight(WK), weight(WV),
        ],
        out_specs=pl.BlockSpec((1, rows, width), lambda b: (b, 0, 0)),
        out_shape=jax.ShapeDtypeStruct((tall // rows, rows, width), BF),
        compiler_params=pltpu.CompilerParams(vmem_limit_bytes=60 * 2**20),
        cost_estimate=pl.CostEstimate(
            flops=4 * tall * width * width, bytes_accessed=6 * tall * width, transcendentals=0
        ),
        name="token_product",
    )(near, dk, dv, got, got)


def weight_kernel(blocks, first, rows, runs, *refs):
    spots = refs[:blocks]
    (near_ref, core_ref, own_ref, dq_ref, wq_ref, h1_ref, dkp_ref, dvp_ref, dkn_ref, dvn_ref,
     q_send, q_keep, kv_send, kv_keep, gown_ref, sums_ref, x_ref, sems) = refs[blocks:]
    core = core_ref[0]
    at = lambda b: pl.ds(pl.multiple_of(b * rows, rows), rows)
    step = pl.program_id(0)

    @pl.when(step == 0)
    def _():
        copies = [
            pltpu.make_async_copy(spot, x_ref.at[pl.ds(i * rows, rows)], sems.at[i])
            for i, spot in enumerate(spots)
        ]
        for copy in copies:
            copy.start()
        for copy in copies:
            copy.wait()
        gown_ref[...] = h1_ref[...]

    scale = HDIM**-0.5
    dq = dq_ref[...].T.astype(BF)
    part = dq.shape[1]
    width = x_ref.shape[1]
    gown_ref[...] += nt(dq, wq_ref[...].reshape(width, part)) * scale
    away, here = halves((tn(own_ref[...], dq) * scale).astype(BF), runs, core)
    q_send[...] = away.reshape(q_send.shape)
    q_keep[...] = here.reshape(q_send.shape)
    sums_ref[0:1, :] = jnp.sum(dq.astype(F32), axis=0, keepdims=True) * scale

    def products(b, carry, dk_ref, dv_ref, base):
        dk, dv, x = dk_ref[at(b), :], dv_ref[at(b), :], x_ref[at(base + b), :]
        wk, wv = carry
        return wk + tn(x, dk), wv + tn(x, dv)

    zero = jnp.zeros((width, part), F32)
    carry = (zero, zero)
    carry = lax.fori_loop(0, first, lambda b, c: products(b, c, dkp_ref, dvp_ref, 0), carry)
    carry = lax.fori_loop(0, near_ref[0], lambda b, c: products(b, c, dkn_ref, dvn_ref, first), carry)
    for i, grad in enumerate(carry):
        away, here = halves(grad.astype(BF), runs, core)
        shape = kv_send.shape[:2] + (part,)
        kv_send[:, :, i * part : (i + 1) * part] = away.reshape(shape)
        kv_keep[:, :, i * part : (i + 1) * part] = here.reshape(shape)
    sums_ref[1:8, :] = jnp.zeros((7, part), F32)


def weight_call(spots, first, near, own, dq, got, h1, dkp, dvp, dkn, dvn, core, runs):
    rows, width = own.shape
    blocks = len(spots)
    tall = blocks * rows
    part = 256
    steps = width // part
    cols = lambda depth, size=part: pl.BlockSpec((depth, size), lambda g: (0, g))
    whole = lambda shape: pl.BlockSpec(shape, lambda g: (0,) * len(shape))
    shape = jax.ShapeDtypeStruct
    owners, each = got.shape[0], width // got.shape[0]
    half = owners // 2
    slab = lambda size: pl.BlockSpec((half, each, size), lambda g: (0, 0, g))
    return pl.pallas_call(
        functools.partial(weight_kernel, blocks, first, rows, runs),
        grid=(steps,),
        in_specs=[pl.BlockSpec(memory_space=pl.ANY)] * blocks
        + [
            pl.BlockSpec(memory_space=pltpu.SMEM),
            pl.BlockSpec(memory_space=pltpu.SMEM),
            whole((rows, width)), pl.BlockSpec((part, rows), lambda g: (g, 0)),
            pl.BlockSpec((owners, each, part), lambda g: (0, WQ, g)),
            whole((rows, width)), cols(PROMPT), cols(PROMPT), cols(tall - PROMPT), cols(tall - PROMPT),
        ],
        out_specs=[
            slab(part), slab(part), slab(2 * part), slab(2 * part), whole((rows, width)), cols(8),
        ],
        out_shape=[
            shape((half, each, width), BF), shape((half, each, width), BF),
            shape((half, each, 2 * width), BF), shape((half, each, 2 * width), BF),
            shape((rows, width), F32), shape((8, width), F32),
        ],
        scratch_shapes=[pltpu.VMEM((tall, width), BF), pltpu.SemaphoreType.DMA((blocks,))],
        compiler_params=pltpu.CompilerParams(vmem_limit_bytes=60 * 2**20),
        cost_estimate=pl.CostEstimate(
            flops=4 * tall * width * width, bytes_accessed=12 * tall * width, transcendentals=0
        ),
        name="weight_product",
    )(*spots, near, core, own, dq, got, h1, dkp, dvp, dkn, dvn)


def real_owners(grads, count, step, width):
    split = count // 32
    take = lambda v: v.reshape(32, -1, split, step, width).transpose(0, 2, 1, 3, 4).reshape(count, -1, width)
    outer, rest = grads[:, : 4 * split * step], grads[:, 4 * split * step :]
    return jnp.concatenate([outer.reshape(count, 4 * step, width), take(rest)], 1)


def solution(mesh):
    plan = Plan(mesh.shape["grp"], mesh.shape["row"])

    def per_device(
        tokens, cont_lengths, cotangent, w_query, w_key, w_value, w_output, w_inner, w_outer,
        bias_query, bias_value, bias_output, gain_first, shift_first, bias_inner, bias_outer,
        gain_second, shift_second,
    ):
        count = plan.count
        _, rows, width = tokens.shape
        step = w_query.shape[0]
        wide = w_inner.shape[1] // width
        row = lax.axis_index("row")
        scale = HDIM ** (-0.5)
        own = tokens[0]

        vectors = (
            bias_query, bias_value, bias_output, gain_first, shift_first, bias_outer, gain_second,
            shift_second, bias_inner,
        )
        small = len(vectors) - 1
        line, place = 0, 0
        for vector in vectors:
            size = vector.shape[0]
            line = line + jnp.pad(vector, (place, width - place - size))
            place += size
        line = jnp.pad(line[None], ((0, 7), (0, 0)))
        inner_rows = [w_inner[:, i * width : (i + 1) * width] for i in range(wide)]
        pack = jnp.concatenate([w_outer, w_output, *inner_rows, w_query, w_key, w_value, line], 0)
        got = lax.all_gather(pack, AXES, axis=0, tiled=True).reshape(count, -1, width)
        lines = got[:, 12 * step]
        if step % 8:
            cuts = [wide * step, (wide + 1) * step, (2 * wide + 1) * step, 12 * step]
            outer, output, inner, rest, _ = jnp.split(got, cuts, axis=1)
            apart = lambda v, n: v.reshape(count, n, step, width).transpose(1, 0, 2, 3)
            inner, rest = [
                v.reshape(v.shape[0], 32, width // 32, width).transpose(1, 0, 2, 3)
                for v in (apart(inner, wide), apart(rest, 3))
            ]
            got = jnp.concatenate(
                [v.reshape(32, -1, width) for v in (outer, output, inner, rest)], 1
            )
        runs = plan.grp
        core = (lax.axis_index("grp") % 2).astype(jnp.int32).reshape(1)

        exchange = Tokens(plan, own)
        exchange.stage_one()
        exchange.stage_two()
        exchange.stage_three()
        spots, near = exchange.spots()
        first_near = PROMPT // rows

        table = lines[:, : small * step].reshape(count, small, step).transpose(1, 0, 2)
        table = table.reshape(small, width).astype(F32)
        v_bin = lines[:, small * step : (small + wide) * step].reshape(wide, width).astype(F32)
        v_bin = jnp.pad(v_bin, ((0, 8 - wide), (0, 0)))
        segments = segment_ids(cont_lengths[0], plan.row * rows)
        seg_own = lax.dynamic_slice_in_dim(segments, row * rows, rows, 0)[None, :]
        seg_near = near_segments(plan, segments, rows)[:, None]
        near = near.astype(jnp.int32).reshape(1)

        queries, keys_p, values_p, keys_n, values_n, context, log_total = attention_call(
            spots, first_near, near, own, got, table[0:1], table[1:2], seg_own, seg_near
        )
        vec = jnp.concatenate([table[2:], jnp.zeros((2, width), F32)], 0)
        layer_out, grad_h1, grad_context, grads, sums, sums_bin = middle_call(
            context, own, cotangent[0], got, vec, v_bin
        )
        if step % 8:
            grads = real_owners(grads, count, step, width)
        o_ab = lax.psum_scatter(
            grads.reshape(-1, width), AXES, scatter_dimension=0, tiled=True
        ).astype(F32)
        core_bit = plan.core[0]
        left = [1 << i for i in reversed(range(plan.bits)) if 1 << i != core_bit]
        parts = width // 256
        dkp, dvp, dqp = back_call(
            0, parts, first_near, near, grad_context, context, queries, keys_p, values_p, log_total,
            seg_own, seg_near,
        )
        shared_p = product_call(first_near, near, dkp, dvp, got, rows)
        returned = Return(plan, rows)
        returned.prompt_one(shared_p)
        dkn, dvn, dq = back_call(
            0, parts, None, near, grad_context, context, queries, keys_n, values_n, log_total,
            seg_own, seg_near, dqp,
        )
        shared_n = product_call(None, near, dkn, dvn, got, rows)
        returned.same, shared_n, dq = tie(returned.same, shared_n, dq)
        returned.prompt_two()
        returned.near(shared_n)
        q_send, q_keep, kv_send, kv_keep, grad_own, sums_qkv = weight_call(
            spots, first_near, near, own, dq, got, grad_h1, dkp, dvp, dkn, dvn, core, runs
        )
        q_send, q_keep, kv_send, kv_keep, returned.same, returned.own = tie(
            q_send, q_keep, kv_send, kv_keep, returned.same, returned.own
        )
        returned.prompt_three()

        order = (6, 5, 3, 4, 2, 0, 1)
        d_table = jnp.concatenate([sums_qkv[:1]] + [sums[i : i + 1] for i in order], 0)
        d_lines = jnp.concatenate(
            [
                d_table.reshape(small, count, step).transpose(1, 0, 2).reshape(count, -1),
                sums_bin[:wide].reshape(count, wide * step),
            ],
            1,
        )
        d_lines = jnp.pad(d_lines, ((0, 0), (0, width - d_lines.shape[1])))[:, None].astype(BF)
        d_lines = jnp.pad(d_lines, ((0, 0), (0, 7), (0, 0)))
        place = core[0]
        pick = Reduce(plan, [])
        if step % 8:
            q_send, q_keep, kv_send, kv_keep = [
                v.reshape(count // 2, step, -1) for v in (q_send, q_keep, kv_send, kv_keep)
            ]
        q_send = jnp.concatenate([q_send, pick.cut(d_lines, core_bit, 1 - place)], 1)
        q_keep = jnp.concatenate([q_keep, pick.cut(d_lines, core_bit, place)], 1)
        r_q = Reduce(plan, [q_keep, plan.swap(q_send, core_bit)], left)
        r_kv = Reduce(plan, [kv_keep, plan.swap(kv_send, core_bit)], left)
        for one, two in zip(plan.x + plan.y + plan.z[::-1], plan.y + plan.x + plan.z[::-1]):
            n = len(r_q.terms)
            if one == plan.z[0]:
                *tied, returned.back = tie(*r_q.terms, *r_kv.terms, returned.back)
            else:
                tied = tie(*r_q.terms, *r_kv.terms)
            r_q.terms, r_kv.terms = list(tied[:n]), list(tied[n:])
            r_q.stage(one)
            r_kv.stage(two)
        grad_tokens = grad_own + returned.total()
        o_query = r_q.result()
        o_line = o_query[step]
        o_both = r_kv.result().reshape(step, parts, 2, width // parts)

        o_small = [o_line[i * step : (i + 1) * step] for i in range(small)]
        o_bin = o_line[small * step : (small + wide) * step]
        return (
            layer_out[None],
            grad_tokens.astype(BF)[None],
            o_query[:step],
            o_both[:, :, 0].reshape(step, width),
            o_both[:, :, 1].reshape(step, width),
            o_ab[wide * step : (wide + 1) * step],
            jnp.concatenate([o_ab[i * step : (i + 1) * step] for i in range(wide + 1, 2 * wide + 1)], 1),
            o_ab[: wide * step],
            o_small[0],
            o_small[1],
            o_small[2],
            o_small[3],
            o_small[4],
            o_bin,
            o_small[5],
            o_small[6],
            o_small[7],
        )

    split = P("grp", "row", None)
    owned2, owned1 = P(AXES, None), P(AXES)
    in_specs = (split, P("grp", None), split) + (owned2,) * 6 + (owned1,) * 9
    out_specs = (split, split) + (owned2,) * 6 + (owned1,) * 9
    return jax.shard_map(
        per_device, mesh=mesh, in_specs=in_specs, out_specs=out_specs, check_vma=False
    )
```

```python
import functools

import jax
import jax.numpy as jnp
import numpy as np
from jax import lax
from jax.experimental import pallas as pl
from jax.experimental.pallas import tpu as pltpu
from jax.sharding import PartitionSpec as P

HEADS = 12
HDIM = 64
PROMPT = 1024
CONT_MOST = 256
BF = jnp.bfloat16
F32 = jnp.float32

NORM_EPS = 1e-12
MASK_FILL = -1000000000.0
SQRT_HALF = 0.7071067811865476
INV_ROOT_TAU = 0.3989422804014327
AXES = ("grp", "row")
WIDE = 4
WO, WI = 4, 5
WQ, WK, WV = 0, 1, 2


def mm(left, right):
    return jnp.dot(left, right, preferred_element_type=F32)


def segment_ids(lengths, group_len):
    ends = jnp.cumsum(lengths)
    places = jnp.arange(group_len, dtype=jnp.int32)
    passed = jnp.sum(((places - PROMPT)[:, None] >= ends[None, :]).astype(jnp.int32), axis=-1)
    return jnp.where(places < PROMPT, 0, 1 + passed)


class Plan:
    def __init__(self, grp, row):
        self.grp, self.row, self.count = grp, row, grp * row
        y = row // 4
        bits = lambda base, size: [base << i for i in range(size.bit_length() - 1)]
        self.y, self.z = bits(1, y), bits(y, 4)
        self.core, self.x = bits(row, 2), bits(2 * row, grp // 2)
        self.bits = self.count.bit_length() - 1

    def swap(self, value, mask):
        return lax.ppermute(value, AXES, [(i, i ^ mask) for i in range(self.count)])

    def send(self, value, moves):
        pairs = [(g * self.row + a, g * self.row + b) for g in range(self.grp) for a, b in moves]
        return lax.ppermute(value, AXES, pairs)

    def me(self):
        return lax.axis_index("grp") * self.row + lax.axis_index("row")


class Reduce:
    def __init__(self, plan, terms, left=None):
        self.plan, self.terms = plan, list(terms)
        self.left = left or [1 << i for i in reversed(range(plan.bits))]

    def cut(self, term, bit, place):
        at = self.left.index(bit)
        high, low = 1 << at, 1 << (len(self.left) - at - 1)
        _, rows, width = term.shape
        term = term.reshape(high, 2, low * rows, width)
        return lax.dynamic_slice_in_dim(term, place, 1, 1).reshape(high * low, rows, width)

    def total(self, terms):
        return sum([t.astype(F32) for t in terms[1:]], terms[0].astype(F32))

    def stage(self, bit):
        place = (self.plan.me() // bit) & 1
        away = self.total([self.cut(t, bit, 1 - place) for t in self.terms]).astype(BF)
        here = [self.cut(t, bit, place) for t in self.terms]
        self.left = [b for b in self.left if b != bit]
        self.terms = here + [self.plan.swap(away, bit)]

    def result(self):
        return self.total(self.terms)[0]


def tie(*values):
    return lax.optimization_barrier(values)


class Tokens:
    def __init__(self, plan, own):
        self.plan, self.own = plan, own
        self.rows = own.shape[0]
        self.ready = plan.row == 8

    def stage_one(self):
        if self.ready:
            plan, own = self.plan, self.own
            across = plan.send(own, [(0, 4), (1, 5), (2, 6), (3, 7)])
            self.same = jnp.where(lax.axis_index("row") < 4, own, across)
            self.beside = plan.swap(own, 1)
            return [self.same, self.beside]
        return []

    def stage_two(self):
        if self.ready:
            plan = self.plan
            self.other = plan.swap(self.same, 2)
            self.same_y = plan.swap(self.same, 1)
            self.diagonal = plan.send(self.own, [(5, 6), (6, 5)])
            return [self.other, self.same_y, self.diagonal]
        return []

    def stage_three(self):
        if self.ready:
            self.other_y = self.plan.swap(self.other, 1)

    def spots(self):
        row, rows, own = lax.axis_index("row"), self.rows, self.own
        if self.ready:
            near = jnp.where(row < 4, 0, jnp.where((row == 5) | (row == 6), 3, 2))
            return [
                self.same, self.other, self.same_y, self.other_y, own, self.beside, self.diagonal,
            ], near
        every = lax.all_gather(own, "row", axis=0, tiled=True)
        start = jnp.maximum(row * rows - CONT_MOST, 0)
        padded = jnp.concatenate([every, jnp.zeros((CONT_MOST, own.shape[1]), own.dtype)], 0)
        near = lax.dynamic_slice_in_dim(padded, start, rows + 2 * CONT_MOST, 0)
        every = jnp.concatenate([every[:PROMPT], near], 0)
        spots = [every[i : i + rows] for i in range(0, every.shape[0], rows)]
        return spots, jnp.where(row * rows < PROMPT, 0, near.shape[0] // rows)


def near_segments(plan, segments, rows):
    row = lax.axis_index("row")
    if plan.row != 8:
        start = jnp.maximum(row * rows - CONT_MOST, 0)
        padded = jnp.concatenate([segments, jnp.full((CONT_MOST,), -1, jnp.int32)], 0)
        near = lax.dynamic_slice_in_dim(padded, start, rows + 2 * CONT_MOST, 0)
        return jnp.where((near == 0) | (row * rows < PROMPT), -1, near)
    pieces = []
    for block, valid in (
        (row, row >= 4),
        (row ^ 1, row >= 4),
        (11 - row, (row == 5) | (row == 6)),
    ):
        block = jnp.clip(block, 0, 7)
        ids = lax.dynamic_slice_in_dim(segments, block * rows, rows, 0)
        pieces.append(jnp.where(valid, ids, -1))
    return jnp.concatenate(pieces, 0)


class Return:
    def __init__(self, plan, rows):
        self.plan, self.rows = plan, rows

    def prompt_one(self, parts):
        self.prompt = self.same = self.own = self.back = parts
        if self.plan.row == 8:
            same, other, same_y, other_y = [parts[i].astype(F32) for i in range(4)]
            self.other = (other + self.plan.swap(parts[3], 1).astype(F32)).astype(BF)
            self.same = same + self.plan.swap(parts[2], 1).astype(F32)

    def prompt_two(self):
        if self.plan.row == 8:
            self.same = self.same + self.plan.swap(self.other, 2).astype(F32)

    def prompt_three(self):
        if self.plan.row == 8:
            self.back = self.plan.send(self.same.astype(BF), [(4, 0), (5, 1), (6, 2), (7, 3)])

    def near(self, parts):
        self.around = parts
        if self.plan.row == 8:
            own = parts[0].astype(F32) + self.plan.swap(parts[1], 1).astype(F32)
            self.own = own + self.plan.send(parts[2], [(5, 6), (6, 5)]).astype(F32)

    def total(self):
        row, rows = lax.axis_index("row"), self.rows
        if self.plan.row == 8:
            return jnp.where(row < 4, self.same + self.back.astype(F32), self.own)
        around = self.around.reshape(-1, self.around.shape[-1]).astype(F32)
        start = jnp.maximum(row * rows - CONT_MOST, 0)
        whole = jnp.zeros((self.plan.row * rows + CONT_MOST, around.shape[1]), F32)
        whole = whole.at[:PROMPT].set(self.prompt.reshape(PROMPT, -1).astype(F32))
        near = jnp.where(row * rows < PROMPT, 0, around)
        near = lax.dynamic_slice_in_dim(whole, start, rows + 2 * CONT_MOST, 0) + near
        whole = lax.dynamic_update_slice_in_dim(whole, near, start, 0)
        return lax.psum_scatter(whole[: self.plan.row * rows], "row", scatter_dimension=0, tiled=True)


def heads_mask(lanes, head):
    lane = lax.broadcasted_iota(jnp.int32, lanes, 1)
    return (lane >= head * HDIM) & (lane < (head + 1) * HDIM)


def nt(left, right):
    return lax.dot_general(left, right, (((1,), (1,)), ((), ())), preferred_element_type=F32)


def tn(left, right):
    return lax.dot_general(left, right, (((0,), (0,)), ((), ())), preferred_element_type=F32)


def pack_kernel(wo_ref, wi_ref, wu_ref, wq_ref, wk_ref, wv_ref, line_ref, early_ref, late_ref):
    step, width = wo_ref.shape
    early_ref[:step, :] = wq_ref[...]
    early_ref[step : step + 8, :] = line_ref[:8, :]
    early_ref[step + 8 : 2 * step + 8, :] = wk_ref[...]
    early_ref[2 * step + 8 :, :] = wv_ref[...]
    late_ref[: WIDE * step, :] = wu_ref[...]
    late_ref[WO * step : WI * step, :] = wo_ref[...]
    for i in range(WIDE):
        late_ref[(WI + i) * step : (WI + i + 1) * step, :] = wi_ref[:, i * width : (i + 1) * width]
    late_ref[(WI + WIDE) * step :, :] = line_ref[8:, :]


def pack_call(w_output, w_inner, w_outer, w_query, w_key, w_value, line):
    step, width = w_output.shape
    shape = lambda rows: jax.ShapeDtypeStruct((rows, width), BF)
    return pl.pallas_call(
        pack_kernel, out_shape=[shape(3 * step + 8), shape((WI + WIDE) * step + 8)], name="pack"
    )(w_output, w_inner, w_outer, w_query, w_key, w_value, line)


def attention_kernel(blocks, first, rows, places, *refs):
    spots = refs[:blocks]
    (near_ref, me_ref, own_ref, a0_ref, a1_ref, b0_ref, b1_ref, segq_ref, segk_ref,
     w_ref, q_ref, kp_ref, vp_ref, kn_ref, vn_ref, ctx_ref, lse_ref,
     x_ref, s_ref, line_ref, bias_ref, sems, w_sems) = refs[blocks:]
    near = near_ref[0]
    at = lambda b: pl.ds(pl.multiple_of(b * rows, rows), rows)
    depth = own_ref.shape[1]
    owners = w_ref.shape[0]
    each = depth // owners
    part = q_ref.shape[1]

    def weights(act):
        @pl.loop(0, owners)
        def _(e):
            away = e ^ me_ref[0]
            for (bits, half), (zero, one), parts in (
                (places[0], (a0_ref, a1_ref), ((0, each, w_ref, 0), (each, 8, line_ref, 0))),
                (places[1], (b0_ref, b1_ref), ((0, 2 * each, w_ref, each),)),
            ):
                j = sum([((away // bit) & 1) * weight for bit, weight in bits])
                for which, source in enumerate((zero, one)):

                    @pl.when(((away // half) & 1) == which)
                    def _():
                        for k, (top, size, target, base) in enumerate(parts):
                            act(pltpu.make_async_copy(
                                source.at[j, pl.ds(top, size)], target.at[e, pl.ds(base, size)],
                                w_sems.at[2 * k if zero is a0_ref else 1, e],
                            ))

    @pl.when(pl.program_id(0) == 0)
    def _():
        copies = [
            pltpu.make_async_copy(spot, x_ref.at[pl.ds(i * rows, rows)], sems.at[i])
            for i, spot in enumerate(spots)
        ]
        weights(lambda c: c.start())
        for copy in copies:
            copy.start()
        weights(lambda c: c.wait())
        for copy in copies:
            copy.wait()
        line = line_ref[:, 0, :128]
        place = lax.broadcasted_iota(jnp.int32, (128, depth), 0)
        lane = lax.broadcasted_iota(jnp.int32, (128, depth), 1)
        mine = lax.broadcasted_iota(jnp.int32, (owners, depth), 0)
        mine = mine == lax.broadcasted_iota(jnp.int32, (owners, depth), 1) // each
        for i in range(2):
            spread = mm(line, jnp.where(place == lane % each + i * each, 1.0, 0.0).astype(BF))
            bias_ref[i : i + 1, :] = jnp.sum(jnp.where(mine, spread, 0.0), axis=0, keepdims=True)

    lanes = pl.ds(pl.multiple_of(pl.program_id(0) * part, part), part)
    wq, wk, wv = [
        w_ref[:, i * each : (i + 1) * each, lanes].reshape(depth, part) for i in (WQ, WK, WV)
    ]
    queries = (mm(own_ref[...], wq) + bias_ref[0:1, lanes]) * (HDIM**-0.5)
    q_ref[...] = queries.astype(BF)

    def project(b, k_ref, v_ref, side):
        x = x_ref[at(b), :]
        k_ref[at(side), :] = mm(x, wk).astype(BF)
        v_ref[at(side), :] = (mm(x, wv) + bias_ref[1:2, lanes]).astype(BF)

    @pl.loop(0, first)
    def _(b):
        project(b, kp_ref, vp_ref, b)

    @pl.loop(0, near)
    def _(b):
        project(first + b, kn_ref, vn_ref, b)

    width = q_ref.shape[1]
    heads = width // HDIM
    q = q_ref[...]
    parts = [jnp.where(heads_mask(q.shape, h), q, 0) for h in range(heads)]

    def scores(b, peaks, k_ref, base):
        k = k_ref[at(b), :]
        out = []
        for h in range(heads):
            s = nt(k, parts[h])
            if base:
                s = jnp.where(segk_ref[at(b), :] == segq_ref[...], s, MASK_FILL)
            s_ref[h, at(base + b), :] = s
            out.append(jnp.maximum(peaks[h], jnp.max(s, axis=0, keepdims=True)))
        return tuple(out)

    peaks = tuple(jnp.full((1, rows), MASK_FILL, F32) for _ in range(heads))
    peaks = lax.fori_loop(0, first, lambda b, c: scores(b, c, kp_ref, 0), peaks)
    peaks = lax.fori_loop(0, near, lambda b, c: scores(b, c, kn_ref, first), peaks)

    def mix(b, carry, v_ref, base):
        totals, mixed = carry
        vt = v_ref[at(b), :].T
        new_totals, new_mixed = [], []
        for h in range(heads):
            p = jnp.exp(s_ref[h, at(base + b), :] - peaks[h])
            new_totals.append(totals[h] + jnp.sum(p, axis=0, keepdims=True))
            new_mixed.append(mixed[h] + mm(vt[h * HDIM : (h + 1) * HDIM], p.astype(BF)))
        return tuple(new_totals), tuple(new_mixed)

    zero = (
        tuple(jnp.zeros((1, rows), F32) for _ in range(heads)),
        tuple(jnp.zeros((HDIM, rows), F32) for _ in range(heads)),
    )
    carry = lax.fori_loop(0, first, lambda b, c: mix(b, c, vp_ref, 0), zero)
    totals, mixed = lax.fori_loop(0, near, lambda b, c: mix(b, c, vn_ref, first), carry)
    whole = jnp.concatenate([mixed[h] / totals[h] for h in range(heads)], 0)
    ctx_ref[...] = whole.T.astype(BF)
    for h in range(heads):
        lse_ref[0, h : h + 1, :] = peaks[h] + jnp.log(totals[h])


def attention_call(spots, first, near, me, own, pieces, places, segq, segk):
    rows, width = own.shape
    blocks = len(spots)
    tall = blocks * rows
    part = 256
    steps = width // part
    heads = part // HDIM
    cols = lambda depth: pl.BlockSpec((depth, part), lambda g: (0, g))
    flops = 2 * tall * width * width * 2 + 4 * tall * rows * width * 4
    owners = 2 * pieces[0].shape[0]
    each = width // owners
    return pl.pallas_call(
        functools.partial(attention_kernel, blocks, first, rows, places),
        grid=(steps,),
        in_specs=[pl.BlockSpec(memory_space=pl.ANY)] * blocks
        + [
            pl.BlockSpec(memory_space=pltpu.SMEM),
            pl.BlockSpec(memory_space=pltpu.SMEM),
            pl.BlockSpec((rows, width), lambda g: (0, 0)),
        ] + [pl.BlockSpec(memory_space=pl.ANY)] * 4 + [
            pl.BlockSpec((1, rows), lambda g: (0, 0)),
            pl.BlockSpec(segk.shape, lambda g: (0, 0)),
        ],
        out_specs=[
            pl.BlockSpec((owners, 3 * each, width), lambda g: (0, 0, 0)),
            cols(rows), cols(PROMPT), cols(PROMPT), cols(tall - PROMPT), cols(tall - PROMPT),
            cols(rows), pl.BlockSpec((1, 8, rows), lambda g: (g, 0, 0)),
        ],
        out_shape=[
            jax.ShapeDtypeStruct((owners, 3 * each, width), BF),
            jax.ShapeDtypeStruct((rows, width), BF),
            jax.ShapeDtypeStruct((PROMPT, width), BF),
            jax.ShapeDtypeStruct((PROMPT, width), BF),
            jax.ShapeDtypeStruct((tall - PROMPT, width), BF),
            jax.ShapeDtypeStruct((tall - PROMPT, width), BF),
            jax.ShapeDtypeStruct((rows, width), BF),
            jax.ShapeDtypeStruct((steps, 8, rows), F32),
        ],
        scratch_shapes=[
            pltpu.VMEM((tall, width), BF),
            pltpu.VMEM((heads, tall, rows), F32),
            pltpu.VMEM((owners, 8, width), BF),
            pltpu.VMEM((8, width), F32),
            pltpu.SemaphoreType.DMA((blocks,)),
            pltpu.SemaphoreType.DMA((3, owners)),
        ],
        compiler_params=pltpu.CompilerParams(vmem_limit_bytes=60 * 2**20),
        cost_estimate=pl.CostEstimate(
            flops=flops, bytes_accessed=12 * 2**20, transcendentals=tall * rows * 12
        ),
        name="attention",
    )(*spots, near, me, own, *pieces, segq, segk)


def halves(value, runs, core):
    depth = value.shape[0] // runs
    pick = lambda first: jnp.concatenate(
        [value[i * depth : (i + 1) * depth] for i in range(first, runs, 2)], 0
    )
    even, odd = pick(0), pick(1)
    return jnp.where(core == 0, odd, even), jnp.where(core == 0, even, odd)


def middle_kernel(wide, ctx_ref, own_ref, cot_ref, wo_ref, wi_ref, wu_ref, vec_ref, bin_ref,
                  out_ref, h1_ref, gctx_ref, grads, sums_ref, sbin_ref,
                  first_ref, n1_ref, inv_ref, low_ref, pre_ref, cdf_ref, act_ref, acc_ref,
                  gffn_ref, glow_ref, out_buf, in_buf, wo_buf, sems):
    step = pl.program_id(0)
    width = ctx_ref.shape[1]
    square = lambda ref: ref[...].reshape(width, width)
    vec = lambda i: vec_ref[i : i + 1, :]
    mean = lambda v: jnp.sum(v, axis=-1, keepdims=True) * (1.0 / width)
    down = lambda v: jnp.sum(v, axis=0, keepdims=True)
    owners = wi_ref.shape[0]
    each = width // owners
    some = owners // wide

    def outer(at):
        turn = (2 * wide - 1 - at) % 2
        place = grads.at[pl.ds(at * some, some), pl.ds(0, wide * each)]
        return pltpu.make_async_copy(out_buf.at[turn], place, sems.at[turn])

    def inner(at):
        turn = (2 * wide - 1 - at) % 2
        place = grads.at[:, pl.ds((wide + 1 + at) * each, each)]
        return pltpu.make_async_copy(in_buf.at[turn], place, sems.at[2 + turn])

    def output():
        return pltpu.make_async_copy(wo_buf, grads.at[:, pl.ds(wide * each, each)], sems.at[4])

    @pl.when(step == 0)
    def _():
        hidden = own_ref[...].astype(F32) + mm(ctx_ref[...], square(wo_ref)) + vec(0)
        centred = hidden - mean(hidden)
        inverse = lax.rsqrt(mean(centred * centred) + NORM_EPS)
        normed = centred * inverse
        n1_ref[...] = normed
        inv_ref[...] = inverse
        first = normed * vec(1) + vec(2)
        first_ref[...] = first
        low_ref[...] = first.astype(BF)

    @pl.when(step < wide)
    def _():
        chunk = pl.ds(pl.multiple_of(step * width, width), width)
        pre = mm(low_ref[...], square(wi_ref)) + bin_ref[pl.ds(step, 1), :]
        cdf = 0.5 * (1.0 + lax.erf(pre * SQRT_HALF))
        act = (pre * cdf).astype(BF)
        pre_ref[:, chunk] = pre
        cdf_ref[:, chunk] = cdf
        act_ref[:, chunk] = act
        more = mm(act, square(wu_ref))

        @pl.when(step == 0)
        def _():
            acc_ref[...] = more

        @pl.when(step > 0)
        def _():
            acc_ref[...] += more

    @pl.when(step == wide - 1)
    def _():
        hidden = first_ref[...] + acc_ref[...] + vec(3)
        centred = hidden - mean(hidden)
        inverse = lax.rsqrt(mean(centred * centred) + NORM_EPS)
        normed = centred * inverse
        out_ref[...] = (normed * vec(4) + vec(5)).astype(BF)
        grad = cot_ref[...].astype(F32)
        sums_ref[0:1, :] = down(grad * normed)
        sums_ref[1:2, :] = down(grad)
        e = grad * vec(4)
        back = inverse * (e - mean(e) - normed * mean(e * normed))
        gffn_ref[...] = back
        low = back.astype(BF)
        glow_ref[...] = low
        sums_ref[2:3, :] = down(low.astype(F32))

    @pl.when(step >= wide)
    def _():
        at = 2 * wide - 1 - step
        chunk = pl.ds(pl.multiple_of(at * width, width), width)
        pre = pre_ref[:, chunk]
        slope = cdf_ref[:, chunk] + pre * jnp.exp(-0.5 * pre * pre) * INV_ROOT_TAU
        low = glow_ref[...]
        grad = (nt(low, square(wu_ref)) * slope).astype(BF)
        sbin_ref[pl.ds(at, 1), :] = down(grad.astype(F32))
        turn = step % 2

        @pl.when(step >= wide + 2)
        def _():
            outer(at + 2).wait()
            inner(at + 2).wait()

        out_buf[turn] = tn(act_ref[:, chunk], low).astype(BF).reshape(some, wide * each, width)
        outer(at).start()
        in_buf[turn] = tn(low_ref[...], grad).astype(BF).reshape(owners, each, width)
        inner(at).start()
        gffn_ref[...] += nt(grad, square(wi_ref))

    @pl.when(step == 2 * wide - 1)
    def _():
        grad = gffn_ref[...]
        normed = n1_ref[...]
        sums_ref[3:4, :] = down(grad * normed)
        sums_ref[4:5, :] = down(grad)
        e = grad * vec(1)
        back = inv_ref[...] * (e - mean(e) - normed * mean(e * normed))
        h1_ref[...] = back
        low = back.astype(BF)
        sums_ref[5:6, :] = down(low.astype(F32))
        wo_buf[...] = tn(ctx_ref[...], low).astype(BF).reshape(owners, each, width)
        output().start()
        gctx = nt(low, square(wo_ref)).astype(BF)
        gctx_ref[...] = gctx
        sums_ref[6:7, :] = down(gctx.astype(F32))
        sums_ref[7:8, :] = jnp.zeros((1, width), F32)
        for at in (1, 0):
            outer(at).wait()
            inner(at).wait()
        output().wait()


def middle_call(ctx, own, cot, got, vec, b_inner):
    rows, width = own.shape
    owners = got.shape[0]
    each = width // owners
    wide = WIDE
    whole = lambda shape: pl.BlockSpec(shape, lambda s: (0,) * len(shape))
    at = lambda s: jnp.where(s < wide, s, 2 * wide - 1 - s)
    shape = jax.ShapeDtypeStruct
    return pl.pallas_call(
        functools.partial(middle_kernel, wide),
        grid=(2 * wide,),
        in_specs=[
            whole((rows, width)), whole((rows, width)), whole((rows, width)),
            pl.BlockSpec((owners, each, width), lambda s: (0, WO, 0)),
            pl.BlockSpec((owners, each, width), lambda s: (0, WI + at(s), 0)),
            pl.BlockSpec((owners // wide, wide * each, width), lambda s: (at(s), 0, 0)),
            whole((8, width)), whole((8, width)),
        ],
        out_specs=[
            whole((rows, width)), whole((rows, width)), whole((rows, width)),
            pl.BlockSpec(memory_space=pl.ANY),
            whole((8, width)), whole((8, width)),
        ],
        out_shape=[
            shape((rows, width), BF), shape((rows, width), F32), shape((rows, width), BF),
            shape((owners, (2 * wide + 1) * each, width), BF),
            shape((8, width), F32), shape((8, width), F32),
        ],
        scratch_shapes=[
            pltpu.VMEM((rows, width), F32), pltpu.VMEM((rows, width), F32), pltpu.VMEM((rows, 1), F32),
            pltpu.VMEM((rows, width), BF), pltpu.VMEM((rows, wide * width), F32),
            pltpu.VMEM((rows, wide * width), F32), pltpu.VMEM((rows, wide * width), BF),
            pltpu.VMEM((rows, width), F32), pltpu.VMEM((rows, width), F32),
            pltpu.VMEM((rows, width), BF),
            pltpu.VMEM((2, owners // wide, wide * each, width), BF),
            pltpu.VMEM((2, owners, each, width), BF),
            pltpu.VMEM((owners, each, width), BF), pltpu.SemaphoreType.DMA((5,)),
        ],
        compiler_params=pltpu.CompilerParams(vmem_limit_bytes=60 * 2**20),
        cost_estimate=pl.CostEstimate(
            flops=2 * rows * width * width * (6 * wide + 3), bytes_accessed=32 * 2**20,
            transcendentals=2 * rows * width * wide,
        ),
        name="middle",
    )(ctx, own, cot, got, got, got, vec, b_inner)


def back_kernel(rows, bound, started, *refs):
    near_ref, gctx_ref, ctx_ref, q_ref, k_ref, v_ref, lse_ref, segq_ref, segk_ref = refs[:9]
    dk_ref, dv_ref, dq_ref = refs[-3:]
    q, g = q_ref[...], gctx_ref[...]
    part = q.shape[1]
    heads = part // HDIM
    masks = [heads_mask(q.shape, h) for h in range(heads)]
    q_parts = [jnp.where(m, q, 0) for m in masks]
    g_parts = [jnp.where(m, g, 0) for m in masks]
    product = (g.astype(F32) * ctx_ref[...].astype(F32)).T
    inner = [
        jnp.sum(product[h * HDIM : (h + 1) * HDIM], axis=0, keepdims=True) for h in range(heads)
    ]

    def one(b, dq):
        here = pl.ds(pl.multiple_of(b * rows, rows), rows)
        k, v = k_ref[here, :], v_ref[here, :]
        kt = k.T
        if bound is None:
            allowed = segk_ref[here, :] == segq_ref[...]
        dk = jnp.zeros((rows, part), F32)
        dv = jnp.zeros((rows, part), F32)
        out = []
        for h in range(heads):
            s = nt(k, q_parts[h])
            if bound is None:
                s = jnp.where(allowed, s, MASK_FILL)
            p = jnp.exp(s - lse_ref[0, h : h + 1, :])
            dp = nt(v, g_parts[h])
            ds = (p * (dp - inner[h])).astype(BF)
            dv = dv + mm(p.astype(BF), g_parts[h])
            dk = dk + mm(ds, q_parts[h])
            out.append(dq[h] + mm(kt[h * HDIM : (h + 1) * HDIM], ds))
        dk_ref[here, :] = dk.astype(BF)
        dv_ref[here, :] = dv.astype(BF)
        return tuple(out)

    if started:
        dq = tuple(refs[9][h * HDIM : (h + 1) * HDIM, :] for h in range(heads))
    else:
        dq = tuple(jnp.zeros((HDIM, rows), F32) for _ in range(heads))
    dq = lax.fori_loop(0, near_ref[0] if bound is None else bound, one, dq)
    dq_ref[...] = jnp.concatenate(dq, 0)


def back_call(start, steps, bound, near, gctx, ctx, q, k, v, lse, segq, segk, dq0=None, into=None):
    rows, width = q.shape
    tall = k.shape[0]
    part = 256
    cols = lambda depth: pl.BlockSpec((depth, part), lambda g: (0, start + g))
    whole = lambda shape: pl.BlockSpec(shape, lambda g: (0,) * len(shape))
    down = pl.BlockSpec((part, rows), lambda g: (start + g, 0))
    shape = jax.ShapeDtypeStruct
    extra = ([dq0] if dq0 is not None else []) + list(into or [])
    specs = ([down] if dq0 is not None else []) + [pl.BlockSpec(memory_space=pl.ANY)] * len(into or [])
    return pl.pallas_call(
        functools.partial(back_kernel, rows, bound, dq0 is not None),
        grid=(steps,),
        in_specs=[
            pl.BlockSpec(memory_space=pltpu.SMEM),
            cols(rows), cols(rows), cols(rows), cols(tall), cols(tall),
            pl.BlockSpec((1, 8, rows), lambda g: (start + g, 0, 0)),
            whole((1, rows)), whole(segk.shape),
        ] + specs,
        out_specs=[cols(tall), cols(tall), down],
        out_shape=[shape((tall, width), BF), shape((tall, width), BF), shape((width, rows), F32)],
        input_output_aliases={9 + i: i for i in range(3)} if into else {},
        compiler_params=pltpu.CompilerParams(vmem_limit_bytes=60 * 2**20),
        cost_estimate=pl.CostEstimate(
            flops=2 * 10 * 2 * tall * rows * part * steps * 2,
            bytes_accessed=8 * tall * part * steps, transcendentals=tall * rows * 4 * steps,
        ),
        name="attention_back",
    )(near, gctx, ctx, q, k, v, lse, segq, segk, *extra)


def product_kernel(rows, bound, near_ref, dk_ref, dv_ref, wk_ref, wv_ref, gx_ref):
    @pl.when((pl.program_id(0) < near_ref[0]) | (bound is not None))
    def _():
        width = dk_ref.shape[1]
        wk, wv = wk_ref[...].reshape(width, width), wv_ref[...].reshape(width, width)
        gx_ref[0] = (nt(dk_ref[...], wk) + nt(dv_ref[...], wv)).astype(BF)


def product_call(bound, near, dk, dv, got, rows):
    tall, width = dk.shape
    owners, each = got.shape[0], width // got.shape[0]
    weight = lambda place: pl.BlockSpec((owners, each, width), lambda b: (0, place, 0))
    return pl.pallas_call(
        functools.partial(product_kernel, rows, bound),
        grid=(tall // rows,),
        in_specs=[
            pl.BlockSpec(memory_space=pltpu.SMEM),
            pl.BlockSpec((rows, width), lambda b: (b, 0)),
            pl.BlockSpec((rows, width), lambda b: (b, 0)),
            weight(WK), weight(WV),
        ],
        out_specs=pl.BlockSpec((1, rows, width), lambda b: (b, 0, 0)),
        out_shape=jax.ShapeDtypeStruct((tall // rows, rows, width), BF),
        compiler_params=pltpu.CompilerParams(vmem_limit_bytes=60 * 2**20),
        cost_estimate=pl.CostEstimate(
            flops=4 * tall * width * width, bytes_accessed=6 * tall * width, transcendentals=0
        ),
        name="token_product",
    )(near, dk, dv, got, got)


def weight_kernel(blocks, first, rows, runs, *refs):
    spots = refs[:blocks]
    (near_ref, core_ref, own_ref, dq_ref, wq_ref, h1_ref, dkp_ref, dvp_ref, dkn_ref, dvn_ref,
     q_send, q_keep, kv_send, kv_keep, gown_ref, sums_ref, x_ref, sems) = refs[blocks:]
    core = core_ref[0]
    at = lambda b: pl.ds(pl.multiple_of(b * rows, rows), rows)
    step = pl.program_id(0)

    @pl.when(step == 0)
    def _():
        copies = [
            pltpu.make_async_copy(spot, x_ref.at[pl.ds(i * rows, rows)], sems.at[i])
            for i, spot in enumerate(spots)
        ]
        for copy in copies:
            copy.start()
        for copy in copies:
            copy.wait()
        gown_ref[...] = h1_ref[...]

    scale = HDIM**-0.5
    dq = dq_ref[...].T.astype(BF)
    part = dq.shape[1]
    width = x_ref.shape[1]
    gown_ref[...] += nt(dq, wq_ref[...].reshape(width, part)) * scale
    away, here = halves((tn(own_ref[...], dq) * scale).astype(BF), runs, core)
    q_send[...] = away.reshape(q_send.shape)
    q_keep[...] = here.reshape(q_send.shape)
    sums_ref[0:1, :] = jnp.sum(dq.astype(F32), axis=0, keepdims=True) * scale

    def products(b, carry, dk_ref, dv_ref, base):
        dk, dv, x = dk_ref[at(b), :], dv_ref[at(b), :], x_ref[at(base + b), :]
        wk, wv = carry
        return wk + tn(x, dk), wv + tn(x, dv)

    zero = jnp.zeros((width, part), F32)
    carry = (zero, zero)
    carry = lax.fori_loop(0, first, lambda b, c: products(b, c, dkp_ref, dvp_ref, 0), carry)
    carry = lax.fori_loop(0, near_ref[0], lambda b, c: products(b, c, dkn_ref, dvn_ref, first), carry)
    for i, grad in enumerate(carry):
        away, here = halves(grad.astype(BF), runs, core)
        shape = kv_send.shape[:2] + (part,)
        kv_send[:, :, i * part : (i + 1) * part] = away.reshape(shape)
        kv_keep[:, :, i * part : (i + 1) * part] = here.reshape(shape)
    sums_ref[1:8, :] = jnp.zeros((7, part), F32)


def weight_call(spots, first, near, own, dq, got, h1, dkp, dvp, dkn, dvn, core, runs):
    rows, width = own.shape
    blocks = len(spots)
    tall = blocks * rows
    part = 256
    steps = width // part
    cols = lambda depth, size=part: pl.BlockSpec((depth, size), lambda g: (0, g))
    whole = lambda shape: pl.BlockSpec(shape, lambda g: (0,) * len(shape))
    shape = jax.ShapeDtypeStruct
    owners, each = got.shape[0], width // got.shape[0]
    half = owners // 2
    slab = lambda size: pl.BlockSpec((half, each, size), lambda g: (0, 0, g))
    return pl.pallas_call(
        functools.partial(weight_kernel, blocks, first, rows, runs),
        grid=(steps,),
        in_specs=[pl.BlockSpec(memory_space=pl.ANY)] * blocks
        + [
            pl.BlockSpec(memory_space=pltpu.SMEM),
            pl.BlockSpec(memory_space=pltpu.SMEM),
            whole((rows, width)), pl.BlockSpec((part, rows), lambda g: (g, 0)),
            pl.BlockSpec((owners, each, part), lambda g: (0, WQ, g)),
            whole((rows, width)), cols(PROMPT), cols(PROMPT), cols(tall - PROMPT), cols(tall - PROMPT),
        ],
        out_specs=[
            slab(part), slab(part), slab(2 * part), slab(2 * part), whole((rows, width)), cols(8),
        ],
        out_shape=[
            shape((half, each, width), BF), shape((half, each, width), BF),
            shape((half, each, 2 * width), BF), shape((half, each, 2 * width), BF),
            shape((rows, width), F32), shape((8, width), F32),
        ],
        scratch_shapes=[pltpu.VMEM((tall, width), BF), pltpu.SemaphoreType.DMA((blocks,))],
        compiler_params=pltpu.CompilerParams(vmem_limit_bytes=60 * 2**20),
        cost_estimate=pl.CostEstimate(
            flops=4 * tall * width * width, bytes_accessed=12 * tall * width, transcendentals=0
        ),
        name="weight_product",
    )(*spots, near, core, own, dq, got, h1, dkp, dvp, dkn, dvn)


def real_owners(grads, count, step, width):
    split = count // 32
    take = lambda v: v.reshape(32, -1, split, step, width).transpose(0, 2, 1, 3, 4).reshape(count, -1, width)
    outer, rest = grads[:, : 4 * split * step], grads[:, 4 * split * step :]
    return jnp.concatenate([outer.reshape(count, 4 * step, width), take(rest)], 1)


def solution(mesh):
    plan = Plan(mesh.shape["grp"], mesh.shape["row"])

    def per_device(
        tokens, cont_lengths, cotangent, w_query, w_key, w_value, w_output, w_inner, w_outer,
        bias_query, bias_value, bias_output, gain_first, shift_first, bias_inner, bias_outer,
        gain_second, shift_second,
    ):
        count = plan.count
        _, rows, width = tokens.shape
        step = w_query.shape[0]
        wide = w_inner.shape[1] // width
        own = tokens[0]

        early = (bias_query, bias_value)
        late = (bias_output, gain_first, shift_first, bias_outer, gain_second, shift_second, bias_inner)
        small = len(late) - 1

        def in_line(vectors):
            line, place = 0, 0
            for vector in vectors:
                size = vector.shape[0]
                line = line + jnp.pad(vector, (place, width - place - size))
                place += size
            return jnp.pad(line[None], ((0, 7), (0, 0)))

        line = jnp.concatenate([in_line(early), in_line(late)], 0)
        runs = plan.grp
        grp, row = lax.axis_index("grp"), lax.axis_index("row")
        core = (grp % 2).astype(jnp.int32).reshape(1)
        exchange = Tokens(plan, own)
        squares = (w_query, w_key, w_value)
        if step % 8 == 0:
            first_pack, pack = pack_call(w_output, w_inner, w_outer, *squares, line)
            got = lax.all_gather(pack, AXES, axis=0, tiled=True).reshape(count, -1, width)
            lines = got[:, (WI + WIDE) * step]

            def swaps(value, bits):
                masks = [0]
                for bit in bits:
                    masks = masks + [m ^ bit for m in masks]
                return [plan.swap(value, m) for m in masks[1:]]

            def stage(held, bit):
                return jnp.concatenate([held, plan.swap(held, bit)], 0)

            away = swaps(first_pack, plan.z)
            *away, same, beside = tie(*away, *exchange.stage_one())
            exchange.same, exchange.beside = same, beside
            cut = step + 8
            one = jnp.stack([v[:cut] for v in (first_pack, *away)])
            two = jnp.stack([v[cut:] for v in (first_pack, *away)])
            one, two = stage(one, plan.y[0]), stage(two, plan.x[0])
            one, two, *seen = tie(one, two, *exchange.stage_two())
            exchange.other, exchange.same_y, exchange.diagonal = seen
            one, two = stage(one, plan.x[0]), stage(two, plan.y[0])
            exchange.stage_three()
            one, two, exchange.other_y = tie(one, two, exchange.other_y)
            pieces = [one, plan.swap(one, plan.core[0]), two, plan.swap(two, plan.core[0])]
            order = lambda *bits: ([(bit, 1 << i) for i, bit in enumerate(bits)], plan.core[0])
            places = (
                order(*plan.z, plan.y[0], plan.x[0]),
                order(*plan.z, plan.x[0], plan.y[0]),
            )
            me = plan.me().astype(jnp.int32).reshape(1)
        else:
            inner_rows = [w_inner[:, i * width : (i + 1) * width] for i in range(wide)]
            pack = jnp.concatenate([w_outer, w_output, *inner_rows, *squares, line], 0)
            got = lax.all_gather(pack, AXES, axis=0, tiled=True).reshape(count, -1, width)
            lines = got[:, 12 * step + 8]
            cuts = [wide * step, (wide + 1) * step, (2 * wide + 1) * step, 12 * step]
            outer, output, inner, rest, marks = jnp.split(got, cuts, axis=1)
            apart = lambda v, n: v.reshape(count, n, step, width).transpose(1, 0, 2, 3)
            inner, rest = [
                v.reshape(v.shape[0], 32, width // 32, width).transpose(1, 0, 2, 3)
                for v in (apart(inner, wide), apart(rest, 3))
            ]
            got = jnp.concatenate([v.reshape(32, -1, width) for v in (outer, output, inner)], 1)
            pairs = marks[:, 0, : 2 * step].reshape(32, count // 32, 2, step).transpose(0, 2, 1, 3)
            pairs = jnp.pad(pairs.reshape(32, 1, -1), ((0, 0), (0, 7), (0, width - 2 * width // 32)))
            one = jnp.concatenate([rest[:, 0], pairs], 1)
            two = rest[:, 1:].reshape(32, -1, width)
            pieces = [one[:16], one[16:], two[:16], two[16:]]
            places = (([(1, 1), (2, 2), (4, 4), (8, 8)], 16),) * 2
            me = jnp.zeros((1,), jnp.int32)
        spots, near = exchange.spots()
        first_near = PROMPT // rows

        table = lines[:, : small * step].reshape(count, small, step).transpose(1, 0, 2)
        table = table.reshape(small, width).astype(F32)
        v_bin = lines[:, small * step : (small + wide) * step].reshape(wide, width).astype(F32)
        v_bin = jnp.pad(v_bin, ((0, 8 - wide), (0, 0)))
        segments = segment_ids(cont_lengths[0], plan.row * rows)
        seg_own = lax.dynamic_slice_in_dim(segments, row * rows, rows, 0)[None, :]
        seg_near = near_segments(plan, segments, rows)[:, None]
        near = near.astype(jnp.int32).reshape(1)

        squares, queries, keys_p, values_p, keys_n, values_n, context, log_total = attention_call(
            spots, first_near, near, me, own, pieces, places, seg_own, seg_near
        )
        vec = jnp.concatenate([table, jnp.zeros((2, width), F32)], 0)
        layer_out, grad_h1, grad_context, grads, sums, sums_bin = middle_call(
            context, own, cotangent[0], got, vec, v_bin
        )
        if step % 8:
            grads = real_owners(grads, count, step, width)
        o_ab = lax.psum_scatter(
            grads.reshape(-1, width), AXES, scatter_dimension=0, tiled=True
        ).astype(F32)
        core_bit = plan.core[0]
        left = [1 << i for i in reversed(range(plan.bits)) if 1 << i != core_bit]
        parts = width // 256
        dkp, dvp, dqp = back_call(
            0, parts, first_near, near, grad_context, context, queries, keys_p, values_p, log_total,
            seg_own, seg_near,
        )
        shared_p = product_call(first_near, near, dkp, dvp, squares, rows)
        returned = Return(plan, rows)
        returned.prompt_one(shared_p)
        dkn, dvn, dq = back_call(
            0, parts, None, near, grad_context, context, queries, keys_n, values_n, log_total,
            seg_own, seg_near, dqp,
        )
        shared_n = product_call(None, near, dkn, dvn, squares, rows)
        returned.same, shared_n, dq = tie(returned.same, shared_n, dq)
        returned.prompt_two()
        returned.near(shared_n)
        q_send, q_keep, kv_send, kv_keep, grad_own, sums_qkv = weight_call(
            spots, first_near, near, own, dq, squares, grad_h1, dkp, dvp, dkn, dvn, core, runs
        )
        q_send, q_keep, kv_send, kv_keep, returned.same, returned.own = tie(
            q_send, q_keep, kv_send, kv_keep, returned.same, returned.own
        )
        returned.prompt_three()

        order = (6, 5, 3, 4, 2, 0, 1)
        small = len(early) + len(late) - 1
        d_table = jnp.concatenate([sums_qkv[:1]] + [sums[i : i + 1] for i in order], 0)
        d_lines = jnp.concatenate(
            [
                d_table.reshape(small, count, step).transpose(1, 0, 2).reshape(count, -1),
                sums_bin[:wide].reshape(count, wide * step),
            ],
            1,
        )
        d_lines = jnp.pad(d_lines, ((0, 0), (0, width - d_lines.shape[1])))[:, None].astype(BF)
        d_lines = jnp.pad(d_lines, ((0, 0), (0, 7), (0, 0)))
        place = core[0]
        pick = Reduce(plan, [])
        if step % 8:
            q_send, q_keep, kv_send, kv_keep = [
                v.reshape(count // 2, step, -1) for v in (q_send, q_keep, kv_send, kv_keep)
            ]
        q_send = jnp.concatenate([q_send, pick.cut(d_lines, core_bit, 1 - place)], 1)
        q_keep = jnp.concatenate([q_keep, pick.cut(d_lines, core_bit, place)], 1)
        r_q = Reduce(plan, [q_keep, plan.swap(q_send, core_bit)], left)
        r_kv = Reduce(plan, [kv_keep, plan.swap(kv_send, core_bit)], left)
        for one, two in zip(plan.x + plan.y + plan.z[::-1], plan.y + plan.x + plan.z[::-1]):
            n = len(r_q.terms)
            if one == plan.z[0]:
                *tied, returned.back = tie(*r_q.terms, *r_kv.terms, returned.back)
            else:
                tied = tie(*r_q.terms, *r_kv.terms)
            r_q.terms, r_kv.terms = list(tied[:n]), list(tied[n:])
            r_q.stage(one)
            r_kv.stage(two)
        grad_tokens = grad_own + returned.total()
        o_query = r_q.result()
        o_line = o_query[step]
        o_both = r_kv.result().reshape(step, parts, 2, width // parts)

        o_small = [o_line[i * step : (i + 1) * step] for i in range(small)]
        o_bin = o_line[small * step : (small + wide) * step]
        return (
            layer_out[None],
            grad_tokens.astype(BF)[None],
            o_query[:step],
            o_both[:, :, 0].reshape(step, width),
            o_both[:, :, 1].reshape(step, width),
            o_ab[wide * step : (wide + 1) * step],
            jnp.concatenate([o_ab[i * step : (i + 1) * step] for i in range(wide + 1, 2 * wide + 1)], 1),
            o_ab[: wide * step],
            o_small[0],
            o_small[1],
            o_small[2],
            o_small[3],
            o_small[4],
            o_bin,
            o_small[5],
            o_small[6],
            o_small[7],
        )

    split = P("grp", "row", None)
    owned2, owned1 = P(AXES, None), P(AXES)
    in_specs = (split, P("grp", None), split) + (owned2,) * 6 + (owned1,) * 9
    out_specs = (split, split) + (owned2,) * 6 + (owned1,) * 9
    return jax.shard_map(
        per_device, mesh=mesh, in_specs=in_specs, out_specs=out_specs, check_vma=False
    )
```

```python
import functools

import jax
import jax.numpy as jnp
import numpy as np
from jax import lax
from jax.experimental import pallas as pl
from jax.experimental.pallas import tpu as pltpu
from jax.sharding import Mesh
from jax.sharding import PartitionSpec as P

HEADS = 12
HDIM = 64
PROMPT = 1024
CONT_MOST = 256
BF = jnp.bfloat16
F32 = jnp.float32

NORM_EPS = 1e-12
MASK_FILL = -1000000000.0
SQRT_HALF = 0.7071067811865476
INV_ROOT_TAU = 0.3989422804014327
AXES = ("x", "core", "z", "y")
GRP, ROW = AXES[:2], AXES[2:]
WIDE = 4
WO, WI = 4, 5
WQ, WK, WV = 0, 1, 2


def mm(left, right):
    return jnp.dot(left, right, preferred_element_type=F32)


def segment_ids(lengths, group_len):
    ends = jnp.cumsum(lengths)
    places = jnp.arange(group_len, dtype=jnp.int32)
    passed = jnp.sum(((places - PROMPT)[:, None] >= ends[None, :]).astype(jnp.int32), axis=-1)
    return jnp.where(places < PROMPT, 0, 1 + passed)


class Plan:
    def __init__(self, grp, row):
        self.grp, self.row, self.count = grp, row, grp * row
        y = row // 4
        bits = lambda base, size: [base << i for i in range(size.bit_length() - 1)]
        self.y, self.z = bits(1, y), bits(y, 4)
        self.core, self.x = bits(row, 2), bits(2 * row, grp // 2)
        self.bits = self.count.bit_length() - 1

    def swap(self, value, mask):
        return lax.ppermute(value, AXES, [(i, i ^ mask) for i in range(self.count)])

    def send(self, value, moves):
        pairs = [(g * self.row + a, g * self.row + b) for g in range(self.grp) for a, b in moves]
        return lax.ppermute(value, AXES, pairs)

    def me(self):
        return lax.axis_index(AXES)


class Reduce:
    def __init__(self, plan, terms, left=None):
        self.plan, self.terms = plan, list(terms)
        self.left = left or [1 << i for i in reversed(range(plan.bits))]

    def cut(self, term, bit, place):
        at = self.left.index(bit)
        high, low = 1 << at, 1 << (len(self.left) - at - 1)
        _, rows, width = term.shape
        term = term.reshape(high, 2, low * rows, width)
        return lax.dynamic_slice_in_dim(term, place, 1, 1).reshape(high * low, rows, width)

    def total(self, terms):
        return sum([t.astype(F32) for t in terms[1:]], terms[0].astype(F32))

    def stage(self, bit):
        place = (self.plan.me() // bit) & 1
        away = self.total([self.cut(t, bit, 1 - place) for t in self.terms]).astype(BF)
        here = [self.cut(t, bit, place) for t in self.terms]
        self.left = [b for b in self.left if b != bit]
        self.terms = here + [self.plan.swap(away, bit)]

    def result(self):
        return self.total(self.terms)[0]


def tie(*values):
    return lax.optimization_barrier(values)


class Tokens:
    def __init__(self, plan, own):
        self.plan, self.own = plan, own
        self.rows = own.shape[0]
        self.ready = plan.row == 8

    def stage_one(self):
        if self.ready:
            plan, own = self.plan, self.own
            across = plan.send(own, [(0, 4), (1, 5), (2, 6), (3, 7)])
            self.same = jnp.where(lax.axis_index(ROW) < 4, own, across)
            self.beside = plan.swap(own, 1)
            return [self.same, self.beside]
        return []

    def stage_two(self):
        if self.ready:
            plan = self.plan
            self.other = plan.swap(self.same, 2)
            self.same_y = plan.swap(self.same, 1)
            self.diagonal = plan.send(self.own, [(5, 6), (6, 5)])
            return [self.other, self.same_y, self.diagonal]
        return []

    def stage_three(self):
        if self.ready:
            self.other_y = self.plan.swap(self.other, 1)

    def spots(self):
        row, rows, own = lax.axis_index(ROW), self.rows, self.own
        if self.ready:
            near = jnp.where(row < 4, 0, jnp.where((row == 5) | (row == 6), 3, 2))
            return [
                self.same, self.other, self.same_y, self.other_y, own, self.beside, self.diagonal,
            ], near
        every = lax.all_gather(own, ROW, axis=0, tiled=True)
        start = jnp.maximum(row * rows - CONT_MOST, 0)
        padded = jnp.concatenate([every, jnp.zeros((CONT_MOST, own.shape[1]), own.dtype)], 0)
        near = lax.dynamic_slice_in_dim(padded, start, rows + 2 * CONT_MOST, 0)
        every = jnp.concatenate([every[:PROMPT], near], 0)
        spots = [every[i : i + rows] for i in range(0, every.shape[0], rows)]
        return spots, jnp.where(row * rows < PROMPT, 0, near.shape[0] // rows)


def near_segments(plan, segments, rows):
    row = lax.axis_index(ROW)
    if plan.row != 8:
        start = jnp.maximum(row * rows - CONT_MOST, 0)
        padded = jnp.concatenate([segments, jnp.full((CONT_MOST,), -1, jnp.int32)], 0)
        near = lax.dynamic_slice_in_dim(padded, start, rows + 2 * CONT_MOST, 0)
        return jnp.where((near == 0) | (row * rows < PROMPT), -1, near)
    pieces = []
    for block, valid in (
        (row, row >= 4),
        (row ^ 1, row >= 4),
        (11 - row, (row == 5) | (row == 6)),
    ):
        block = jnp.clip(block, 0, 7)
        ids = lax.dynamic_slice_in_dim(segments, block * rows, rows, 0)
        pieces.append(jnp.where(valid, ids, -1))
    return jnp.concatenate(pieces, 0)


class Return:
    def __init__(self, plan, rows):
        self.plan, self.rows = plan, rows

    def prompt_one(self, parts):
        self.prompt = self.same = self.own = self.back = parts
        if self.plan.row == 8:
            same, other, same_y, other_y = [parts[i].astype(F32) for i in range(4)]
            self.other = (other + self.plan.swap(parts[3], 1).astype(F32)).astype(BF)
            self.same = same + self.plan.swap(parts[2], 1).astype(F32)

    def prompt_two(self):
        if self.plan.row == 8:
            self.same = self.same + self.plan.swap(self.other, 2).astype(F32)

    def prompt_three(self):
        if self.plan.row == 8:
            self.back = self.plan.send(self.same.astype(BF), [(4, 0), (5, 1), (6, 2), (7, 3)])

    def near(self, parts):
        self.around = parts
        if self.plan.row == 8:
            own = parts[0].astype(F32) + self.plan.swap(parts[1], 1).astype(F32)
            self.own = own + self.plan.send(parts[2], [(5, 6), (6, 5)]).astype(F32)

    def total(self):
        row, rows = lax.axis_index(ROW), self.rows
        if self.plan.row == 8:
            return jnp.where(row < 4, self.same + self.back.astype(F32), self.own)
        around = self.around.reshape(-1, self.around.shape[-1]).astype(F32)
        start = jnp.maximum(row * rows - CONT_MOST, 0)
        whole = jnp.zeros((self.plan.row * rows + CONT_MOST, around.shape[1]), F32)
        whole = whole.at[:PROMPT].set(self.prompt.reshape(PROMPT, -1).astype(F32))
        near = jnp.where(row * rows < PROMPT, 0, around)
        near = lax.dynamic_slice_in_dim(whole, start, rows + 2 * CONT_MOST, 0) + near
        whole = lax.dynamic_update_slice_in_dim(whole, near, start, 0)
        return lax.psum_scatter(whole[: self.plan.row * rows], ROW, scatter_dimension=0, tiled=True)


def heads_mask(lanes, head):
    lane = lax.broadcasted_iota(jnp.int32, lanes, 1)
    return (lane >= head * HDIM) & (lane < (head + 1) * HDIM)


def nt(left, right):
    return lax.dot_general(left, right, (((1,), (1,)), ((), ())), preferred_element_type=F32)


def tn(left, right):
    return lax.dot_general(left, right, (((0,), (0,)), ((), ())), preferred_element_type=F32)


def pack_kernel(wo_ref, wi_ref, wu_ref, wq_ref, wk_ref, wv_ref, line_ref, early_ref, late_ref):
    step, width = wo_ref.shape
    early_ref[:step, :] = wq_ref[...]
    early_ref[step : step + 8, :] = line_ref[:8, :]
    early_ref[step + 8 : 2 * step + 8, :] = wk_ref[...]
    early_ref[2 * step + 8 :, :] = wv_ref[...]
    late_ref[: WIDE * step, :] = wu_ref[...]
    late_ref[WO * step : WI * step, :] = wo_ref[...]
    for i in range(WIDE):
        late_ref[(WI + i) * step : (WI + i + 1) * step, :] = wi_ref[:, i * width : (i + 1) * width]
    late_ref[(WI + WIDE) * step :, :] = line_ref[8:, :]


def pack_call(w_output, w_inner, w_outer, w_query, w_key, w_value, line):
    step, width = w_output.shape
    shape = lambda rows: jax.ShapeDtypeStruct((rows, width), BF)
    return pl.pallas_call(
        pack_kernel, out_shape=[shape(3 * step + 8), shape((WI + WIDE) * step + 8)], name="pack"
    )(w_output, w_inner, w_outer, w_query, w_key, w_value, line)


def attention_kernel(blocks, first, rows, places, *refs):
    spots = refs[:blocks]
    (near_ref, me_ref, own_ref, a0_ref, a1_ref, b0_ref, b1_ref, segq_ref, segk_ref,
     w_ref, q_ref, kp_ref, vp_ref, kn_ref, vn_ref, ctx_ref, lse_ref,
     x_ref, s_ref, line_ref, bias_ref, sems, w_sems) = refs[blocks:]
    near = near_ref[0]
    at = lambda b: pl.ds(pl.multiple_of(b * rows, rows), rows)
    depth = own_ref.shape[1]
    owners = w_ref.shape[0]
    each = depth // owners
    part = q_ref.shape[1]

    def weights(act):
        @pl.loop(0, owners)
        def _(e):
            away = e ^ me_ref[0]
            for (bits, half), (zero, one), parts in (
                (places[0], (a0_ref, a1_ref), ((0, each, w_ref, 0), (each, 8, line_ref, 0))),
                (places[1], (b0_ref, b1_ref), ((0, 2 * each, w_ref, each),)),
            ):
                j = sum([((away // bit) & 1) * weight for bit, weight in bits])
                for which, source in enumerate((zero, one)):

                    @pl.when(((away // half) & 1) == which)
                    def _():
                        for k, (top, size, target, base) in enumerate(parts):
                            act(pltpu.make_async_copy(
                                source.at[j, pl.ds(top, size)], target.at[e, pl.ds(base, size)],
                                w_sems.at[2 * k if zero is a0_ref else 1, e],
                            ))

    @pl.when(pl.program_id(0) == 0)
    def _():
        copies = [
            pltpu.make_async_copy(spot, x_ref.at[pl.ds(i * rows, rows)], sems.at[i])
            for i, spot in enumerate(spots)
        ]
        weights(lambda c: c.start())
        for copy in copies:
            copy.start()
        weights(lambda c: c.wait())
        for copy in copies:
            copy.wait()
        line = line_ref[:, 0, :128]
        place = lax.broadcasted_iota(jnp.int32, (128, depth), 0)
        lane = lax.broadcasted_iota(jnp.int32, (128, depth), 1)
        mine = lax.broadcasted_iota(jnp.int32, (owners, depth), 0)
        mine = mine == lax.broadcasted_iota(jnp.int32, (owners, depth), 1) // each
        for i in range(2):
            spread = mm(line, jnp.where(place == lane % each + i * each, 1.0, 0.0).astype(BF))
            bias_ref[i : i + 1, :] = jnp.sum(jnp.where(mine, spread, 0.0), axis=0, keepdims=True)

    lanes = pl.ds(pl.multiple_of(pl.program_id(0) * part, part), part)
    wq, wk, wv = [
        w_ref[:, i * each : (i + 1) * each, lanes].reshape(depth, part) for i in (WQ, WK, WV)
    ]
    queries = (mm(own_ref[...], wq) + bias_ref[0:1, lanes]) * (HDIM**-0.5)
    q_ref[...] = queries.astype(BF)

    def project(b, k_ref, v_ref, side):
        x = x_ref[at(b), :]
        k_ref[at(side), :] = mm(x, wk).astype(BF)
        v_ref[at(side), :] = (mm(x, wv) + bias_ref[1:2, lanes]).astype(BF)

    @pl.loop(0, first)
    def _(b):
        project(b, kp_ref, vp_ref, b)

    @pl.loop(0, near)
    def _(b):
        project(first + b, kn_ref, vn_ref, b)

    width = q_ref.shape[1]
    heads = width // HDIM
    q = q_ref[...]
    parts = [jnp.where(heads_mask(q.shape, h), q, 0) for h in range(heads)]

    def scores(b, peaks, k_ref, base):
        k = k_ref[at(b), :]
        out = []
        for h in range(heads):
            s = nt(k, parts[h])
            if base:
                s = jnp.where(segk_ref[at(b), :] == segq_ref[...], s, MASK_FILL)
            s_ref[h, at(base + b), :] = s
            out.append(jnp.maximum(peaks[h], jnp.max(s, axis=0, keepdims=True)))
        return tuple(out)

    peaks = tuple(jnp.full((1, rows), MASK_FILL, F32) for _ in range(heads))
    peaks = lax.fori_loop(0, first, lambda b, c: scores(b, c, kp_ref, 0), peaks)
    peaks = lax.fori_loop(0, near, lambda b, c: scores(b, c, kn_ref, first), peaks)

    def mix(b, carry, v_ref, base):
        totals, mixed = carry
        vt = v_ref[at(b), :].T
        new_totals, new_mixed = [], []
        for h in range(heads):
            p = jnp.exp(s_ref[h, at(base + b), :] - peaks[h])
            new_totals.append(totals[h] + jnp.sum(p, axis=0, keepdims=True))
            new_mixed.append(mixed[h] + mm(vt[h * HDIM : (h + 1) * HDIM], p.astype(BF)))
        return tuple(new_totals), tuple(new_mixed)

    zero = (
        tuple(jnp.zeros((1, rows), F32) for _ in range(heads)),
        tuple(jnp.zeros((HDIM, rows), F32) for _ in range(heads)),
    )
    carry = lax.fori_loop(0, first, lambda b, c: mix(b, c, vp_ref, 0), zero)
    totals, mixed = lax.fori_loop(0, near, lambda b, c: mix(b, c, vn_ref, first), carry)
    whole = jnp.concatenate([mixed[h] / totals[h] for h in range(heads)], 0)
    ctx_ref[...] = whole.T.astype(BF)
    for h in range(heads):
        lse_ref[0, h : h + 1, :] = peaks[h] + jnp.log(totals[h])


def attention_call(spots, first, near, me, own, pieces, places, segq, segk):
    rows, width = own.shape
    blocks = len(spots)
    tall = blocks * rows
    part = 256
    steps = width // part
    heads = part // HDIM
    cols = lambda depth: pl.BlockSpec((depth, part), lambda g: (0, g))
    flops = 2 * tall * width * width * 2 + 4 * tall * rows * width * 4
    owners = 2 * pieces[0].shape[0]
    each = width // owners
    return pl.pallas_call(
        functools.partial(attention_kernel, blocks, first, rows, places),
        grid=(steps,),
        in_specs=[pl.BlockSpec(memory_space=pl.ANY)] * blocks
        + [
            pl.BlockSpec(memory_space=pltpu.SMEM),
            pl.BlockSpec(memory_space=pltpu.SMEM),
            pl.BlockSpec((rows, width), lambda g: (0, 0)),
        ] + [pl.BlockSpec(memory_space=pl.ANY)] * 4 + [
            pl.BlockSpec((1, rows), lambda g: (0, 0)),
            pl.BlockSpec(segk.shape, lambda g: (0, 0)),
        ],
        out_specs=[
            pl.BlockSpec((owners, 3 * each, width), lambda g: (0, 0, 0)),
            cols(rows), cols(PROMPT), cols(PROMPT), cols(tall - PROMPT), cols(tall - PROMPT),
            cols(rows), pl.BlockSpec((1, 8, rows), lambda g: (g, 0, 0)),
        ],
        out_shape=[
            jax.ShapeDtypeStruct((owners, 3 * each, width), BF),
            jax.ShapeDtypeStruct((rows, width), BF),
            jax.ShapeDtypeStruct((PROMPT, width), BF),
            jax.ShapeDtypeStruct((PROMPT, width), BF),
            jax.ShapeDtypeStruct((tall - PROMPT, width), BF),
            jax.ShapeDtypeStruct((tall - PROMPT, width), BF),
            jax.ShapeDtypeStruct((rows, width), BF),
            jax.ShapeDtypeStruct((steps, 8, rows), F32),
        ],
        scratch_shapes=[
            pltpu.VMEM((tall, width), BF),
            pltpu.VMEM((heads, tall, rows), F32),
            pltpu.VMEM((owners, 8, width), BF),
            pltpu.VMEM((8, width), F32),
            pltpu.SemaphoreType.DMA((blocks,)),
            pltpu.SemaphoreType.DMA((3, owners)),
        ],
        compiler_params=pltpu.CompilerParams(vmem_limit_bytes=60 * 2**20),
        cost_estimate=pl.CostEstimate(
            flops=flops, bytes_accessed=12 * 2**20, transcendentals=tall * rows * 12
        ),
        name="attention",
    )(*spots, near, me, own, *pieces, segq, segk)


def halves(value, runs, core):
    depth = value.shape[0] // runs
    pick = lambda first: jnp.concatenate(
        [value[i * depth : (i + 1) * depth] for i in range(first, runs, 2)], 0
    )
    even, odd = pick(0), pick(1)
    return jnp.where(core == 0, odd, even), jnp.where(core == 0, even, odd)


def middle_kernel(wide, mapped, ctx_ref, own_ref, cot_ref, wo_ref, wi_ref, wu_ref, vec_ref, bin_ref,
                  out_ref, h1_ref, gctx_ref, grads, sums_ref, sbin_ref,
                  first_ref, n1_ref, inv_ref, low_ref, pre_ref, cdf_ref, act_ref, acc_ref,
                  gffn_ref, glow_ref, out_buf, in_buf, wo_buf, sems):
    step = pl.program_id(0)
    width = ctx_ref.shape[1]
    square = lambda ref: ref[...].reshape(width, width)
    vec = lambda i: vec_ref[i : i + 1, :]
    mean = lambda v: jnp.sum(v, axis=-1, keepdims=True) * (1.0 / width)
    down = lambda v: jnp.sum(v, axis=0, keepdims=True)
    owners = wi_ref.shape[0]
    each = width // owners
    some = owners // wide

    def slot(group, i):
        return group % 2 * 16 + group // 2 * 8 + i % 2 * 4 + i // 2 if mapped else group * 8 + i

    def outer(at):
        turn = (2 * wide - 1 - at) % 2
        return [
            pltpu.make_async_copy(
                out_buf.at[turn, i], grads.at[slot(at, i), pl.ds(0, wide * each)], sems.at[turn, i]
            )
            for i in range(some)
        ]

    def inner(at):
        turn = (2 * wide - 1 - at) % 2
        top = pl.multiple_of((wide + 1 + at) * each, each)
        return [
            pltpu.make_async_copy(
                in_buf.at[turn, e], grads.at[slot(e // 8, e % 8), pl.ds(top, each)], sems.at[2 + turn, e]
            )
            for e in range(owners)
        ]

    def output():
        return [
            pltpu.make_async_copy(
                wo_buf.at[e], grads.at[slot(e // 8, e % 8), pl.ds(wide * each, each)], sems.at[4, e]
            )
            for e in range(owners)
        ]

    def start(copies):
        for copy in copies:
            copy.start()

    def wait(copies):
        for copy in copies:
            copy.wait()

    @pl.when(step == 0)
    def _():
        hidden = own_ref[...].astype(F32) + mm(ctx_ref[...], square(wo_ref)) + vec(0)
        centred = hidden - mean(hidden)
        inverse = lax.rsqrt(mean(centred * centred) + NORM_EPS)
        normed = centred * inverse
        n1_ref[...] = normed
        inv_ref[...] = inverse
        first = normed * vec(1) + vec(2)
        first_ref[...] = first
        low_ref[...] = first.astype(BF)

    @pl.when(step < wide)
    def _():
        chunk = pl.ds(pl.multiple_of(step * width, width), width)
        pre = mm(low_ref[...], square(wi_ref)) + bin_ref[pl.ds(step, 1), :]
        cdf = 0.5 * (1.0 + lax.erf(pre * SQRT_HALF))
        act = (pre * cdf).astype(BF)
        pre_ref[:, chunk] = pre
        cdf_ref[:, chunk] = cdf
        act_ref[:, chunk] = act
        more = mm(act, square(wu_ref))

        @pl.when(step == 0)
        def _():
            acc_ref[...] = more

        @pl.when(step > 0)
        def _():
            acc_ref[...] += more

    @pl.when(step == wide - 1)
    def _():
        hidden = first_ref[...] + acc_ref[...] + vec(3)
        centred = hidden - mean(hidden)
        inverse = lax.rsqrt(mean(centred * centred) + NORM_EPS)
        normed = centred * inverse
        out_ref[...] = (normed * vec(4) + vec(5)).astype(BF)
        grad = cot_ref[...].astype(F32)
        sums_ref[0:1, :] = down(grad * normed)
        sums_ref[1:2, :] = down(grad)
        e = grad * vec(4)
        back = inverse * (e - mean(e) - normed * mean(e * normed))
        gffn_ref[...] = back
        low = back.astype(BF)
        glow_ref[...] = low
        sums_ref[2:3, :] = down(low.astype(F32))

    @pl.when(step >= wide)
    def _():
        at = 2 * wide - 1 - step
        chunk = pl.ds(pl.multiple_of(at * width, width), width)
        pre = pre_ref[:, chunk]
        slope = cdf_ref[:, chunk] + pre * jnp.exp(-0.5 * pre * pre) * INV_ROOT_TAU
        low = glow_ref[...]
        grad = (nt(low, square(wu_ref)) * slope).astype(BF)
        sbin_ref[pl.ds(at, 1), :] = down(grad.astype(F32))
        turn = step % 2

        @pl.when(step >= wide + 2)
        def _():
            wait(outer(at + 2) + inner(at + 2))

        out_buf[turn] = tn(act_ref[:, chunk], low).astype(BF).reshape(some, wide * each, width)
        start(outer(at))
        in_buf[turn] = tn(low_ref[...], grad).astype(BF).reshape(owners, each, width)
        start(inner(at))
        gffn_ref[...] += nt(grad, square(wi_ref))

    @pl.when(step == 2 * wide - 1)
    def _():
        grad = gffn_ref[...]
        normed = n1_ref[...]
        sums_ref[3:4, :] = down(grad * normed)
        sums_ref[4:5, :] = down(grad)
        e = grad * vec(1)
        back = inv_ref[...] * (e - mean(e) - normed * mean(e * normed))
        h1_ref[...] = back
        low = back.astype(BF)
        sums_ref[5:6, :] = down(low.astype(F32))
        wo_buf[...] = tn(ctx_ref[...], low).astype(BF).reshape(owners, each, width)
        start(output())
        gctx = nt(low, square(wo_ref)).astype(BF)
        gctx_ref[...] = gctx
        sums_ref[6:7, :] = down(gctx.astype(F32))
        sums_ref[7:8, :] = jnp.zeros((1, width), F32)
        wait(outer(1) + inner(1) + outer(0) + inner(0) + output())


def middle_call(ctx, own, cot, got, vec, b_inner, mapped):
    rows, width = own.shape
    owners = got.shape[0]
    each = width // owners
    wide = WIDE
    whole = lambda shape: pl.BlockSpec(shape, lambda s: (0,) * len(shape))
    at = lambda s: jnp.where(s < wide, s, 2 * wide - 1 - s)
    shape = jax.ShapeDtypeStruct
    return pl.pallas_call(
        functools.partial(middle_kernel, wide, mapped),
        grid=(2 * wide,),
        in_specs=[
            whole((rows, width)), whole((rows, width)), whole((rows, width)),
            pl.BlockSpec((owners, each, width), lambda s: (0, WO, 0)),
            pl.BlockSpec((owners, each, width), lambda s: (0, WI + at(s), 0)),
            pl.BlockSpec((owners // wide, wide * each, width), lambda s: (at(s), 0, 0)),
            whole((8, width)), whole((8, width)),
        ],
        out_specs=[
            whole((rows, width)), whole((rows, width)), whole((rows, width)),
            pl.BlockSpec(memory_space=pl.ANY),
            whole((8, width)), whole((8, width)),
        ],
        out_shape=[
            shape((rows, width), BF), shape((rows, width), F32), shape((rows, width), BF),
            shape((owners, (2 * wide + 1) * each, width), BF),
            shape((8, width), F32), shape((8, width), F32),
        ],
        scratch_shapes=[
            pltpu.VMEM((rows, width), F32), pltpu.VMEM((rows, width), F32), pltpu.VMEM((rows, 1), F32),
            pltpu.VMEM((rows, width), BF), pltpu.VMEM((rows, wide * width), F32),
            pltpu.VMEM((rows, wide * width), F32), pltpu.VMEM((rows, wide * width), BF),
            pltpu.VMEM((rows, width), F32), pltpu.VMEM((rows, width), F32),
            pltpu.VMEM((rows, width), BF),
            pltpu.VMEM((2, owners // wide, wide * each, width), BF),
            pltpu.VMEM((2, owners, each, width), BF),
            pltpu.VMEM((owners, each, width), BF), pltpu.SemaphoreType.DMA((5, owners)),
        ],
        compiler_params=pltpu.CompilerParams(vmem_limit_bytes=60 * 2**20),
        cost_estimate=pl.CostEstimate(
            flops=2 * rows * width * width * (6 * wide + 3), bytes_accessed=32 * 2**20,
            transcendentals=2 * rows * width * wide,
        ),
        name="middle",
    )(ctx, own, cot, got, got, got, vec, b_inner)


def back_kernel(rows, bound, started, *refs):
    near_ref, gctx_ref, ctx_ref, q_ref, k_ref, v_ref, lse_ref, segq_ref, segk_ref = refs[:9]
    dk_ref, dv_ref, dq_ref = refs[-3:]
    q, g = q_ref[...], gctx_ref[...]
    part = q.shape[1]
    heads = part // HDIM
    masks = [heads_mask(q.shape, h) for h in range(heads)]
    q_parts = [jnp.where(m, q, 0) for m in masks]
    g_parts = [jnp.where(m, g, 0) for m in masks]
    product = (g.astype(F32) * ctx_ref[...].astype(F32)).T
    inner = [
        jnp.sum(product[h * HDIM : (h + 1) * HDIM], axis=0, keepdims=True) for h in range(heads)
    ]

    def one(b, dq):
        here = pl.ds(pl.multiple_of(b * rows, rows), rows)
        k, v = k_ref[here, :], v_ref[here, :]
        kt = k.T
        if bound is None:
            allowed = segk_ref[here, :] == segq_ref[...]
        dk = jnp.zeros((rows, part), F32)
        dv = jnp.zeros((rows, part), F32)
        out = []
        for h in range(heads):
            s = nt(k, q_parts[h])
            if bound is None:
                s = jnp.where(allowed, s, MASK_FILL)
            p = jnp.exp(s - lse_ref[0, h : h + 1, :])
            dp = nt(v, g_parts[h])
            ds = (p * (dp - inner[h])).astype(BF)
            dv = dv + mm(p.astype(BF), g_parts[h])
            dk = dk + mm(ds, q_parts[h])
            out.append(dq[h] + mm(kt[h * HDIM : (h + 1) * HDIM], ds))
        dk_ref[here, :] = dk.astype(BF)
        dv_ref[here, :] = dv.astype(BF)
        return tuple(out)

    if started:
        dq = tuple(refs[9][h * HDIM : (h + 1) * HDIM, :] for h in range(heads))
    else:
        dq = tuple(jnp.zeros((HDIM, rows), F32) for _ in range(heads))
    dq = lax.fori_loop(0, near_ref[0] if bound is None else bound, one, dq)
    dq_ref[...] = jnp.concatenate(dq, 0)


def back_call(start, steps, bound, near, gctx, ctx, q, k, v, lse, segq, segk, dq0=None, into=None):
    rows, width = q.shape
    tall = k.shape[0]
    part = 256
    cols = lambda depth: pl.BlockSpec((depth, part), lambda g: (0, start + g))
    whole = lambda shape: pl.BlockSpec(shape, lambda g: (0,) * len(shape))
    down = pl.BlockSpec((part, rows), lambda g: (start + g, 0))
    shape = jax.ShapeDtypeStruct
    extra = ([dq0] if dq0 is not None else []) + list(into or [])
    specs = ([down] if dq0 is not None else []) + [pl.BlockSpec(memory_space=pl.ANY)] * len(into or [])
    return pl.pallas_call(
        functools.partial(back_kernel, rows, bound, dq0 is not None),
        grid=(steps,),
        in_specs=[
            pl.BlockSpec(memory_space=pltpu.SMEM),
            cols(rows), cols(rows), cols(rows), cols(tall), cols(tall),
            pl.BlockSpec((1, 8, rows), lambda g: (start + g, 0, 0)),
            whole((1, rows)), whole(segk.shape),
        ] + specs,
        out_specs=[cols(tall), cols(tall), down],
        out_shape=[shape((tall, width), BF), shape((tall, width), BF), shape((width, rows), F32)],
        input_output_aliases={9 + i: i for i in range(3)} if into else {},
        compiler_params=pltpu.CompilerParams(vmem_limit_bytes=60 * 2**20),
        cost_estimate=pl.CostEstimate(
            flops=2 * 10 * 2 * tall * rows * part * steps * 2,
            bytes_accessed=8 * tall * part * steps, transcendentals=tall * rows * 4 * steps,
        ),
        name="attention_back",
    )(near, gctx, ctx, q, k, v, lse, segq, segk, *extra)


def product_kernel(rows, bound, near_ref, dk_ref, dv_ref, wk_ref, wv_ref, gx_ref):
    @pl.when((pl.program_id(0) < near_ref[0]) | (bound is not None))
    def _():
        width = dk_ref.shape[1]
        wk, wv = wk_ref[...].reshape(width, width), wv_ref[...].reshape(width, width)
        gx_ref[0] = (nt(dk_ref[...], wk) + nt(dv_ref[...], wv)).astype(BF)


def product_call(bound, near, dk, dv, got, rows):
    tall, width = dk.shape
    owners, each = got.shape[0], width // got.shape[0]
    weight = lambda place: pl.BlockSpec((owners, each, width), lambda b: (0, place, 0))
    return pl.pallas_call(
        functools.partial(product_kernel, rows, bound),
        grid=(tall // rows,),
        in_specs=[
            pl.BlockSpec(memory_space=pltpu.SMEM),
            pl.BlockSpec((rows, width), lambda b: (b, 0)),
            pl.BlockSpec((rows, width), lambda b: (b, 0)),
            weight(WK), weight(WV),
        ],
        out_specs=pl.BlockSpec((1, rows, width), lambda b: (b, 0, 0)),
        out_shape=jax.ShapeDtypeStruct((tall // rows, rows, width), BF),
        compiler_params=pltpu.CompilerParams(vmem_limit_bytes=60 * 2**20),
        cost_estimate=pl.CostEstimate(
            flops=4 * tall * width * width, bytes_accessed=6 * tall * width, transcendentals=0
        ),
        name="token_product",
    )(near, dk, dv, got, got)


def weight_kernel(blocks, first, rows, runs, *refs):
    spots = refs[:blocks]
    (near_ref, core_ref, own_ref, dq_ref, wq_ref, h1_ref, dkp_ref, dvp_ref, dkn_ref, dvn_ref,
     q_send, q_keep, kv_send, kv_keep, gown_ref, sums_ref, x_ref, sems) = refs[blocks:]
    core = core_ref[0]
    at = lambda b: pl.ds(pl.multiple_of(b * rows, rows), rows)
    step = pl.program_id(0)

    @pl.when(step == 0)
    def _():
        copies = [
            pltpu.make_async_copy(spot, x_ref.at[pl.ds(i * rows, rows)], sems.at[i])
            for i, spot in enumerate(spots)
        ]
        for copy in copies:
            copy.start()
        for copy in copies:
            copy.wait()
        gown_ref[...] = h1_ref[...]

    scale = HDIM**-0.5
    dq = dq_ref[...].T.astype(BF)
    part = dq.shape[1]
    width = x_ref.shape[1]
    gown_ref[...] += nt(dq, wq_ref[...].reshape(width, part)) * scale
    away, here = halves((tn(own_ref[...], dq) * scale).astype(BF), runs, core)
    q_send[...] = away.reshape(q_send.shape)
    q_keep[...] = here.reshape(q_send.shape)
    sums_ref[0:1, :] = jnp.sum(dq.astype(F32), axis=0, keepdims=True) * scale

    def products(b, carry, dk_ref, dv_ref, base):
        dk, dv, x = dk_ref[at(b), :], dv_ref[at(b), :], x_ref[at(base + b), :]
        wk, wv = carry
        return wk + tn(x, dk), wv + tn(x, dv)

    zero = jnp.zeros((width, part), F32)
    carry = (zero, zero)
    carry = lax.fori_loop(0, first, lambda b, c: products(b, c, dkp_ref, dvp_ref, 0), carry)
    carry = lax.fori_loop(0, near_ref[0], lambda b, c: products(b, c, dkn_ref, dvn_ref, first), carry)
    for i, grad in enumerate(carry):
        away, here = halves(grad.astype(BF), runs, core)
        shape = kv_send.shape[:2] + (part,)
        kv_send[:, :, i * part : (i + 1) * part] = away.reshape(shape)
        kv_keep[:, :, i * part : (i + 1) * part] = here.reshape(shape)
    sums_ref[1:8, :] = jnp.zeros((7, part), F32)


def weight_call(spots, first, near, own, dq, got, h1, dkp, dvp, dkn, dvn, core, runs):
    rows, width = own.shape
    blocks = len(spots)
    tall = blocks * rows
    part = 256
    steps = width // part
    cols = lambda depth, size=part: pl.BlockSpec((depth, size), lambda g: (0, g))
    whole = lambda shape: pl.BlockSpec(shape, lambda g: (0,) * len(shape))
    shape = jax.ShapeDtypeStruct
    owners, each = got.shape[0], width // got.shape[0]
    half = owners // 2
    slab = lambda size: pl.BlockSpec((half, each, size), lambda g: (0, 0, g))
    return pl.pallas_call(
        functools.partial(weight_kernel, blocks, first, rows, runs),
        grid=(steps,),
        in_specs=[pl.BlockSpec(memory_space=pl.ANY)] * blocks
        + [
            pl.BlockSpec(memory_space=pltpu.SMEM),
            pl.BlockSpec(memory_space=pltpu.SMEM),
            whole((rows, width)), pl.BlockSpec((part, rows), lambda g: (g, 0)),
            pl.BlockSpec((owners, each, part), lambda g: (0, WQ, g)),
            whole((rows, width)), cols(PROMPT), cols(PROMPT), cols(tall - PROMPT), cols(tall - PROMPT),
        ],
        out_specs=[
            slab(part), slab(part), slab(2 * part), slab(2 * part), whole((rows, width)), cols(8),
        ],
        out_shape=[
            shape((half, each, width), BF), shape((half, each, width), BF),
            shape((half, each, 2 * width), BF), shape((half, each, 2 * width), BF),
            shape((rows, width), F32), shape((8, width), F32),
        ],
        scratch_shapes=[pltpu.VMEM((tall, width), BF), pltpu.SemaphoreType.DMA((blocks,))],
        compiler_params=pltpu.CompilerParams(vmem_limit_bytes=60 * 2**20),
        cost_estimate=pl.CostEstimate(
            flops=4 * tall * width * width, bytes_accessed=12 * tall * width, transcendentals=0
        ),
        name="weight_product",
    )(*spots, near, core, own, dq, got, h1, dkp, dvp, dkn, dvn)


def real_owners(grads, count, step, width):
    split = count // 32
    take = lambda v: v.reshape(32, -1, split, step, width).transpose(0, 2, 1, 3, 4).reshape(count, -1, width)
    outer, rest = grads[:, : 4 * split * step], grads[:, 4 * split * step :]
    return jnp.concatenate([outer.reshape(count, 4 * step, width), take(rest)], 1)


def solution(mesh):
    plan = Plan(mesh.shape["grp"], mesh.shape["row"])
    fine = Mesh(mesh.devices.reshape(plan.grp // 2, 2, 4, plan.row // 4), AXES)

    def per_device(
        tokens, cont_lengths, cotangent, w_query, w_key, w_value, w_output, w_inner, w_outer,
        bias_query, bias_value, bias_output, gain_first, shift_first, bias_inner, bias_outer,
        gain_second, shift_second,
    ):
        count = plan.count
        _, rows, width = tokens.shape
        step = w_query.shape[0]
        wide = w_inner.shape[1] // width
        own = tokens[0]

        early = (bias_query, bias_value)
        late = (bias_output, gain_first, shift_first, bias_outer, gain_second, shift_second, bias_inner)
        small = len(late) - 1

        def in_line(vectors):
            line, place = 0, 0
            for vector in vectors:
                size = vector.shape[0]
                line = line + jnp.pad(vector, (place, width - place - size))
                place += size
            return jnp.pad(line[None], ((0, 7), (0, 0)))

        line = jnp.concatenate([in_line(early), in_line(late)], 0)
        runs = plan.grp
        row = lax.axis_index(ROW)
        core = lax.axis_index("core").astype(jnp.int32).reshape(1)
        exchange = Tokens(plan, own)
        squares = (w_query, w_key, w_value)
        if step % 8 == 0:
            first_pack, pack = pack_call(w_output, w_inner, w_outer, *squares, line)
            got = lax.all_gather(pack, AXES, axis=0, tiled=True).reshape(count, -1, width)
            lines = got[:, (WI + WIDE) * step]

            def swaps(value, bits):
                masks = [0]
                for bit in bits:
                    masks = masks + [m ^ bit for m in masks]
                return [plan.swap(value, m) for m in masks[1:]]

            def stage(held, bit):
                return jnp.concatenate([held, plan.swap(held, bit)], 0)

            away = swaps(first_pack, plan.z)
            *away, same, beside = tie(*away, *exchange.stage_one())
            exchange.same, exchange.beside = same, beside
            cut = step + 8
            one = jnp.stack([v[:cut] for v in (first_pack, *away)])
            two = jnp.stack([v[cut:] for v in (first_pack, *away)])
            one, two = stage(one, plan.y[0]), stage(two, plan.x[0])
            one, two, *seen = tie(one, two, *exchange.stage_two())
            exchange.other, exchange.same_y, exchange.diagonal = seen
            one, two = stage(one, plan.x[0]), stage(two, plan.y[0])
            exchange.stage_three()
            one, two, exchange.other_y = tie(one, two, exchange.other_y)
            pieces = [one, plan.swap(one, plan.core[0]), two, plan.swap(two, plan.core[0])]
            order = lambda *bits: ([(bit, 1 << i) for i, bit in enumerate(bits)], plan.core[0])
            places = (
                order(*plan.z, plan.y[0], plan.x[0]),
                order(*plan.z, plan.x[0], plan.y[0]),
            )
            me = plan.me().astype(jnp.int32).reshape(1)
        else:
            inner_rows = [w_inner[:, i * width : (i + 1) * width] for i in range(wide)]
            pack = jnp.concatenate([w_outer, w_output, *inner_rows, *squares, line], 0)
            got = lax.all_gather(pack, AXES, axis=0, tiled=True).reshape(count, -1, width)
            lines = got[:, 12 * step + 8]
            cuts = [wide * step, (wide + 1) * step, (2 * wide + 1) * step, 12 * step]
            outer, output, inner, rest, marks = jnp.split(got, cuts, axis=1)
            apart = lambda v, n: v.reshape(count, n, step, width).transpose(1, 0, 2, 3)
            inner, rest = [
                v.reshape(v.shape[0], 32, width // 32, width).transpose(1, 0, 2, 3)
                for v in (apart(inner, wide), apart(rest, 3))
            ]
            got = jnp.concatenate([v.reshape(32, -1, width) for v in (outer, output, inner)], 1)
            pairs = marks[:, 0, : 2 * step].reshape(32, count // 32, 2, step).transpose(0, 2, 1, 3)
            pairs = jnp.pad(pairs.reshape(32, 1, -1), ((0, 0), (0, 7), (0, width - 2 * width // 32)))
            one = jnp.concatenate([rest[:, 0], pairs], 1)
            two = rest[:, 1:].reshape(32, -1, width)
            pieces = [one[:16], one[16:], two[:16], two[16:]]
            places = (([(1, 1), (2, 2), (4, 4), (8, 8)], 16),) * 2
            me = jnp.zeros((1,), jnp.int32)
        spots, near = exchange.spots()
        first_near = PROMPT // rows

        table = lines[:, : small * step].reshape(count, small, step).transpose(1, 0, 2)
        table = table.reshape(small, width).astype(F32)
        v_bin = lines[:, small * step : (small + wide) * step].reshape(wide, width).astype(F32)
        v_bin = jnp.pad(v_bin, ((0, 8 - wide), (0, 0)))
        segments = segment_ids(cont_lengths[0], plan.row * rows)
        seg_own = lax.dynamic_slice_in_dim(segments, row * rows, rows, 0)[None, :]
        seg_near = near_segments(plan, segments, rows)[:, None]
        near = near.astype(jnp.int32).reshape(1)

        squares, queries, keys_p, values_p, keys_n, values_n, context, log_total = attention_call(
            spots, first_near, near, me, own, pieces, places, seg_own, seg_near
        )
        vec = jnp.concatenate([table, jnp.zeros((2, width), F32)], 0)
        layer_out, grad_h1, grad_context, grads, sums, sums_bin = middle_call(
            context, own, cotangent[0], got, vec, v_bin, step % 8 == 0
        )
        if step % 8:
            grads = real_owners(grads, count, step, width)
            grads = grads.reshape(plan.grp // 2, 2, 4, plan.row // 4, -1, width)
            grads = grads.transpose(1, 0, 3, 2, 4, 5).reshape(count, -1, width)
        level = lambda value, axes: lax.psum_scatter(value, axes, scatter_dimension=0, tiled=True)
        grads = level(grads, "core")
        core_bit = plan.core[0]
        left = [1 << i for i in reversed(range(plan.bits)) if 1 << i != core_bit]
        parts = width // 256
        dkp, dvp, dqp = back_call(
            0, parts, first_near, near, grad_context, context, queries, keys_p, values_p, log_total,
            seg_own, seg_near,
        )
        grads, dkp, dvp, dqp = tie(grads, dkp, dvp, dqp)
        grads = level(grads, ("x", "y"))
        shared_p = product_call(first_near, near, dkp, dvp, squares, rows)
        returned = Return(plan, rows)
        returned.prompt_one(shared_p)
        dkn, dvn, dq = back_call(
            0, parts, None, near, grad_context, context, queries, keys_n, values_n, log_total,
            seg_own, seg_near, dqp,
        )
        returned.same, dkn, dvn, dq = tie(returned.same, dkn, dvn, dq)
        returned.prompt_two()
        q_send, q_keep, kv_send, kv_keep, grad_own, sums_qkv = weight_call(
            spots, first_near, near, own, dq, squares, grad_h1, dkp, dvp, dkn, dvn, core, runs
        )
        q_send, q_keep, kv_send, kv_keep, returned.same, dkn, dvn = tie(
            q_send, q_keep, kv_send, kv_keep, returned.same, dkn, dvn
        )
        shared_n = product_call(None, near, dkn, dvn, squares, rows)
        returned.prompt_three()

        order = (6, 5, 3, 4, 2, 0, 1)
        small = len(early) + len(late) - 1
        d_table = jnp.concatenate([sums_qkv[:1]] + [sums[i : i + 1] for i in order], 0)
        d_lines = jnp.concatenate(
            [
                d_table.reshape(small, count, step).transpose(1, 0, 2).reshape(count, -1),
                sums_bin[:wide].reshape(count, wide * step),
            ],
            1,
        )
        d_lines = jnp.pad(d_lines, ((0, 0), (0, width - d_lines.shape[1])))[:, None].astype(BF)
        d_lines = jnp.pad(d_lines, ((0, 0), (0, 7), (0, 0)))
        place = core[0]
        pick = Reduce(plan, [])
        if step % 8:
            q_send, q_keep, kv_send, kv_keep = [
                v.reshape(count // 2, step, -1) for v in (q_send, q_keep, kv_send, kv_keep)
            ]
        q_send = jnp.concatenate([q_send, pick.cut(d_lines, core_bit, 1 - place)], 1)
        q_keep = jnp.concatenate([q_keep, pick.cut(d_lines, core_bit, place)], 1)
        r_q = Reduce(plan, [q_keep, plan.swap(q_send, core_bit)], left)
        r_kv = Reduce(plan, [kv_keep, plan.swap(kv_send, core_bit)], left)
        for one, two in zip(plan.x + plan.y + plan.z[::-1], plan.y + plan.x + plan.z[::-1]):
            n = len(r_q.terms)
            held = [*r_q.terms, *r_kv.terms]
            if one == plan.x[0]:
                *held, shared_n = tie(*held, shared_n)
                returned.near(shared_n)
            elif one == plan.y[0]:
                *held, returned.own = tie(*held, returned.own)
            elif one == plan.z[-1]:
                *held, grads = tie(*held, grads)
                grads = level(grads, "z")
            else:
                *held, returned.back = tie(*held, returned.back)
            r_q.terms, r_kv.terms = held[:n], held[n:]
            r_q.stage(one)
            r_kv.stage(two)
        o_ab = grads.reshape(-1, width).astype(F32)
        grad_tokens = grad_own + returned.total()
        o_query = r_q.result()
        o_line = o_query[step]
        o_both = r_kv.result().reshape(step, parts, 2, width // parts)

        o_small = [o_line[i * step : (i + 1) * step] for i in range(small)]
        o_bin = o_line[small * step : (small + wide) * step]
        return (
            layer_out[None],
            grad_tokens.astype(BF)[None],
            o_query[:step],
            o_both[:, :, 0].reshape(step, width),
            o_both[:, :, 1].reshape(step, width),
            o_ab[wide * step : (wide + 1) * step],
            jnp.concatenate([o_ab[i * step : (i + 1) * step] for i in range(wide + 1, 2 * wide + 1)], 1),
            o_ab[: wide * step],
            o_small[0],
            o_small[1],
            o_small[2],
            o_small[3],
            o_small[4],
            o_bin,
            o_small[5],
            o_small[6],
            o_small[7],
        )

    split = P(GRP, ROW, None)
    owned2, owned1 = P(AXES, None), P(AXES)
    in_specs = (split, P(GRP, None), split) + (owned2,) * 6 + (owned1,) * 9
    out_specs = (split, split) + (owned2,) * 6 + (owned1,) * 9
    return jax.shard_map(
        per_device, mesh=fine, in_specs=in_specs, out_specs=out_specs, check_vma=False
    )
```

```python
import functools

import jax
import jax.numpy as jnp
import numpy as np
from jax import lax
from jax.experimental import pallas as pl
from jax.experimental.pallas import tpu as pltpu
from jax.sharding import Mesh
from jax.sharding import PartitionSpec as P

HEADS = 12
HDIM = 64
PROMPT = 1024
CONT_MOST = 256
BF = jnp.bfloat16
F32 = jnp.float32

NORM_EPS = 1e-12
MASK_FILL = -1000000000.0
SQRT_HALF = 0.7071067811865476
INV_ROOT_TAU = 0.3989422804014327
AXES = ("x", "core", "z", "y")
GRP, ROW = AXES[:2], AXES[2:]
WIDE = 4
WO, WI = 4, 5
WQ, WK, WV = 0, 1, 2


def mm(left, right):
    return jnp.dot(left, right, preferred_element_type=F32)


def segment_ids(lengths, group_len):
    ends = jnp.cumsum(lengths)
    places = jnp.arange(group_len, dtype=jnp.int32)
    passed = jnp.sum(((places - PROMPT)[:, None] >= ends[None, :]).astype(jnp.int32), axis=-1)
    return jnp.where(places < PROMPT, 0, 1 + passed)


class Plan:
    def __init__(self, grp, row):
        self.grp, self.row, self.count = grp, row, grp * row
        y = row // 4
        bits = lambda base, size: [base << i for i in range(size.bit_length() - 1)]
        self.y, self.z = bits(1, y), bits(y, 4)
        self.core, self.x = bits(row, 2), bits(2 * row, grp // 2)
        self.bits = self.count.bit_length() - 1

    def swap(self, value, mask):
        return lax.ppermute(value, AXES, [(i, i ^ mask) for i in range(self.count)])

    def send(self, value, moves):
        pairs = [(g * self.row + a, g * self.row + b) for g in range(self.grp) for a, b in moves]
        return lax.ppermute(value, AXES, pairs)

    def me(self):
        return lax.axis_index(AXES)


class Reduce:
    def __init__(self, plan, terms, left=None):
        self.plan, self.terms = plan, list(terms)
        self.left = left or [1 << i for i in reversed(range(plan.bits))]

    def cut(self, term, bit, place):
        at = self.left.index(bit)
        high, low = 1 << at, 1 << (len(self.left) - at - 1)
        _, rows, width = term.shape
        term = term.reshape(high, 2, low * rows, width)
        return lax.dynamic_slice_in_dim(term, place, 1, 1).reshape(high * low, rows, width)

    def total(self, terms):
        return sum([t.astype(F32) for t in terms[1:]], terms[0].astype(F32))

    def stage(self, bit):
        place = (self.plan.me() // bit) & 1
        away = self.total([self.cut(t, bit, 1 - place) for t in self.terms]).astype(BF)
        here = [self.cut(t, bit, place) for t in self.terms]
        self.left = [b for b in self.left if b != bit]
        self.terms = here + [self.plan.swap(away, bit)]

    def result(self):
        return self.total(self.terms)[0]


def tie(*values):
    return lax.optimization_barrier(values)


class Tokens:
    def __init__(self, plan, own):
        self.plan, self.own = plan, own
        self.rows = own.shape[0]
        self.ready = plan.row == 8

    def stage_one(self):
        if self.ready:
            plan, own = self.plan, self.own
            across = plan.send(own, [(0, 4), (1, 5), (2, 6), (3, 7)])
            self.same = jnp.where(lax.axis_index(ROW) < 4, own, across)
            self.beside = plan.swap(own, 1)
            return [self.same, self.beside]
        return []

    def stage_two(self):
        if self.ready:
            plan = self.plan
            self.other = plan.swap(self.same, 2)
            self.same_y = plan.swap(self.same, 1)
            self.diagonal = plan.send(self.own, [(5, 6), (6, 5)])
            return [self.other, self.same_y, self.diagonal]
        return []

    def stage_three(self):
        if self.ready:
            self.other_y = self.plan.swap(self.other, 1)

    def spots(self):
        row, rows, own = lax.axis_index(ROW), self.rows, self.own
        if self.ready:
            near = jnp.where(row < 4, 0, jnp.where((row == 5) | (row == 6), 3, 2))
            return [
                self.same, self.other, self.same_y, self.other_y, own, self.beside, self.diagonal,
            ], near
        every = lax.all_gather(own, ROW, axis=0, tiled=True)
        start = jnp.maximum(row * rows - CONT_MOST, 0)
        padded = jnp.concatenate([every, jnp.zeros((CONT_MOST, own.shape[1]), own.dtype)], 0)
        near = lax.dynamic_slice_in_dim(padded, start, rows + 2 * CONT_MOST, 0)
        every = jnp.concatenate([every[:PROMPT], near], 0)
        spots = [every[i : i + rows] for i in range(0, every.shape[0], rows)]
        return spots, jnp.where(row * rows < PROMPT, 0, near.shape[0] // rows)


def near_segments(plan, segments, rows):
    row = lax.axis_index(ROW)
    if plan.row != 8:
        start = jnp.maximum(row * rows - CONT_MOST, 0)
        padded = jnp.concatenate([segments, jnp.full((CONT_MOST,), -1, jnp.int32)], 0)
        near = lax.dynamic_slice_in_dim(padded, start, rows + 2 * CONT_MOST, 0)
        return jnp.where((near == 0) | (row * rows < PROMPT), -1, near)
    pieces = []
    for block, valid in (
        (row, row >= 4),
        (row ^ 1, row >= 4),
        (11 - row, (row == 5) | (row == 6)),
    ):
        block = jnp.clip(block, 0, 7)
        ids = lax.dynamic_slice_in_dim(segments, block * rows, rows, 0)
        pieces.append(jnp.where(valid, ids, -1))
    return jnp.concatenate(pieces, 0)


class Return:
    def __init__(self, plan, rows):
        self.plan, self.rows = plan, rows

    def prompt_one(self, parts):
        self.prompt = self.same = self.own = self.back = parts
        if self.plan.row == 8:
            same, other, same_y, other_y = [parts[i].astype(F32) for i in range(4)]
            self.other = (other + self.plan.swap(parts[3], 1).astype(F32)).astype(BF)
            self.same = same + self.plan.swap(parts[2], 1).astype(F32)

    def prompt_two(self):
        if self.plan.row == 8:
            self.same = self.same + self.plan.swap(self.other, 2).astype(F32)

    def prompt_three(self):
        if self.plan.row == 8:
            self.back = self.plan.send(self.same.astype(BF), [(4, 0), (5, 1), (6, 2), (7, 3)])

    def near(self, parts):
        self.around = parts
        if self.plan.row == 8:
            own = parts[0].astype(F32) + self.plan.swap(parts[1], 1).astype(F32)
            self.own = own + self.plan.send(parts[2], [(5, 6), (6, 5)]).astype(F32)

    def total(self):
        row, rows = lax.axis_index(ROW), self.rows
        if self.plan.row == 8:
            return jnp.where(row < 4, self.same + self.back.astype(F32), self.own)
        around = self.around.reshape(-1, self.around.shape[-1]).astype(F32)
        start = jnp.maximum(row * rows - CONT_MOST, 0)
        whole = jnp.zeros((self.plan.row * rows + CONT_MOST, around.shape[1]), F32)
        whole = whole.at[:PROMPT].set(self.prompt.reshape(PROMPT, -1).astype(F32))
        near = jnp.where(row * rows < PROMPT, 0, around)
        near = lax.dynamic_slice_in_dim(whole, start, rows + 2 * CONT_MOST, 0) + near
        whole = lax.dynamic_update_slice_in_dim(whole, near, start, 0)
        return lax.psum_scatter(whole[: self.plan.row * rows], ROW, scatter_dimension=0, tiled=True)


def heads_mask(lanes, head):
    lane = lax.broadcasted_iota(jnp.int32, lanes, 1)
    return (lane >= head * HDIM) & (lane < (head + 1) * HDIM)


def nt(left, right):
    return lax.dot_general(left, right, (((1,), (1,)), ((), ())), preferred_element_type=F32)


def tn(left, right):
    return lax.dot_general(left, right, (((0,), (0,)), ((), ())), preferred_element_type=F32)


def pack_kernel(wo_ref, wi_ref, wu_ref, wq_ref, wk_ref, wv_ref, line_ref, early_ref, late_ref):
    step, width = wo_ref.shape
    early_ref[:step, :] = wq_ref[...]
    early_ref[step : step + 8, :] = line_ref[:8, :]
    early_ref[step + 8 : 2 * step + 8, :] = wk_ref[...]
    early_ref[2 * step + 8 :, :] = wv_ref[...]
    late_ref[: WIDE * step, :] = wu_ref[...]
    late_ref[WO * step : WI * step, :] = wo_ref[...]
    for i in range(WIDE):
        late_ref[(WI + i) * step : (WI + i + 1) * step, :] = wi_ref[:, i * width : (i + 1) * width]
    late_ref[(WI + WIDE) * step :, :] = line_ref[8:, :]


def pack_call(w_output, w_inner, w_outer, w_query, w_key, w_value, line):
    step, width = w_output.shape
    shape = lambda rows: jax.ShapeDtypeStruct((rows, width), BF)
    return pl.pallas_call(
        pack_kernel, out_shape=[shape(3 * step + 8), shape((WI + WIDE) * step + 8)], name="pack"
    )(w_output, w_inner, w_outer, w_query, w_key, w_value, line)


def attention_kernel(blocks, first, rows, places, *refs):
    spots = refs[:blocks]
    (near_ref, me_ref, own_ref, a0_ref, a1_ref, b0_ref, b1_ref, segq_ref, segk_ref,
     w_ref, q_ref, kp_ref, vp_ref, kn_ref, vn_ref, ctx_ref, lse_ref,
     x_ref, s_ref, line_ref, bias_ref, sems, w_sems) = refs[blocks:]
    near = near_ref[0]
    at = lambda b: pl.ds(pl.multiple_of(b * rows, rows), rows)
    depth = own_ref.shape[1]
    owners = w_ref.shape[0]
    each = depth // owners
    part = q_ref.shape[1]

    def weights(act):
        @pl.loop(0, owners)
        def _(e):
            away = e ^ me_ref[0]
            for (bits, half), (zero, one), parts in (
                (places[0], (a0_ref, a1_ref), ((0, each, w_ref, 0), (each, 8, line_ref, 0))),
                (places[1], (b0_ref, b1_ref), ((0, 2 * each, w_ref, each),)),
            ):
                j = sum([((away // bit) & 1) * weight for bit, weight in bits])
                for which, source in enumerate((zero, one)):

                    @pl.when(((away // half) & 1) == which)
                    def _():
                        for k, (top, size, target, base) in enumerate(parts):
                            act(pltpu.make_async_copy(
                                source.at[j, pl.ds(top, size)], target.at[e, pl.ds(base, size)],
                                w_sems.at[2 * k if zero is a0_ref else 1, e],
                            ))

    @pl.when(pl.program_id(0) == 0)
    def _():
        copies = [
            pltpu.make_async_copy(spot, x_ref.at[pl.ds(i * rows, rows)], sems.at[i])
            for i, spot in enumerate(spots)
        ]
        weights(lambda c: c.start())
        for copy in copies:
            copy.start()
        weights(lambda c: c.wait())
        for copy in copies:
            copy.wait()
        line = line_ref[:, 0, :128]
        place = lax.broadcasted_iota(jnp.int32, (128, depth), 0)
        lane = lax.broadcasted_iota(jnp.int32, (128, depth), 1)
        mine = lax.broadcasted_iota(jnp.int32, (owners, depth), 0)
        mine = mine == lax.broadcasted_iota(jnp.int32, (owners, depth), 1) // each
        for i in range(2):
            spread = mm(line, jnp.where(place == lane % each + i * each, 1.0, 0.0).astype(BF))
            bias_ref[i : i + 1, :] = jnp.sum(jnp.where(mine, spread, 0.0), axis=0, keepdims=True)

    lanes = pl.ds(pl.multiple_of(pl.program_id(0) * part, part), part)
    wq, wk, wv = [
        w_ref[:, i * each : (i + 1) * each, lanes].reshape(depth, part) for i in (WQ, WK, WV)
    ]
    queries = (mm(own_ref[...], wq) + bias_ref[0:1, lanes]) * (HDIM**-0.5)
    q_ref[...] = queries.astype(BF)

    def project(b, k_ref, v_ref, side):
        x = x_ref[at(b), :]
        k_ref[at(side), :] = mm(x, wk).astype(BF)
        v_ref[at(side), :] = (mm(x, wv) + bias_ref[1:2, lanes]).astype(BF)

    @pl.loop(0, first)
    def _(b):
        project(b, kp_ref, vp_ref, b)

    @pl.loop(0, near)
    def _(b):
        project(first + b, kn_ref, vn_ref, b)

    width = q_ref.shape[1]
    heads = width // HDIM
    q = q_ref[...]
    parts = [jnp.where(heads_mask(q.shape, h), q, 0) for h in range(heads)]

    def scores(b, peaks, k_ref, base):
        k = k_ref[at(b), :]
        out = []
        for h in range(heads):
            s = nt(k, parts[h])
            if base:
                s = jnp.where(segk_ref[at(b), :] == segq_ref[...], s, MASK_FILL)
            s_ref[h, at(base + b), :] = s
            out.append(jnp.maximum(peaks[h], jnp.max(s, axis=0, keepdims=True)))
        return tuple(out)

    peaks = tuple(jnp.full((1, rows), MASK_FILL, F32) for _ in range(heads))
    peaks = lax.fori_loop(0, first, lambda b, c: scores(b, c, kp_ref, 0), peaks)
    peaks = lax.fori_loop(0, near, lambda b, c: scores(b, c, kn_ref, first), peaks)

    def mix(b, carry, v_ref, base):
        totals, mixed = carry
        vt = v_ref[at(b), :].T
        new_totals, new_mixed = [], []
        for h in range(heads):
            p = jnp.exp(s_ref[h, at(base + b), :] - peaks[h])
            new_totals.append(totals[h] + jnp.sum(p, axis=0, keepdims=True))
            new_mixed.append(mixed[h] + mm(vt[h * HDIM : (h + 1) * HDIM], p.astype(BF)))
        return tuple(new_totals), tuple(new_mixed)

    zero = (
        tuple(jnp.zeros((1, rows), F32) for _ in range(heads)),
        tuple(jnp.zeros((HDIM, rows), F32) for _ in range(heads)),
    )
    carry = lax.fori_loop(0, first, lambda b, c: mix(b, c, vp_ref, 0), zero)
    totals, mixed = lax.fori_loop(0, near, lambda b, c: mix(b, c, vn_ref, first), carry)
    whole = jnp.concatenate([mixed[h] / totals[h] for h in range(heads)], 0)
    ctx_ref[...] = whole.T.astype(BF)
    for h in range(heads):
        lse_ref[0, h : h + 1, :] = peaks[h] + jnp.log(totals[h])


def attention_call(spots, first, near, me, own, pieces, places, segq, segk):
    rows, width = own.shape
    blocks = len(spots)
    tall = blocks * rows
    part = 256
    steps = width // part
    heads = part // HDIM
    cols = lambda depth: pl.BlockSpec((depth, part), lambda g: (0, g))
    flops = 2 * tall * width * width * 2 + 4 * tall * rows * width * 4
    owners = 2 * pieces[0].shape[0]
    each = width // owners
    return pl.pallas_call(
        functools.partial(attention_kernel, blocks, first, rows, places),
        grid=(steps,),
        in_specs=[pl.BlockSpec(memory_space=pl.ANY)] * blocks
        + [
            pl.BlockSpec(memory_space=pltpu.SMEM),
            pl.BlockSpec(memory_space=pltpu.SMEM),
            pl.BlockSpec((rows, width), lambda g: (0, 0)),
        ] + [pl.BlockSpec(memory_space=pl.ANY)] * 4 + [
            pl.BlockSpec((1, rows), lambda g: (0, 0)),
            pl.BlockSpec(segk.shape, lambda g: (0, 0)),
        ],
        out_specs=[
            pl.BlockSpec((owners, 3 * each, width), lambda g: (0, 0, 0)),
            cols(rows), cols(PROMPT), cols(PROMPT), cols(tall - PROMPT), cols(tall - PROMPT),
            cols(rows), pl.BlockSpec((1, 8, rows), lambda g: (g, 0, 0)),
        ],
        out_shape=[
            jax.ShapeDtypeStruct((owners, 3 * each, width), BF),
            jax.ShapeDtypeStruct((rows, width), BF),
            jax.ShapeDtypeStruct((PROMPT, width), BF),
            jax.ShapeDtypeStruct((PROMPT, width), BF),
            jax.ShapeDtypeStruct((tall - PROMPT, width), BF),
            jax.ShapeDtypeStruct((tall - PROMPT, width), BF),
            jax.ShapeDtypeStruct((rows, width), BF),
            jax.ShapeDtypeStruct((steps, 8, rows), F32),
        ],
        scratch_shapes=[
            pltpu.VMEM((tall, width), BF),
            pltpu.VMEM((heads, tall, rows), F32),
            pltpu.VMEM((owners, 8, width), BF),
            pltpu.VMEM((8, width), F32),
            pltpu.SemaphoreType.DMA((blocks,)),
            pltpu.SemaphoreType.DMA((3, owners)),
        ],
        compiler_params=pltpu.CompilerParams(vmem_limit_bytes=60 * 2**20),
        cost_estimate=pl.CostEstimate(
            flops=flops, bytes_accessed=12 * 2**20, transcendentals=tall * rows * 12
        ),
        name="attention",
    )(*spots, near, me, own, *pieces, segq, segk)


def halves(value, runs, core):
    depth = value.shape[0] // runs
    pick = lambda first: jnp.concatenate(
        [value[i * depth : (i + 1) * depth] for i in range(first, runs, 2)], 0
    )
    even, odd = pick(0), pick(1)
    return jnp.where(core == 0, odd, even), jnp.where(core == 0, even, odd)


def middle_kernel(wide, mapped, ctx_ref, own_ref, cot_ref, wo_ref, wi_ref, wu_ref, vec_ref, bin_ref,
                  out_ref, h1_ref, gctx_ref, grads, sums_ref, sbin_ref,
                  first_ref, n1_ref, inv_ref, low_ref, pre_ref, cdf_ref, act_ref, acc_ref,
                  gffn_ref, glow_ref, out_buf, in_buf, wo_buf, sems):
    step = pl.program_id(0)
    width = ctx_ref.shape[1]
    square = lambda ref: ref[...].reshape(width, width)
    vec = lambda i: vec_ref[i : i + 1, :]
    mean = lambda v: jnp.sum(v, axis=-1, keepdims=True) * (1.0 / width)
    down = lambda v: jnp.sum(v, axis=0, keepdims=True)
    owners = wi_ref.shape[0]
    each = width // owners
    some = owners // wide

    def slot(group, i):
        return group % 2 * 16 + group // 2 * 8 + i % 2 * 4 + i // 2 if mapped else group * 8 + i

    def outer(at):
        turn = (2 * wide - 1 - at) % 2
        return [
            pltpu.make_async_copy(
                out_buf.at[turn, i], grads.at[slot(at, i), pl.ds(0, wide * each)], sems.at[turn, i]
            )
            for i in range(some)
        ]

    def inner(at):
        turn = (2 * wide - 1 - at) % 2
        top = pl.multiple_of((wide + 1 + at) * each, each)
        return [
            pltpu.make_async_copy(
                in_buf.at[turn, e], grads.at[slot(e // 8, e % 8), pl.ds(top, each)], sems.at[2 + turn, e]
            )
            for e in range(owners)
        ]

    def output():
        return [
            pltpu.make_async_copy(
                wo_buf.at[e], grads.at[slot(e // 8, e % 8), pl.ds(wide * each, each)], sems.at[4, e]
            )
            for e in range(owners)
        ]

    def start(copies):
        for copy in copies:
            copy.start()

    def wait(copies):
        for copy in copies:
            copy.wait()

    @pl.when(step == 0)
    def _():
        hidden = own_ref[...].astype(F32) + mm(ctx_ref[...], square(wo_ref)) + vec(0)
        centred = hidden - mean(hidden)
        inverse = lax.rsqrt(mean(centred * centred) + NORM_EPS)
        normed = centred * inverse
        n1_ref[...] = normed
        inv_ref[...] = inverse
        first = normed * vec(1) + vec(2)
        first_ref[...] = first
        low_ref[...] = first.astype(BF)

    @pl.when(step < wide)
    def _():
        chunk = pl.ds(pl.multiple_of(step * width, width), width)
        pre = mm(low_ref[...], square(wi_ref)) + bin_ref[pl.ds(step, 1), :]
        cdf = 0.5 * (1.0 + lax.erf(pre * SQRT_HALF))
        act = (pre * cdf).astype(BF)
        pre_ref[:, chunk] = pre
        cdf_ref[:, chunk] = cdf
        act_ref[:, chunk] = act
        more = mm(act, square(wu_ref))

        @pl.when(step == 0)
        def _():
            acc_ref[...] = more

        @pl.when(step > 0)
        def _():
            acc_ref[...] += more

    @pl.when(step == wide - 1)
    def _():
        hidden = first_ref[...] + acc_ref[...] + vec(3)
        centred = hidden - mean(hidden)
        inverse = lax.rsqrt(mean(centred * centred) + NORM_EPS)
        normed = centred * inverse
        out_ref[...] = (normed * vec(4) + vec(5)).astype(BF)
        grad = cot_ref[...].astype(F32)
        sums_ref[0:1, :] = down(grad * normed)
        sums_ref[1:2, :] = down(grad)
        e = grad * vec(4)
        back = inverse * (e - mean(e) - normed * mean(e * normed))
        gffn_ref[...] = back
        low = back.astype(BF)
        glow_ref[...] = low
        sums_ref[2:3, :] = down(low.astype(F32))

    @pl.when(step >= wide)
    def _():
        at = 2 * wide - 1 - step
        chunk = pl.ds(pl.multiple_of(at * width, width), width)
        pre = pre_ref[:, chunk]
        slope = cdf_ref[:, chunk] + pre * jnp.exp(-0.5 * pre * pre) * INV_ROOT_TAU
        low = glow_ref[...]
        grad = (nt(low, square(wu_ref)) * slope).astype(BF)
        sbin_ref[pl.ds(at, 1), :] = down(grad.astype(F32))
        turn = step % 2

        @pl.when(step >= wide + 2)
        def _():
            wait(outer(at + 2) + inner(at + 2))

        out_buf[turn] = tn(act_ref[:, chunk], low).astype(BF).reshape(some, wide * each, width)
        start(outer(at))
        in_buf[turn] = tn(low_ref[...], grad).astype(BF).reshape(owners, each, width)
        start(inner(at))
        gffn_ref[...] += nt(grad, square(wi_ref))

    @pl.when(step == 2 * wide - 1)
    def _():
        grad = gffn_ref[...]
        normed = n1_ref[...]
        sums_ref[3:4, :] = down(grad * normed)
        sums_ref[4:5, :] = down(grad)
        e = grad * vec(1)
        back = inv_ref[...] * (e - mean(e) - normed * mean(e * normed))
        h1_ref[...] = back
        low = back.astype(BF)
        sums_ref[5:6, :] = down(low.astype(F32))
        wo_buf[...] = tn(ctx_ref[...], low).astype(BF).reshape(owners, each, width)
        start(output())
        gctx = nt(low, square(wo_ref)).astype(BF)
        gctx_ref[...] = gctx
        sums_ref[6:7, :] = down(gctx.astype(F32))
        sums_ref[7:8, :] = jnp.zeros((1, width), F32)
        wait(outer(1) + inner(1) + outer(0) + inner(0) + output())


def middle_call(ctx, own, cot, got, vec, b_inner, mapped):
    rows, width = own.shape
    owners = got.shape[0]
    each = width // owners
    wide = WIDE
    whole = lambda shape: pl.BlockSpec(shape, lambda s: (0,) * len(shape))
    at = lambda s: jnp.where(s < wide, s, 2 * wide - 1 - s)
    shape = jax.ShapeDtypeStruct
    return pl.pallas_call(
        functools.partial(middle_kernel, wide, mapped),
        grid=(2 * wide,),
        in_specs=[
            whole((rows, width)), whole((rows, width)), whole((rows, width)),
            pl.BlockSpec((owners, each, width), lambda s: (0, WO, 0)),
            pl.BlockSpec((owners, each, width), lambda s: (0, WI + at(s), 0)),
            pl.BlockSpec((owners // wide, wide * each, width), lambda s: (at(s), 0, 0)),
            whole((8, width)), whole((8, width)),
        ],
        out_specs=[
            whole((rows, width)), whole((rows, width)), whole((rows, width)),
            pl.BlockSpec(memory_space=pl.ANY),
            whole((8, width)), whole((8, width)),
        ],
        out_shape=[
            shape((rows, width), BF), shape((rows, width), F32), shape((rows, width), BF),
            shape((owners, (2 * wide + 1) * each, width), BF),
            shape((8, width), F32), shape((8, width), F32),
        ],
        scratch_shapes=[
            pltpu.VMEM((rows, width), F32), pltpu.VMEM((rows, width), F32), pltpu.VMEM((rows, 1), F32),
            pltpu.VMEM((rows, width), BF), pltpu.VMEM((rows, wide * width), F32),
            pltpu.VMEM((rows, wide * width), F32), pltpu.VMEM((rows, wide * width), BF),
            pltpu.VMEM((rows, width), F32), pltpu.VMEM((rows, width), F32),
            pltpu.VMEM((rows, width), BF),
            pltpu.VMEM((2, owners // wide, wide * each, width), BF),
            pltpu.VMEM((2, owners, each, width), BF),
            pltpu.VMEM((owners, each, width), BF), pltpu.SemaphoreType.DMA((5, owners)),
        ],
        compiler_params=pltpu.CompilerParams(vmem_limit_bytes=60 * 2**20),
        cost_estimate=pl.CostEstimate(
            flops=2 * rows * width * width * (6 * wide + 3), bytes_accessed=32 * 2**20,
            transcendentals=2 * rows * width * wide,
        ),
        name="middle",
    )(ctx, own, cot, got, got, got, vec, b_inner)


def back_kernel(rows, bound, started, *refs):
    near_ref, gctx_ref, ctx_ref, q_ref, k_ref, v_ref, lse_ref, segq_ref, segk_ref = refs[:9]
    dk_ref, dv_ref, dq_ref = refs[-3:]
    q, g = q_ref[...], gctx_ref[...]
    part = q.shape[1]
    heads = part // HDIM
    masks = [heads_mask(q.shape, h) for h in range(heads)]
    q_parts = [jnp.where(m, q, 0) for m in masks]
    g_parts = [jnp.where(m, g, 0) for m in masks]
    product = (g.astype(F32) * ctx_ref[...].astype(F32)).T
    inner = [
        jnp.sum(product[h * HDIM : (h + 1) * HDIM], axis=0, keepdims=True) for h in range(heads)
    ]

    def one(b, dq):
        here = pl.ds(pl.multiple_of(b * rows, rows), rows)
        k, v = k_ref[here, :], v_ref[here, :]
        kt = k.T
        if bound is None:
            allowed = segk_ref[here, :] == segq_ref[...]
        dk = jnp.zeros((rows, part), F32)
        dv = jnp.zeros((rows, part), F32)
        out = []
        for h in range(heads):
            s = nt(k, q_parts[h])
            if bound is None:
                s = jnp.where(allowed, s, MASK_FILL)
            p = jnp.exp(s - lse_ref[0, h : h + 1, :])
            dp = nt(v, g_parts[h])
            ds = (p * (dp - inner[h])).astype(BF)
            dv = dv + mm(p.astype(BF), g_parts[h])
            dk = dk + mm(ds, q_parts[h])
            out.append(dq[h] + mm(kt[h * HDIM : (h + 1) * HDIM], ds))
        dk_ref[here, :] = dk.astype(BF)
        dv_ref[here, :] = dv.astype(BF)
        return tuple(out)

    if started:
        dq = tuple(refs[9][h * HDIM : (h + 1) * HDIM, :] for h in range(heads))
    else:
        dq = tuple(jnp.zeros((HDIM, rows), F32) for _ in range(heads))
    dq = lax.fori_loop(0, near_ref[0] if bound is None else bound, one, dq)
    dq_ref[...] = jnp.concatenate(dq, 0)


def back_call(start, steps, bound, near, gctx, ctx, q, k, v, lse, segq, segk, dq0=None, into=None):
    rows, width = q.shape
    tall = k.shape[0]
    part = 256
    cols = lambda depth: pl.BlockSpec((depth, part), lambda g: (0, start + g))
    whole = lambda shape: pl.BlockSpec(shape, lambda g: (0,) * len(shape))
    down = pl.BlockSpec((part, rows), lambda g: (start + g, 0))
    shape = jax.ShapeDtypeStruct
    extra = ([dq0] if dq0 is not None else []) + list(into or [])
    specs = ([down] if dq0 is not None else []) + [pl.BlockSpec(memory_space=pl.ANY)] * len(into or [])
    return pl.pallas_call(
        functools.partial(back_kernel, rows, bound, dq0 is not None),
        grid=(steps,),
        in_specs=[
            pl.BlockSpec(memory_space=pltpu.SMEM),
            cols(rows), cols(rows), cols(rows), cols(tall), cols(tall),
            pl.BlockSpec((1, 8, rows), lambda g: (start + g, 0, 0)),
            whole((1, rows)), whole(segk.shape),
        ] + specs,
        out_specs=[cols(tall), cols(tall), down],
        out_shape=[shape((tall, width), BF), shape((tall, width), BF), shape((width, rows), F32)],
        input_output_aliases={9 + i: i for i in range(3)} if into else {},
        compiler_params=pltpu.CompilerParams(vmem_limit_bytes=60 * 2**20),
        cost_estimate=pl.CostEstimate(
            flops=2 * 10 * 2 * tall * rows * part * steps * 2,
            bytes_accessed=8 * tall * part * steps, transcendentals=tall * rows * 4 * steps,
        ),
        name="attention_back",
    )(near, gctx, ctx, q, k, v, lse, segq, segk, *extra)


def product_kernel(rows, bound, near_ref, dk_ref, dv_ref, wk_ref, wv_ref, gx_ref):
    @pl.when((pl.program_id(0) < near_ref[0]) | (bound is not None))
    def _():
        width = dk_ref.shape[1]
        wk, wv = wk_ref[...].reshape(width, width), wv_ref[...].reshape(width, width)
        gx_ref[0] = (nt(dk_ref[...], wk) + nt(dv_ref[...], wv)).astype(BF)


def product_call(bound, near, dk, dv, got, rows):
    tall, width = dk.shape
    owners, each = got.shape[0], width // got.shape[0]
    weight = lambda place: pl.BlockSpec((owners, each, width), lambda b: (0, place, 0))
    return pl.pallas_call(
        functools.partial(product_kernel, rows, bound),
        grid=(tall // rows,),
        in_specs=[
            pl.BlockSpec(memory_space=pltpu.SMEM),
            pl.BlockSpec((rows, width), lambda b: (b, 0)),
            pl.BlockSpec((rows, width), lambda b: (b, 0)),
            weight(WK), weight(WV),
        ],
        out_specs=pl.BlockSpec((1, rows, width), lambda b: (b, 0, 0)),
        out_shape=jax.ShapeDtypeStruct((tall // rows, rows, width), BF),
        compiler_params=pltpu.CompilerParams(vmem_limit_bytes=60 * 2**20),
        cost_estimate=pl.CostEstimate(
            flops=4 * tall * width * width, bytes_accessed=6 * tall * width, transcendentals=0
        ),
        name="token_product",
    )(near, dk, dv, got, got)


def weight_kernel(blocks, first, rows, runs, *refs):
    spots = refs[:blocks]
    (near_ref, core_ref, own_ref, dq_ref, wq_ref, h1_ref, dkp_ref, dvp_ref, dkn_ref, dvn_ref,
     q_send, q_keep, kv_send, kv_keep, gown_ref, sums_ref, x_ref, sems) = refs[blocks:]
    core = core_ref[0]
    at = lambda b: pl.ds(pl.multiple_of(b * rows, rows), rows)
    step = pl.program_id(0)

    @pl.when(step == 0)
    def _():
        copies = [
            pltpu.make_async_copy(spot, x_ref.at[pl.ds(i * rows, rows)], sems.at[i])
            for i, spot in enumerate(spots)
        ]
        for copy in copies:
            copy.start()
        for copy in copies:
            copy.wait()
        gown_ref[...] = h1_ref[...]

    scale = HDIM**-0.5
    dq = dq_ref[...].T.astype(BF)
    part = dq.shape[1]
    width = x_ref.shape[1]
    gown_ref[...] += nt(dq, wq_ref[...].reshape(width, part)) * scale
    away, here = halves((tn(own_ref[...], dq) * scale).astype(BF), runs, core)
    q_send[...] = away.reshape(q_send.shape)
    q_keep[...] = here.reshape(q_send.shape)
    sums_ref[0:1, :] = jnp.sum(dq.astype(F32), axis=0, keepdims=True) * scale

    def products(b, carry, dk_ref, dv_ref, base):
        dk, dv, x = dk_ref[at(b), :], dv_ref[at(b), :], x_ref[at(base + b), :]
        wk, wv = carry
        return wk + tn(x, dk), wv + tn(x, dv)

    zero = jnp.zeros((width, part), F32)
    carry = (zero, zero)
    carry = lax.fori_loop(0, first, lambda b, c: products(b, c, dkp_ref, dvp_ref, 0), carry)
    carry = lax.fori_loop(0, near_ref[0], lambda b, c: products(b, c, dkn_ref, dvn_ref, first), carry)
    for i, grad in enumerate(carry):
        away, here = halves(grad.astype(BF), runs, core)
        shape = kv_send.shape[:2] + (part,)
        kv_send[:, :, i * part : (i + 1) * part] = away.reshape(shape)
        kv_keep[:, :, i * part : (i + 1) * part] = here.reshape(shape)
    sums_ref[1:8, :] = jnp.zeros((7, part), F32)


def weight_call(spots, first, near, own, dq, got, h1, dkp, dvp, dkn, dvn, core, runs):
    rows, width = own.shape
    blocks = len(spots)
    tall = blocks * rows
    part = 256
    steps = width // part
    cols = lambda depth, size=part: pl.BlockSpec((depth, size), lambda g: (0, g))
    whole = lambda shape: pl.BlockSpec(shape, lambda g: (0,) * len(shape))
    shape = jax.ShapeDtypeStruct
    owners, each = got.shape[0], width // got.shape[0]
    half = owners // 2
    slab = lambda size: pl.BlockSpec((half, each, size), lambda g: (0, 0, g))
    return pl.pallas_call(
        functools.partial(weight_kernel, blocks, first, rows, runs),
        grid=(steps,),
        in_specs=[pl.BlockSpec(memory_space=pl.ANY)] * blocks
        + [
            pl.BlockSpec(memory_space=pltpu.SMEM),
            pl.BlockSpec(memory_space=pltpu.SMEM),
            whole((rows, width)), pl.BlockSpec((part, rows), lambda g: (g, 0)),
            pl.BlockSpec((owners, each, part), lambda g: (0, WQ, g)),
            whole((rows, width)), cols(PROMPT), cols(PROMPT), cols(tall - PROMPT), cols(tall - PROMPT),
        ],
        out_specs=[
            slab(part), slab(part), slab(2 * part), slab(2 * part), whole((rows, width)), cols(8),
        ],
        out_shape=[
            shape((half, each, width), BF), shape((half, each, width), BF),
            shape((half, each, 2 * width), BF), shape((half, each, 2 * width), BF),
            shape((rows, width), F32), shape((8, width), F32),
        ],
        scratch_shapes=[pltpu.VMEM((tall, width), BF), pltpu.SemaphoreType.DMA((blocks,))],
        compiler_params=pltpu.CompilerParams(vmem_limit_bytes=60 * 2**20),
        cost_estimate=pl.CostEstimate(
            flops=4 * tall * width * width, bytes_accessed=12 * tall * width, transcendentals=0
        ),
        name="weight_product",
    )(*spots, near, core, own, dq, got, h1, dkp, dvp, dkn, dvn)


def real_owners(grads, count, step, width):
    split = count // 32
    take = lambda v: v.reshape(32, -1, split, step, width).transpose(0, 2, 1, 3, 4).reshape(count, -1, width)
    outer, rest = grads[:, : 4 * split * step], grads[:, 4 * split * step :]
    return jnp.concatenate([outer.reshape(count, 4 * step, width), take(rest)], 1)


def solution(mesh):
    plan = Plan(mesh.shape["grp"], mesh.shape["row"])
    fine = Mesh(mesh.devices.reshape(plan.grp // 2, 2, 4, plan.row // 4), AXES)

    def per_device(
        tokens, cont_lengths, cotangent, w_query, w_key, w_value, w_output, w_inner, w_outer,
        bias_query, bias_value, bias_output, gain_first, shift_first, bias_inner, bias_outer,
        gain_second, shift_second,
    ):
        count = plan.count
        _, rows, width = tokens.shape
        step = w_query.shape[0]
        wide = w_inner.shape[1] // width
        own = tokens[0]

        early = (bias_query, bias_value)
        late = (bias_output, gain_first, shift_first, bias_outer, gain_second, shift_second, bias_inner)
        small = len(late) - 1

        def in_line(vectors):
            line, place = 0, 0
            for vector in vectors:
                size = vector.shape[0]
                line = line + jnp.pad(vector, (place, width - place - size))
                place += size
            return jnp.pad(line[None], ((0, 7), (0, 0)))

        line = jnp.concatenate([in_line(early), in_line(late)], 0)
        runs = plan.grp
        row = lax.axis_index(ROW)
        core = lax.axis_index("core").astype(jnp.int32).reshape(1)
        exchange = Tokens(plan, own)
        squares = (w_query, w_key, w_value)
        if step % 8 == 0:
            first_pack, pack = pack_call(w_output, w_inner, w_outer, *squares, line)
            got = lax.all_gather(pack, AXES, axis=0, tiled=True).reshape(count, -1, width)
            lines = got[:, (WI + WIDE) * step]

            def swaps(value, bits):
                masks = [0]
                for bit in bits:
                    masks = masks + [m ^ bit for m in masks]
                return [plan.swap(value, m) for m in masks[1:]]

            def stage(held, bit):
                return jnp.concatenate([held, plan.swap(held, bit)], 0)

            away = swaps(first_pack, plan.z)
            *away, same, beside = tie(*away, *exchange.stage_one())
            exchange.same, exchange.beside = same, beside
            cut = step + 8
            one = jnp.stack([v[:cut] for v in (first_pack, *away)])
            two = jnp.stack([v[cut:] for v in (first_pack, *away)])
            one, two = stage(one, plan.x[0]), stage(two, plan.y[0])
            one, two, *seen = tie(one, two, *exchange.stage_two())
            exchange.other, exchange.same_y, exchange.diagonal = seen
            one, two = stage(one, plan.y[0]), stage(two, plan.x[0])
            exchange.stage_three()
            one, two, exchange.other_y = tie(one, two, exchange.other_y)
            pieces = [one, plan.swap(one, plan.core[0]), two, plan.swap(two, plan.core[0])]
            order = lambda *bits: ([(bit, 1 << i) for i, bit in enumerate(bits)], plan.core[0])
            places = (
                order(*plan.z, plan.x[0], plan.y[0]),
                order(*plan.z, plan.y[0], plan.x[0]),
            )
            me = plan.me().astype(jnp.int32).reshape(1)
        else:
            inner_rows = [w_inner[:, i * width : (i + 1) * width] for i in range(wide)]
            pack = jnp.concatenate([w_outer, w_output, *inner_rows, *squares, line], 0)
            got = lax.all_gather(pack, AXES, axis=0, tiled=True).reshape(count, -1, width)
            lines = got[:, 12 * step + 8]
            cuts = [wide * step, (wide + 1) * step, (2 * wide + 1) * step, 12 * step]
            outer, output, inner, rest, marks = jnp.split(got, cuts, axis=1)
            apart = lambda v, n: v.reshape(count, n, step, width).transpose(1, 0, 2, 3)
            inner, rest = [
                v.reshape(v.shape[0], 32, width // 32, width).transpose(1, 0, 2, 3)
                for v in (apart(inner, wide), apart(rest, 3))
            ]
            got = jnp.concatenate([v.reshape(32, -1, width) for v in (outer, output, inner)], 1)
            pairs = marks[:, 0, : 2 * step].reshape(32, count // 32, 2, step).transpose(0, 2, 1, 3)
            pairs = jnp.pad(pairs.reshape(32, 1, -1), ((0, 0), (0, 7), (0, width - 2 * width // 32)))
            one = jnp.concatenate([rest[:, 0], pairs], 1)
            two = rest[:, 1:].reshape(32, -1, width)
            pieces = [one[:16], one[16:], two[:16], two[16:]]
            places = (([(1, 1), (2, 2), (4, 4), (8, 8)], 16),) * 2
            me = jnp.zeros((1,), jnp.int32)
        spots, near = exchange.spots()
        first_near = PROMPT // rows

        table = lines[:, : small * step].reshape(count, small, step).transpose(1, 0, 2)
        table = table.reshape(small, width).astype(F32)
        v_bin = lines[:, small * step : (small + wide) * step].reshape(wide, width).astype(F32)
        v_bin = jnp.pad(v_bin, ((0, 8 - wide), (0, 0)))
        segments = segment_ids(cont_lengths[0], plan.row * rows)
        seg_own = lax.dynamic_slice_in_dim(segments, row * rows, rows, 0)[None, :]
        seg_near = near_segments(plan, segments, rows)[:, None]
        near = near.astype(jnp.int32).reshape(1)

        squares, queries, keys_p, values_p, keys_n, values_n, context, log_total = attention_call(
            spots, first_near, near, me, own, pieces, places, seg_own, seg_near
        )
        vec = jnp.concatenate([table, jnp.zeros((2, width), F32)], 0)
        layer_out, grad_h1, grad_context, grads, sums, sums_bin = middle_call(
            context, own, cotangent[0], got, vec, v_bin, step % 8 == 0
        )
        if step % 8:
            grads = real_owners(grads, count, step, width)
            grads = grads.reshape(plan.grp // 2, 2, 4, plan.row // 4, -1, width)
            grads = grads.transpose(1, 0, 3, 2, 4, 5).reshape(count, -1, width)
        level = lambda value, axes: lax.psum_scatter(value, axes, scatter_dimension=0, tiled=True)
        grads = level(grads, "core")
        core_bit = plan.core[0]
        left = [1 << i for i in reversed(range(plan.bits)) if 1 << i != core_bit]
        parts = width // 256
        dkp, dvp, dqp = back_call(
            0, parts, first_near, near, grad_context, context, queries, keys_p, values_p, log_total,
            seg_own, seg_near,
        )
        grads, dkp, dvp, dqp = tie(grads, dkp, dvp, dqp)
        grads = level(grads, ("x", "y"))
        shared_p = product_call(first_near, near, dkp, dvp, squares, rows)
        returned = Return(plan, rows)
        returned.prompt_one(shared_p)
        dkn, dvn, dq = back_call(
            0, parts, None, near, grad_context, context, queries, keys_n, values_n, log_total,
            seg_own, seg_near, dqp,
        )
        q_send, q_keep, kv_send, kv_keep, grad_own, sums_qkv = weight_call(
            spots, first_near, near, own, dq, squares, grad_h1, dkp, dvp, dkn, dvn, core, runs
        )
        q_send, q_keep, kv_send, kv_keep, returned.same, dkn, dvn = tie(
            q_send, q_keep, kv_send, kv_keep, returned.same, dkn, dvn
        )
        returned.prompt_two()
        shared_n = product_call(None, near, dkn, dvn, squares, rows)

        order = (6, 5, 3, 4, 2, 0, 1)
        small = len(early) + len(late) - 1
        d_table = jnp.concatenate([sums_qkv[:1]] + [sums[i : i + 1] for i in order], 0)
        d_lines = jnp.concatenate(
            [
                d_table.reshape(small, count, step).transpose(1, 0, 2).reshape(count, -1),
                sums_bin[:wide].reshape(count, wide * step),
            ],
            1,
        )
        d_lines = jnp.pad(d_lines, ((0, 0), (0, width - d_lines.shape[1])))[:, None].astype(BF)
        d_lines = jnp.pad(d_lines, ((0, 0), (0, 7), (0, 0)))
        place = core[0]
        pick = Reduce(plan, [])
        if step % 8:
            q_send, q_keep, kv_send, kv_keep = [
                v.reshape(count // 2, step, -1) for v in (q_send, q_keep, kv_send, kv_keep)
            ]
        q_send = jnp.concatenate([q_send, pick.cut(d_lines, core_bit, 1 - place)], 1)
        q_keep = jnp.concatenate([q_keep, pick.cut(d_lines, core_bit, place)], 1)
        r_q = Reduce(plan, [q_keep, plan.swap(q_send, core_bit)], left)
        r_kv = Reduce(plan, [kv_keep, plan.swap(kv_send, core_bit)], left)
        for one, two in zip(plan.x + plan.y + plan.z[::-1], plan.y + plan.x + plan.z[::-1]):
            n = len(r_q.terms)
            held = [*r_q.terms, *r_kv.terms]
            if one == plan.x[0]:
                *held, shared_n, returned.same = tie(*held, shared_n, returned.same)
                returned.near(shared_n)
                returned.prompt_three()
            elif one == plan.y[0]:
                *held, grads, returned.own = tie(*held, grads, returned.own)
                grads = level(grads, "z")
            elif one == plan.z[-1]:
                held = tie(*held)
            else:
                *held, returned.back = tie(*held, returned.back)
            r_q.terms, r_kv.terms = held[:n], held[n:]
            r_q.stage(one)
            r_kv.stage(two)
        o_ab = grads.reshape(-1, width).astype(F32)
        grad_tokens = grad_own + returned.total()
        o_query = r_q.result()
        o_line = o_query[step]
        o_both = r_kv.result().reshape(step, parts, 2, width // parts)

        o_small = [o_line[i * step : (i + 1) * step] for i in range(small)]
        o_bin = o_line[small * step : (small + wide) * step]
        return (
            layer_out[None],
            grad_tokens.astype(BF)[None],
            o_query[:step],
            o_both[:, :, 0].reshape(step, width),
            o_both[:, :, 1].reshape(step, width),
            o_ab[wide * step : (wide + 1) * step],
            jnp.concatenate([o_ab[i * step : (i + 1) * step] for i in range(wide + 1, 2 * wide + 1)], 1),
            o_ab[: wide * step],
            o_small[0],
            o_small[1],
            o_small[2],
            o_small[3],
            o_small[4],
            o_bin,
            o_small[5],
            o_small[6],
            o_small[7],
        )

    split = P(GRP, ROW, None)
    owned2, owned1 = P(AXES, None), P(AXES)
    in_specs = (split, P(GRP, None), split) + (owned2,) * 6 + (owned1,) * 9
    out_specs = (split, split) + (owned2,) * 6 + (owned1,) * 9
    return jax.shard_map(
        per_device, mesh=fine, in_specs=in_specs, out_specs=out_specs, check_vma=False
    )
```

```python
import functools

import jax
import jax.numpy as jnp
import numpy as np
from jax import lax
from jax.experimental import pallas as pl
from jax.experimental.pallas import tpu as pltpu
from jax.sharding import Mesh
from jax.sharding import PartitionSpec as P

HEADS = 12
HDIM = 64
PROMPT = 1024
CONT_MOST = 256
BF = jnp.bfloat16
F32 = jnp.float32

NORM_EPS = 1e-12
MASK_FILL = -1000000000.0
SQRT_HALF = 0.7071067811865476
INV_ROOT_TAU = 0.3989422804014327
AXES = ("x", "core", "z", "y")
GRP, ROW = AXES[:2], AXES[2:]
WIDE = 4
WO, WI = 4, 5
WQ, WK, WV = 0, 1, 2


def mm(left, right):
    return jnp.dot(left, right, preferred_element_type=F32)


def segment_ids(lengths, group_len):
    ends = jnp.cumsum(lengths)
    places = jnp.arange(group_len, dtype=jnp.int32)
    passed = jnp.sum(((places - PROMPT)[:, None] >= ends[None, :]).astype(jnp.int32), axis=-1)
    return jnp.where(places < PROMPT, 0, 1 + passed)


class Plan:
    def __init__(self, grp, row):
        self.grp, self.row, self.count = grp, row, grp * row
        y = row // 4
        bits = lambda base, size: [base << i for i in range(size.bit_length() - 1)]
        self.y, self.z = bits(1, y), bits(y, 4)
        self.core, self.x = bits(row, 2), bits(2 * row, grp // 2)
        self.bits = self.count.bit_length() - 1

    def swap(self, value, mask):
        return lax.ppermute(value, AXES, [(i, i ^ mask) for i in range(self.count)])

    def send(self, value, moves):
        pairs = [(g * self.row + a, g * self.row + b) for g in range(self.grp) for a, b in moves]
        return lax.ppermute(value, AXES, pairs)

    def me(self):
        return lax.axis_index(AXES)


class Reduce:
    def __init__(self, plan, terms, left=None):
        self.plan, self.terms = plan, list(terms)
        self.left = left or [1 << i for i in reversed(range(plan.bits))]

    def cut(self, term, bit, place):
        at = self.left.index(bit)
        high, low = 1 << at, 1 << (len(self.left) - at - 1)
        _, rows, width = term.shape
        term = term.reshape(high, 2, low * rows, width)
        return lax.dynamic_slice_in_dim(term, place, 1, 1).reshape(high * low, rows, width)

    def total(self, terms):
        return sum([t.astype(F32) for t in terms[1:]], terms[0].astype(F32))

    def stage(self, bit):
        place = (self.plan.me() // bit) & 1
        away = self.total([self.cut(t, bit, 1 - place) for t in self.terms]).astype(BF)
        here = [self.cut(t, bit, place) for t in self.terms]
        self.left = [b for b in self.left if b != bit]
        self.terms = here + [self.plan.swap(away, bit)]

    def result(self):
        return self.total(self.terms)[0]


def tie(*values):
    return lax.optimization_barrier(values)


class Tokens:
    def __init__(self, plan, own):
        self.plan, self.own = plan, own
        self.rows = own.shape[0]
        self.ready = plan.row == 8

    def stage_one(self):
        if self.ready:
            plan, own = self.plan, self.own
            across = plan.send(own, [(0, 4), (1, 5), (2, 6), (3, 7)])
            self.same = jnp.where(lax.axis_index(ROW) < 4, own, across)
            self.beside = plan.swap(own, 1)
            return [self.same, self.beside]
        return []

    def stage_two(self):
        if self.ready:
            plan = self.plan
            self.other = plan.swap(self.same, 2)
            self.same_y = plan.swap(self.same, 1)
            self.diagonal = plan.send(self.own, [(5, 6), (6, 5)])
            return [self.other, self.same_y, self.diagonal]
        return []

    def stage_three(self):
        if self.ready:
            self.other_y = self.plan.swap(self.other, 1)

    def spots(self):
        row, rows, own = lax.axis_index(ROW), self.rows, self.own
        if self.ready:
            near = jnp.where(row < 4, 0, jnp.where((row == 5) | (row == 6), 3, 2))
            return [
                self.same, self.other, self.same_y, self.other_y, own, self.beside, self.diagonal,
            ], near
        every = lax.all_gather(own, ROW, axis=0, tiled=True)
        start = jnp.maximum(row * rows - CONT_MOST, 0)
        padded = jnp.concatenate([every, jnp.zeros((CONT_MOST, own.shape[1]), own.dtype)], 0)
        near = lax.dynamic_slice_in_dim(padded, start, rows + 2 * CONT_MOST, 0)
        every = jnp.concatenate([every[:PROMPT], near], 0)
        spots = [every[i : i + rows] for i in range(0, every.shape[0], rows)]
        return spots, jnp.where(row * rows < PROMPT, 0, near.shape[0] // rows)


def near_segments(plan, segments, rows):
    row = lax.axis_index(ROW)
    if plan.row != 8:
        start = jnp.maximum(row * rows - CONT_MOST, 0)
        padded = jnp.concatenate([segments, jnp.full((CONT_MOST,), -1, jnp.int32)], 0)
        near = lax.dynamic_slice_in_dim(padded, start, rows + 2 * CONT_MOST, 0)
        return jnp.where((near == 0) | (row * rows < PROMPT), -1, near)
    pieces = []
    for block, valid in (
        (row, row >= 4),
        (row ^ 1, row >= 4),
        (11 - row, (row == 5) | (row == 6)),
    ):
        block = jnp.clip(block, 0, 7)
        ids = lax.dynamic_slice_in_dim(segments, block * rows, rows, 0)
        pieces.append(jnp.where(valid, ids, -1))
    return jnp.concatenate(pieces, 0)


class Return:
    def __init__(self, plan, rows):
        self.plan, self.rows = plan, rows

    def prompt_one(self, parts):
        self.prompt = self.same = self.own = self.back = parts
        if self.plan.row == 8:
            same, other, same_y, other_y = [parts[i].astype(F32) for i in range(4)]
            self.other = (other + self.plan.swap(parts[3], 1).astype(F32)).astype(BF)
            self.same = same + self.plan.swap(parts[2], 1).astype(F32)

    def prompt_two(self):
        if self.plan.row == 8:
            self.same = self.same + self.plan.swap(self.other, 2).astype(F32)

    def prompt_three(self):
        if self.plan.row == 8:
            self.back = self.plan.send(self.same.astype(BF), [(4, 0), (5, 1), (6, 2), (7, 3)])

    def near(self, parts):
        self.around = parts
        if self.plan.row == 8:
            own = parts[0].astype(F32) + self.plan.swap(parts[1], 1).astype(F32)
            self.own = own + self.plan.send(parts[2], [(5, 6), (6, 5)]).astype(F32)

    def total(self):
        row, rows = lax.axis_index(ROW), self.rows
        if self.plan.row == 8:
            return jnp.where(row < 4, self.same + self.back.astype(F32), self.own)
        around = self.around.reshape(-1, self.around.shape[-1]).astype(F32)
        start = jnp.maximum(row * rows - CONT_MOST, 0)
        whole = jnp.zeros((self.plan.row * rows + CONT_MOST, around.shape[1]), F32)
        whole = whole.at[:PROMPT].set(self.prompt.reshape(PROMPT, -1).astype(F32))
        near = jnp.where(row * rows < PROMPT, 0, around)
        near = lax.dynamic_slice_in_dim(whole, start, rows + 2 * CONT_MOST, 0) + near
        whole = lax.dynamic_update_slice_in_dim(whole, near, start, 0)
        return lax.psum_scatter(whole[: self.plan.row * rows], ROW, scatter_dimension=0, tiled=True)


def heads_mask(lanes, head):
    lane = lax.broadcasted_iota(jnp.int32, lanes, 1)
    return (lane >= head * HDIM) & (lane < (head + 1) * HDIM)


def nt(left, right):
    return lax.dot_general(left, right, (((1,), (1,)), ((), ())), preferred_element_type=F32)


def tn(left, right):
    return lax.dot_general(left, right, (((0,), (0,)), ((), ())), preferred_element_type=F32)


def pack_kernel(wo_ref, wi_ref, wu_ref, wq_ref, wk_ref, wv_ref, line_ref, early_ref, late_ref):
    step, width = wo_ref.shape
    early_ref[:step, :] = wq_ref[...]
    early_ref[step : step + 8, :] = line_ref[:8, :]
    early_ref[step + 8 : 2 * step + 8, :] = wk_ref[...]
    early_ref[2 * step + 8 :, :] = wv_ref[...]
    late_ref[: WIDE * step, :] = wu_ref[...]
    late_ref[WO * step : WI * step, :] = wo_ref[...]
    for i in range(WIDE):
        late_ref[(WI + i) * step : (WI + i + 1) * step, :] = wi_ref[:, i * width : (i + 1) * width]
    late_ref[(WI + WIDE) * step :, :] = line_ref[8:, :]


def pack_call(w_output, w_inner, w_outer, w_query, w_key, w_value, line):
    step, width = w_output.shape
    shape = lambda rows: jax.ShapeDtypeStruct((rows, width), BF)
    return pl.pallas_call(
        pack_kernel, out_shape=[shape(3 * step + 8), shape((WI + WIDE) * step + 8)], name="pack"
    )(w_output, w_inner, w_outer, w_query, w_key, w_value, line)


def attention_kernel(blocks, first, rows, places, *refs):
    spots = refs[:blocks]
    (near_ref, me_ref, own_ref, a0_ref, a1_ref, b0_ref, b1_ref, segq_ref, segk_ref,
     w_out, q_ref, kp_ref, vp_ref, kn_ref, vn_ref, ctx_ref, lse_ref,
     x_ref, w_ref, s_ref, vt_ref, out_ref, line_ref, bias_ref, sems, w_sems, o_sem) = refs[blocks:]
    near = near_ref[0]
    depth = own_ref.shape[1]
    owners = w_ref.shape[0]
    each = depth // owners
    part = q_ref.shape[1]

    def weights(act):
        @pl.loop(0, owners)
        def _(e):
            away = e ^ me_ref[0]
            for (bits, half), (zero, one), parts in (
                (places[0], (a0_ref, a1_ref), ((0, each, w_ref, 0), (each, 8, line_ref, 0))),
                (places[1], (b0_ref, b1_ref), ((0, 2 * each, w_ref, each),)),
            ):
                j = sum([((away // bit) & 1) * weight for bit, weight in bits])
                for which, source in enumerate((zero, one)):

                    @pl.when(((away // half) & 1) == which)
                    def _():
                        for k, (top, size, target, base) in enumerate(parts):
                            act(pltpu.make_async_copy(
                                source.at[j, pl.ds(top, size)], target.at[e, pl.ds(base, size)],
                                w_sems.at[2 * k if zero is a0_ref else 1, e],
                            ))

    @pl.when(pl.program_id(0) == 0)
    def _():
        copies = [
            pltpu.make_async_copy(spot, x_ref.at[pl.ds(i * rows, rows)], sems.at[i])
            for i, spot in enumerate(spots)
        ]
        weights(lambda c: c.start())
        for copy in copies:
            copy.start()
        weights(lambda c: c.wait())
        for copy in copies:
            copy.wait()
        pltpu.make_async_copy(w_ref, w_out, o_sem).start()
        line = line_ref[:, 0, :128]
        place = lax.broadcasted_iota(jnp.int32, (128, depth), 0)
        lane = lax.broadcasted_iota(jnp.int32, (128, depth), 1)
        mine = lax.broadcasted_iota(jnp.int32, (owners, depth), 0)
        mine = mine == lax.broadcasted_iota(jnp.int32, (owners, depth), 1) // each
        for i in range(2):
            spread = mm(line, jnp.where(place == lane % each + i * each, 1.0, 0.0).astype(BF))
            bias_ref[i : i + 1, :] = jnp.sum(jnp.where(mine, spread, 0.0), axis=0, keepdims=True)

    lanes = pl.ds(pl.multiple_of(pl.program_id(0) * part, part), part)
    wq, wk, wv = [
        w_ref[:, i * each : (i + 1) * each, lanes].reshape(depth, part) for i in (WQ, WK, WV)
    ]
    queries = (mm(own_ref[...], wq) + bias_ref[0:1, lanes]) * (HDIM**-0.5)
    q_ref[...] = queries.astype(BF)

    heads = part // HDIM
    q = q_ref[...]
    tall = x_ref.shape[0]

    def body(sets):
        for k_ref, v_ref, base, size, _ in sets:
            x = x_ref[base : base + size, :]
            k_ref[...] = mm(x, wk).astype(BF)
            v = (mm(x, wv) + bias_ref[1:2, lanes]).astype(BF)
            v_ref[...] = v
            vt_ref[:, base : base + size] = v.T
        for h in range(heads):
            q_h = jnp.where(heads_mask(q.shape, h), q, 0)
            peak = jnp.full((1, rows), MASK_FILL, F32)
            for k_ref, _, base, size, masked in sets:
                s = nt(k_ref[...], q_h)
                if masked:
                    s = jnp.where(segk_ref[...] == segq_ref[...], s, MASK_FILL)
                s_ref[h % 2, base : base + size, :] = s
                peak = jnp.maximum(peak, jnp.max(s, axis=0, keepdims=True))
            total, mixed = jnp.zeros((1, rows), F32), jnp.zeros((HDIM, rows), F32)
            for _, _, base, size, _ in sets:
                p = jnp.exp(s_ref[h % 2, base : base + size, :] - peak)
                total = total + jnp.sum(p, axis=0, keepdims=True)
                mixed = mixed + mm(vt_ref[h * HDIM : (h + 1) * HDIM, base : base + size], p.astype(BF))
            out_ref[h * HDIM : (h + 1) * HDIM, :] = mixed / total
            lse_ref[0, h : h + 1, :] = peak + jnp.log(total)

    prompt = (kp_ref, vp_ref, 0, PROMPT, False)

    @pl.when(near == 0)
    def _():
        body([prompt])

    @pl.when(near > 0)
    def _():
        body([prompt, (kn_ref, vn_ref, PROMPT, tall - PROMPT, True)])

    ctx_ref[...] = out_ref[...].T.astype(BF)

    @pl.when(pl.program_id(0) == pl.num_programs(0) - 1)
    def _():
        pltpu.make_async_copy(w_ref, w_out, o_sem).wait()


def attention_call(spots, first, near, me, own, pieces, places, segq, segk):
    rows, width = own.shape
    blocks = len(spots)
    tall = blocks * rows
    part = 256
    steps = width // part
    heads = part // HDIM
    cols = lambda depth: pl.BlockSpec((depth, part), lambda g: (0, g))
    flops = 2 * tall * width * width * 2 + 4 * tall * rows * width * 4
    owners = 2 * pieces[0].shape[0]
    each = width // owners
    return pl.pallas_call(
        functools.partial(attention_kernel, blocks, first, rows, places),
        grid=(steps,),
        in_specs=[pl.BlockSpec(memory_space=pl.ANY)] * blocks
        + [
            pl.BlockSpec(memory_space=pltpu.SMEM),
            pl.BlockSpec(memory_space=pltpu.SMEM),
            pl.BlockSpec((rows, width), lambda g: (0, 0)),
        ] + [pl.BlockSpec(memory_space=pl.ANY)] * 4 + [
            pl.BlockSpec((1, rows), lambda g: (0, 0)),
            pl.BlockSpec(segk.shape, lambda g: (0, 0)),
        ],
        out_specs=[
            pl.BlockSpec(memory_space=pl.ANY),
            cols(rows), cols(PROMPT), cols(PROMPT), cols(tall - PROMPT), cols(tall - PROMPT),
            cols(rows), pl.BlockSpec((1, 8, rows), lambda g: (g, 0, 0)),
        ],
        out_shape=[
            jax.ShapeDtypeStruct((owners, 3 * each, width), BF),
            jax.ShapeDtypeStruct((rows, width), BF),
            jax.ShapeDtypeStruct((PROMPT, width), BF),
            jax.ShapeDtypeStruct((PROMPT, width), BF),
            jax.ShapeDtypeStruct((tall - PROMPT, width), BF),
            jax.ShapeDtypeStruct((tall - PROMPT, width), BF),
            jax.ShapeDtypeStruct((rows, width), BF),
            jax.ShapeDtypeStruct((steps, 8, rows), F32),
        ],
        scratch_shapes=[
            pltpu.VMEM((tall, width), BF),
            pltpu.VMEM((owners, 3 * each, width), BF),
            pltpu.VMEM((2, tall, rows), F32),
            pltpu.VMEM((part, tall), BF),
            pltpu.VMEM((part, rows), F32),
            pltpu.VMEM((owners, 8, width), BF),
            pltpu.VMEM((8, width), F32),
            pltpu.SemaphoreType.DMA((blocks,)),
            pltpu.SemaphoreType.DMA((3, owners)),
            pltpu.SemaphoreType.DMA,
        ],
        compiler_params=pltpu.CompilerParams(vmem_limit_bytes=60 * 2**20),
        cost_estimate=pl.CostEstimate(
            flops=flops, bytes_accessed=12 * 2**20, transcendentals=tall * rows * 12
        ),
        name="attention",
    )(*spots, near, me, own, *pieces, segq, segk)


def halves(value, runs, core):
    depth = value.shape[0] // runs
    pick = lambda first: jnp.concatenate(
        [value[i * depth : (i + 1) * depth] for i in range(first, runs, 2)], 0
    )
    even, odd = pick(0), pick(1)
    return jnp.where(core == 0, odd, even), jnp.where(core == 0, even, odd)


def middle_kernel(wide, mapped, ctx_ref, own_ref, cot_ref, got_ref, vec_ref, bin_ref,
                  out_ref, h1_ref, gctx_ref, grads, sums_ref, sbin_ref,
                  first_ref, n1_ref, inv_ref, low_ref, pre_ref, cdf_ref, act_ref, acc_ref,
                  gffn_ref, glow_ref, lowt_ref, w_ref, out_buf, in_buf, wo_buf, sems, w_sems):
    step = pl.program_id(0)
    width = ctx_ref.shape[1]
    vec = lambda i: vec_ref[i : i + 1, :]
    mean = lambda v: jnp.sum(v, axis=-1, keepdims=True) * (1.0 / width)
    down = lambda v: jnp.sum(v, axis=0, keepdims=True)
    owners = got_ref.shape[0]
    each = width // owners
    some = owners // wide
    square = lambda value: value.reshape(width, width)
    rows_of = lambda place: pl.ds(pl.multiple_of(place * each, each), each)
    w_output = lambda ref: ref.at[:, rows_of(WO)]
    w_inner = lambda ref, at: ref.at[:, rows_of(WI + at)]
    w_outer = lambda ref, at: ref.at[pl.ds(at * some, some), pl.ds(0, wide * each)]

    def fetch_inner(at):
        return pltpu.make_async_copy(w_inner(got_ref, at), w_inner(w_ref, at), w_sems.at[0, at])

    def fetch_outer(at):
        return pltpu.make_async_copy(w_outer(got_ref, at), w_outer(w_ref, at), w_sems.at[1, at])

    def fetch_output():
        return pltpu.make_async_copy(w_output(got_ref), w_output(w_ref), w_sems.at[0, wide])

    def slot(group, i):
        return group % 2 * 16 + group // 2 * 8 + i % 2 * 4 + i // 2 if mapped else group * 8 + i

    def outer(at):
        turn = (2 * wide - 1 - at) % 2
        return [
            pltpu.make_async_copy(
                out_buf.at[turn, i], grads.at[slot(at, i), pl.ds(0, wide * each)], sems.at[turn, i]
            )
            for i in range(some)
        ]

    def inner(at):
        turn = (2 * wide - 1 - at) % 2
        top = pl.multiple_of((wide + 1 + at) * each, each)
        return [
            pltpu.make_async_copy(
                in_buf.at[turn, e], grads.at[slot(e // 8, e % 8), pl.ds(top, each)], sems.at[2 + turn, e]
            )
            for e in range(owners)
        ]

    def output():
        return [
            pltpu.make_async_copy(
                wo_buf.at[e], grads.at[slot(e // 8, e % 8), pl.ds(wide * each, each)], sems.at[4, e]
            )
            for e in range(owners)
        ]

    def start(copies):
        for copy in copies:
            copy.start()

    def wait(copies):
        for copy in copies:
            copy.wait()

    @pl.when(step == 0)
    def _():
        fetch_output().start()
        for at in range(wide):
            fetch_inner(at).start()
            fetch_outer(at).start()
        fetch_output().wait()
        hidden = own_ref[...].astype(F32) + mm(ctx_ref[...], square(w_output(w_ref)[...])) + vec(0)
        centred = hidden - mean(hidden)
        inverse = lax.rsqrt(mean(centred * centred) + NORM_EPS)
        normed = centred * inverse
        n1_ref[...] = normed
        inv_ref[...] = inverse
        first = normed * vec(1) + vec(2)
        first_ref[...] = first
        low_ref[...] = first.astype(BF)
        lowt_ref[...] = first.astype(BF).T

    @pl.when(step < wide)
    def _():
        chunk = pl.ds(pl.multiple_of(step * width, width), width)
        fetch_inner(step).wait()
        fetch_outer(step).wait()
        pre = mm(low_ref[...], square(w_inner(w_ref, step)[...])) + bin_ref[pl.ds(step, 1), :]
        cdf = 0.5 * (1.0 + lax.erf(pre * SQRT_HALF))
        act = (pre * cdf).astype(BF)
        pre_ref[:, chunk] = pre
        cdf_ref[:, chunk] = cdf
        act_ref[:, chunk] = act
        more = mm(act, square(w_outer(w_ref, step)[...]))

        @pl.when(step == 0)
        def _():
            acc_ref[...] = more

        @pl.when(step > 0)
        def _():
            acc_ref[...] += more

    @pl.when(step == wide - 1)
    def _():
        hidden = first_ref[...] + acc_ref[...] + vec(3)
        centred = hidden - mean(hidden)
        inverse = lax.rsqrt(mean(centred * centred) + NORM_EPS)
        normed = centred * inverse
        out_ref[...] = (normed * vec(4) + vec(5)).astype(BF)
        grad = cot_ref[...].astype(F32)
        sums_ref[0:1, :] = down(grad * normed)
        sums_ref[1:2, :] = down(grad)
        e = grad * vec(4)
        back = inverse * (e - mean(e) - normed * mean(e * normed))
        gffn_ref[...] = back
        low = back.astype(BF)
        glow_ref[...] = low
        sums_ref[2:3, :] = down(low.astype(F32))

    @pl.when(step >= wide)
    def _():
        at = 2 * wide - 1 - step
        chunk = pl.ds(pl.multiple_of(at * width, width), width)
        pre = pre_ref[:, chunk]
        slope = cdf_ref[:, chunk] + pre * jnp.exp(-0.5 * pre * pre) * INV_ROOT_TAU
        low = glow_ref[...]
        grad = (nt(low, square(w_outer(w_ref, at)[...])) * slope).astype(BF)
        sbin_ref[pl.ds(at, 1), :] = down(grad.astype(F32))
        turn = step % 2

        @pl.when(step >= wide + 2)
        def _():
            wait(outer(at + 2) + inner(at + 2))

        out_buf[turn] = tn(act_ref[:, chunk], low).astype(BF).reshape(some, wide * each, width)
        start(outer(at))
        in_buf[turn] = mm(lowt_ref[...], grad).astype(BF).reshape(owners, each, width)
        start(inner(at))
        gffn_ref[...] += nt(grad, square(w_inner(w_ref, at)[...]))

    @pl.when(step == 2 * wide - 1)
    def _():
        grad = gffn_ref[...]
        normed = n1_ref[...]
        sums_ref[3:4, :] = down(grad * normed)
        sums_ref[4:5, :] = down(grad)
        e = grad * vec(1)
        back = inv_ref[...] * (e - mean(e) - normed * mean(e * normed))
        h1_ref[...] = back
        low = back.astype(BF)
        sums_ref[5:6, :] = down(low.astype(F32))
        wo_buf[...] = tn(ctx_ref[...], low).astype(BF).reshape(owners, each, width)
        start(output())
        gctx = nt(low, square(w_output(w_ref)[...])).astype(BF)
        gctx_ref[...] = gctx
        sums_ref[6:7, :] = down(gctx.astype(F32))
        sums_ref[7:8, :] = jnp.zeros((1, width), F32)
        wait(outer(1) + inner(1) + outer(0) + inner(0) + output())


def middle_call(ctx, own, cot, got, vec, b_inner, mapped):
    rows, width = own.shape
    owners = got.shape[0]
    each = width // owners
    wide = WIDE
    whole = lambda shape: pl.BlockSpec(shape, lambda s: (0,) * len(shape))
    shape = jax.ShapeDtypeStruct
    return pl.pallas_call(
        functools.partial(middle_kernel, wide, mapped),
        grid=(2 * wide,),
        in_specs=[
            whole((rows, width)), whole((rows, width)), whole((rows, width)),
            pl.BlockSpec(memory_space=pl.ANY),
            whole((8, width)), whole((8, width)),
        ],
        out_specs=[
            whole((rows, width)), whole((rows, width)), whole((rows, width)),
            pl.BlockSpec(memory_space=pl.ANY),
            whole((8, width)), whole((8, width)),
        ],
        out_shape=[
            shape((rows, width), BF), shape((rows, width), F32), shape((rows, width), BF),
            shape((owners, (2 * wide + 1) * each, width), BF),
            shape((8, width), F32), shape((8, width), F32),
        ],
        scratch_shapes=[
            pltpu.VMEM((rows, width), F32), pltpu.VMEM((rows, width), F32), pltpu.VMEM((rows, 1), F32),
            pltpu.VMEM((rows, width), BF), pltpu.VMEM((rows, wide * width), F32),
            pltpu.VMEM((rows, wide * width), F32), pltpu.VMEM((rows, wide * width), BF),
            pltpu.VMEM((rows, width), F32), pltpu.VMEM((rows, width), F32),
            pltpu.VMEM((rows, width), BF), pltpu.VMEM((width, rows), BF),
            pltpu.VMEM((owners, (2 * wide + 1) * each, width), BF),
            pltpu.VMEM((2, owners // wide, wide * each, width), BF),
            pltpu.VMEM((2, owners, each, width), BF),
            pltpu.VMEM((owners, each, width), BF), pltpu.SemaphoreType.DMA((5, owners)),
            pltpu.SemaphoreType.DMA((2, wide + 1)),
        ],
        compiler_params=pltpu.CompilerParams(vmem_limit_bytes=60 * 2**20),
        cost_estimate=pl.CostEstimate(
            flops=2 * rows * width * width * (6 * wide + 3), bytes_accessed=32 * 2**20,
            transcendentals=2 * rows * width * wide,
        ),
        name="middle",
    )(ctx, own, cot, got, vec, b_inner)


def back_kernel(rows, bound, started, *refs):
    near_ref, gctx_ref, ctx_ref, q_ref, k_ref, v_ref, lse_ref, segq_ref, segk_ref = refs[:9]
    dk_ref, dv_ref, dq_ref, kt_ref, p_ref, ds_ref = refs[-6:]
    q, g = q_ref[...], gctx_ref[...]
    part = q.shape[1]
    heads = part // HDIM
    masks = [heads_mask(q.shape, h) for h in range(heads)]
    q_parts = [jnp.where(m, q, 0) for m in masks]
    g_parts = [jnp.where(m, g, 0) for m in masks]
    product = (g.astype(F32) * ctx_ref[...].astype(F32)).T
    inner = [
        jnp.sum(product[h * HDIM : (h + 1) * HDIM], axis=0, keepdims=True) for h in range(heads)
    ]

    def body():
        k, v = k_ref[...], v_ref[...]
        kt_ref[...] = k.T
        for h in range(heads):
            s = nt(k, q_parts[h])
            if bound is None:
                s = jnp.where(segk_ref[...] == segq_ref[...], s, MASK_FILL)
            p = jnp.exp(s - lse_ref[0, h : h + 1, :])
            across = slice(h * rows, (h + 1) * rows)
            ds = (p * (nt(v, g_parts[h]) - inner[h])).astype(BF)
            p_ref[:, across] = p.astype(BF)
            ds_ref[:, across] = ds
            mine = slice(h * HDIM, (h + 1) * HDIM)
            more = mm(kt_ref[mine, :], ds)
            dq_ref[mine, :] = refs[9][mine, :] + more if started else more
        dk_ref[...] = mm(ds_ref[...], jnp.concatenate(q_parts, 0)).astype(BF)
        dv_ref[...] = mm(p_ref[...], jnp.concatenate(g_parts, 0)).astype(BF)

    if bound is None:

        @pl.when(near_ref[0] == 0)
        def _():
            dq_ref[...] = refs[9][...]

        pl.when(near_ref[0] > 0)(body)
    else:
        body()


def back_call(start, steps, bound, near, gctx, ctx, q, k, v, lse, segq, segk, dq0=None, into=None):
    rows, width = q.shape
    tall = k.shape[0]
    part = 256
    cols = lambda depth: pl.BlockSpec((depth, part), lambda g: (0, start + g))
    whole = lambda shape: pl.BlockSpec(shape, lambda g: (0,) * len(shape))
    down = pl.BlockSpec((part, rows), lambda g: (start + g, 0))
    shape = jax.ShapeDtypeStruct
    extra = ([dq0] if dq0 is not None else []) + list(into or [])
    specs = ([down] if dq0 is not None else []) + [pl.BlockSpec(memory_space=pl.ANY)] * len(into or [])
    return pl.pallas_call(
        functools.partial(back_kernel, rows, bound, dq0 is not None),
        grid=(steps,),
        in_specs=[
            pl.BlockSpec(memory_space=pltpu.SMEM),
            cols(rows), cols(rows), cols(rows), cols(tall), cols(tall),
            pl.BlockSpec((1, 8, rows), lambda g: (start + g, 0, 0)),
            whole((1, rows)), whole(segk.shape),
        ] + specs,
        out_specs=[cols(tall), cols(tall), down],
        out_shape=[shape((tall, width), BF), shape((tall, width), BF), shape((width, rows), F32)],
        input_output_aliases={9 + i: i for i in range(3)} if into else {},
        scratch_shapes=[
            pltpu.VMEM((part, tall), BF),
            pltpu.VMEM((tall, part // HDIM * rows), BF),
            pltpu.VMEM((tall, part // HDIM * rows), BF),
        ],
        compiler_params=pltpu.CompilerParams(vmem_limit_bytes=60 * 2**20),
        cost_estimate=pl.CostEstimate(
            flops=2 * 10 * 2 * tall * rows * part * steps * 2,
            bytes_accessed=8 * tall * part * steps, transcendentals=tall * rows * 4 * steps,
        ),
        name="attention_back",
    )(near, gctx, ctx, q, k, v, lse, segq, segk, *extra)


def product_kernel(rows, bound, near_ref, dk_ref, dv_ref, wk_ref, wv_ref, gx_ref):
    @pl.when((pl.program_id(0) < near_ref[0]) | (bound is not None))
    def _():
        width = dk_ref.shape[1]
        wk, wv = wk_ref[...].reshape(width, width), wv_ref[...].reshape(width, width)
        gx_ref[0] = (nt(dk_ref[...], wk) + nt(dv_ref[...], wv)).astype(BF)


def product_call(bound, near, dk, dv, got, rows):
    tall, width = dk.shape
    owners, each = got.shape[0], width // got.shape[0]
    weight = lambda place: pl.BlockSpec((owners, each, width), lambda b: (0, place, 0))
    return pl.pallas_call(
        functools.partial(product_kernel, rows, bound),
        grid=(tall // rows,),
        in_specs=[
            pl.BlockSpec(memory_space=pltpu.SMEM),
            pl.BlockSpec((rows, width), lambda b: (b, 0)),
            pl.BlockSpec((rows, width), lambda b: (b, 0)),
            weight(WK), weight(WV),
        ],
        out_specs=pl.BlockSpec((1, rows, width), lambda b: (b, 0, 0)),
        out_shape=jax.ShapeDtypeStruct((tall // rows, rows, width), BF),
        compiler_params=pltpu.CompilerParams(vmem_limit_bytes=60 * 2**20),
        cost_estimate=pl.CostEstimate(
            flops=4 * tall * width * width, bytes_accessed=6 * tall * width, transcendentals=0
        ),
        name="token_product",
    )(near, dk, dv, got, got)


def weight_kernel(blocks, first, rows, runs, *refs):
    spots = refs[:blocks]
    (near_ref, core_ref, own_ref, dq_ref, wq_ref, h1_ref, dkp_ref, dvp_ref, dkn_ref, dvn_ref,
     q_send, q_keep, kv_send, kv_keep, gown_ref, sums_ref, x_ref, xt_ref, sems) = refs[blocks:]
    core = core_ref[0]
    step = pl.program_id(0)

    @pl.when(step == 0)
    def _():
        copies = [
            pltpu.make_async_copy(spot, x_ref.at[pl.ds(i * rows, rows)], sems.at[i])
            for i, spot in enumerate(spots)
        ]
        for copy in copies:
            copy.start()
        gown_ref[...] = h1_ref[...]
        for i, copy in enumerate(copies):
            copy.wait()
            xt_ref[:, i * rows : (i + 1) * rows] = x_ref[i * rows : (i + 1) * rows, :].T

    scale = HDIM**-0.5
    dq = dq_ref[...].T.astype(BF)
    part = dq.shape[1]
    width = x_ref.shape[1]
    gown_ref[...] += nt(dq, wq_ref[...].reshape(width, part)) * scale
    away, here = halves((tn(own_ref[...], dq) * scale).astype(BF), runs, core)
    q_send[...] = away.reshape(q_send.shape)
    q_keep[...] = here.reshape(q_send.shape)
    sums_ref[0:1, :] = jnp.sum(dq.astype(F32), axis=0, keepdims=True) * scale

    def body(near):
        for i, (p_ref, n_ref) in enumerate(((dkp_ref, dkn_ref), (dvp_ref, dvn_ref))):
            grad = mm(xt_ref[:, :PROMPT], p_ref[...])
            if near:
                grad = grad + mm(xt_ref[:, PROMPT:], n_ref[...])
            away, here = halves(grad.astype(BF), runs, core)
            shape = kv_send.shape[:2] + (part,)
            kv_send[:, :, i * part : (i + 1) * part] = away.reshape(shape)
            kv_keep[:, :, i * part : (i + 1) * part] = here.reshape(shape)

    pl.when(near_ref[0] == 0)(lambda: body(False))
    pl.when(near_ref[0] > 0)(lambda: body(True))
    sums_ref[1:8, :] = jnp.zeros((7, part), F32)


def weight_call(spots, first, near, own, dq, got, h1, dkp, dvp, dkn, dvn, core, runs):
    rows, width = own.shape
    blocks = len(spots)
    tall = blocks * rows
    part = 256
    steps = width // part
    cols = lambda depth, size=part: pl.BlockSpec((depth, size), lambda g: (0, g))
    whole = lambda shape: pl.BlockSpec(shape, lambda g: (0,) * len(shape))
    shape = jax.ShapeDtypeStruct
    owners, each = got.shape[0], width // got.shape[0]
    half = owners // 2
    slab = lambda size: pl.BlockSpec((half, each, size), lambda g: (0, 0, g))
    return pl.pallas_call(
        functools.partial(weight_kernel, blocks, first, rows, runs),
        grid=(steps,),
        in_specs=[pl.BlockSpec(memory_space=pl.ANY)] * blocks
        + [
            pl.BlockSpec(memory_space=pltpu.SMEM),
            pl.BlockSpec(memory_space=pltpu.SMEM),
            whole((rows, width)), pl.BlockSpec((part, rows), lambda g: (g, 0)),
            pl.BlockSpec((owners, each, part), lambda g: (0, WQ, g)),
            whole((rows, width)), cols(PROMPT), cols(PROMPT), cols(tall - PROMPT), cols(tall - PROMPT),
        ],
        out_specs=[
            slab(part), slab(part), slab(2 * part), slab(2 * part), whole((rows, width)), cols(8),
        ],
        out_shape=[
            shape((half, each, width), BF), shape((half, each, width), BF),
            shape((half, each, 2 * width), BF), shape((half, each, 2 * width), BF),
            shape((rows, width), F32), shape((8, width), F32),
        ],
        scratch_shapes=[
            pltpu.VMEM((tall, width), BF), pltpu.VMEM((width, tall), BF), pltpu.SemaphoreType.DMA((blocks,)),
        ],
        compiler_params=pltpu.CompilerParams(vmem_limit_bytes=60 * 2**20),
        cost_estimate=pl.CostEstimate(
            flops=4 * tall * width * width, bytes_accessed=12 * tall * width, transcendentals=0
        ),
        name="weight_product",
    )(*spots, near, core, own, dq, got, h1, dkp, dvp, dkn, dvn)


def real_owners(grads, count, step, width):
    split = count // 32
    take = lambda v: v.reshape(32, -1, split, step, width).transpose(0, 2, 1, 3, 4).reshape(count, -1, width)
    outer, rest = grads[:, : 4 * split * step], grads[:, 4 * split * step :]
    return jnp.concatenate([outer.reshape(count, 4 * step, width), take(rest)], 1)


def solution(mesh):
    plan = Plan(mesh.shape["grp"], mesh.shape["row"])
    fine = Mesh(mesh.devices.reshape(plan.grp // 2, 2, 4, plan.row // 4), AXES)

    def per_device(
        tokens, cont_lengths, cotangent, w_query, w_key, w_value, w_output, w_inner, w_outer,
        bias_query, bias_value, bias_output, gain_first, shift_first, bias_inner, bias_outer,
        gain_second, shift_second,
    ):
        count = plan.count
        _, rows, width = tokens.shape
        step = w_query.shape[0]
        wide = w_inner.shape[1] // width
        own = tokens[0]

        early = (bias_query, bias_value)
        late = (bias_output, gain_first, shift_first, bias_outer, gain_second, shift_second, bias_inner)
        small = len(late) - 1

        def in_line(vectors):
            line, place = 0, 0
            for vector in vectors:
                size = vector.shape[0]
                line = line + jnp.pad(vector, (place, width - place - size))
                place += size
            return jnp.pad(line[None], ((0, 7), (0, 0)))

        line = jnp.concatenate([in_line(early), in_line(late)], 0)
        runs = plan.grp
        row = lax.axis_index(ROW)
        core = lax.axis_index("core").astype(jnp.int32).reshape(1)
        exchange = Tokens(plan, own)
        squares = (w_query, w_key, w_value)
        if step % 8 == 0:
            first_pack, pack = pack_call(w_output, w_inner, w_outer, *squares, line)
            got = lax.all_gather(pack, AXES, axis=0, tiled=True).reshape(count, -1, width)
            lines = got[:, (WI + WIDE) * step]

            def swaps(value, bits):
                masks = [0]
                for bit in bits:
                    masks = masks + [m ^ bit for m in masks]
                return [plan.swap(value, m) for m in masks[1:]]

            def stage(held, bit):
                return jnp.concatenate([held, plan.swap(held, bit)], 0)

            away = swaps(first_pack, plan.z)
            *away, same, beside = tie(*away, *exchange.stage_one())
            exchange.same, exchange.beside = same, beside
            cut = step + 8
            one = jnp.stack([v[:cut] for v in (first_pack, *away)])
            two = jnp.stack([v[cut:] for v in (first_pack, *away)])
            one, two = stage(one, plan.x[0]), stage(two, plan.y[0])
            one, two, *seen = tie(one, two, *exchange.stage_two())
            exchange.other, exchange.same_y, exchange.diagonal = seen
            one, two = stage(one, plan.y[0]), stage(two, plan.x[0])
            exchange.stage_three()
            one, two, exchange.other_y = tie(one, two, exchange.other_y)
            pieces = [one, plan.swap(one, plan.core[0]), two, plan.swap(two, plan.core[0])]
            order = lambda *bits: ([(bit, 1 << i) for i, bit in enumerate(bits)], plan.core[0])
            places = (
                order(*plan.z, plan.x[0], plan.y[0]),
                order(*plan.z, plan.y[0], plan.x[0]),
            )
            me = plan.me().astype(jnp.int32).reshape(1)
        else:
            inner_rows = [w_inner[:, i * width : (i + 1) * width] for i in range(wide)]
            pack = jnp.concatenate([w_outer, w_output, *inner_rows, *squares, line], 0)
            got = lax.all_gather(pack, AXES, axis=0, tiled=True).reshape(count, -1, width)
            lines = got[:, 12 * step + 8]
            cuts = [wide * step, (wide + 1) * step, (2 * wide + 1) * step, 12 * step]
            outer, output, inner, rest, marks = jnp.split(got, cuts, axis=1)
            apart = lambda v, n: v.reshape(count, n, step, width).transpose(1, 0, 2, 3)
            inner, rest = [
                v.reshape(v.shape[0], 32, width // 32, width).transpose(1, 0, 2, 3)
                for v in (apart(inner, wide), apart(rest, 3))
            ]
            got = jnp.concatenate([v.reshape(32, -1, width) for v in (outer, output, inner)], 1)
            pairs = marks[:, 0, : 2 * step].reshape(32, count // 32, 2, step).transpose(0, 2, 1, 3)
            pairs = jnp.pad(pairs.reshape(32, 1, -1), ((0, 0), (0, 7), (0, width - 2 * width // 32)))
            one = jnp.concatenate([rest[:, 0], pairs], 1)
            two = rest[:, 1:].reshape(32, -1, width)
            pieces = [one[:16], one[16:], two[:16], two[16:]]
            places = (([(1, 1), (2, 2), (4, 4), (8, 8)], 16),) * 2
            me = jnp.zeros((1,), jnp.int32)
        spots, near = exchange.spots()
        first_near = PROMPT // rows

        table = lines[:, : small * step].reshape(count, small, step).transpose(1, 0, 2)
        table = table.reshape(small, width).astype(F32)
        v_bin = lines[:, small * step : (small + wide) * step].reshape(wide, width).astype(F32)
        v_bin = jnp.pad(v_bin, ((0, 8 - wide), (0, 0)))
        segments = segment_ids(cont_lengths[0], plan.row * rows)
        seg_own = lax.dynamic_slice_in_dim(segments, row * rows, rows, 0)[None, :]
        seg_near = near_segments(plan, segments, rows)[:, None]
        near = near.astype(jnp.int32).reshape(1)

        squares, queries, keys_p, values_p, keys_n, values_n, context, log_total = attention_call(
            spots, first_near, near, me, own, pieces, places, seg_own, seg_near
        )
        vec = jnp.concatenate([table, jnp.zeros((2, width), F32)], 0)
        layer_out, grad_h1, grad_context, grads, sums, sums_bin = middle_call(
            context, own, cotangent[0], got, vec, v_bin, step % 8 == 0
        )
        if step % 8:
            grads = real_owners(grads, count, step, width)
            grads = grads.reshape(plan.grp // 2, 2, 4, plan.row // 4, -1, width)
            grads = grads.transpose(1, 0, 3, 2, 4, 5).reshape(count, -1, width)
        level = lambda value, axes: lax.psum_scatter(value, axes, scatter_dimension=0, tiled=True)
        grads = level(grads, "core")
        core_bit = plan.core[0]
        left = [1 << i for i in reversed(range(plan.bits)) if 1 << i != core_bit]
        parts = width // 256
        dkp, dvp, dqp = back_call(
            0, parts, first_near, near, grad_context, context, queries, keys_p, values_p, log_total,
            seg_own, seg_near,
        )
        grads, dkp, dvp, dqp = tie(grads, dkp, dvp, dqp)
        grads = level(grads, ("x", "y"))
        shared_p = product_call(first_near, near, dkp, dvp, squares, rows)
        returned = Return(plan, rows)
        returned.prompt_one(shared_p)
        dkn, dvn, dq = back_call(
            0, parts, None, near, grad_context, context, queries, keys_n, values_n, log_total,
            seg_own, seg_near, dqp,
        )
        q_send, q_keep, kv_send, kv_keep, grad_own, sums_qkv = weight_call(
            spots, first_near, near, own, dq, squares, grad_h1, dkp, dvp, dkn, dvn, core, runs
        )
        q_send, q_keep, kv_send, kv_keep, returned.same, dkn, dvn = tie(
            q_send, q_keep, kv_send, kv_keep, returned.same, dkn, dvn
        )
        returned.prompt_two()
        shared_n = product_call(None, near, dkn, dvn, squares, rows)

        order = (6, 5, 3, 4, 2, 0, 1)
        small = len(early) + len(late) - 1
        d_table = jnp.concatenate([sums_qkv[:1]] + [sums[i : i + 1] for i in order], 0)
        d_lines = jnp.concatenate(
            [
                d_table.reshape(small, count, step).transpose(1, 0, 2).reshape(count, -1),
                sums_bin[:wide].reshape(count, wide * step),
            ],
            1,
        )
        d_lines = jnp.pad(d_lines, ((0, 0), (0, width - d_lines.shape[1])))[:, None].astype(BF)
        d_lines = jnp.pad(d_lines, ((0, 0), (0, 7), (0, 0)))
        place = core[0]
        pick = Reduce(plan, [])
        if step % 8:
            q_send, q_keep, kv_send, kv_keep = [
                v.reshape(count // 2, step, -1) for v in (q_send, q_keep, kv_send, kv_keep)
            ]
        q_send = jnp.concatenate([q_send, pick.cut(d_lines, core_bit, 1 - place)], 1)
        q_keep = jnp.concatenate([q_keep, pick.cut(d_lines, core_bit, place)], 1)
        r_q = Reduce(plan, [q_keep, plan.swap(q_send, core_bit)], left)
        r_kv = Reduce(plan, [kv_keep, plan.swap(kv_send, core_bit)], left)
        for one, two in zip(plan.x + plan.y + plan.z[::-1], plan.y + plan.x + plan.z[::-1]):
            n = len(r_q.terms)
            held = [*r_q.terms, *r_kv.terms]
            if one == plan.x[0]:
                *held, shared_n, returned.same = tie(*held, shared_n, returned.same)
                returned.near(shared_n)
                returned.prompt_three()
            elif one == plan.y[0]:
                *held, grads, returned.own = tie(*held, grads, returned.own)
                grads = level(grads, "z")
            elif one == plan.z[-1]:
                held = tie(*held)
            else:
                *held, returned.back = tie(*held, returned.back)
            r_q.terms, r_kv.terms = held[:n], held[n:]
            r_q.stage(one)
            r_kv.stage(two)
        o_ab = grads.reshape(-1, width).astype(F32)
        grad_tokens = grad_own + returned.total()
        o_query = r_q.result()
        o_line = o_query[step]
        o_both = r_kv.result().reshape(step, parts, 2, width // parts)

        o_small = [o_line[i * step : (i + 1) * step] for i in range(small)]
        o_bin = o_line[small * step : (small + wide) * step]
        return (
            layer_out[None],
            grad_tokens.astype(BF)[None],
            o_query[:step],
            o_both[:, :, 0].reshape(step, width),
            o_both[:, :, 1].reshape(step, width),
            o_ab[wide * step : (wide + 1) * step],
            jnp.concatenate([o_ab[i * step : (i + 1) * step] for i in range(wide + 1, 2 * wide + 1)], 1),
            o_ab[: wide * step],
            o_small[0],
            o_small[1],
            o_small[2],
            o_small[3],
            o_small[4],
            o_bin,
            o_small[5],
            o_small[6],
            o_small[7],
        )

    split = P(GRP, ROW, None)
    owned2, owned1 = P(AXES, None), P(AXES)
    in_specs = (split, P(GRP, None), split) + (owned2,) * 6 + (owned1,) * 9
    out_specs = (split, split) + (owned2,) * 6 + (owned1,) * 9
    return jax.shard_map(
        per_device, mesh=fine, in_specs=in_specs, out_specs=out_specs, check_vma=False
    )
```

```python
import functools

import jax
import jax.numpy as jnp
import numpy as np
from jax import lax
from jax.experimental import pallas as pl
from jax.experimental.pallas import tpu as pltpu
from jax.sharding import Mesh
from jax.sharding import PartitionSpec as P

HEADS = 12
HDIM = 64
PROMPT = 1024
CONT_MOST = 256
BF = jnp.bfloat16
F32 = jnp.float32

NORM_EPS = 1e-12
MASK_FILL = -1000000000.0
SQRT_HALF = 0.7071067811865476
INV_ROOT_TAU = 0.3989422804014327
AXES = ("x", "core", "z", "y")
GRP, ROW = AXES[:2], AXES[2:]
WIDE = 4
WO, WI = 4, 5
WQ, WK, WV = 0, 1, 2


def mm(left, right):
    return jnp.dot(left, right, preferred_element_type=F32)


def segment_ids(lengths, group_len):
    ends = jnp.cumsum(lengths)
    places = jnp.arange(group_len, dtype=jnp.int32)
    passed = jnp.sum(((places - PROMPT)[:, None] >= ends[None, :]).astype(jnp.int32), axis=-1)
    return jnp.where(places < PROMPT, 0, 1 + passed)


class Plan:
    def __init__(self, grp, row):
        self.grp, self.row, self.count = grp, row, grp * row
        y = row // 4
        bits = lambda base, size: [base << i for i in range(size.bit_length() - 1)]
        self.y, self.z = bits(1, y), bits(y, 4)
        self.core, self.x = bits(row, 2), bits(2 * row, grp // 2)
        self.bits = self.count.bit_length() - 1

    def swap(self, value, mask):
        return lax.ppermute(value, AXES, [(i, i ^ mask) for i in range(self.count)])

    def send(self, value, moves):
        pairs = [(g * self.row + a, g * self.row + b) for g in range(self.grp) for a, b in moves]
        return lax.ppermute(value, AXES, pairs)

    def me(self):
        return lax.axis_index(AXES)


class Reduce:
    def __init__(self, plan, terms, left=None):
        self.plan, self.terms = plan, list(terms)
        self.left = left or [1 << i for i in reversed(range(plan.bits))]

    def cut(self, term, bit, place):
        at = self.left.index(bit)
        high, low = 1 << at, 1 << (len(self.left) - at - 1)
        _, rows, width = term.shape
        term = term.reshape(high, 2, low * rows, width)
        return lax.dynamic_slice_in_dim(term, place, 1, 1).reshape(high * low, rows, width)

    def total(self, terms):
        return sum([t.astype(F32) for t in terms[1:]], terms[0].astype(F32))

    def stage(self, bit):
        place = (self.plan.me() // bit) & 1
        away = self.total([self.cut(t, bit, 1 - place) for t in self.terms]).astype(BF)
        here = [self.cut(t, bit, place) for t in self.terms]
        self.left = [b for b in self.left if b != bit]
        self.terms = here + [self.plan.swap(away, bit)]

    def result(self):
        return self.total(self.terms)[0]


def tie(*values):
    return lax.optimization_barrier(values)


class Tokens:
    def __init__(self, plan, own):
        self.plan, self.own = plan, own
        self.rows = own.shape[0]
        self.ready = plan.row == 8

    def stage_one(self):
        if self.ready:
            plan, own = self.plan, self.own
            across = plan.send(own, [(0, 4), (1, 5), (2, 6), (3, 7)])
            self.same = jnp.where(lax.axis_index(ROW) < 4, own, across)
            self.beside = plan.swap(own, 1)
            return [self.same, self.beside]
        return []

    def stage_two(self):
        if self.ready:
            plan = self.plan
            self.other = plan.swap(self.same, 2)
            self.same_y = plan.swap(self.same, 1)
            self.diagonal = plan.send(self.own, [(5, 6), (6, 5)])
            return [self.other, self.same_y, self.diagonal]
        return []

    def stage_three(self):
        if self.ready:
            self.other_y = self.plan.swap(self.other, 1)

    def spots(self):
        row, rows, own = lax.axis_index(ROW), self.rows, self.own
        if self.ready:
            near = jnp.where(row < 4, 0, jnp.where((row == 5) | (row == 6), 3, 2))
            return [
                self.same, self.other, self.same_y, self.other_y, own, self.beside, self.diagonal,
            ], near
        every = lax.all_gather(own, ROW, axis=0, tiled=True)
        start = jnp.maximum(row * rows - CONT_MOST, 0)
        padded = jnp.concatenate([every, jnp.zeros((CONT_MOST, own.shape[1]), own.dtype)], 0)
        near = lax.dynamic_slice_in_dim(padded, start, rows + 2 * CONT_MOST, 0)
        every = jnp.concatenate([every[:PROMPT], near], 0)
        spots = [every[i : i + rows] for i in range(0, every.shape[0], rows)]
        return spots, jnp.where(row * rows < PROMPT, 0, near.shape[0] // rows)


def near_segments(plan, segments, rows):
    row = lax.axis_index(ROW)
    if plan.row != 8:
        start = jnp.maximum(row * rows - CONT_MOST, 0)
        padded = jnp.concatenate([segments, jnp.full((CONT_MOST,), -1, jnp.int32)], 0)
        near = lax.dynamic_slice_in_dim(padded, start, rows + 2 * CONT_MOST, 0)
        return jnp.where((near == 0) | (row * rows < PROMPT), -1, near)
    pieces = []
    for block, valid in (
        (row, row >= 4),
        (row ^ 1, row >= 4),
        (11 - row, (row == 5) | (row == 6)),
    ):
        block = jnp.clip(block, 0, 7)
        ids = lax.dynamic_slice_in_dim(segments, block * rows, rows, 0)
        pieces.append(jnp.where(valid, ids, -1))
    return jnp.concatenate(pieces, 0)


class Return:
    def __init__(self, plan, rows):
        self.plan, self.rows = plan, rows

    def prompt_one(self, parts):
        self.prompt = self.same = self.own = self.back = parts
        if self.plan.row == 8:
            same, other, same_y, other_y = [parts[i].astype(F32) for i in range(4)]
            self.other = (other + self.plan.swap(parts[3], 1).astype(F32)).astype(BF)
            self.same = same + self.plan.swap(parts[2], 1).astype(F32)

    def prompt_two(self):
        if self.plan.row == 8:
            self.same = self.same + self.plan.swap(self.other, 2).astype(F32)

    def prompt_three(self):
        if self.plan.row == 8:
            self.back = self.plan.send(self.same.astype(BF), [(4, 0), (5, 1), (6, 2), (7, 3)])

    def near(self, parts):
        self.around = parts
        if self.plan.row == 8:
            own = parts[0].astype(F32) + self.plan.swap(parts[1], 1).astype(F32)
            self.own = own + self.plan.send(parts[2], [(5, 6), (6, 5)]).astype(F32)

    def total(self):
        row, rows = lax.axis_index(ROW), self.rows
        if self.plan.row == 8:
            return jnp.where(row < 4, self.same + self.back.astype(F32), self.own)
        around = self.around.reshape(-1, self.around.shape[-1]).astype(F32)
        start = jnp.maximum(row * rows - CONT_MOST, 0)
        whole = jnp.zeros((self.plan.row * rows + CONT_MOST, around.shape[1]), F32)
        whole = whole.at[:PROMPT].set(self.prompt.reshape(PROMPT, -1).astype(F32))
        near = jnp.where(row * rows < PROMPT, 0, around)
        near = lax.dynamic_slice_in_dim(whole, start, rows + 2 * CONT_MOST, 0) + near
        whole = lax.dynamic_update_slice_in_dim(whole, near, start, 0)
        return lax.psum_scatter(whole[: self.plan.row * rows], ROW, scatter_dimension=0, tiled=True)


def heads_mask(lanes, head):
    lane = lax.broadcasted_iota(jnp.int32, lanes, 1)
    return (lane >= head * HDIM) & (lane < (head + 1) * HDIM)


def nt(left, right):
    return lax.dot_general(left, right, (((1,), (1,)), ((), ())), preferred_element_type=F32)


def tn(left, right):
    return lax.dot_general(left, right, (((0,), (0,)), ((), ())), preferred_element_type=F32)


def pack_kernel(wo_ref, wi_ref, wu_ref, wq_ref, wk_ref, wv_ref, line_ref, early_ref, late_ref):
    step, width = wo_ref.shape
    early_ref[:step, :] = wq_ref[...]
    early_ref[step : step + 8, :] = line_ref[:8, :]
    early_ref[step + 8 : 2 * step + 8, :] = wk_ref[...]
    early_ref[2 * step + 8 :, :] = wv_ref[...]
    late_ref[: WIDE * step, :] = wu_ref[...]
    late_ref[WO * step : WI * step, :] = wo_ref[...]
    for i in range(WIDE):
        late_ref[(WI + i) * step : (WI + i + 1) * step, :] = wi_ref[:, i * width : (i + 1) * width]
    late_ref[(WI + WIDE) * step :, :] = line_ref[8:, :]


def pack_call(w_output, w_inner, w_outer, w_query, w_key, w_value, line):
    step, width = w_output.shape
    shape = lambda rows: jax.ShapeDtypeStruct((rows, width), BF)
    return pl.pallas_call(
        pack_kernel, out_shape=[shape(3 * step + 8), shape((WI + WIDE) * step + 8)], name="pack"
    )(w_output, w_inner, w_outer, w_query, w_key, w_value, line)


def attention_kernel(blocks, first, rows, places, *refs):
    spots = refs[:blocks]
    (near_ref, me_ref, own_ref, a0_ref, a1_ref, b0_ref, b1_ref, segq_ref, segk_ref,
     w_out, q_ref, kp_ref, vp_ref, kn_ref, vn_ref, ctx_ref, lse_ref,
     x_ref, w_ref, s_ref, vt_ref, out_ref, line_ref, bias_ref, sems, w_sems, o_sem) = refs[blocks:]
    near = near_ref[0]
    depth = own_ref.shape[1]
    owners = w_ref.shape[0]
    each = depth // owners
    part = q_ref.shape[1]

    def weights(act):
        @pl.loop(0, owners)
        def _(e):
            away = e ^ me_ref[0]
            for (bits, half), (zero, one), parts in (
                (places[0], (a0_ref, a1_ref), ((0, each, w_ref, 0), (each, 8, line_ref, 0))),
                (places[1], (b0_ref, b1_ref), ((0, 2 * each, w_ref, each),)),
            ):
                j = sum([((away // bit) & 1) * weight for bit, weight in bits])
                for which, source in enumerate((zero, one)):

                    @pl.when(((away // half) & 1) == which)
                    def _():
                        for k, (top, size, target, base) in enumerate(parts):
                            act(pltpu.make_async_copy(
                                source.at[j, pl.ds(top, size)], target.at[e, pl.ds(base, size)],
                                w_sems.at[2 * k if zero is a0_ref else 1, e],
                            ))

    @pl.when(pl.program_id(0) == 0)
    def _():
        copies = [
            pltpu.make_async_copy(spot, x_ref.at[pl.ds(i * rows, rows)], sems.at[i])
            for i, spot in enumerate(spots)
        ]
        weights(lambda c: c.start())
        for copy in copies:
            copy.start()
        weights(lambda c: c.wait())
        for copy in copies:
            copy.wait()
        pltpu.make_async_copy(w_ref, w_out, o_sem).start()
        line = line_ref[:, 0, :128]
        place = lax.broadcasted_iota(jnp.int32, (128, depth), 0)
        lane = lax.broadcasted_iota(jnp.int32, (128, depth), 1)
        mine = lax.broadcasted_iota(jnp.int32, (owners, depth), 0)
        mine = mine == lax.broadcasted_iota(jnp.int32, (owners, depth), 1) // each
        for i in range(2):
            spread = mm(line, jnp.where(place == lane % each + i * each, 1.0, 0.0).astype(BF))
            bias_ref[i : i + 1, :] = jnp.sum(jnp.where(mine, spread, 0.0), axis=0, keepdims=True)

    lanes = pl.ds(pl.multiple_of(pl.program_id(0) * part, part), part)
    wq, wk, wv = [
        w_ref[:, i * each : (i + 1) * each, lanes].reshape(depth, part) for i in (WQ, WK, WV)
    ]
    queries = (mm(own_ref[...], wq) + bias_ref[0:1, lanes]) * (HDIM**-0.5)
    q_ref[...] = queries.astype(BF)

    heads = part // HDIM
    q = q_ref[...]
    tall = x_ref.shape[0]

    def body(sets):
        for k_ref, v_ref, base, size, _ in sets:
            x = x_ref[base : base + size, :]
            k_ref[...] = mm(x, wk).astype(BF)
            v = (mm(x, wv) + bias_ref[1:2, lanes]).astype(BF)
            v_ref[...] = v
            vt_ref[:, base : base + size] = v.T
        for h in range(heads):
            q_h = jnp.where(heads_mask(q.shape, h), q, 0)
            peak = jnp.full((1, rows), MASK_FILL, F32)
            for k_ref, _, base, size, masked in sets:
                s = nt(k_ref[...], q_h)
                if masked:
                    s = jnp.where(segk_ref[...] == segq_ref[...], s, MASK_FILL)
                s_ref[h % 2, base : base + size, :] = s
                peak = jnp.maximum(peak, jnp.max(s, axis=0, keepdims=True))
            total, mixed = jnp.zeros((1, rows), F32), jnp.zeros((HDIM, rows), F32)
            for _, _, base, size, _ in sets:
                p = jnp.exp(s_ref[h % 2, base : base + size, :] - peak)
                total = total + jnp.sum(p, axis=0, keepdims=True)
                mixed = mixed + mm(vt_ref[h * HDIM : (h + 1) * HDIM, base : base + size], p.astype(BF))
            out_ref[h * HDIM : (h + 1) * HDIM, :] = mixed / total
            lse_ref[0, h : h + 1, :] = peak + jnp.log(total)

    prompt = (kp_ref, vp_ref, 0, PROMPT, False)

    @pl.when(near == 0)
    def _():
        body([prompt])

    @pl.when(near > 0)
    def _():
        body([prompt, (kn_ref, vn_ref, PROMPT, tall - PROMPT, True)])

    ctx_ref[...] = out_ref[...].T.astype(BF)

    @pl.when(pl.program_id(0) == pl.num_programs(0) - 1)
    def _():
        pltpu.make_async_copy(w_ref, w_out, o_sem).wait()


def attention_call(spots, first, near, me, own, pieces, places, segq, segk):
    rows, width = own.shape
    blocks = len(spots)
    tall = blocks * rows
    part = 256
    steps = width // part
    heads = part // HDIM
    cols = lambda depth: pl.BlockSpec((depth, part), lambda g: (0, g))
    flops = 2 * tall * width * width * 2 + 4 * tall * rows * width * 4
    owners = 2 * pieces[0].shape[0]
    each = width // owners
    return pl.pallas_call(
        functools.partial(attention_kernel, blocks, first, rows, places),
        grid=(steps,),
        in_specs=[pl.BlockSpec(memory_space=pl.ANY)] * blocks
        + [
            pl.BlockSpec(memory_space=pltpu.SMEM),
            pl.BlockSpec(memory_space=pltpu.SMEM),
            pl.BlockSpec((rows, width), lambda g: (0, 0)),
        ] + [pl.BlockSpec(memory_space=pl.ANY)] * 4 + [
            pl.BlockSpec((1, rows), lambda g: (0, 0)),
            pl.BlockSpec(segk.shape, lambda g: (0, 0)),
        ],
        out_specs=[
            pl.BlockSpec(memory_space=pl.ANY),
            cols(rows), cols(PROMPT), cols(PROMPT), cols(tall - PROMPT), cols(tall - PROMPT),
            cols(rows), pl.BlockSpec((1, 8, rows), lambda g: (g, 0, 0)),
        ],
        out_shape=[
            jax.ShapeDtypeStruct((owners, 3 * each, width), BF),
            jax.ShapeDtypeStruct((rows, width), BF),
            jax.ShapeDtypeStruct((PROMPT, width), BF),
            jax.ShapeDtypeStruct((PROMPT, width), BF),
            jax.ShapeDtypeStruct((tall - PROMPT, width), BF),
            jax.ShapeDtypeStruct((tall - PROMPT, width), BF),
            jax.ShapeDtypeStruct((rows, width), BF),
            jax.ShapeDtypeStruct((steps, 8, rows), F32),
        ],
        scratch_shapes=[
            pltpu.VMEM((tall, width), BF),
            pltpu.VMEM((owners, 3 * each, width), BF),
            pltpu.VMEM((2, tall, rows), F32),
            pltpu.VMEM((part, tall), BF),
            pltpu.VMEM((part, rows), F32),
            pltpu.VMEM((owners, 8, width), BF),
            pltpu.VMEM((8, width), F32),
            pltpu.SemaphoreType.DMA((blocks,)),
            pltpu.SemaphoreType.DMA((3, owners)),
            pltpu.SemaphoreType.DMA,
        ],
        compiler_params=pltpu.CompilerParams(vmem_limit_bytes=60 * 2**20),
        cost_estimate=pl.CostEstimate(
            flops=flops, bytes_accessed=12 * 2**20, transcendentals=tall * rows * 12
        ),
        name="attention",
    )(*spots, near, me, own, *pieces, segq, segk)


def halves(value, runs, core):
    depth = value.shape[0] // runs
    pick = lambda first: jnp.concatenate(
        [value[i * depth : (i + 1) * depth] for i in range(first, runs, 2)], 0
    )
    even, odd = pick(0), pick(1)
    return jnp.where(core == 0, odd, even), jnp.where(core == 0, even, odd)


def middle_kernel(wide, mapped, ctx_ref, own_ref, cot_ref, got_ref, vec_ref, bin_ref,
                  out_ref, h1_ref, gctx_ref, grads, sums_ref, sbin_ref,
                  first_ref, n1_ref, inv_ref, low_ref, pre_ref, cdf_ref, act_ref, acc_ref,
                  gffn_ref, glow_ref, lowt_ref, w_ref, out_buf, in_buf, wo_buf, sems, w_sems):
    step = pl.program_id(0)
    width = ctx_ref.shape[1]
    vec = lambda i: vec_ref[i : i + 1, :]
    mean = lambda v: jnp.sum(v, axis=-1, keepdims=True) * (1.0 / width)
    down = lambda v: jnp.sum(v, axis=0, keepdims=True)
    owners = got_ref.shape[0]
    each = width // owners
    some = owners // wide
    square = lambda value: value.reshape(width, width)
    rows_of = lambda place: pl.ds(pl.multiple_of(place * each, each), each)
    w_output = lambda ref: ref.at[:, rows_of(WO)]
    w_inner = lambda ref, at: ref.at[:, rows_of(WI + at)]
    w_outer = lambda ref, at: ref.at[pl.ds(at * some, some), pl.ds(0, wide * each)]

    def fetch_inner(at):
        return pltpu.make_async_copy(w_inner(got_ref, at), w_inner(w_ref, at), w_sems.at[0, at])

    def fetch_outer(at):
        return pltpu.make_async_copy(w_outer(got_ref, at), w_outer(w_ref, at), w_sems.at[1, at])

    def fetch_output():
        return pltpu.make_async_copy(w_output(got_ref), w_output(w_ref), w_sems.at[0, wide])

    def slot(group, i):
        return group % 2 * 16 + group // 2 * 8 + i % 2 * 4 + i // 2 if mapped else group * 8 + i

    def outer(at):
        turn = (2 * wide - 1 - at) % 2
        return [
            pltpu.make_async_copy(
                out_buf.at[turn, i], grads.at[slot(at, i), pl.ds(0, wide * each)], sems.at[turn, i]
            )
            for i in range(some)
        ]

    def inner(at):
        turn = (2 * wide - 1 - at) % 2
        top = pl.multiple_of((wide + 1 + at) * each, each)
        return [
            pltpu.make_async_copy(
                in_buf.at[turn, e], grads.at[slot(e // 8, e % 8), pl.ds(top, each)], sems.at[2 + turn, e]
            )
            for e in range(owners)
        ]

    def output():
        return [
            pltpu.make_async_copy(
                wo_buf.at[e], grads.at[slot(e // 8, e % 8), pl.ds(wide * each, each)], sems.at[4, e]
            )
            for e in range(owners)
        ]

    def start(copies):
        for copy in copies:
            copy.start()

    def wait(copies):
        for copy in copies:
            copy.wait()

    @pl.when(step == 0)
    def _():
        fetch_output().start()
        for at in range(wide):
            fetch_inner(at).start()
            fetch_outer(at).start()
        fetch_output().wait()
        hidden = own_ref[...].astype(F32) + mm(ctx_ref[...], square(w_output(w_ref)[...])) + vec(0)
        centred = hidden - mean(hidden)
        inverse = lax.rsqrt(mean(centred * centred) + NORM_EPS)
        normed = centred * inverse
        n1_ref[...] = normed
        inv_ref[...] = inverse
        first = normed * vec(1) + vec(2)
        first_ref[...] = first
        low_ref[...] = first.astype(BF)
        lowt_ref[...] = first.astype(BF).T

    @pl.when(step < wide)
    def _():
        chunk = pl.ds(pl.multiple_of(step * width, width), width)
        fetch_inner(step).wait()
        fetch_outer(step).wait()
        pre = mm(low_ref[...], square(w_inner(w_ref, step)[...])) + bin_ref[pl.ds(step, 1), :]
        cdf = 0.5 * (1.0 + lax.erf(pre * SQRT_HALF))
        act = (pre * cdf).astype(BF)
        pre_ref[:, chunk] = pre
        cdf_ref[:, chunk] = cdf
        act_ref[:, chunk] = act
        more = mm(act, square(w_outer(w_ref, step)[...]))

        @pl.when(step == 0)
        def _():
            acc_ref[...] = more

        @pl.when(step > 0)
        def _():
            acc_ref[...] += more

    @pl.when(step == wide - 1)
    def _():
        hidden = first_ref[...] + acc_ref[...] + vec(3)
        centred = hidden - mean(hidden)
        inverse = lax.rsqrt(mean(centred * centred) + NORM_EPS)
        normed = centred * inverse
        out_ref[...] = (normed * vec(4) + vec(5)).astype(BF)
        grad = cot_ref[...].astype(F32)
        sums_ref[0:1, :] = down(grad * normed)
        sums_ref[1:2, :] = down(grad)
        e = grad * vec(4)
        back = inverse * (e - mean(e) - normed * mean(e * normed))
        gffn_ref[...] = back
        low = back.astype(BF)
        glow_ref[...] = low
        sums_ref[2:3, :] = down(low.astype(F32))

    @pl.when(step >= wide)
    def _():
        at = 2 * wide - 1 - step
        chunk = pl.ds(pl.multiple_of(at * width, width), width)
        pre = pre_ref[:, chunk]
        slope = cdf_ref[:, chunk] + pre * jnp.exp(-0.5 * pre * pre) * INV_ROOT_TAU
        low = glow_ref[...]
        grad = (nt(low, square(w_outer(w_ref, at)[...])) * slope).astype(BF)
        sbin_ref[pl.ds(at, 1), :] = down(grad.astype(F32))
        turn = step % 2

        @pl.when(step >= wide + 2)
        def _():
            wait(outer(at + 2) + inner(at + 2))

        out_buf[turn] = tn(act_ref[:, chunk], low).astype(BF).reshape(some, wide * each, width)
        start(outer(at))
        in_buf[turn] = mm(lowt_ref[...], grad).astype(BF).reshape(owners, each, width)
        start(inner(at))
        gffn_ref[...] += nt(grad, square(w_inner(w_ref, at)[...]))

    @pl.when(step == 2 * wide - 1)
    def _():
        grad = gffn_ref[...]
        normed = n1_ref[...]
        sums_ref[3:4, :] = down(grad * normed)
        sums_ref[4:5, :] = down(grad)
        e = grad * vec(1)
        back = inv_ref[...] * (e - mean(e) - normed * mean(e * normed))
        h1_ref[...] = back
        low = back.astype(BF)
        sums_ref[5:6, :] = down(low.astype(F32))
        wo_buf[...] = tn(ctx_ref[...], low).astype(BF).reshape(owners, each, width)
        start(output())
        gctx = nt(low, square(w_output(w_ref)[...])).astype(BF)
        gctx_ref[...] = gctx
        sums_ref[6:7, :] = down(gctx.astype(F32))
        sums_ref[7:8, :] = jnp.zeros((1, width), F32)
        wait(outer(1) + inner(1) + outer(0) + inner(0) + output())


def middle_call(ctx, own, cot, got, vec, b_inner, mapped):
    rows, width = own.shape
    owners = got.shape[0]
    each = width // owners
    wide = WIDE
    whole = lambda shape: pl.BlockSpec(shape, lambda s: (0,) * len(shape))
    shape = jax.ShapeDtypeStruct
    return pl.pallas_call(
        functools.partial(middle_kernel, wide, mapped),
        grid=(2 * wide,),
        in_specs=[
            whole((rows, width)), whole((rows, width)), whole((rows, width)),
            pl.BlockSpec(memory_space=pl.ANY),
            whole((8, width)), whole((8, width)),
        ],
        out_specs=[
            whole((rows, width)), whole((rows, width)), whole((rows, width)),
            pl.BlockSpec(memory_space=pl.ANY),
            whole((8, width)), whole((8, width)),
        ],
        out_shape=[
            shape((rows, width), BF), shape((rows, width), F32), shape((rows, width), BF),
            shape((owners, (2 * wide + 1) * each, width), BF),
            shape((8, width), F32), shape((8, width), F32),
        ],
        scratch_shapes=[
            pltpu.VMEM((rows, width), F32), pltpu.VMEM((rows, width), F32), pltpu.VMEM((rows, 1), F32),
            pltpu.VMEM((rows, width), BF), pltpu.VMEM((rows, wide * width), F32),
            pltpu.VMEM((rows, wide * width), F32), pltpu.VMEM((rows, wide * width), BF),
            pltpu.VMEM((rows, width), F32), pltpu.VMEM((rows, width), F32),
            pltpu.VMEM((rows, width), BF), pltpu.VMEM((width, rows), BF),
            pltpu.VMEM((owners, (2 * wide + 1) * each, width), BF),
            pltpu.VMEM((2, owners // wide, wide * each, width), BF),
            pltpu.VMEM((2, owners, each, width), BF),
            pltpu.VMEM((owners, each, width), BF), pltpu.SemaphoreType.DMA((5, owners)),
            pltpu.SemaphoreType.DMA((2, wide + 1)),
        ],
        compiler_params=pltpu.CompilerParams(vmem_limit_bytes=60 * 2**20),
        cost_estimate=pl.CostEstimate(
            flops=2 * rows * width * width * (6 * wide + 3), bytes_accessed=32 * 2**20,
            transcendentals=2 * rows * width * wide,
        ),
        name="middle",
    )(ctx, own, cot, got, vec, b_inner)


def back_kernel(rows, bound, started, *refs):
    near_ref, gctx_ref, ctx_ref, q_ref, k_ref, v_ref, lse_ref, segq_ref, segk_ref = refs[:9]
    dk_ref, dv_ref, dq_ref, kt_ref, p_ref, ds_ref = refs[-6:]
    q, g = q_ref[...], gctx_ref[...]
    part = q.shape[1]
    heads = part // HDIM
    masks = [heads_mask(q.shape, h) for h in range(heads)]
    q_parts = [jnp.where(m, q, 0) for m in masks]
    g_parts = [jnp.where(m, g, 0) for m in masks]
    product = (g.astype(F32) * ctx_ref[...].astype(F32)).T
    inner = [
        jnp.sum(product[h * HDIM : (h + 1) * HDIM], axis=0, keepdims=True) for h in range(heads)
    ]

    def body():
        k, v = k_ref[...], v_ref[...]
        kt_ref[...] = k.T
        for h in range(heads):
            s = nt(k, q_parts[h])
            if bound is None:
                s = jnp.where(segk_ref[...] == segq_ref[...], s, MASK_FILL)
            p = jnp.exp(s - lse_ref[0, h : h + 1, :])
            across = slice(h * rows, (h + 1) * rows)
            ds = (p * (nt(v, g_parts[h]) - inner[h])).astype(BF)
            p_ref[:, across] = p.astype(BF)
            ds_ref[:, across] = ds
            mine = slice(h * HDIM, (h + 1) * HDIM)
            more = mm(kt_ref[mine, :], ds)
            dq_ref[mine, :] = refs[9][mine, :] + more if started else more
        dk_ref[...] = mm(ds_ref[...], jnp.concatenate(q_parts, 0)).astype(BF)
        dv_ref[...] = mm(p_ref[...], jnp.concatenate(g_parts, 0)).astype(BF)

    if bound is None:

        @pl.when(near_ref[0] == 0)
        def _():
            dq_ref[...] = refs[9][...]

        pl.when(near_ref[0] > 0)(body)
    else:
        body()


def back_call(start, steps, bound, near, gctx, ctx, q, k, v, lse, segq, segk, dq0=None, into=None):
    rows, width = q.shape
    tall = k.shape[0]
    part = 256
    cols = lambda depth: pl.BlockSpec((depth, part), lambda g: (0, start + g))
    whole = lambda shape: pl.BlockSpec(shape, lambda g: (0,) * len(shape))
    down = pl.BlockSpec((part, rows), lambda g: (start + g, 0))
    shape = jax.ShapeDtypeStruct
    extra = ([dq0] if dq0 is not None else []) + list(into or [])
    specs = ([down] if dq0 is not None else []) + [pl.BlockSpec(memory_space=pl.ANY)] * len(into or [])
    return pl.pallas_call(
        functools.partial(back_kernel, rows, bound, dq0 is not None),
        grid=(steps,),
        in_specs=[
            pl.BlockSpec(memory_space=pltpu.SMEM),
            cols(rows), cols(rows), cols(rows), cols(tall), cols(tall),
            pl.BlockSpec((1, 8, rows), lambda g: (start + g, 0, 0)),
            whole((1, rows)), whole(segk.shape),
        ] + specs,
        out_specs=[cols(tall), cols(tall), down],
        out_shape=[shape((tall, width), BF), shape((tall, width), BF), shape((width, rows), F32)],
        input_output_aliases={9 + i: i for i in range(3)} if into else {},
        scratch_shapes=[
            pltpu.VMEM((part, tall), BF),
            pltpu.VMEM((tall, part // HDIM * rows), BF),
            pltpu.VMEM((tall, part // HDIM * rows), BF),
        ],
        compiler_params=pltpu.CompilerParams(vmem_limit_bytes=60 * 2**20),
        cost_estimate=pl.CostEstimate(
            flops=2 * 10 * 2 * tall * rows * part * steps * 2,
            bytes_accessed=8 * tall * part * steps, transcendentals=tall * rows * 4 * steps,
        ),
        name="attention_back",
    )(near, gctx, ctx, q, k, v, lse, segq, segk, *extra)


def product_kernel(rows, bound, near_ref, dk_ref, dv_ref, wk_ref, wv_ref, gx_ref):
    @pl.when((pl.program_id(0) < near_ref[0]) | (bound is not None))
    def _():
        width = dk_ref.shape[1]
        wk, wv = wk_ref[...].reshape(width, width), wv_ref[...].reshape(width, width)
        gx_ref[0] = (nt(dk_ref[...], wk) + nt(dv_ref[...], wv)).astype(BF)


def product_call(bound, near, dk, dv, got, rows):
    tall, width = dk.shape
    owners, each = got.shape[0], width // got.shape[0]
    weight = lambda place: pl.BlockSpec((owners, each, width), lambda b: (0, place, 0))
    return pl.pallas_call(
        functools.partial(product_kernel, rows, bound),
        grid=(tall // rows,),
        in_specs=[
            pl.BlockSpec(memory_space=pltpu.SMEM),
            pl.BlockSpec((rows, width), lambda b: (b, 0)),
            pl.BlockSpec((rows, width), lambda b: (b, 0)),
            weight(WK), weight(WV),
        ],
        out_specs=pl.BlockSpec((1, rows, width), lambda b: (b, 0, 0)),
        out_shape=jax.ShapeDtypeStruct((tall // rows, rows, width), BF),
        compiler_params=pltpu.CompilerParams(vmem_limit_bytes=60 * 2**20),
        cost_estimate=pl.CostEstimate(
            flops=4 * tall * width * width, bytes_accessed=6 * tall * width, transcendentals=0
        ),
        name="token_product",
    )(near, dk, dv, got, got)


def weight_kernel(blocks, first, rows, runs, *refs):
    spots = refs[:blocks]
    (near_ref, core_ref, own_ref, dq_ref, wq_ref, h1_ref, dkp_ref, dvp_ref, dkn_ref, dvn_ref,
     send_ref, keep_ref, gown_ref, sums_ref, x_ref, xt_ref, sems) = refs[blocks:]
    core = core_ref[0]
    step = pl.program_id(0)

    @pl.when(step == 0)
    def _():
        copies = [
            pltpu.make_async_copy(spot, x_ref.at[pl.ds(i * rows, rows)], sems.at[i])
            for i, spot in enumerate(spots)
        ]
        for copy in copies:
            copy.start()
        gown_ref[...] = h1_ref[...]
        for i, copy in enumerate(copies):
            copy.wait()
            xt_ref[:, i * rows : (i + 1) * rows] = x_ref[i * rows : (i + 1) * rows, :].T

    scale = HDIM**-0.5
    dq = dq_ref[...].T.astype(BF)
    part = dq.shape[1]
    width = x_ref.shape[1]
    gown_ref[...] += nt(dq, wq_ref[...].reshape(width, part)) * scale
    half = send_ref.shape[0]
    each = width // (2 * half)

    def put(i, grad):
        away, here = halves(grad.astype(BF), runs, core)
        send_ref[:, i * each : (i + 1) * each, :] = away.reshape(half, each, part)
        keep_ref[:, i * each : (i + 1) * each, :] = here.reshape(half, each, part)

    put(WQ, tn(own_ref[...], dq) * scale)
    sums_ref[0:1, :] = jnp.sum(dq.astype(F32), axis=0, keepdims=True) * scale

    def body(near):
        for i, p_ref, n_ref in ((WK, dkp_ref, dkn_ref), (WV, dvp_ref, dvn_ref)):
            grad = mm(xt_ref[:, :PROMPT], p_ref[...])
            if near:
                grad = grad + mm(xt_ref[:, PROMPT:], n_ref[...])
            put(i, grad)

    pl.when(near_ref[0] == 0)(lambda: body(False))
    pl.when(near_ref[0] > 0)(lambda: body(True))
    sums_ref[1:8, :] = jnp.zeros((7, part), F32)


def weight_call(spots, first, near, own, dq, got, h1, dkp, dvp, dkn, dvn, core, runs):
    rows, width = own.shape
    blocks = len(spots)
    tall = blocks * rows
    part = 256
    steps = width // part
    cols = lambda depth, size=part: pl.BlockSpec((depth, size), lambda g: (0, g))
    whole = lambda shape: pl.BlockSpec(shape, lambda g: (0,) * len(shape))
    shape = jax.ShapeDtypeStruct
    owners, each = got.shape[0], width // got.shape[0]
    half = owners // 2
    slab = pl.BlockSpec((half, 3 * each, part), lambda g: (0, 0, g))
    return pl.pallas_call(
        functools.partial(weight_kernel, blocks, first, rows, runs),
        grid=(steps,),
        in_specs=[pl.BlockSpec(memory_space=pl.ANY)] * blocks
        + [
            pl.BlockSpec(memory_space=pltpu.SMEM),
            pl.BlockSpec(memory_space=pltpu.SMEM),
            whole((rows, width)), pl.BlockSpec((part, rows), lambda g: (g, 0)),
            pl.BlockSpec((owners, each, part), lambda g: (0, WQ, g)),
            whole((rows, width)), cols(PROMPT), cols(PROMPT), cols(tall - PROMPT), cols(tall - PROMPT),
        ],
        out_specs=[
            slab, slab, whole((rows, width)), cols(8),
        ],
        out_shape=[
            shape((half, 3 * each, width), BF), shape((half, 3 * each, width), BF),
            shape((rows, width), F32), shape((8, width), F32),
        ],
        scratch_shapes=[
            pltpu.VMEM((tall, width), BF), pltpu.VMEM((width, tall), BF), pltpu.SemaphoreType.DMA((blocks,)),
        ],
        compiler_params=pltpu.CompilerParams(vmem_limit_bytes=60 * 2**20),
        cost_estimate=pl.CostEstimate(
            flops=4 * tall * width * width, bytes_accessed=12 * tall * width, transcendentals=0
        ),
        name="weight_product",
    )(*spots, near, core, own, dq, got, h1, dkp, dvp, dkn, dvn)


def real_owners(grads, count, step, width):
    split = count // 32
    take = lambda v: v.reshape(32, -1, split, step, width).transpose(0, 2, 1, 3, 4).reshape(count, -1, width)
    outer, rest = grads[:, : 4 * split * step], grads[:, 4 * split * step :]
    return jnp.concatenate([outer.reshape(count, 4 * step, width), take(rest)], 1)


def solution(mesh):
    plan = Plan(mesh.shape["grp"], mesh.shape["row"])
    fine = Mesh(mesh.devices.reshape(plan.grp // 2, 2, 4, plan.row // 4), AXES)

    def per_device(
        tokens, cont_lengths, cotangent, w_query, w_key, w_value, w_output, w_inner, w_outer,
        bias_query, bias_value, bias_output, gain_first, shift_first, bias_inner, bias_outer,
        gain_second, shift_second,
    ):
        count = plan.count
        _, rows, width = tokens.shape
        step = w_query.shape[0]
        wide = w_inner.shape[1] // width
        own = tokens[0]

        early = (bias_query, bias_value)
        late = (bias_output, gain_first, shift_first, bias_outer, gain_second, shift_second, bias_inner)
        small = len(late) - 1

        def in_line(vectors):
            line, place = 0, 0
            for vector in vectors:
                size = vector.shape[0]
                line = line + jnp.pad(vector, (place, width - place - size))
                place += size
            return jnp.pad(line[None], ((0, 7), (0, 0)))

        line = jnp.concatenate([in_line(early), in_line(late)], 0)
        runs = plan.grp
        row = lax.axis_index(ROW)
        core = lax.axis_index("core").astype(jnp.int32).reshape(1)
        exchange = Tokens(plan, own)
        squares = (w_query, w_key, w_value)
        if step % 8 == 0:
            first_pack, pack = pack_call(w_output, w_inner, w_outer, *squares, line)
            got = lax.all_gather(pack, AXES, axis=0, tiled=True).reshape(count, -1, width)
            lines = got[:, (WI + WIDE) * step]

            def swaps(value, bits):
                masks = [0]
                for bit in bits:
                    masks = masks + [m ^ bit for m in masks]
                return [plan.swap(value, m) for m in masks[1:]]

            def stage(held, bit):
                return jnp.concatenate([held, plan.swap(held, bit)], 0)

            away = swaps(first_pack, plan.z)
            *away, same, beside = tie(*away, *exchange.stage_one())
            exchange.same, exchange.beside = same, beside
            cut = step + 8
            one = jnp.stack([v[:cut] for v in (first_pack, *away)])
            two = jnp.stack([v[cut:] for v in (first_pack, *away)])
            one, two = stage(one, plan.x[0]), stage(two, plan.y[0])
            one, two, *seen = tie(one, two, *exchange.stage_two())
            exchange.other, exchange.same_y, exchange.diagonal = seen
            one, two = stage(one, plan.y[0]), stage(two, plan.x[0])
            exchange.stage_three()
            one, two, exchange.other_y = tie(one, two, exchange.other_y)
            pieces = [one, plan.swap(one, plan.core[0]), two, plan.swap(two, plan.core[0])]
            order = lambda *bits: ([(bit, 1 << i) for i, bit in enumerate(bits)], plan.core[0])
            places = (
                order(*plan.z, plan.x[0], plan.y[0]),
                order(*plan.z, plan.y[0], plan.x[0]),
            )
            me = plan.me().astype(jnp.int32).reshape(1)
        else:
            inner_rows = [w_inner[:, i * width : (i + 1) * width] for i in range(wide)]
            pack = jnp.concatenate([w_outer, w_output, *inner_rows, *squares, line], 0)
            got = lax.all_gather(pack, AXES, axis=0, tiled=True).reshape(count, -1, width)
            lines = got[:, 12 * step + 8]
            cuts = [wide * step, (wide + 1) * step, (2 * wide + 1) * step, 12 * step]
            outer, output, inner, rest, marks = jnp.split(got, cuts, axis=1)
            apart = lambda v, n: v.reshape(count, n, step, width).transpose(1, 0, 2, 3)
            inner, rest = [
                v.reshape(v.shape[0], 32, width // 32, width).transpose(1, 0, 2, 3)
                for v in (apart(inner, wide), apart(rest, 3))
            ]
            got = jnp.concatenate([v.reshape(32, -1, width) for v in (outer, output, inner)], 1)
            pairs = marks[:, 0, : 2 * step].reshape(32, count // 32, 2, step).transpose(0, 2, 1, 3)
            pairs = jnp.pad(pairs.reshape(32, 1, -1), ((0, 0), (0, 7), (0, width - 2 * width // 32)))
            one = jnp.concatenate([rest[:, 0], pairs], 1)
            two = rest[:, 1:].reshape(32, -1, width)
            pieces = [one[:16], one[16:], two[:16], two[16:]]
            places = (([(1, 1), (2, 2), (4, 4), (8, 8)], 16),) * 2
            me = jnp.zeros((1,), jnp.int32)
        spots, near = exchange.spots()
        first_near = PROMPT // rows

        table = lines[:, : small * step].reshape(count, small, step).transpose(1, 0, 2)
        table = table.reshape(small, width).astype(F32)
        v_bin = lines[:, small * step : (small + wide) * step].reshape(wide, width).astype(F32)
        v_bin = jnp.pad(v_bin, ((0, 8 - wide), (0, 0)))
        segments = segment_ids(cont_lengths[0], plan.row * rows)
        seg_own = lax.dynamic_slice_in_dim(segments, row * rows, rows, 0)[None, :]
        seg_near = near_segments(plan, segments, rows)[:, None]
        near = near.astype(jnp.int32).reshape(1)

        squares, queries, keys_p, values_p, keys_n, values_n, context, log_total = attention_call(
            spots, first_near, near, me, own, pieces, places, seg_own, seg_near
        )
        vec = jnp.concatenate([table, jnp.zeros((2, width), F32)], 0)
        layer_out, grad_h1, grad_context, grads, sums, sums_bin = middle_call(
            context, own, cotangent[0], got, vec, v_bin, step % 8 == 0
        )
        if step % 8:
            grads = real_owners(grads, count, step, width)
            grads = grads.reshape(plan.grp // 2, 2, 4, plan.row // 4, -1, width)
            grads = grads.transpose(1, 0, 3, 2, 4, 5).reshape(count, -1, width)
        level = lambda value, axes: lax.psum_scatter(value, axes, scatter_dimension=0, tiled=True)
        grads = level(grads, "core")
        core_bit = plan.core[0]
        left = [1 << i for i in reversed(range(plan.bits)) if 1 << i != core_bit]
        parts = width // 256
        dkp, dvp, dqp = back_call(
            0, parts, first_near, near, grad_context, context, queries, keys_p, values_p, log_total,
            seg_own, seg_near,
        )
        shared_p = product_call(first_near, near, dkp, dvp, squares, rows)
        grads, shared_p, dqp = tie(grads, shared_p, dqp)
        grads = level(grads, ("x", "y"))
        returned = Return(plan, rows)
        returned.prompt_one(shared_p)
        dkn, dvn, dq = back_call(
            0, parts, None, near, grad_context, context, queries, keys_n, values_n, log_total,
            seg_own, seg_near, dqp,
        )
        send, keep, grad_own, sums_qkv = weight_call(
            spots, first_near, near, own, dq, squares, grad_h1, dkp, dvp, dkn, dvn, core, runs
        )
        send, keep, returned.same, dkn, dvn = tie(send, keep, returned.same, dkn, dvn)
        returned.prompt_two()
        shared_n = product_call(None, near, dkn, dvn, squares, rows)

        order = (6, 5, 3, 4, 2, 0, 1)
        small = len(early) + len(late) - 1
        d_table = jnp.concatenate([sums_qkv[:1]] + [sums[i : i + 1] for i in order], 0)
        d_lines = jnp.concatenate(
            [
                d_table.reshape(small, count, step).transpose(1, 0, 2).reshape(count, -1),
                sums_bin[:wide].reshape(count, wide * step),
            ],
            1,
        )
        d_lines = jnp.pad(d_lines, ((0, 0), (0, width - d_lines.shape[1])))[:, None].astype(BF)
        d_lines = jnp.pad(d_lines, ((0, 0), (0, 7), (0, 0)))
        place = core[0]
        pick = Reduce(plan, [])
        if step % 8:
            real = lambda v: v.reshape(16, 3, count // 32, step, width).transpose(0, 2, 1, 3, 4)
            send, keep = [real(v).reshape(count // 2, 3 * step, width) for v in (send, keep)]
        send = jnp.concatenate([send, pick.cut(d_lines, core_bit, 1 - place)], 1)
        keep = jnp.concatenate([keep, pick.cut(d_lines, core_bit, place)], 1)
        reduce = Reduce(plan, [keep, plan.swap(send, core_bit)], left)
        for bit in plan.x + plan.y + plan.z[::-1]:
            held = reduce.terms
            if bit == plan.x[0]:
                *held, returned.same = tie(*held, returned.same)
                returned.prompt_three()
            elif bit == plan.y[0]:
                *held, grads, shared_n = tie(*held, grads, shared_n)
                grads = level(grads, "z")
                returned.near(shared_n)
            elif bit == plan.z[-1]:
                *held, returned.own = tie(*held, returned.own)
            elif bit == plan.z[0]:
                *held, returned.back = tie(*held, returned.back)
            reduce.terms = list(held)
            reduce.stage(bit)
        o_ab = grads.reshape(-1, width).astype(F32)
        grad_tokens = grad_own + returned.total()
        o_first = reduce.result()
        o_line = o_first[3 * step]
        o_small = [o_line[i * step : (i + 1) * step] for i in range(small)]
        o_bin = o_line[small * step : (small + wide) * step]
        return (
            layer_out[None],
            grad_tokens.astype(BF)[None],
            o_first[:step],
            o_first[step : 2 * step],
            o_first[2 * step : 3 * step],
            o_ab[wide * step : (wide + 1) * step],
            jnp.concatenate([o_ab[i * step : (i + 1) * step] for i in range(wide + 1, 2 * wide + 1)], 1),
            o_ab[: wide * step],
            o_small[0],
            o_small[1],
            o_small[2],
            o_small[3],
            o_small[4],
            o_bin,
            o_small[5],
            o_small[6],
            o_small[7],
        )

    split = P(GRP, ROW, None)
    owned2, owned1 = P(AXES, None), P(AXES)
    in_specs = (split, P(GRP, None), split) + (owned2,) * 6 + (owned1,) * 9
    out_specs = (split, split) + (owned2,) * 6 + (owned1,) * 9
    return jax.shard_map(
        per_device, mesh=fine, in_specs=in_specs, out_specs=out_specs, check_vma=False
    )
```

```python
import functools

import jax
import jax.numpy as jnp
import numpy as np
from jax import lax
from jax.experimental import pallas as pl
from jax.experimental.pallas import tpu as pltpu
from jax.sharding import Mesh
from jax.sharding import PartitionSpec as P

HEADS = 12
HDIM = 64
PROMPT = 1024
CONT_MOST = 256
BF = jnp.bfloat16
F32 = jnp.float32

NORM_EPS = 1e-12
MASK_FILL = -1000000000.0
SQRT_HALF = 0.7071067811865476
INV_ROOT_TAU = 0.3989422804014327
AXES = ("x", "core", "z", "y")
GRP, ROW = AXES[:2], AXES[2:]
WIDE = 4
WO, WI = 4, 5
WQ, WK, WV = 0, 1, 2


def mm(left, right):
    return jnp.dot(left, right, preferred_element_type=F32)


def segment_ids(lengths, group_len):
    ends = jnp.cumsum(lengths)
    places = jnp.arange(group_len, dtype=jnp.int32)
    passed = jnp.sum(((places - PROMPT)[:, None] >= ends[None, :]).astype(jnp.int32), axis=-1)
    return jnp.where(places < PROMPT, 0, 1 + passed)


class Plan:
    def __init__(self, grp, row):
        self.grp, self.row, self.count = grp, row, grp * row
        y = row // 4
        bits = lambda base, size: [base << i for i in range(size.bit_length() - 1)]
        self.y, self.z = bits(1, y), bits(y, 4)
        self.core, self.x = bits(row, 2), bits(2 * row, grp // 2)
        self.bits = self.count.bit_length() - 1

    def swap(self, value, mask):
        return lax.ppermute(value, AXES, [(i, i ^ mask) for i in range(self.count)])

    def send(self, value, moves):
        pairs = [(g * self.row + a, g * self.row + b) for g in range(self.grp) for a, b in moves]
        return lax.ppermute(value, AXES, pairs)

    def me(self):
        return lax.axis_index(AXES)


class Reduce:
    def __init__(self, plan, terms, left=None):
        self.plan, self.terms = plan, list(terms)
        self.left = left or [1 << i for i in reversed(range(plan.bits))]

    def cut(self, term, bit, place):
        at = self.left.index(bit)
        high, low = 1 << at, 1 << (len(self.left) - at - 1)
        _, rows, width = term.shape
        term = term.reshape(high, 2, low * rows, width)
        return lax.dynamic_slice_in_dim(term, place, 1, 1).reshape(high * low, rows, width)

    def total(self, terms):
        return sum([t.astype(F32) for t in terms[1:]], terms[0].astype(F32))

    def stage(self, bit):
        place = (self.plan.me() // bit) & 1
        away = self.total([self.cut(t, bit, 1 - place) for t in self.terms]).astype(BF)
        here = [self.cut(t, bit, place) for t in self.terms]
        self.left = [b for b in self.left if b != bit]
        self.terms = here + [self.plan.swap(away, bit)]

    def result(self):
        return self.total(self.terms)[0]


def tie(*values):
    return lax.optimization_barrier(values)


class Tokens:
    def __init__(self, plan, own):
        self.plan, self.own = plan, own
        self.rows = own.shape[0]
        self.ready = plan.row == 8

    def stage_one(self):
        if self.ready:
            plan, own = self.plan, self.own
            across = plan.send(own, [(0, 4), (1, 5), (2, 6), (3, 7)])
            self.same = jnp.where(lax.axis_index(ROW) < 4, own, across)
            self.beside = plan.swap(own, 1)
            return [self.same, self.beside]
        return []

    def stage_two(self):
        if self.ready:
            plan = self.plan
            self.other = plan.swap(self.same, 2)
            self.same_y = plan.swap(self.same, 1)
            self.diagonal = plan.send(self.own, [(5, 6), (6, 5)])
            return [self.other, self.same_y, self.diagonal]
        return []

    def stage_three(self):
        if self.ready:
            self.other_y = self.plan.swap(self.other, 1)

    def spots(self):
        row, rows, own = lax.axis_index(ROW), self.rows, self.own
        if self.ready:
            near = jnp.where(row < 4, 0, jnp.where((row == 5) | (row == 6), 3, 2))
            return [
                self.same, self.other, self.same_y, self.other_y, own, self.beside, self.diagonal,
            ], near
        every = lax.all_gather(own, ROW, axis=0, tiled=True)
        start = jnp.maximum(row * rows - CONT_MOST, 0)
        padded = jnp.concatenate([every, jnp.zeros((CONT_MOST, own.shape[1]), own.dtype)], 0)
        near = lax.dynamic_slice_in_dim(padded, start, rows + 2 * CONT_MOST, 0)
        every = jnp.concatenate([every[:PROMPT], near], 0)
        spots = [every[i : i + rows] for i in range(0, every.shape[0], rows)]
        return spots, jnp.where(row * rows < PROMPT, 0, near.shape[0] // rows)


def near_segments(plan, segments, rows):
    row = lax.axis_index(ROW)
    if plan.row != 8:
        start = jnp.maximum(row * rows - CONT_MOST, 0)
        padded = jnp.concatenate([segments, jnp.full((CONT_MOST,), -1, jnp.int32)], 0)
        near = lax.dynamic_slice_in_dim(padded, start, rows + 2 * CONT_MOST, 0)
        return jnp.where((near == 0) | (row * rows < PROMPT), -1, near)
    pieces = []
    for block, valid in (
        (row, row >= 4),
        (row ^ 1, row >= 4),
        (11 - row, (row == 5) | (row == 6)),
    ):
        block = jnp.clip(block, 0, 7)
        ids = lax.dynamic_slice_in_dim(segments, block * rows, rows, 0)
        pieces.append(jnp.where(valid, ids, -1))
    return jnp.concatenate(pieces, 0)


class Return:
    def __init__(self, plan, rows):
        self.plan, self.rows = plan, rows

    def prompt_one(self, parts):
        self.prompt = self.same = self.own = self.back = parts
        if self.plan.row == 8:
            same, other, same_y, other_y = [parts[i].astype(F32) for i in range(4)]
            self.other = (other + self.plan.swap(parts[3], 1).astype(F32)).astype(BF)
            self.same = same + self.plan.swap(parts[2], 1).astype(F32)

    def prompt_two(self):
        if self.plan.row == 8:
            self.same = self.same + self.plan.swap(self.other, 2).astype(F32)

    def prompt_three(self):
        if self.plan.row == 8:
            self.back = self.plan.send(self.same.astype(BF), [(4, 0), (5, 1), (6, 2), (7, 3)])

    def near(self, parts):
        self.around = parts
        if self.plan.row == 8:
            own = parts[0].astype(F32) + self.plan.swap(parts[1], 1).astype(F32)
            self.own = own + self.plan.send(parts[2], [(5, 6), (6, 5)]).astype(F32)

    def total(self):
        row, rows = lax.axis_index(ROW), self.rows
        if self.plan.row == 8:
            return jnp.where(row < 4, self.same + self.back.astype(F32), self.own)
        around = self.around.reshape(-1, self.around.shape[-1]).astype(F32)
        start = jnp.maximum(row * rows - CONT_MOST, 0)
        whole = jnp.zeros((self.plan.row * rows + CONT_MOST, around.shape[1]), F32)
        whole = whole.at[:PROMPT].set(self.prompt.reshape(PROMPT, -1).astype(F32))
        near = jnp.where(row * rows < PROMPT, 0, around)
        near = lax.dynamic_slice_in_dim(whole, start, rows + 2 * CONT_MOST, 0) + near
        whole = lax.dynamic_update_slice_in_dim(whole, near, start, 0)
        return lax.psum_scatter(whole[: self.plan.row * rows], ROW, scatter_dimension=0, tiled=True)


def heads_mask(lanes, head):
    lane = lax.broadcasted_iota(jnp.int32, lanes, 1)
    return (lane >= head * HDIM) & (lane < (head + 1) * HDIM)


def nt(left, right):
    return lax.dot_general(left, right, (((1,), (1,)), ((), ())), preferred_element_type=F32)


def tn(left, right):
    return lax.dot_general(left, right, (((0,), (0,)), ((), ())), preferred_element_type=F32)


def pack_kernel(wo_ref, wi_ref, wu_ref, wq_ref, wk_ref, wv_ref, line_ref, early_ref, late_ref):
    step, width = wo_ref.shape
    early_ref[:step, :] = wq_ref[...]
    early_ref[step : step + 8, :] = line_ref[:8, :]
    early_ref[step + 8 : 2 * step + 8, :] = wk_ref[...]
    early_ref[2 * step + 8 :, :] = wv_ref[...]
    late_ref[: WIDE * step, :] = wu_ref[...]
    late_ref[WO * step : WI * step, :] = wo_ref[...]
    for i in range(WIDE):
        late_ref[(WI + i) * step : (WI + i + 1) * step, :] = wi_ref[:, i * width : (i + 1) * width]
    late_ref[(WI + WIDE) * step :, :] = line_ref[8:, :]


def pack_call(w_output, w_inner, w_outer, w_query, w_key, w_value, line):
    step, width = w_output.shape
    shape = lambda rows: jax.ShapeDtypeStruct((rows, width), BF)
    return pl.pallas_call(
        pack_kernel, out_shape=[shape(3 * step + 8), shape((WI + WIDE) * step + 8)], name="pack"
    )(w_output, w_inner, w_outer, w_query, w_key, w_value, line)


def attention_kernel(blocks, first, rows, places, *refs):
    spots = refs[:blocks]
    (near_ref, me_ref, own_ref, a0_ref, a1_ref, b0_ref, b1_ref, segq_ref, segk_ref,
     w_out, q_ref, kp_ref, vp_ref, kn_ref, vn_ref, ctx_ref, lse_ref,
     x_ref, w_ref, s_ref, vt_ref, out_ref, line_ref, bias_ref, sems, w_sems, o_sem) = refs[blocks:]
    near = near_ref[0]
    depth = own_ref.shape[1]
    owners = w_ref.shape[0]
    each = depth // owners
    part = q_ref.shape[1]

    def weights(act):
        @pl.loop(0, owners)
        def _(e):
            away = e ^ me_ref[0]
            for (bits, half), (zero, one), parts in (
                (places[0], (a0_ref, a1_ref), ((0, each, w_ref, 0), (each, 8, line_ref, 0))),
                (places[1], (b0_ref, b1_ref), ((0, 2 * each, w_ref, each),)),
            ):
                j = sum([((away // bit) & 1) * weight for bit, weight in bits])
                for which, source in enumerate((zero, one)):

                    @pl.when(((away // half) & 1) == which)
                    def _():
                        for k, (top, size, target, base) in enumerate(parts):
                            act(pltpu.make_async_copy(
                                source.at[j, pl.ds(top, size)], target.at[e, pl.ds(base, size)],
                                w_sems.at[2 * k if zero is a0_ref else 1, e],
                            ))

    @pl.when(pl.program_id(0) == 0)
    def _():
        copies = [
            pltpu.make_async_copy(spot, x_ref.at[pl.ds(i * rows, rows)], sems.at[i])
            for i, spot in enumerate(spots)
        ]
        weights(lambda c: c.start())
        for copy in copies:
            copy.start()
        weights(lambda c: c.wait())
        for copy in copies:
            copy.wait()
        pltpu.make_async_copy(w_ref, w_out, o_sem).start()
        line = line_ref[:, 0, :128]
        place = lax.broadcasted_iota(jnp.int32, (128, depth), 0)
        lane = lax.broadcasted_iota(jnp.int32, (128, depth), 1)
        mine = lax.broadcasted_iota(jnp.int32, (owners, depth), 0)
        mine = mine == lax.broadcasted_iota(jnp.int32, (owners, depth), 1) // each
        for i in range(2):
            spread = mm(line, jnp.where(place == lane % each + i * each, 1.0, 0.0).astype(BF))
            bias_ref[i : i + 1, :] = jnp.sum(jnp.where(mine, spread, 0.0), axis=0, keepdims=True)

    lanes = pl.ds(pl.multiple_of(pl.program_id(0) * part, part), part)
    wq, wk, wv = [
        w_ref[:, i * each : (i + 1) * each, lanes].reshape(depth, part) for i in (WQ, WK, WV)
    ]
    queries = (mm(own_ref[...], wq) + bias_ref[0:1, lanes]) * (HDIM**-0.5)
    q_ref[...] = queries.astype(BF)

    heads = part // HDIM
    q = q_ref[...]
    tall = x_ref.shape[0]

    def body(sets):
        for k_ref, v_ref, base, size, _ in sets:
            x = x_ref[base : base + size, :]
            k_ref[...] = mm(x, wk).astype(BF)
            v = (mm(x, wv) + bias_ref[1:2, lanes]).astype(BF)
            v_ref[...] = v
            vt_ref[:, base : base + size] = v.T
        for h in range(heads):
            q_h = jnp.where(heads_mask(q.shape, h), q, 0)
            peak = jnp.full((1, rows), MASK_FILL, F32)
            for k_ref, _, base, size, masked in sets:
                s = nt(k_ref[...], q_h)
                if masked:
                    s = jnp.where(segk_ref[...] == segq_ref[...], s, MASK_FILL)
                s_ref[h % 2, base : base + size, :] = s
                peak = jnp.maximum(peak, jnp.max(s, axis=0, keepdims=True))
            total, mixed = jnp.zeros((1, rows), F32), jnp.zeros((HDIM, rows), F32)
            for _, _, base, size, _ in sets:
                p = jnp.exp(s_ref[h % 2, base : base + size, :] - peak)
                total = total + jnp.sum(p, axis=0, keepdims=True)
                mixed = mixed + mm(vt_ref[h * HDIM : (h + 1) * HDIM, base : base + size], p.astype(BF))
            out_ref[h * HDIM : (h + 1) * HDIM, :] = mixed / total
            lse_ref[0, h : h + 1, :] = peak + jnp.log(total)

    prompt = (kp_ref, vp_ref, 0, PROMPT, False)

    @pl.when(near == 0)
    def _():
        body([prompt])

    @pl.when(near > 0)
    def _():
        body([prompt, (kn_ref, vn_ref, PROMPT, tall - PROMPT, True)])

    ctx_ref[...] = out_ref[...].T.astype(BF)

    @pl.when(pl.program_id(0) == pl.num_programs(0) - 1)
    def _():
        pltpu.make_async_copy(w_ref, w_out, o_sem).wait()


def attention_call(spots, first, near, me, own, pieces, places, segq, segk):
    rows, width = own.shape
    blocks = len(spots)
    tall = blocks * rows
    part = 256
    steps = width // part
    heads = part // HDIM
    cols = lambda depth: pl.BlockSpec((depth, part), lambda g: (0, g))
    flops = 2 * tall * width * width * 2 + 4 * tall * rows * width * 4
    owners = 2 * pieces[0].shape[0]
    each = width // owners
    return pl.pallas_call(
        functools.partial(attention_kernel, blocks, first, rows, places),
        grid=(steps,),
        in_specs=[pl.BlockSpec(memory_space=pl.ANY)] * blocks
        + [
            pl.BlockSpec(memory_space=pltpu.SMEM),
            pl.BlockSpec(memory_space=pltpu.SMEM),
            pl.BlockSpec((rows, width), lambda g: (0, 0)),
        ] + [pl.BlockSpec(memory_space=pl.ANY)] * 4 + [
            pl.BlockSpec((1, rows), lambda g: (0, 0)),
            pl.BlockSpec(segk.shape, lambda g: (0, 0)),
        ],
        out_specs=[
            pl.BlockSpec(memory_space=pl.ANY),
            cols(rows), cols(PROMPT), cols(PROMPT), cols(tall - PROMPT), cols(tall - PROMPT),
            cols(rows), pl.BlockSpec((1, 8, rows), lambda g: (g, 0, 0)),
        ],
        out_shape=[
            jax.ShapeDtypeStruct((owners, 3 * each, width), BF),
            jax.ShapeDtypeStruct((rows, width), BF),
            jax.ShapeDtypeStruct((PROMPT, width), BF),
            jax.ShapeDtypeStruct((PROMPT, width), BF),
            jax.ShapeDtypeStruct((tall - PROMPT, width), BF),
            jax.ShapeDtypeStruct((tall - PROMPT, width), BF),
            jax.ShapeDtypeStruct((rows, width), BF),
            jax.ShapeDtypeStruct((steps, 8, rows), F32),
        ],
        scratch_shapes=[
            pltpu.VMEM((tall, width), BF),
            pltpu.VMEM((owners, 3 * each, width), BF),
            pltpu.VMEM((2, tall, rows), F32),
            pltpu.VMEM((part, tall), BF),
            pltpu.VMEM((part, rows), F32),
            pltpu.VMEM((owners, 8, width), BF),
            pltpu.VMEM((8, width), F32),
            pltpu.SemaphoreType.DMA((blocks,)),
            pltpu.SemaphoreType.DMA((3, owners)),
            pltpu.SemaphoreType.DMA,
        ],
        compiler_params=pltpu.CompilerParams(vmem_limit_bytes=60 * 2**20),
        cost_estimate=pl.CostEstimate(
            flops=flops, bytes_accessed=12 * 2**20, transcendentals=tall * rows * 12
        ),
        name="attention",
    )(*spots, near, me, own, *pieces, segq, segk)


def halves(value, runs, core):
    depth = value.shape[0] // runs
    pick = lambda first: jnp.concatenate(
        [value[i * depth : (i + 1) * depth] for i in range(first, runs, 2)], 0
    )
    even, odd = pick(0), pick(1)
    return jnp.where(core == 0, odd, even), jnp.where(core == 0, even, odd)


def middle_kernel(wide, mapped, ctx_ref, own_ref, cot_ref, got_ref, vec_ref, bin_ref,
                  out_ref, h1_ref, gctx_ref, grads, sums_ref, sbin_ref,
                  first_ref, n1_ref, inv_ref, low_ref, pre_ref, cdf_ref, act_ref, acc_ref,
                  gffn_ref, glow_ref, lowt_ref, w_ref, out_buf, in_buf, wo_buf, sems, w_sems):
    step = pl.program_id(0)
    width = ctx_ref.shape[1]
    vec = lambda i: vec_ref[i : i + 1, :]
    mean = lambda v: jnp.sum(v, axis=-1, keepdims=True) * (1.0 / width)
    down = lambda v: jnp.sum(v, axis=0, keepdims=True)
    owners = got_ref.shape[0]
    each = width // owners
    some = owners // wide
    square = lambda value: value.reshape(width, width)
    rows_of = lambda place: pl.ds(pl.multiple_of(place * each, each), each)
    w_output = lambda ref: ref.at[:, rows_of(WO)]
    w_inner = lambda ref, at: ref.at[:, rows_of(WI + at)]
    w_outer = lambda ref, at: ref.at[pl.ds(at * some, some), pl.ds(0, wide * each)]

    def fetch_inner(at):
        return pltpu.make_async_copy(w_inner(got_ref, at), w_inner(w_ref, at), w_sems.at[0, at])

    def fetch_outer(at):
        return pltpu.make_async_copy(w_outer(got_ref, at), w_outer(w_ref, at), w_sems.at[1, at])

    def fetch_output():
        return pltpu.make_async_copy(w_output(got_ref), w_output(w_ref), w_sems.at[0, wide])

    def slot(group, i):
        return group % 2 * 16 + group // 2 * 8 + i % 2 * 4 + i // 2 if mapped else group * 8 + i

    def outer(at):
        turn = (2 * wide - 1 - at) % 2
        return [
            pltpu.make_async_copy(
                out_buf.at[turn, i], grads.at[slot(at, i), pl.ds(0, wide * each)], sems.at[turn, i]
            )
            for i in range(some)
        ]

    def inner(at):
        turn = (2 * wide - 1 - at) % 2
        top = pl.multiple_of((wide + 1 + at) * each, each)
        return [
            pltpu.make_async_copy(
                in_buf.at[turn, e], grads.at[slot(e // 8, e % 8), pl.ds(top, each)], sems.at[2 + turn, e]
            )
            for e in range(owners)
        ]

    def output():
        return [
            pltpu.make_async_copy(
                wo_buf.at[e], grads.at[slot(e // 8, e % 8), pl.ds(wide * each, each)], sems.at[4, e]
            )
            for e in range(owners)
        ]

    def start(copies):
        for copy in copies:
            copy.start()

    def wait(copies):
        for copy in copies:
            copy.wait()

    @pl.when(step == 0)
    def _():
        fetch_output().start()
        for at in range(wide):
            fetch_inner(at).start()
            fetch_outer(at).start()
        fetch_output().wait()
        hidden = own_ref[...].astype(F32) + mm(ctx_ref[...], square(w_output(w_ref)[...])) + vec(0)
        centred = hidden - mean(hidden)
        inverse = lax.rsqrt(mean(centred * centred) + NORM_EPS)
        normed = centred * inverse
        n1_ref[...] = normed
        inv_ref[...] = inverse
        first = normed * vec(1) + vec(2)
        first_ref[...] = first
        low_ref[...] = first.astype(BF)
        lowt_ref[...] = first.astype(BF).T

    @pl.when(step < wide)
    def _():
        chunk = pl.ds(pl.multiple_of(step * width, width), width)
        fetch_inner(step).wait()
        fetch_outer(step).wait()
        pre = mm(low_ref[...], square(w_inner(w_ref, step)[...])) + bin_ref[pl.ds(step, 1), :]
        cdf = 0.5 * (1.0 + lax.erf(pre * SQRT_HALF))
        act = (pre * cdf).astype(BF)
        pre_ref[:, chunk] = pre
        cdf_ref[:, chunk] = cdf
        act_ref[:, chunk] = act
        more = mm(act, square(w_outer(w_ref, step)[...]))

        @pl.when(step == 0)
        def _():
            acc_ref[...] = more

        @pl.when(step > 0)
        def _():
            acc_ref[...] += more

    @pl.when(step == wide - 1)
    def _():
        hidden = first_ref[...] + acc_ref[...] + vec(3)
        centred = hidden - mean(hidden)
        inverse = lax.rsqrt(mean(centred * centred) + NORM_EPS)
        normed = centred * inverse
        out_ref[...] = (normed * vec(4) + vec(5)).astype(BF)
        grad = cot_ref[...].astype(F32)
        sums_ref[0:1, :] = down(grad * normed)
        sums_ref[1:2, :] = down(grad)
        e = grad * vec(4)
        back = inverse * (e - mean(e) - normed * mean(e * normed))
        gffn_ref[...] = back
        low = back.astype(BF)
        glow_ref[...] = low
        sums_ref[2:3, :] = down(low.astype(F32))

    @pl.when(step >= wide)
    def _():
        at = 2 * wide - 1 - step
        chunk = pl.ds(pl.multiple_of(at * width, width), width)
        pre = pre_ref[:, chunk]
        slope = cdf_ref[:, chunk] + pre * jnp.exp(-0.5 * pre * pre) * INV_ROOT_TAU
        low = glow_ref[...]
        grad = (nt(low, square(w_outer(w_ref, at)[...])) * slope).astype(BF)
        sbin_ref[pl.ds(at, 1), :] = down(grad.astype(F32))
        turn = step % 2

        @pl.when(step >= wide + 2)
        def _():
            wait(outer(at + 2) + inner(at + 2))

        out_buf[turn] = tn(act_ref[:, chunk], low).astype(BF).reshape(some, wide * each, width)
        start(outer(at))
        in_buf[turn] = mm(lowt_ref[...], grad).astype(BF).reshape(owners, each, width)
        start(inner(at))
        gffn_ref[...] += nt(grad, square(w_inner(w_ref, at)[...]))

    @pl.when(step == 2 * wide - 1)
    def _():
        grad = gffn_ref[...]
        normed = n1_ref[...]
        sums_ref[3:4, :] = down(grad * normed)
        sums_ref[4:5, :] = down(grad)
        e = grad * vec(1)
        back = inv_ref[...] * (e - mean(e) - normed * mean(e * normed))
        h1_ref[...] = back
        low = back.astype(BF)
        sums_ref[5:6, :] = down(low.astype(F32))
        wo_buf[...] = tn(ctx_ref[...], low).astype(BF).reshape(owners, each, width)
        start(output())
        gctx = nt(low, square(w_output(w_ref)[...])).astype(BF)
        gctx_ref[...] = gctx
        sums_ref[6:7, :] = down(gctx.astype(F32))
        sums_ref[7:8, :] = jnp.zeros((1, width), F32)
        wait(outer(1) + inner(1) + outer(0) + inner(0) + output())


def middle_call(ctx, own, cot, got, vec, b_inner, mapped):
    rows, width = own.shape
    owners = got.shape[0]
    each = width // owners
    wide = WIDE
    whole = lambda shape: pl.BlockSpec(shape, lambda s: (0,) * len(shape))
    shape = jax.ShapeDtypeStruct
    return pl.pallas_call(
        functools.partial(middle_kernel, wide, mapped),
        grid=(2 * wide,),
        in_specs=[
            whole((rows, width)), whole((rows, width)), whole((rows, width)),
            pl.BlockSpec(memory_space=pl.ANY),
            whole((8, width)), whole((8, width)),
        ],
        out_specs=[
            whole((rows, width)), whole((rows, width)), whole((rows, width)),
            pl.BlockSpec(memory_space=pl.ANY),
            whole((8, width)), whole((8, width)),
        ],
        out_shape=[
            shape((rows, width), BF), shape((rows, width), F32), shape((rows, width), BF),
            shape((owners, (2 * wide + 1) * each, width), BF),
            shape((8, width), F32), shape((8, width), F32),
        ],
        scratch_shapes=[
            pltpu.VMEM((rows, width), F32), pltpu.VMEM((rows, width), F32), pltpu.VMEM((rows, 1), F32),
            pltpu.VMEM((rows, width), BF), pltpu.VMEM((rows, wide * width), F32),
            pltpu.VMEM((rows, wide * width), F32), pltpu.VMEM((rows, wide * width), BF),
            pltpu.VMEM((rows, width), F32), pltpu.VMEM((rows, width), F32),
            pltpu.VMEM((rows, width), BF), pltpu.VMEM((width, rows), BF),
            pltpu.VMEM((owners, (2 * wide + 1) * each, width), BF),
            pltpu.VMEM((2, owners // wide, wide * each, width), BF),
            pltpu.VMEM((2, owners, each, width), BF),
            pltpu.VMEM((owners, each, width), BF), pltpu.SemaphoreType.DMA((5, owners)),
            pltpu.SemaphoreType.DMA((2, wide + 1)),
        ],
        compiler_params=pltpu.CompilerParams(vmem_limit_bytes=60 * 2**20),
        cost_estimate=pl.CostEstimate(
            flops=2 * rows * width * width * (6 * wide + 3), bytes_accessed=32 * 2**20,
            transcendentals=2 * rows * width * wide,
        ),
        name="middle",
    )(ctx, own, cot, got, vec, b_inner)


def back_kernel(rows, bound, started, *refs):
    near_ref, gctx_ref, ctx_ref, q_ref, k_ref, v_ref, lse_ref, segq_ref, segk_ref = refs[:9]
    dk_ref, dv_ref, dq_ref, kt_ref, p_ref, ds_ref = refs[-6:]
    q, g = q_ref[...], gctx_ref[...]
    part = q.shape[1]
    heads = part // HDIM
    masks = [heads_mask(q.shape, h) for h in range(heads)]
    q_parts = [jnp.where(m, q, 0) for m in masks]
    g_parts = [jnp.where(m, g, 0) for m in masks]
    product = (g.astype(F32) * ctx_ref[...].astype(F32)).T
    inner = [
        jnp.sum(product[h * HDIM : (h + 1) * HDIM], axis=0, keepdims=True) for h in range(heads)
    ]

    def body():
        k, v = k_ref[...], v_ref[...]
        kt_ref[...] = k.T
        for h in range(heads):
            s = nt(k, q_parts[h])
            if bound is None:
                s = jnp.where(segk_ref[...] == segq_ref[...], s, MASK_FILL)
            p = jnp.exp(s - lse_ref[0, h : h + 1, :])
            across = slice(h * rows, (h + 1) * rows)
            ds = (p * (nt(v, g_parts[h]) - inner[h])).astype(BF)
            p_ref[:, across] = p.astype(BF)
            ds_ref[:, across] = ds
            mine = slice(h * HDIM, (h + 1) * HDIM)
            more = mm(kt_ref[mine, :], ds)
            dq_ref[mine, :] = refs[9][mine, :] + more if started else more
        dk_ref[...] = mm(ds_ref[...], jnp.concatenate(q_parts, 0)).astype(BF)
        dv_ref[...] = mm(p_ref[...], jnp.concatenate(g_parts, 0)).astype(BF)

    if bound is None:

        @pl.when(near_ref[0] == 0)
        def _():
            dq_ref[...] = refs[9][...]

        pl.when(near_ref[0] > 0)(body)
    else:
        body()


def back_call(start, steps, bound, near, gctx, ctx, q, k, v, lse, segq, segk, dq0=None, into=None):
    rows, width = q.shape
    tall = k.shape[0]
    part = 256
    cols = lambda depth: pl.BlockSpec((depth, part), lambda g: (0, start + g))
    whole = lambda shape: pl.BlockSpec(shape, lambda g: (0,) * len(shape))
    down = pl.BlockSpec((part, rows), lambda g: (start + g, 0))
    shape = jax.ShapeDtypeStruct
    extra = ([dq0] if dq0 is not None else []) + list(into or [])
    specs = ([down] if dq0 is not None else []) + [pl.BlockSpec(memory_space=pl.ANY)] * len(into or [])
    return pl.pallas_call(
        functools.partial(back_kernel, rows, bound, dq0 is not None),
        grid=(steps,),
        in_specs=[
            pl.BlockSpec(memory_space=pltpu.SMEM),
            cols(rows), cols(rows), cols(rows), cols(tall), cols(tall),
            pl.BlockSpec((1, 8, rows), lambda g: (start + g, 0, 0)),
            whole((1, rows)), whole(segk.shape),
        ] + specs,
        out_specs=[cols(tall), cols(tall), down],
        out_shape=[shape((tall, width), BF), shape((tall, width), BF), shape((width, rows), F32)],
        input_output_aliases={9 + i: i for i in range(3)} if into else {},
        scratch_shapes=[
            pltpu.VMEM((part, tall), BF),
            pltpu.VMEM((tall, part // HDIM * rows), BF),
            pltpu.VMEM((tall, part // HDIM * rows), BF),
        ],
        compiler_params=pltpu.CompilerParams(vmem_limit_bytes=60 * 2**20),
        cost_estimate=pl.CostEstimate(
            flops=2 * 10 * 2 * tall * rows * part * steps * 2,
            bytes_accessed=8 * tall * part * steps, transcendentals=tall * rows * 4 * steps,
        ),
        name="attention_back",
    )(near, gctx, ctx, q, k, v, lse, segq, segk, *extra)


def product_kernel(rows, bound, near_ref, dk_ref, dv_ref, wk_ref, wv_ref, gx_ref):
    @pl.when((pl.program_id(0) < near_ref[0]) | (bound is not None))
    def _():
        width = dk_ref.shape[1]
        wk, wv = wk_ref[...].reshape(width, width), wv_ref[...].reshape(width, width)
        gx_ref[0] = (nt(dk_ref[...], wk) + nt(dv_ref[...], wv)).astype(BF)


def product_call(bound, near, dk, dv, got, rows):
    tall, width = dk.shape
    owners, each = got.shape[0], width // got.shape[0]
    weight = lambda place: pl.BlockSpec((owners, each, width), lambda b: (0, place, 0))
    return pl.pallas_call(
        functools.partial(product_kernel, rows, bound),
        grid=(tall // rows,),
        in_specs=[
            pl.BlockSpec(memory_space=pltpu.SMEM),
            pl.BlockSpec((rows, width), lambda b: (b, 0)),
            pl.BlockSpec((rows, width), lambda b: (b, 0)),
            weight(WK), weight(WV),
        ],
        out_specs=pl.BlockSpec((1, rows, width), lambda b: (b, 0, 0)),
        out_shape=jax.ShapeDtypeStruct((tall // rows, rows, width), BF),
        compiler_params=pltpu.CompilerParams(vmem_limit_bytes=60 * 2**20),
        cost_estimate=pl.CostEstimate(
            flops=4 * tall * width * width, bytes_accessed=6 * tall * width, transcendentals=0
        ),
        name="token_product",
    )(near, dk, dv, got, got)


def weight_kernel(blocks, first, rows, runs, *refs):
    spots = refs[:blocks]
    (near_ref, core_ref, own_ref, dq_ref, wq_ref, h1_ref, dkp_ref, dvp_ref, dkn_ref, dvn_ref,
     send_ref, keep_ref, gown_ref, sums_ref, x_ref, xt_ref, sems) = refs[blocks:]
    core = core_ref[0]
    step = pl.program_id(0)

    @pl.when(step == 0)
    def _():
        copies = [
            pltpu.make_async_copy(spot, x_ref.at[pl.ds(i * rows, rows)], sems.at[i])
            for i, spot in enumerate(spots)
        ]
        for copy in copies:
            copy.start()
        gown_ref[...] = h1_ref[...]
        for i, copy in enumerate(copies):
            copy.wait()
            xt_ref[:, i * rows : (i + 1) * rows] = x_ref[i * rows : (i + 1) * rows, :].T

    scale = HDIM**-0.5
    dq = dq_ref[...].T.astype(BF)
    part = dq.shape[1]
    width = x_ref.shape[1]
    gown_ref[...] += nt(dq, wq_ref[...].reshape(width, part)) * scale
    half = send_ref.shape[0]
    each = width // (2 * half)

    def put(i, grad):
        away, here = halves(grad.astype(BF), runs, core)
        send_ref[:, i * each : (i + 1) * each, :] = away.reshape(half, each, part)
        keep_ref[:, i * each : (i + 1) * each, :] = here.reshape(half, each, part)

    put(WQ, tn(own_ref[...], dq) * scale)
    sums_ref[0:1, :] = jnp.sum(dq.astype(F32), axis=0, keepdims=True) * scale

    def body(near):
        for i, p_ref, n_ref in ((WK, dkp_ref, dkn_ref), (WV, dvp_ref, dvn_ref)):
            grad = mm(xt_ref[:, :PROMPT], p_ref[...])
            if near:
                grad = grad + mm(xt_ref[:, PROMPT:], n_ref[...])
            put(i, grad)

    pl.when(near_ref[0] == 0)(lambda: body(False))
    pl.when(near_ref[0] > 0)(lambda: body(True))
    sums_ref[1:8, :] = jnp.zeros((7, part), F32)


def weight_call(spots, first, near, own, dq, got, h1, dkp, dvp, dkn, dvn, core, runs):
    rows, width = own.shape
    blocks = len(spots)
    tall = blocks * rows
    part = 256
    steps = width // part
    cols = lambda depth, size=part: pl.BlockSpec((depth, size), lambda g: (0, g))
    whole = lambda shape: pl.BlockSpec(shape, lambda g: (0,) * len(shape))
    shape = jax.ShapeDtypeStruct
    owners, each = got.shape[0], width // got.shape[0]
    half = owners // 2
    slab = pl.BlockSpec((half, 3 * each, part), lambda g: (0, 0, g))
    return pl.pallas_call(
        functools.partial(weight_kernel, blocks, first, rows, runs),
        grid=(steps,),
        in_specs=[pl.BlockSpec(memory_space=pl.ANY)] * blocks
        + [
            pl.BlockSpec(memory_space=pltpu.SMEM),
            pl.BlockSpec(memory_space=pltpu.SMEM),
            whole((rows, width)), pl.BlockSpec((part, rows), lambda g: (g, 0)),
            pl.BlockSpec((owners, each, part), lambda g: (0, WQ, g)),
            whole((rows, width)), cols(PROMPT), cols(PROMPT), cols(tall - PROMPT), cols(tall - PROMPT),
        ],
        out_specs=[
            slab, slab, whole((rows, width)), cols(8),
        ],
        out_shape=[
            shape((half, 3 * each, width), BF), shape((half, 3 * each, width), BF),
            shape((rows, width), F32), shape((8, width), F32),
        ],
        scratch_shapes=[
            pltpu.VMEM((tall, width), BF), pltpu.VMEM((width, tall), BF), pltpu.SemaphoreType.DMA((blocks,)),
        ],
        compiler_params=pltpu.CompilerParams(vmem_limit_bytes=60 * 2**20),
        cost_estimate=pl.CostEstimate(
            flops=4 * tall * width * width, bytes_accessed=12 * tall * width, transcendentals=0
        ),
        name="weight_product",
    )(*spots, near, core, own, dq, got, h1, dkp, dvp, dkn, dvn)


def real_owners(grads, count, step, width):
    split = count // 32
    take = lambda v: v.reshape(32, -1, split, step, width).transpose(0, 2, 1, 3, 4).reshape(count, -1, width)
    outer, rest = grads[:, : 4 * split * step], grads[:, 4 * split * step :]
    return jnp.concatenate([outer.reshape(count, 4 * step, width), take(rest)], 1)


def solution(mesh):
    plan = Plan(mesh.shape["grp"], mesh.shape["row"])
    fine = Mesh(mesh.devices.reshape(plan.grp // 2, 2, 4, plan.row // 4), AXES)

    def per_device(
        tokens, cont_lengths, cotangent, w_query, w_key, w_value, w_output, w_inner, w_outer,
        bias_query, bias_value, bias_output, gain_first, shift_first, bias_inner, bias_outer,
        gain_second, shift_second,
    ):
        count = plan.count
        _, rows, width = tokens.shape
        step = w_query.shape[0]
        wide = w_inner.shape[1] // width
        own = tokens[0]

        early = (bias_query, bias_value)
        late = (bias_output, gain_first, shift_first, bias_outer, gain_second, shift_second, bias_inner)
        small = len(late) - 1

        def in_line(vectors):
            line, place = 0, 0
            for vector in vectors:
                size = vector.shape[0]
                line = line + jnp.pad(vector, (place, width - place - size))
                place += size
            return jnp.pad(line[None], ((0, 7), (0, 0)))

        line = jnp.concatenate([in_line(early), in_line(late)], 0)
        runs = plan.grp
        row = lax.axis_index(ROW)
        core = lax.axis_index("core").astype(jnp.int32).reshape(1)
        exchange = Tokens(plan, own)
        squares = (w_query, w_key, w_value)
        if step % 8 == 0:
            first_pack, pack = pack_call(w_output, w_inner, w_outer, *squares, line)
            got = lax.all_gather(pack, AXES, axis=0, tiled=True).reshape(count, -1, width)
            lines = got[:, (WI + WIDE) * step]

            def swaps(value, bits):
                masks = [0]
                for bit in bits:
                    masks = masks + [m ^ bit for m in masks]
                return [plan.swap(value, m) for m in masks[1:]]

            def stage(held, bit):
                return jnp.concatenate([held, plan.swap(held, bit)], 0)

            away = swaps(first_pack, plan.z)
            *away, same, beside = tie(*away, *exchange.stage_one())
            exchange.same, exchange.beside = same, beside
            cut = step + 8
            one = jnp.stack([v[:cut] for v in (first_pack, *away)])
            two = jnp.stack([v[cut:] for v in (first_pack, *away)])
            one, two = stage(one, plan.x[0]), stage(two, plan.y[0])
            one, two, *seen = tie(one, two, *exchange.stage_two())
            exchange.other, exchange.same_y, exchange.diagonal = seen
            one, two = stage(one, plan.y[0]), stage(two, plan.x[0])
            exchange.stage_three()
            one, exchange.other_y = tie(one, exchange.other_y)
            pieces = [one, plan.swap(one, plan.core[0]), two, plan.swap(two, plan.core[0])]
            order = lambda *bits: ([(bit, 1 << i) for i, bit in enumerate(bits)], plan.core[0])
            places = (
                order(*plan.z, plan.x[0], plan.y[0]),
                order(*plan.z, plan.y[0], plan.x[0]),
            )
            me = plan.me().astype(jnp.int32).reshape(1)
        else:
            inner_rows = [w_inner[:, i * width : (i + 1) * width] for i in range(wide)]
            pack = jnp.concatenate([w_outer, w_output, *inner_rows, *squares, line], 0)
            got = lax.all_gather(pack, AXES, axis=0, tiled=True).reshape(count, -1, width)
            lines = got[:, 12 * step + 8]
            cuts = [wide * step, (wide + 1) * step, (2 * wide + 1) * step, 12 * step]
            outer, output, inner, rest, marks = jnp.split(got, cuts, axis=1)
            apart = lambda v, n: v.reshape(count, n, step, width).transpose(1, 0, 2, 3)
            inner, rest = [
                v.reshape(v.shape[0], 32, width // 32, width).transpose(1, 0, 2, 3)
                for v in (apart(inner, wide), apart(rest, 3))
            ]
            got = jnp.concatenate([v.reshape(32, -1, width) for v in (outer, output, inner)], 1)
            pairs = marks[:, 0, : 2 * step].reshape(32, count // 32, 2, step).transpose(0, 2, 1, 3)
            pairs = jnp.pad(pairs.reshape(32, 1, -1), ((0, 0), (0, 7), (0, width - 2 * width // 32)))
            one = jnp.concatenate([rest[:, 0], pairs], 1)
            two = rest[:, 1:].reshape(32, -1, width)
            pieces = [one[:16], one[16:], two[:16], two[16:]]
            places = (([(1, 1), (2, 2), (4, 4), (8, 8)], 16),) * 2
            me = jnp.zeros((1,), jnp.int32)
        spots, near = exchange.spots()
        first_near = PROMPT // rows

        table = lines[:, : small * step].reshape(count, small, step).transpose(1, 0, 2)
        table = table.reshape(small, width).astype(F32)
        v_bin = lines[:, small * step : (small + wide) * step].reshape(wide, width).astype(F32)
        v_bin = jnp.pad(v_bin, ((0, 8 - wide), (0, 0)))
        segments = segment_ids(cont_lengths[0], plan.row * rows)
        seg_own = lax.dynamic_slice_in_dim(segments, row * rows, rows, 0)[None, :]
        seg_near = near_segments(plan, segments, rows)[:, None]
        near = near.astype(jnp.int32).reshape(1)

        squares, queries, keys_p, values_p, keys_n, values_n, context, log_total = attention_call(
            spots, first_near, near, me, own, pieces, places, seg_own, seg_near
        )
        vec = jnp.concatenate([table, jnp.zeros((2, width), F32)], 0)
        layer_out, grad_h1, grad_context, grads, sums, sums_bin = middle_call(
            context, own, cotangent[0], got, vec, v_bin, step % 8 == 0
        )
        if step % 8:
            grads = real_owners(grads, count, step, width)
            grads = grads.reshape(plan.grp // 2, 2, 4, plan.row // 4, -1, width)
            grads = grads.transpose(1, 0, 3, 2, 4, 5).reshape(count, -1, width)
        level = lambda value, axes: lax.psum_scatter(value, axes, scatter_dimension=0, tiled=True)
        grads = level(grads, "core")
        core_bit = plan.core[0]
        left = [1 << i for i in reversed(range(plan.bits)) if 1 << i != core_bit]
        parts = width // 256
        dkp, dvp, dqp = back_call(
            0, parts, first_near, near, grad_context, context, queries, keys_p, values_p, log_total,
            seg_own, seg_near,
        )
        shared_p = product_call(first_near, near, dkp, dvp, squares, rows)
        grads, shared_p, dqp = tie(grads, shared_p, dqp)
        grads = level(grads, ("x", "y"))
        returned = Return(plan, rows)
        returned.prompt_one(shared_p)
        dkn, dvn, dq = back_call(
            0, parts, None, near, grad_context, context, queries, keys_n, values_n, log_total,
            seg_own, seg_near, dqp,
        )
        send, keep, grad_own, sums_qkv = weight_call(
            spots, first_near, near, own, dq, squares, grad_h1, dkp, dvp, dkn, dvn, core, runs
        )
        send, keep, returned.same, dkn, dvn = tie(send, keep, returned.same, dkn, dvn)
        returned.prompt_two()
        shared_n = product_call(None, near, dkn, dvn, squares, rows)

        order = (6, 5, 3, 4, 2, 0, 1)
        small = len(early) + len(late) - 1
        d_table = jnp.concatenate([sums_qkv[:1]] + [sums[i : i + 1] for i in order], 0)
        d_lines = jnp.concatenate(
            [
                d_table.reshape(small, count, step).transpose(1, 0, 2).reshape(count, -1),
                sums_bin[:wide].reshape(count, wide * step),
            ],
            1,
        )
        d_lines = jnp.pad(d_lines, ((0, 0), (0, width - d_lines.shape[1])))[:, None].astype(BF)
        d_lines = jnp.pad(d_lines, ((0, 0), (0, 7), (0, 0)))
        place = core[0]
        pick = Reduce(plan, [])
        if step % 8:
            real = lambda v: v.reshape(16, 3, count // 32, step, width).transpose(0, 2, 1, 3, 4)
            send, keep = [real(v).reshape(count // 2, 3 * step, width) for v in (send, keep)]
        send = jnp.concatenate([send, pick.cut(d_lines, core_bit, 1 - place)], 1)
        keep = jnp.concatenate([keep, pick.cut(d_lines, core_bit, place)], 1)
        reduce = Reduce(plan, [keep, plan.swap(send, core_bit)], left)
        for bit in plan.x + plan.y + plan.z[::-1]:
            held = reduce.terms
            if bit == plan.x[0]:
                *held, returned.same = tie(*held, returned.same)
                returned.prompt_three()
            elif bit == plan.y[0]:
                *held, grads, shared_n, returned.back = tie(*held, grads, shared_n, returned.back)
                grads = level(grads, "z")
            elif bit == plan.z[-1]:
                *held, shared_n = tie(*held, shared_n)
                returned.near(shared_n)
            elif bit == plan.z[0]:
                *held, returned.own = tie(*held, returned.own)
            reduce.terms = list(held)
            reduce.stage(bit)
        o_ab = grads.reshape(-1, width).astype(F32)
        grad_tokens = grad_own + returned.total()
        o_first = reduce.result()
        o_line = o_first[3 * step]
        o_small = [o_line[i * step : (i + 1) * step] for i in range(small)]
        o_bin = o_line[small * step : (small + wide) * step]
        return (
            layer_out[None],
            grad_tokens.astype(BF)[None],
            o_first[:step],
            o_first[step : 2 * step],
            o_first[2 * step : 3 * step],
            o_ab[wide * step : (wide + 1) * step],
            jnp.concatenate([o_ab[i * step : (i + 1) * step] for i in range(wide + 1, 2 * wide + 1)], 1),
            o_ab[: wide * step],
            o_small[0],
            o_small[1],
            o_small[2],
            o_small[3],
            o_small[4],
            o_bin,
            o_small[5],
            o_small[6],
            o_small[7],
        )

    split = P(GRP, ROW, None)
    owned2, owned1 = P(AXES, None), P(AXES)
    in_specs = (split, P(GRP, None), split) + (owned2,) * 6 + (owned1,) * 9
    out_specs = (split, split) + (owned2,) * 6 + (owned1,) * 9
    return jax.shard_map(
        per_device, mesh=fine, in_specs=in_specs, out_specs=out_specs, check_vma=False
    )
```

```python
import functools

import jax
import jax.numpy as jnp
import numpy as np
from jax import lax
from jax.experimental import pallas as pl
from jax.experimental.pallas import tpu as pltpu
from jax.sharding import Mesh
from jax.sharding import PartitionSpec as P

HEADS = 12
HDIM = 64
PROMPT = 1024
CONT_MOST = 256
BF = jnp.bfloat16
F32 = jnp.float32

NORM_EPS = 1e-12
MASK_FILL = -1000000000.0
SQRT_HALF = 0.7071067811865476
INV_ROOT_TAU = 0.3989422804014327
AXES = ("x", "core", "z", "y")
GRP, ROW = AXES[:2], AXES[2:]
WIDE = 4
WO, WI = 4, 5
WQ, WK, WV = 0, 1, 2


def mm(left, right):
    return jnp.dot(left, right, preferred_element_type=F32)


def segment_ids(lengths, group_len):
    ends = jnp.cumsum(lengths)
    places = jnp.arange(group_len, dtype=jnp.int32)
    passed = jnp.sum(((places - PROMPT)[:, None] >= ends[None, :]).astype(jnp.int32), axis=-1)
    return jnp.where(places < PROMPT, 0, 1 + passed)


class Plan:
    def __init__(self, grp, row):
        self.grp, self.row, self.count = grp, row, grp * row
        y = row // 4
        bits = lambda base, size: [base << i for i in range(size.bit_length() - 1)]
        self.y, self.z = bits(1, y), bits(y, 4)
        self.core, self.x = bits(row, 2), bits(2 * row, grp // 2)
        self.bits = self.count.bit_length() - 1

    def swap(self, value, mask):
        return lax.ppermute(value, AXES, [(i, i ^ mask) for i in range(self.count)])

    def send(self, value, moves):
        pairs = [(g * self.row + a, g * self.row + b) for g in range(self.grp) for a, b in moves]
        return lax.ppermute(value, AXES, pairs)

    def me(self):
        return lax.axis_index(AXES)


class Reduce:
    def __init__(self, plan, terms, left=None):
        self.plan, self.terms = plan, list(terms)
        self.left = left or [1 << i for i in reversed(range(plan.bits))]

    def cut(self, term, bit, place):
        at = self.left.index(bit)
        high, low = 1 << at, 1 << (len(self.left) - at - 1)
        _, rows, width = term.shape
        term = term.reshape(high, 2, low * rows, width)
        return lax.dynamic_slice_in_dim(term, place, 1, 1).reshape(high * low, rows, width)

    def total(self, terms):
        return sum([t.astype(F32) for t in terms[1:]], terms[0].astype(F32))

    def stage(self, bit):
        place = (self.plan.me() // bit) & 1
        away = self.total([self.cut(t, bit, 1 - place) for t in self.terms]).astype(BF)
        here = [self.cut(t, bit, place) for t in self.terms]
        self.left = [b for b in self.left if b != bit]
        self.terms = here + [self.plan.swap(away, bit)]

    def result(self):
        return self.total(self.terms)[0]


def tie(*values):
    return lax.optimization_barrier(values)


class Tokens:
    def __init__(self, plan, own):
        self.plan, self.own = plan, own
        self.rows = own.shape[0]
        self.ready = plan.row == 8

    def stage_one(self):
        if self.ready:
            plan, own = self.plan, self.own
            across = plan.send(own, [(0, 4), (1, 5), (2, 6), (3, 7)])
            self.same = jnp.where(lax.axis_index(ROW) < 4, own, across)
            self.beside = plan.swap(own, 1)
            return [self.same, self.beside]
        return []

    def stage_two(self):
        if self.ready:
            plan = self.plan
            self.other = plan.swap(self.same, 2)
            self.same_y = plan.swap(self.same, 1)
            self.diagonal = plan.send(self.own, [(5, 6), (6, 5)])
            return [self.other, self.same_y, self.diagonal]
        return []

    def stage_three(self):
        if self.ready:
            self.other_y = self.plan.swap(self.same_y, 2)

    def spots(self):
        row, rows, own = lax.axis_index(ROW), self.rows, self.own
        if self.ready:
            near = jnp.where(row < 4, 0, jnp.where((row == 5) | (row == 6), 3, 2))
            return [
                self.same, self.other, self.same_y, self.other_y, own, self.beside, self.diagonal,
            ], near
        every = lax.all_gather(own, ROW, axis=0, tiled=True)
        start = jnp.maximum(row * rows - CONT_MOST, 0)
        padded = jnp.concatenate([every, jnp.zeros((CONT_MOST, own.shape[1]), own.dtype)], 0)
        near = lax.dynamic_slice_in_dim(padded, start, rows + 2 * CONT_MOST, 0)
        every = jnp.concatenate([every[:PROMPT], near], 0)
        spots = [every[i : i + rows] for i in range(0, every.shape[0], rows)]
        return spots, jnp.where(row * rows < PROMPT, 0, near.shape[0] // rows)


def near_segments(plan, segments, rows):
    row = lax.axis_index(ROW)
    if plan.row != 8:
        start = jnp.maximum(row * rows - CONT_MOST, 0)
        padded = jnp.concatenate([segments, jnp.full((CONT_MOST,), -1, jnp.int32)], 0)
        near = lax.dynamic_slice_in_dim(padded, start, rows + 2 * CONT_MOST, 0)
        return jnp.where((near == 0) | (row * rows < PROMPT), -1, near)
    pieces = []
    for block, valid in (
        (row, row >= 4),
        (row ^ 1, row >= 4),
        (11 - row, (row == 5) | (row == 6)),
    ):
        block = jnp.clip(block, 0, 7)
        ids = lax.dynamic_slice_in_dim(segments, block * rows, rows, 0)
        pieces.append(jnp.where(valid, ids, -1))
    return jnp.concatenate(pieces, 0)


class Return:
    def __init__(self, plan, rows):
        self.plan, self.rows = plan, rows

    def prompt_one(self, parts):
        self.prompt = self.same = self.same_y = self.own = self.back = parts
        if self.plan.row == 8:
            same, same_y = parts[0].astype(F32), parts[2].astype(F32)
            self.same_y = (same_y + self.plan.swap(parts[3], 2).astype(F32)).astype(BF)
            self.same = same + self.plan.swap(parts[1], 2).astype(F32)

    def prompt_two(self):
        if self.plan.row == 8:
            self.same = self.same + self.plan.swap(self.same_y, 1).astype(F32)

    def prompt_three(self):
        if self.plan.row == 8:
            self.back = self.plan.send(self.same.astype(BF), [(4, 0), (5, 1), (6, 2), (7, 3)])

    def near(self, parts):
        self.around = parts
        if self.plan.row == 8:
            own = parts[0].astype(F32) + self.plan.swap(parts[1], 1).astype(F32)
            self.own = own + self.plan.send(parts[2], [(5, 6), (6, 5)]).astype(F32)

    def total(self):
        row, rows = lax.axis_index(ROW), self.rows
        if self.plan.row == 8:
            return jnp.where(row < 4, self.same + self.back.astype(F32), self.own)
        around = self.around.reshape(-1, self.around.shape[-1]).astype(F32)
        start = jnp.maximum(row * rows - CONT_MOST, 0)
        whole = jnp.zeros((self.plan.row * rows + CONT_MOST, around.shape[1]), F32)
        whole = whole.at[:PROMPT].set(self.prompt.reshape(PROMPT, -1).astype(F32))
        near = jnp.where(row * rows < PROMPT, 0, around)
        near = lax.dynamic_slice_in_dim(whole, start, rows + 2 * CONT_MOST, 0) + near
        whole = lax.dynamic_update_slice_in_dim(whole, near, start, 0)
        return lax.psum_scatter(whole[: self.plan.row * rows], ROW, scatter_dimension=0, tiled=True)


def heads_mask(lanes, head):
    lane = lax.broadcasted_iota(jnp.int32, lanes, 1)
    return (lane >= head * HDIM) & (lane < (head + 1) * HDIM)


def nt(left, right):
    return lax.dot_general(left, right, (((1,), (1,)), ((), ())), preferred_element_type=F32)


def tn(left, right):
    return lax.dot_general(left, right, (((0,), (0,)), ((), ())), preferred_element_type=F32)


def pack_kernel(wo_ref, wi_ref, wu_ref, wq_ref, wk_ref, wv_ref, line_ref, early_ref, late_ref):
    step, width = wo_ref.shape
    early_ref[:step, :] = wq_ref[...]
    early_ref[step : step + 8, :] = line_ref[:8, :]
    early_ref[step + 8 : 2 * step + 8, :] = wk_ref[...]
    early_ref[2 * step + 8 :, :] = wv_ref[...]
    late_ref[: WIDE * step, :] = wu_ref[...]
    late_ref[WO * step : WI * step, :] = wo_ref[...]
    for i in range(WIDE):
        late_ref[(WI + i) * step : (WI + i + 1) * step, :] = wi_ref[:, i * width : (i + 1) * width]
    late_ref[(WI + WIDE) * step :, :] = line_ref[8:, :]


def pack_call(w_output, w_inner, w_outer, w_query, w_key, w_value, line):
    step, width = w_output.shape
    shape = lambda rows: jax.ShapeDtypeStruct((rows, width), BF)
    return pl.pallas_call(
        pack_kernel, out_shape=[shape(3 * step + 8), shape((WI + WIDE) * step + 8)], name="pack"
    )(w_output, w_inner, w_outer, w_query, w_key, w_value, line)


def attention_kernel(blocks, first, rows, places, *refs):
    spots = refs[:blocks]
    (near_ref, me_ref, own_ref, a0_ref, a1_ref, b0_ref, b1_ref, segq_ref, segk_ref,
     w_out, q_ref, kp_ref, vp_ref, kn_ref, vn_ref, ctx_ref, lse_ref,
     x_ref, w_ref, s_ref, vt_ref, out_ref, line_ref, bias_ref, sems, w_sems, o_sem) = refs[blocks:]
    near = near_ref[0]
    depth = own_ref.shape[1]
    owners = w_ref.shape[0]
    each = depth // owners
    part = q_ref.shape[1]

    def weights(act):
        @pl.loop(0, owners)
        def _(e):
            away = e ^ me_ref[0]
            for (bits, half), (zero, one), parts in (
                (places[0], (a0_ref, a1_ref), ((0, each, w_ref, 0), (each, 8, line_ref, 0))),
                (places[1], (b0_ref, b1_ref), ((0, 2 * each, w_ref, each),)),
            ):
                j = sum([((away // bit) & 1) * weight for bit, weight in bits])
                for which, source in enumerate((zero, one)):

                    @pl.when(((away // half) & 1) == which)
                    def _():
                        for k, (top, size, target, base) in enumerate(parts):
                            act(pltpu.make_async_copy(
                                source.at[j, pl.ds(top, size)], target.at[e, pl.ds(base, size)],
                                w_sems.at[2 * k if zero is a0_ref else 1, e],
                            ))

    @pl.when(pl.program_id(0) == 0)
    def _():
        copies = [
            pltpu.make_async_copy(spot, x_ref.at[pl.ds(i * rows, rows)], sems.at[i])
            for i, spot in enumerate(spots)
        ]
        weights(lambda c: c.start())
        for copy in copies:
            copy.start()
        weights(lambda c: c.wait())
        for copy in copies:
            copy.wait()
        pltpu.make_async_copy(w_ref, w_out, o_sem).start()
        line = line_ref[:, 0, :128]
        place = lax.broadcasted_iota(jnp.int32, (128, depth), 0)
        lane = lax.broadcasted_iota(jnp.int32, (128, depth), 1)
        mine = lax.broadcasted_iota(jnp.int32, (owners, depth), 0)
        mine = mine == lax.broadcasted_iota(jnp.int32, (owners, depth), 1) // each
        for i in range(2):
            spread = mm(line, jnp.where(place == lane % each + i * each, 1.0, 0.0).astype(BF))
            bias_ref[i : i + 1, :] = jnp.sum(jnp.where(mine, spread, 0.0), axis=0, keepdims=True)

    lanes = pl.ds(pl.multiple_of(pl.program_id(0) * part, part), part)
    wq, wk, wv = [
        w_ref[:, i * each : (i + 1) * each, lanes].reshape(depth, part) for i in (WQ, WK, WV)
    ]
    queries = (mm(own_ref[...], wq) + bias_ref[0:1, lanes]) * (HDIM**-0.5)
    q_ref[...] = queries.astype(BF)

    heads = part // HDIM
    q = q_ref[...]
    tall = x_ref.shape[0]

    def body(sets):
        for k_ref, v_ref, base, size, _ in sets:
            x = x_ref[base : base + size, :]
            k_ref[...] = mm(x, wk).astype(BF)
            v = (mm(x, wv) + bias_ref[1:2, lanes]).astype(BF)
            v_ref[...] = v
            vt_ref[:, base : base + size] = v.T
        for h in range(heads):
            q_h = jnp.where(heads_mask(q.shape, h), q, 0)
            peak = jnp.full((1, rows), MASK_FILL, F32)
            for k_ref, _, base, size, masked in sets:
                s = nt(k_ref[...], q_h)
                if masked:
                    s = jnp.where(segk_ref[...] == segq_ref[...], s, MASK_FILL)
                s_ref[h % 2, base : base + size, :] = s
                peak = jnp.maximum(peak, jnp.max(s, axis=0, keepdims=True))
            total, mixed = jnp.zeros((1, rows), F32), jnp.zeros((HDIM, rows), F32)
            for _, _, base, size, _ in sets:
                p = jnp.exp(s_ref[h % 2, base : base + size, :] - peak)
                total = total + jnp.sum(p, axis=0, keepdims=True)
                mixed = mixed + mm(vt_ref[h * HDIM : (h + 1) * HDIM, base : base + size], p.astype(BF))
            out_ref[h * HDIM : (h + 1) * HDIM, :] = mixed / total
            lse_ref[0, h : h + 1, :] = peak + jnp.log(total)

    prompt = (kp_ref, vp_ref, 0, PROMPT, False)

    @pl.when(near == 0)
    def _():
        body([prompt])

    @pl.when(near > 0)
    def _():
        body([prompt, (kn_ref, vn_ref, PROMPT, tall - PROMPT, True)])

    ctx_ref[...] = out_ref[...].T.astype(BF)

    @pl.when(pl.program_id(0) == pl.num_programs(0) - 1)
    def _():
        pltpu.make_async_copy(w_ref, w_out, o_sem).wait()


def attention_call(spots, first, near, me, own, pieces, places, segq, segk):
    rows, width = own.shape
    blocks = len(spots)
    tall = blocks * rows
    part = 256
    steps = width // part
    heads = part // HDIM
    cols = lambda depth: pl.BlockSpec((depth, part), lambda g: (0, g))
    flops = 2 * tall * width * width * 2 + 4 * tall * rows * width * 4
    owners = 2 * pieces[0].shape[0]
    each = width // owners
    return pl.pallas_call(
        functools.partial(attention_kernel, blocks, first, rows, places),
        grid=(steps,),
        in_specs=[pl.BlockSpec(memory_space=pl.ANY)] * blocks
        + [
            pl.BlockSpec(memory_space=pltpu.SMEM),
            pl.BlockSpec(memory_space=pltpu.SMEM),
            pl.BlockSpec((rows, width), lambda g: (0, 0)),
        ] + [pl.BlockSpec(memory_space=pl.ANY)] * 4 + [
            pl.BlockSpec((1, rows), lambda g: (0, 0)),
            pl.BlockSpec(segk.shape, lambda g: (0, 0)),
        ],
        out_specs=[
            pl.BlockSpec(memory_space=pl.ANY),
            cols(rows), cols(PROMPT), cols(PROMPT), cols(tall - PROMPT), cols(tall - PROMPT),
            cols(rows), pl.BlockSpec((1, 8, rows), lambda g: (g, 0, 0)),
        ],
        out_shape=[
            jax.ShapeDtypeStruct((owners, 3 * each, width), BF),
            jax.ShapeDtypeStruct((rows, width), BF),
            jax.ShapeDtypeStruct((PROMPT, width), BF),
            jax.ShapeDtypeStruct((PROMPT, width), BF),
            jax.ShapeDtypeStruct((tall - PROMPT, width), BF),
            jax.ShapeDtypeStruct((tall - PROMPT, width), BF),
            jax.ShapeDtypeStruct((rows, width), BF),
            jax.ShapeDtypeStruct((steps, 8, rows), F32),
        ],
        scratch_shapes=[
            pltpu.VMEM((tall, width), BF),
            pltpu.VMEM((owners, 3 * each, width), BF),
            pltpu.VMEM((2, tall, rows), F32),
            pltpu.VMEM((part, tall), BF),
            pltpu.VMEM((part, rows), F32),
            pltpu.VMEM((owners, 8, width), BF),
            pltpu.VMEM((8, width), F32),
            pltpu.SemaphoreType.DMA((blocks,)),
            pltpu.SemaphoreType.DMA((3, owners)),
            pltpu.SemaphoreType.DMA,
        ],
        compiler_params=pltpu.CompilerParams(vmem_limit_bytes=60 * 2**20),
        cost_estimate=pl.CostEstimate(
            flops=flops, bytes_accessed=12 * 2**20, transcendentals=tall * rows * 12
        ),
        name="attention",
    )(*spots, near, me, own, *pieces, segq, segk)


def halves(value, runs, core):
    depth = value.shape[0] // runs
    pick = lambda first: jnp.concatenate(
        [value[i * depth : (i + 1) * depth] for i in range(first, runs, 2)], 0
    )
    even, odd = pick(0), pick(1)
    return jnp.where(core == 0, odd, even), jnp.where(core == 0, even, odd)


def middle_kernel(wide, mapped, ctx_ref, own_ref, cot_ref, got_ref, vec_ref, bin_ref,
                  out_ref, h1_ref, gctx_ref, grads, sums_ref, sbin_ref,
                  first_ref, n1_ref, inv_ref, low_ref, pre_ref, cdf_ref, act_ref, acc_ref,
                  gffn_ref, glow_ref, lowt_ref, w_ref, out_buf, in_buf, wo_buf, sems, w_sems):
    step = pl.program_id(0)
    width = ctx_ref.shape[1]
    vec = lambda i: vec_ref[i : i + 1, :]
    mean = lambda v: jnp.sum(v, axis=-1, keepdims=True) * (1.0 / width)
    down = lambda v: jnp.sum(v, axis=0, keepdims=True)
    owners = got_ref.shape[0]
    each = width // owners
    some = owners // wide
    square = lambda value: value.reshape(width, width)
    rows_of = lambda place: pl.ds(pl.multiple_of(place * each, each), each)
    w_output = lambda ref: ref.at[:, rows_of(WO)]
    w_inner = lambda ref, at: ref.at[:, rows_of(WI + at)]
    w_outer = lambda ref, at: ref.at[pl.ds(at * some, some), pl.ds(0, wide * each)]

    def fetch_inner(at):
        return pltpu.make_async_copy(w_inner(got_ref, at), w_inner(w_ref, at), w_sems.at[0, at])

    def fetch_outer(at):
        return pltpu.make_async_copy(w_outer(got_ref, at), w_outer(w_ref, at), w_sems.at[1, at])

    def fetch_output():
        return pltpu.make_async_copy(w_output(got_ref), w_output(w_ref), w_sems.at[0, wide])

    def slot(group, i):
        return group % 2 * 16 + group // 2 * 8 + i % 2 * 4 + i // 2 if mapped else group * 8 + i

    def outer(at):
        turn = (2 * wide - 1 - at) % 2
        return [
            pltpu.make_async_copy(
                out_buf.at[turn, i], grads.at[slot(at, i), pl.ds(0, wide * each)], sems.at[turn, i]
            )
            for i in range(some)
        ]

    def inner(at):
        turn = (2 * wide - 1 - at) % 2
        top = pl.multiple_of((wide + 1 + at) * each, each)
        return [
            pltpu.make_async_copy(
                in_buf.at[turn, e], grads.at[slot(e // 8, e % 8), pl.ds(top, each)], sems.at[2 + turn, e]
            )
            for e in range(owners)
        ]

    def output():
        return [
            pltpu.make_async_copy(
                wo_buf.at[e], grads.at[slot(e // 8, e % 8), pl.ds(wide * each, each)], sems.at[4, e]
            )
            for e in range(owners)
        ]

    def start(copies):
        for copy in copies:
            copy.start()

    def wait(copies):
        for copy in copies:
            copy.wait()

    @pl.when(step == 0)
    def _():
        fetch_output().start()
        for at in range(wide):
            fetch_inner(at).start()
            fetch_outer(at).start()
        fetch_output().wait()
        hidden = own_ref[...].astype(F32) + mm(ctx_ref[...], square(w_output(w_ref)[...])) + vec(0)
        centred = hidden - mean(hidden)
        inverse = lax.rsqrt(mean(centred * centred) + NORM_EPS)
        normed = centred * inverse
        n1_ref[...] = normed
        inv_ref[...] = inverse
        first = normed * vec(1) + vec(2)
        first_ref[...] = first
        low_ref[...] = first.astype(BF)
        lowt_ref[...] = first.astype(BF).T

    @pl.when(step < wide)
    def _():
        chunk = pl.ds(pl.multiple_of(step * width, width), width)
        fetch_inner(step).wait()
        fetch_outer(step).wait()
        pre = mm(low_ref[...], square(w_inner(w_ref, step)[...])) + bin_ref[pl.ds(step, 1), :]
        cdf = 0.5 * (1.0 + lax.erf(pre * SQRT_HALF))
        act = (pre * cdf).astype(BF)
        pre_ref[:, chunk] = pre
        cdf_ref[:, chunk] = cdf
        act_ref[:, chunk] = act
        more = mm(act, square(w_outer(w_ref, step)[...]))

        @pl.when(step == 0)
        def _():
            acc_ref[...] = more

        @pl.when(step > 0)
        def _():
            acc_ref[...] += more

    @pl.when(step == wide - 1)
    def _():
        hidden = first_ref[...] + acc_ref[...] + vec(3)
        centred = hidden - mean(hidden)
        inverse = lax.rsqrt(mean(centred * centred) + NORM_EPS)
        normed = centred * inverse
        out_ref[...] = (normed * vec(4) + vec(5)).astype(BF)
        grad = cot_ref[...].astype(F32)
        sums_ref[0:1, :] = down(grad * normed)
        sums_ref[1:2, :] = down(grad)
        e = grad * vec(4)
        back = inverse * (e - mean(e) - normed * mean(e * normed))
        gffn_ref[...] = back
        low = back.astype(BF)
        glow_ref[...] = low
        sums_ref[2:3, :] = down(low.astype(F32))

    @pl.when(step >= wide)
    def _():
        at = 2 * wide - 1 - step
        chunk = pl.ds(pl.multiple_of(at * width, width), width)
        pre = pre_ref[:, chunk]
        slope = cdf_ref[:, chunk] + pre * jnp.exp(-0.5 * pre * pre) * INV_ROOT_TAU
        low = glow_ref[...]
        grad = (nt(low, square(w_outer(w_ref, at)[...])) * slope).astype(BF)
        sbin_ref[pl.ds(at, 1), :] = down(grad.astype(F32))
        turn = step % 2

        @pl.when(step >= wide + 2)
        def _():
            wait(outer(at + 2) + inner(at + 2))

        out_buf[turn] = tn(act_ref[:, chunk], low).astype(BF).reshape(some, wide * each, width)
        start(outer(at))
        in_buf[turn] = mm(lowt_ref[...], grad).astype(BF).reshape(owners, each, width)
        start(inner(at))
        gffn_ref[...] += nt(grad, square(w_inner(w_ref, at)[...]))

    @pl.when(step == 2 * wide - 1)
    def _():
        grad = gffn_ref[...]
        normed = n1_ref[...]
        sums_ref[3:4, :] = down(grad * normed)
        sums_ref[4:5, :] = down(grad)
        e = grad * vec(1)
        back = inv_ref[...] * (e - mean(e) - normed * mean(e * normed))
        h1_ref[...] = back
        low = back.astype(BF)
        sums_ref[5:6, :] = down(low.astype(F32))
        wo_buf[...] = tn(ctx_ref[...], low).astype(BF).reshape(owners, each, width)
        start(output())
        gctx = nt(low, square(w_output(w_ref)[...])).astype(BF)
        gctx_ref[...] = gctx
        sums_ref[6:7, :] = down(gctx.astype(F32))
        sums_ref[7:8, :] = jnp.zeros((1, width), F32)
        wait(outer(1) + inner(1) + outer(0) + inner(0) + output())


def middle_call(ctx, own, cot, got, vec, b_inner, mapped):
    rows, width = own.shape
    owners = got.shape[0]
    each = width // owners
    wide = WIDE
    whole = lambda shape: pl.BlockSpec(shape, lambda s: (0,) * len(shape))
    shape = jax.ShapeDtypeStruct
    return pl.pallas_call(
        functools.partial(middle_kernel, wide, mapped),
        grid=(2 * wide,),
        in_specs=[
            whole((rows, width)), whole((rows, width)), whole((rows, width)),
            pl.BlockSpec(memory_space=pl.ANY),
            whole((8, width)), whole((8, width)),
        ],
        out_specs=[
            whole((rows, width)), whole((rows, width)), whole((rows, width)),
            pl.BlockSpec(memory_space=pl.ANY),
            whole((8, width)), whole((8, width)),
        ],
        out_shape=[
            shape((rows, width), BF), shape((rows, width), F32), shape((rows, width), BF),
            shape((owners, (2 * wide + 1) * each, width), BF),
            shape((8, width), F32), shape((8, width), F32),
        ],
        scratch_shapes=[
            pltpu.VMEM((rows, width), F32), pltpu.VMEM((rows, width), F32), pltpu.VMEM((rows, 1), F32),
            pltpu.VMEM((rows, width), BF), pltpu.VMEM((rows, wide * width), F32),
            pltpu.VMEM((rows, wide * width), F32), pltpu.VMEM((rows, wide * width), BF),
            pltpu.VMEM((rows, width), F32), pltpu.VMEM((rows, width), F32),
            pltpu.VMEM((rows, width), BF), pltpu.VMEM((width, rows), BF),
            pltpu.VMEM((owners, (2 * wide + 1) * each, width), BF),
            pltpu.VMEM((2, owners // wide, wide * each, width), BF),
            pltpu.VMEM((2, owners, each, width), BF),
            pltpu.VMEM((owners, each, width), BF), pltpu.SemaphoreType.DMA((5, owners)),
            pltpu.SemaphoreType.DMA((2, wide + 1)),
        ],
        compiler_params=pltpu.CompilerParams(vmem_limit_bytes=60 * 2**20),
        cost_estimate=pl.CostEstimate(
            flops=2 * rows * width * width * (6 * wide + 3), bytes_accessed=32 * 2**20,
            transcendentals=2 * rows * width * wide,
        ),
        name="middle",
    )(ctx, own, cot, got, vec, b_inner)


def back_kernel(rows, bound, started, *refs):
    near_ref, gctx_ref, ctx_ref, q_ref, k_ref, v_ref, lse_ref, segq_ref, segk_ref = refs[:9]
    dk_ref, dv_ref, dq_ref, kt_ref, p_ref, ds_ref = refs[-6:]
    q, g = q_ref[...], gctx_ref[...]
    part = q.shape[1]
    heads = part // HDIM
    masks = [heads_mask(q.shape, h) for h in range(heads)]
    q_parts = [jnp.where(m, q, 0) for m in masks]
    g_parts = [jnp.where(m, g, 0) for m in masks]
    product = (g.astype(F32) * ctx_ref[...].astype(F32)).T
    inner = [
        jnp.sum(product[h * HDIM : (h + 1) * HDIM], axis=0, keepdims=True) for h in range(heads)
    ]

    def body():
        k, v = k_ref[...], v_ref[...]
        kt_ref[...] = k.T
        for h in range(heads):
            s = nt(k, q_parts[h])
            if bound is None:
                s = jnp.where(segk_ref[...] == segq_ref[...], s, MASK_FILL)
            p = jnp.exp(s - lse_ref[0, h : h + 1, :])
            across = slice(h * rows, (h + 1) * rows)
            ds = (p * (nt(v, g_parts[h]) - inner[h])).astype(BF)
            p_ref[:, across] = p.astype(BF)
            ds_ref[:, across] = ds
            mine = slice(h * HDIM, (h + 1) * HDIM)
            more = mm(kt_ref[mine, :], ds)
            dq_ref[mine, :] = refs[9][mine, :] + more if started else more
        dk_ref[...] = mm(ds_ref[...], jnp.concatenate(q_parts, 0)).astype(BF)
        dv_ref[...] = mm(p_ref[...], jnp.concatenate(g_parts, 0)).astype(BF)

    if bound is None:

        @pl.when(near_ref[0] == 0)
        def _():
            dq_ref[...] = refs[9][...]

        pl.when(near_ref[0] > 0)(body)
    else:
        body()


def back_call(start, steps, bound, near, gctx, ctx, q, k, v, lse, segq, segk, dq0=None, into=None):
    rows, width = q.shape
    tall = k.shape[0]
    part = 256
    cols = lambda depth: pl.BlockSpec((depth, part), lambda g: (0, start + g))
    whole = lambda shape: pl.BlockSpec(shape, lambda g: (0,) * len(shape))
    down = pl.BlockSpec((part, rows), lambda g: (start + g, 0))
    shape = jax.ShapeDtypeStruct
    extra = ([dq0] if dq0 is not None else []) + list(into or [])
    specs = ([down] if dq0 is not None else []) + [pl.BlockSpec(memory_space=pl.ANY)] * len(into or [])
    return pl.pallas_call(
        functools.partial(back_kernel, rows, bound, dq0 is not None),
        grid=(steps,),
        in_specs=[
            pl.BlockSpec(memory_space=pltpu.SMEM),
            cols(rows), cols(rows), cols(rows), cols(tall), cols(tall),
            pl.BlockSpec((1, 8, rows), lambda g: (start + g, 0, 0)),
            whole((1, rows)), whole(segk.shape),
        ] + specs,
        out_specs=[cols(tall), cols(tall), down],
        out_shape=[shape((tall, width), BF), shape((tall, width), BF), shape((width, rows), F32)],
        input_output_aliases={9 + i: i for i in range(3)} if into else {},
        scratch_shapes=[
            pltpu.VMEM((part, tall), BF),
            pltpu.VMEM((tall, part // HDIM * rows), BF),
            pltpu.VMEM((tall, part // HDIM * rows), BF),
        ],
        compiler_params=pltpu.CompilerParams(vmem_limit_bytes=60 * 2**20),
        cost_estimate=pl.CostEstimate(
            flops=2 * 10 * 2 * tall * rows * part * steps * 2,
            bytes_accessed=8 * tall * part * steps, transcendentals=tall * rows * 4 * steps,
        ),
        name="attention_back",
    )(near, gctx, ctx, q, k, v, lse, segq, segk, *extra)


def product_kernel(rows, bound, near_ref, dk_ref, dv_ref, wk_ref, wv_ref, gx_ref):
    @pl.when((pl.program_id(0) < near_ref[0]) | (bound is not None))
    def _():
        width = dk_ref.shape[1]
        wk, wv = wk_ref[...].reshape(width, width), wv_ref[...].reshape(width, width)
        gx_ref[0] = (nt(dk_ref[...], wk) + nt(dv_ref[...], wv)).astype(BF)


def product_call(bound, near, dk, dv, got, rows):
    tall, width = dk.shape
    owners, each = got.shape[0], width // got.shape[0]
    weight = lambda place: pl.BlockSpec((owners, each, width), lambda b: (0, place, 0))
    return pl.pallas_call(
        functools.partial(product_kernel, rows, bound),
        grid=(tall // rows,),
        in_specs=[
            pl.BlockSpec(memory_space=pltpu.SMEM),
            pl.BlockSpec((rows, width), lambda b: (b, 0)),
            pl.BlockSpec((rows, width), lambda b: (b, 0)),
            weight(WK), weight(WV),
        ],
        out_specs=pl.BlockSpec((1, rows, width), lambda b: (b, 0, 0)),
        out_shape=jax.ShapeDtypeStruct((tall // rows, rows, width), BF),
        compiler_params=pltpu.CompilerParams(vmem_limit_bytes=60 * 2**20),
        cost_estimate=pl.CostEstimate(
            flops=4 * tall * width * width, bytes_accessed=6 * tall * width, transcendentals=0
        ),
        name="token_product",
    )(near, dk, dv, got, got)


def weight_kernel(blocks, first, rows, runs, *refs):
    spots = refs[:blocks]
    (near_ref, core_ref, own_ref, dq_ref, wq_ref, h1_ref, dkp_ref, dvp_ref, dkn_ref, dvn_ref,
     send_ref, keep_ref, gown_ref, sums_ref, x_ref, xt_ref, sems) = refs[blocks:]
    core = core_ref[0]
    step = pl.program_id(0)

    @pl.when(step == 0)
    def _():
        copies = [
            pltpu.make_async_copy(spot, x_ref.at[pl.ds(i * rows, rows)], sems.at[i])
            for i, spot in enumerate(spots)
        ]
        for copy in copies:
            copy.start()
        gown_ref[...] = h1_ref[...]
        for i, copy in enumerate(copies):
            copy.wait()
            xt_ref[:, i * rows : (i + 1) * rows] = x_ref[i * rows : (i + 1) * rows, :].T

    scale = HDIM**-0.5
    dq = dq_ref[...].T.astype(BF)
    part = dq.shape[1]
    width = x_ref.shape[1]
    gown_ref[...] += nt(dq, wq_ref[...].reshape(width, part)) * scale
    half = send_ref.shape[0]
    each = width // (2 * half)

    def put(i, grad):
        away, here = halves(grad.astype(BF), runs, core)
        send_ref[:, i * each : (i + 1) * each, :] = away.reshape(half, each, part)
        keep_ref[:, i * each : (i + 1) * each, :] = here.reshape(half, each, part)

    put(WQ, tn(own_ref[...], dq) * scale)
    sums_ref[0:1, :] = jnp.sum(dq.astype(F32), axis=0, keepdims=True) * scale

    def body(near):
        for i, p_ref, n_ref in ((WK, dkp_ref, dkn_ref), (WV, dvp_ref, dvn_ref)):
            grad = mm(xt_ref[:, :PROMPT], p_ref[...])
            if near:
                grad = grad + mm(xt_ref[:, PROMPT:], n_ref[...])
            put(i, grad)

    pl.when(near_ref[0] == 0)(lambda: body(False))
    pl.when(near_ref[0] > 0)(lambda: body(True))
    sums_ref[1:8, :] = jnp.zeros((7, part), F32)


def weight_call(spots, first, near, own, dq, got, h1, dkp, dvp, dkn, dvn, core, runs):
    rows, width = own.shape
    blocks = len(spots)
    tall = blocks * rows
    part = 256
    steps = width // part
    cols = lambda depth, size=part: pl.BlockSpec((depth, size), lambda g: (0, g))
    whole = lambda shape: pl.BlockSpec(shape, lambda g: (0,) * len(shape))
    shape = jax.ShapeDtypeStruct
    owners, each = got.shape[0], width // got.shape[0]
    half = owners // 2
    slab = pl.BlockSpec((half, 3 * each, part), lambda g: (0, 0, g))
    return pl.pallas_call(
        functools.partial(weight_kernel, blocks, first, rows, runs),
        grid=(steps,),
        in_specs=[pl.BlockSpec(memory_space=pl.ANY)] * blocks
        + [
            pl.BlockSpec(memory_space=pltpu.SMEM),
            pl.BlockSpec(memory_space=pltpu.SMEM),
            whole((rows, width)), pl.BlockSpec((part, rows), lambda g: (g, 0)),
            pl.BlockSpec((owners, each, part), lambda g: (0, WQ, g)),
            whole((rows, width)), cols(PROMPT), cols(PROMPT), cols(tall - PROMPT), cols(tall - PROMPT),
        ],
        out_specs=[
            slab, slab, whole((rows, width)), cols(8),
        ],
        out_shape=[
            shape((half, 3 * each, width), BF), shape((half, 3 * each, width), BF),
            shape((rows, width), F32), shape((8, width), F32),
        ],
        scratch_shapes=[
            pltpu.VMEM((tall, width), BF), pltpu.VMEM((width, tall), BF), pltpu.SemaphoreType.DMA((blocks,)),
        ],
        compiler_params=pltpu.CompilerParams(vmem_limit_bytes=60 * 2**20),
        cost_estimate=pl.CostEstimate(
            flops=4 * tall * width * width, bytes_accessed=12 * tall * width, transcendentals=0
        ),
        name="weight_product",
    )(*spots, near, core, own, dq, got, h1, dkp, dvp, dkn, dvn)


def real_owners(grads, count, step, width):
    split = count // 32
    take = lambda v: v.reshape(32, -1, split, step, width).transpose(0, 2, 1, 3, 4).reshape(count, -1, width)
    outer, rest = grads[:, : 4 * split * step], grads[:, 4 * split * step :]
    return jnp.concatenate([outer.reshape(count, 4 * step, width), take(rest)], 1)


def solution(mesh):
    plan = Plan(mesh.shape["grp"], mesh.shape["row"])
    fine = Mesh(mesh.devices.reshape(plan.grp // 2, 2, 4, plan.row // 4), AXES)

    def per_device(
        tokens, cont_lengths, cotangent, w_query, w_key, w_value, w_output, w_inner, w_outer,
        bias_query, bias_value, bias_output, gain_first, shift_first, bias_inner, bias_outer,
        gain_second, shift_second,
    ):
        count = plan.count
        _, rows, width = tokens.shape
        step = w_query.shape[0]
        wide = w_inner.shape[1] // width
        own = tokens[0]

        early = (bias_query, bias_value)
        late = (bias_output, gain_first, shift_first, bias_outer, gain_second, shift_second, bias_inner)
        small = len(late) - 1

        def in_line(vectors):
            line, place = 0, 0
            for vector in vectors:
                size = vector.shape[0]
                line = line + jnp.pad(vector, (place, width - place - size))
                place += size
            return jnp.pad(line[None], ((0, 7), (0, 0)))

        line = jnp.concatenate([in_line(early), in_line(late)], 0)
        runs = plan.grp
        row = lax.axis_index(ROW)
        core = lax.axis_index("core").astype(jnp.int32).reshape(1)
        exchange = Tokens(plan, own)
        squares = (w_query, w_key, w_value)
        if step % 8 == 0:
            first_pack, pack = pack_call(w_output, w_inner, w_outer, *squares, line)
            got = lax.all_gather(pack, AXES, axis=0, tiled=True).reshape(count, -1, width)
            lines = got[:, (WI + WIDE) * step]

            def swaps(value, bits):
                masks = [0]
                for bit in bits:
                    masks = masks + [m ^ bit for m in masks]
                return [plan.swap(value, m) for m in masks[1:]]

            def stage(held, bit):
                return jnp.concatenate([held, plan.swap(held, bit)], 0)

            away = swaps(first_pack, plan.z)
            *away, same, beside = tie(*away, *exchange.stage_one())
            exchange.same, exchange.beside = same, beside
            cut = step + 8
            one = jnp.stack([v[:cut] for v in (first_pack, *away)])
            two = jnp.stack([v[cut:] for v in (first_pack, *away)])
            one, two = stage(one, plan.x[0]), stage(two, plan.y[0])
            one, two, *seen = tie(one, two, *exchange.stage_two())
            exchange.other, exchange.same_y, exchange.diagonal = seen
            one, two = stage(one, plan.y[0]), stage(two, plan.x[0])
            exchange.stage_three()
            one, exchange.other_y = tie(one, exchange.other_y)
            pieces = [one, plan.swap(one, plan.core[0]), two, plan.swap(two, plan.core[0])]
            order = lambda *bits: ([(bit, 1 << i) for i, bit in enumerate(bits)], plan.core[0])
            places = (
                order(*plan.z, plan.x[0], plan.y[0]),
                order(*plan.z, plan.y[0], plan.x[0]),
            )
            me = plan.me().astype(jnp.int32).reshape(1)
        else:
            inner_rows = [w_inner[:, i * width : (i + 1) * width] for i in range(wide)]
            pack = jnp.concatenate([w_outer, w_output, *inner_rows, *squares, line], 0)
            got = lax.all_gather(pack, AXES, axis=0, tiled=True).reshape(count, -1, width)
            lines = got[:, 12 * step + 8]
            cuts = [wide * step, (wide + 1) * step, (2 * wide + 1) * step, 12 * step]
            outer, output, inner, rest, marks = jnp.split(got, cuts, axis=1)
            apart = lambda v, n: v.reshape(count, n, step, width).transpose(1, 0, 2, 3)
            inner, rest = [
                v.reshape(v.shape[0], 32, width // 32, width).transpose(1, 0, 2, 3)
                for v in (apart(inner, wide), apart(rest, 3))
            ]
            got = jnp.concatenate([v.reshape(32, -1, width) for v in (outer, output, inner)], 1)
            pairs = marks[:, 0, : 2 * step].reshape(32, count // 32, 2, step).transpose(0, 2, 1, 3)
            pairs = jnp.pad(pairs.reshape(32, 1, -1), ((0, 0), (0, 7), (0, width - 2 * width // 32)))
            one = jnp.concatenate([rest[:, 0], pairs], 1)
            two = rest[:, 1:].reshape(32, -1, width)
            pieces = [one[:16], one[16:], two[:16], two[16:]]
            places = (([(1, 1), (2, 2), (4, 4), (8, 8)], 16),) * 2
            me = jnp.zeros((1,), jnp.int32)
        spots, near = exchange.spots()
        first_near = PROMPT // rows

        table = lines[:, : small * step].reshape(count, small, step).transpose(1, 0, 2)
        table = table.reshape(small, width).astype(F32)
        v_bin = lines[:, small * step : (small + wide) * step].reshape(wide, width).astype(F32)
        v_bin = jnp.pad(v_bin, ((0, 8 - wide), (0, 0)))
        segments = segment_ids(cont_lengths[0], plan.row * rows)
        seg_own = lax.dynamic_slice_in_dim(segments, row * rows, rows, 0)[None, :]
        seg_near = near_segments(plan, segments, rows)[:, None]
        near = near.astype(jnp.int32).reshape(1)

        squares, queries, keys_p, values_p, keys_n, values_n, context, log_total = attention_call(
            spots, first_near, near, me, own, pieces, places, seg_own, seg_near
        )
        vec = jnp.concatenate([table, jnp.zeros((2, width), F32)], 0)
        layer_out, grad_h1, grad_context, grads, sums, sums_bin = middle_call(
            context, own, cotangent[0], got, vec, v_bin, step % 8 == 0
        )
        if step % 8:
            grads = real_owners(grads, count, step, width)
            grads = grads.reshape(plan.grp // 2, 2, 4, plan.row // 4, -1, width)
            grads = grads.transpose(1, 0, 3, 2, 4, 5).reshape(count, -1, width)
        level = lambda value, axes: lax.psum_scatter(value, axes, scatter_dimension=0, tiled=True)
        grads = level(grads, "core")
        core_bit = plan.core[0]
        left = [1 << i for i in reversed(range(plan.bits)) if 1 << i != core_bit]
        parts = width // 256
        dkp, dvp, dqp = back_call(
            0, parts, first_near, near, grad_context, context, queries, keys_p, values_p, log_total,
            seg_own, seg_near,
        )
        shared_p = product_call(first_near, near, dkp, dvp, squares, rows)
        grads, shared_p, dqp = tie(grads, shared_p, dqp)
        grads = level(grads, ("x", "y"))
        returned = Return(plan, rows)
        returned.prompt_one(shared_p)
        dkn, dvn, dq = back_call(
            0, parts, None, near, grad_context, context, queries, keys_n, values_n, log_total,
            seg_own, seg_near, dqp,
        )
        send, keep, grad_own, sums_qkv = weight_call(
            spots, first_near, near, own, dq, squares, grad_h1, dkp, dvp, dkn, dvn, core, runs
        )
        send, keep, returned.same, returned.same_y, dkn, dvn = tie(
            send, keep, returned.same, returned.same_y, dkn, dvn
        )
        returned.prompt_two()
        shared_n = product_call(None, near, dkn, dvn, squares, rows)

        order = (6, 5, 3, 4, 2, 0, 1)
        small = len(early) + len(late) - 1
        d_table = jnp.concatenate([sums_qkv[:1]] + [sums[i : i + 1] for i in order], 0)
        d_lines = jnp.concatenate(
            [
                d_table.reshape(small, count, step).transpose(1, 0, 2).reshape(count, -1),
                sums_bin[:wide].reshape(count, wide * step),
            ],
            1,
        )
        d_lines = jnp.pad(d_lines, ((0, 0), (0, width - d_lines.shape[1])))[:, None].astype(BF)
        d_lines = jnp.pad(d_lines, ((0, 0), (0, 7), (0, 0)))
        place = core[0]
        pick = Reduce(plan, [])
        if step % 8:
            real = lambda v: v.reshape(16, 3, count // 32, step, width).transpose(0, 2, 1, 3, 4)
            send, keep = [real(v).reshape(count // 2, 3 * step, width) for v in (send, keep)]
        send = jnp.concatenate([send, pick.cut(d_lines, core_bit, 1 - place)], 1)
        keep = jnp.concatenate([keep, pick.cut(d_lines, core_bit, place)], 1)
        reduce = Reduce(plan, [keep, plan.swap(send, core_bit)], left)
        for bit in plan.x + plan.y + plan.z[::-1]:
            held = reduce.terms
            if bit == plan.x[0]:
                *held, returned.same = tie(*held, returned.same)
                returned.prompt_three()
            elif bit == plan.y[0]:
                *held, grads, shared_n, returned.back = tie(*held, grads, shared_n, returned.back)
                grads = level(grads, "z")
            elif bit == plan.z[-1]:
                *held, shared_n = tie(*held, shared_n)
                returned.near(shared_n)
            elif bit == plan.z[0]:
                *held, returned.own = tie(*held, returned.own)
            reduce.terms = list(held)
            reduce.stage(bit)
        o_ab = grads.reshape(-1, width).astype(F32)
        grad_tokens = grad_own + returned.total()
        o_first = reduce.result()
        o_line = o_first[3 * step]
        o_small = [o_line[i * step : (i + 1) * step] for i in range(small)]
        o_bin = o_line[small * step : (small + wide) * step]
        return (
            layer_out[None],
            grad_tokens.astype(BF)[None],
            o_first[:step],
            o_first[step : 2 * step],
            o_first[2 * step : 3 * step],
            o_ab[wide * step : (wide + 1) * step],
            jnp.concatenate([o_ab[i * step : (i + 1) * step] for i in range(wide + 1, 2 * wide + 1)], 1),
            o_ab[: wide * step],
            o_small[0],
            o_small[1],
            o_small[2],
            o_small[3],
            o_small[4],
            o_bin,
            o_small[5],
            o_small[6],
            o_small[7],
        )

    split = P(GRP, ROW, None)
    owned2, owned1 = P(AXES, None), P(AXES)
    in_specs = (split, P(GRP, None), split) + (owned2,) * 6 + (owned1,) * 9
    out_specs = (split, split) + (owned2,) * 6 + (owned1,) * 9
    return jax.shard_map(
        per_device, mesh=fine, in_specs=in_specs, out_specs=out_specs, check_vma=False
    )
```

```python
import functools

import jax
import jax.numpy as jnp
import numpy as np
from jax import lax
from jax.experimental import pallas as pl
from jax.experimental.pallas import tpu as pltpu
from jax.sharding import Mesh
from jax.sharding import PartitionSpec as P

HEADS = 12
HDIM = 64
PROMPT = 1024
CONT_MOST = 256
BF = jnp.bfloat16
F32 = jnp.float32

NORM_EPS = 1e-12
MASK_FILL = -1000000000.0
SQRT_HALF = 0.7071067811865476
INV_ROOT_TAU = 0.3989422804014327
AXES = ("x", "core", "z", "y")
GRP, ROW = AXES[:2], AXES[2:]
WIDE = 4
WO, WI = 4, 5
WQ, WK, WV = 0, 1, 2


def mm(left, right):
    return jnp.dot(left, right, preferred_element_type=F32)


def segment_ids(lengths, group_len):
    ends = jnp.cumsum(lengths)
    places = jnp.arange(group_len, dtype=jnp.int32)
    passed = jnp.sum(((places - PROMPT)[:, None] >= ends[None, :]).astype(jnp.int32), axis=-1)
    return jnp.where(places < PROMPT, 0, 1 + passed)


class Plan:
    def __init__(self, grp, row):
        self.grp, self.row, self.count = grp, row, grp * row
        y = row // 4
        bits = lambda base, size: [base << i for i in range(size.bit_length() - 1)]
        self.y, self.z = bits(1, y), bits(y, 4)
        self.core, self.x = bits(row, 2), bits(2 * row, grp // 2)
        self.bits = self.count.bit_length() - 1

    def swap(self, value, mask):
        return lax.ppermute(value, AXES, [(i, i ^ mask) for i in range(self.count)])

    def send(self, value, moves):
        pairs = [(g * self.row + a, g * self.row + b) for g in range(self.grp) for a, b in moves]
        return lax.ppermute(value, AXES, pairs)

    def me(self):
        return lax.axis_index(AXES)


class Reduce:
    def __init__(self, plan, terms, left=None):
        self.plan, self.terms = plan, list(terms)
        self.left = left or [1 << i for i in reversed(range(plan.bits))]

    def cut(self, term, bit, place):
        at = self.left.index(bit)
        high, low = 1 << at, 1 << (len(self.left) - at - 1)
        _, rows, width = term.shape
        term = term.reshape(high, 2, low * rows, width)
        return lax.dynamic_slice_in_dim(term, place, 1, 1).reshape(high * low, rows, width)

    def total(self, terms):
        return sum([t.astype(F32) for t in terms[1:]], terms[0].astype(F32))

    def stage(self, bit):
        place = (self.plan.me() // bit) & 1
        away = self.total([self.cut(t, bit, 1 - place) for t in self.terms]).astype(BF)
        here = [self.cut(t, bit, place) for t in self.terms]
        self.left = [b for b in self.left if b != bit]
        self.terms = here + [self.plan.swap(away, bit)]

    def result(self):
        return self.total(self.terms)[0]


def tie(*values):
    return lax.optimization_barrier(values)


class Tokens:
    def __init__(self, plan, own):
        self.plan, self.own = plan, own
        self.rows = own.shape[0]
        self.ready = plan.row == 8

    def stage_one(self):
        if self.ready:
            plan, own = self.plan, self.own
            across = plan.send(own, [(0, 4), (1, 5), (2, 6), (3, 7)])
            self.same = jnp.where(lax.axis_index(ROW) < 4, own, across)
            self.beside = plan.swap(own, 1)
            return [self.same, self.beside]
        return []

    def stage_two(self):
        if self.ready:
            plan = self.plan
            self.other = plan.swap(self.same, 2)
            self.same_y = plan.swap(self.same, 1)
            self.diagonal = plan.send(self.own, [(5, 6), (6, 5)])
            return [self.other, self.same_y, self.diagonal]
        return []

    def stage_three(self):
        if self.ready:
            self.other_y = self.plan.swap(self.same_y, 2)

    def spots(self):
        row, rows, own = lax.axis_index(ROW), self.rows, self.own
        if self.ready:
            near = jnp.where(row < 4, 0, jnp.where((row == 5) | (row == 6), 3, 2))
            return [
                self.same, self.other, self.same_y, self.other_y, own, self.beside, self.diagonal,
            ], near
        every = lax.all_gather(own, ROW, axis=0, tiled=True)
        start = jnp.maximum(row * rows - CONT_MOST, 0)
        padded = jnp.concatenate([every, jnp.zeros((CONT_MOST, own.shape[1]), own.dtype)], 0)
        near = lax.dynamic_slice_in_dim(padded, start, rows + 2 * CONT_MOST, 0)
        every = jnp.concatenate([every[:PROMPT], near], 0)
        spots = [every[i : i + rows] for i in range(0, every.shape[0], rows)]
        return spots, jnp.where(row * rows < PROMPT, 0, near.shape[0] // rows)


def near_segments(plan, segments, rows):
    row = lax.axis_index(ROW)
    if plan.row != 8:
        start = jnp.maximum(row * rows - CONT_MOST, 0)
        padded = jnp.concatenate([segments, jnp.full((CONT_MOST,), -1, jnp.int32)], 0)
        near = lax.dynamic_slice_in_dim(padded, start, rows + 2 * CONT_MOST, 0)
        return jnp.where((near == 0) | (row * rows < PROMPT), -1, near)
    pieces = []
    for block, valid in (
        (row, row >= 4),
        (row ^ 1, row >= 4),
        (11 - row, (row == 5) | (row == 6)),
    ):
        block = jnp.clip(block, 0, 7)
        ids = lax.dynamic_slice_in_dim(segments, block * rows, rows, 0)
        pieces.append(jnp.where(valid, ids, -1))
    return jnp.concatenate(pieces, 0)


class Return:
    def __init__(self, plan, rows):
        self.plan, self.rows = plan, rows

    def prompt_one(self, parts):
        self.prompt = self.same = self.same_y = self.own = self.back = parts
        if self.plan.row == 8:
            same, same_y = parts[0].astype(F32), parts[2].astype(F32)
            self.same_y = (same_y + self.plan.swap(parts[3], 2).astype(F32)).astype(BF)
            self.same = same + self.plan.swap(parts[1], 2).astype(F32)

    def prompt_two(self):
        if self.plan.row == 8:
            self.same = self.same + self.plan.swap(self.same_y, 1).astype(F32)

    def prompt_three(self):
        if self.plan.row == 8:
            self.back = self.plan.send(self.same.astype(BF), [(4, 0), (5, 1), (6, 2), (7, 3)])

    def near(self, parts):
        self.around = parts
        if self.plan.row == 8:
            own = parts[0].astype(F32) + self.plan.swap(parts[1], 1).astype(F32)
            self.own = own + self.plan.send(parts[2], [(5, 6), (6, 5)]).astype(F32)

    def total(self):
        row, rows = lax.axis_index(ROW), self.rows
        if self.plan.row == 8:
            return jnp.where(row < 4, self.same + self.back.astype(F32), self.own)
        around = self.around.reshape(-1, self.around.shape[-1]).astype(F32)
        start = jnp.maximum(row * rows - CONT_MOST, 0)
        whole = jnp.zeros((self.plan.row * rows + CONT_MOST, around.shape[1]), F32)
        whole = whole.at[:PROMPT].set(self.prompt.reshape(PROMPT, -1).astype(F32))
        near = jnp.where(row * rows < PROMPT, 0, around)
        near = lax.dynamic_slice_in_dim(whole, start, rows + 2 * CONT_MOST, 0) + near
        whole = lax.dynamic_update_slice_in_dim(whole, near, start, 0)
        return lax.psum_scatter(whole[: self.plan.row * rows], ROW, scatter_dimension=0, tiled=True)


def heads_mask(lanes, head):
    lane = lax.broadcasted_iota(jnp.int32, lanes, 1)
    return (lane >= head * HDIM) & (lane < (head + 1) * HDIM)


def nt(left, right):
    return lax.dot_general(left, right, (((1,), (1,)), ((), ())), preferred_element_type=F32)


def tn(left, right):
    return lax.dot_general(left, right, (((0,), (0,)), ((), ())), preferred_element_type=F32)


def pack_kernel(wo_ref, wi_ref, wu_ref, wq_ref, wk_ref, wv_ref, line_ref, early_ref, late_ref):
    step, width = wo_ref.shape
    early_ref[:step, :] = wq_ref[...]
    early_ref[step : step + 8, :] = line_ref[:8, :]
    early_ref[step + 8 : 2 * step + 8, :] = wk_ref[...]
    early_ref[2 * step + 8 :, :] = wv_ref[...]
    late_ref[: WIDE * step, :] = wu_ref[...]
    late_ref[WO * step : WI * step, :] = wo_ref[...]
    for i in range(WIDE):
        late_ref[(WI + i) * step : (WI + i + 1) * step, :] = wi_ref[:, i * width : (i + 1) * width]
    late_ref[(WI + WIDE) * step :, :] = line_ref[8:, :]


def pack_call(w_output, w_inner, w_outer, w_query, w_key, w_value, line):
    step, width = w_output.shape
    shape = lambda rows: jax.ShapeDtypeStruct((rows, width), BF)
    return pl.pallas_call(
        pack_kernel, out_shape=[shape(3 * step + 8), shape((WI + WIDE) * step + 8)], name="pack"
    )(w_output, w_inner, w_outer, w_query, w_key, w_value, line)


def attention_kernel(blocks, first, rows, places, *refs):
    spots = refs[:blocks]
    (near_ref, me_ref, own_ref, a0_ref, a1_ref, b0_ref, b1_ref, segq_ref, segk_ref,
     w_out, q_ref, kp_ref, vp_ref, kn_ref, vn_ref, ctx_ref, lse_ref,
     x_ref, w_ref, s_ref, vt_ref, out_ref, line_ref, bias_ref, sems, w_sems, o_sem) = refs[blocks:]
    near = near_ref[0]
    depth = own_ref.shape[1]
    owners = w_ref.shape[0]
    each = depth // owners
    part = q_ref.shape[1]

    def weights(act):
        @pl.loop(0, owners)
        def _(e):
            away = e ^ me_ref[0]
            for (bits, half), (zero, one), parts in (
                (places[0], (a0_ref, a1_ref), ((0, each, w_ref, 0), (each, 8, line_ref, 0), (each + 8, 8, w_ref, each))),
                (places[1], (b0_ref, b1_ref), ((0, 2 * each - 8, w_ref, each + 8),)),
            ):
                j = sum([((away // bit) & 1) * weight for bit, weight in bits])
                for which, source in enumerate((zero, one)):

                    @pl.when(((away // half) & 1) == which)
                    def _():
                        for k, (top, size, target, base) in enumerate(parts):
                            act(pltpu.make_async_copy(
                                source.at[j, pl.ds(top, size)], target.at[e, pl.ds(base, size)],
                                w_sems.at[k if zero is a0_ref else 3, e],
                            ))

    @pl.when(pl.program_id(0) == 0)
    def _():
        copies = [
            pltpu.make_async_copy(spot, x_ref.at[pl.ds(i * rows, rows)], sems.at[i])
            for i, spot in enumerate(spots)
        ]
        weights(lambda c: c.start())
        for copy in copies:
            copy.start()
        weights(lambda c: c.wait())
        for copy in copies:
            copy.wait()
        pltpu.make_async_copy(w_ref, w_out, o_sem).start()
        line = line_ref[:, 0, :128]
        place = lax.broadcasted_iota(jnp.int32, (128, depth), 0)
        lane = lax.broadcasted_iota(jnp.int32, (128, depth), 1)
        mine = lax.broadcasted_iota(jnp.int32, (owners, depth), 0)
        mine = mine == lax.broadcasted_iota(jnp.int32, (owners, depth), 1) // each
        for i in range(2):
            spread = mm(line, jnp.where(place == lane % each + i * each, 1.0, 0.0).astype(BF))
            bias_ref[i : i + 1, :] = jnp.sum(jnp.where(mine, spread, 0.0), axis=0, keepdims=True)

    lanes = pl.ds(pl.multiple_of(pl.program_id(0) * part, part), part)
    wq, wk, wv = [
        w_ref[:, i * each : (i + 1) * each, lanes].reshape(depth, part) for i in (WQ, WK, WV)
    ]
    queries = (mm(own_ref[...], wq) + bias_ref[0:1, lanes]) * (HDIM**-0.5)
    q_ref[...] = queries.astype(BF)

    heads = part // HDIM
    q = q_ref[...]
    tall = x_ref.shape[0]

    def body(sets):
        for k_ref, v_ref, base, size, _ in sets:
            x = x_ref[base : base + size, :]
            k_ref[...] = mm(x, wk).astype(BF)
            v = (mm(x, wv) + bias_ref[1:2, lanes]).astype(BF)
            v_ref[...] = v
            vt_ref[:, base : base + size] = v.T
        for h in range(heads):
            q_h = jnp.where(heads_mask(q.shape, h), q, 0)
            peak = jnp.full((1, rows), MASK_FILL, F32)
            for k_ref, _, base, size, masked in sets:
                s = nt(k_ref[...], q_h)
                if masked:
                    s = jnp.where(segk_ref[...] == segq_ref[...], s, MASK_FILL)
                s_ref[h % 2, base : base + size, :] = s
                peak = jnp.maximum(peak, jnp.max(s, axis=0, keepdims=True))
            total, mixed = jnp.zeros((1, rows), F32), jnp.zeros((HDIM, rows), F32)
            for _, _, base, size, _ in sets:
                p = jnp.exp(s_ref[h % 2, base : base + size, :] - peak)
                total = total + jnp.sum(p, axis=0, keepdims=True)
                mixed = mixed + mm(vt_ref[h * HDIM : (h + 1) * HDIM, base : base + size], p.astype(BF))
            out_ref[h * HDIM : (h + 1) * HDIM, :] = mixed / total
            lse_ref[0, h : h + 1, :] = peak + jnp.log(total)

    prompt = (kp_ref, vp_ref, 0, PROMPT, False)

    @pl.when(near == 0)
    def _():
        body([prompt])

    @pl.when(near > 0)
    def _():
        body([prompt, (kn_ref, vn_ref, PROMPT, tall - PROMPT, True)])

    ctx_ref[...] = out_ref[...].T.astype(BF)

    @pl.when(pl.program_id(0) == pl.num_programs(0) - 1)
    def _():
        pltpu.make_async_copy(w_ref, w_out, o_sem).wait()


def attention_call(spots, first, near, me, own, pieces, places, segq, segk):
    rows, width = own.shape
    blocks = len(spots)
    tall = blocks * rows
    part = 256
    steps = width // part
    heads = part // HDIM
    cols = lambda depth: pl.BlockSpec((depth, part), lambda g: (0, g))
    flops = 2 * tall * width * width * 2 + 4 * tall * rows * width * 4
    owners = 2 * pieces[0].shape[0]
    each = width // owners
    return pl.pallas_call(
        functools.partial(attention_kernel, blocks, first, rows, places),
        grid=(steps,),
        in_specs=[pl.BlockSpec(memory_space=pl.ANY)] * blocks
        + [
            pl.BlockSpec(memory_space=pltpu.SMEM),
            pl.BlockSpec(memory_space=pltpu.SMEM),
            pl.BlockSpec((rows, width), lambda g: (0, 0)),
        ] + [pl.BlockSpec(memory_space=pl.ANY)] * 4 + [
            pl.BlockSpec((1, rows), lambda g: (0, 0)),
            pl.BlockSpec(segk.shape, lambda g: (0, 0)),
        ],
        out_specs=[
            pl.BlockSpec(memory_space=pl.ANY),
            cols(rows), cols(PROMPT), cols(PROMPT), cols(tall - PROMPT), cols(tall - PROMPT),
            cols(rows), pl.BlockSpec((1, 8, rows), lambda g: (g, 0, 0)),
        ],
        out_shape=[
            jax.ShapeDtypeStruct((owners, 3 * each, width), BF),
            jax.ShapeDtypeStruct((rows, width), BF),
            jax.ShapeDtypeStruct((PROMPT, width), BF),
            jax.ShapeDtypeStruct((PROMPT, width), BF),
            jax.ShapeDtypeStruct((tall - PROMPT, width), BF),
            jax.ShapeDtypeStruct((tall - PROMPT, width), BF),
            jax.ShapeDtypeStruct((rows, width), BF),
            jax.ShapeDtypeStruct((steps, 8, rows), F32),
        ],
        scratch_shapes=[
            pltpu.VMEM((tall, width), BF),
            pltpu.VMEM((owners, 3 * each, width), BF),
            pltpu.VMEM((2, tall, rows), F32),
            pltpu.VMEM((part, tall), BF),
            pltpu.VMEM((part, rows), F32),
            pltpu.VMEM((owners, 8, width), BF),
            pltpu.VMEM((8, width), F32),
            pltpu.SemaphoreType.DMA((blocks,)),
            pltpu.SemaphoreType.DMA((4, owners)),
            pltpu.SemaphoreType.DMA,
        ],
        compiler_params=pltpu.CompilerParams(vmem_limit_bytes=60 * 2**20),
        cost_estimate=pl.CostEstimate(
            flops=flops, bytes_accessed=12 * 2**20, transcendentals=tall * rows * 12
        ),
        name="attention",
    )(*spots, near, me, own, *pieces, segq, segk)


def halves(value, runs, core):
    depth = value.shape[0] // runs
    pick = lambda first: jnp.concatenate(
        [value[i * depth : (i + 1) * depth] for i in range(first, runs, 2)], 0
    )
    even, odd = pick(0), pick(1)
    return jnp.where(core == 0, odd, even), jnp.where(core == 0, even, odd)


def middle_kernel(wide, mapped, ctx_ref, own_ref, cot_ref, got_ref, vec_ref, bin_ref,
                  out_ref, h1_ref, gctx_ref, grads, sums_ref, sbin_ref,
                  first_ref, n1_ref, inv_ref, low_ref, pre_ref, cdf_ref, act_ref, acc_ref,
                  gffn_ref, glow_ref, lowt_ref, w_ref, out_buf, in_buf, wo_buf, sems, w_sems):
    step = pl.program_id(0)
    width = ctx_ref.shape[1]
    vec = lambda i: vec_ref[i : i + 1, :]
    mean = lambda v: jnp.sum(v, axis=-1, keepdims=True) * (1.0 / width)
    down = lambda v: jnp.sum(v, axis=0, keepdims=True)
    owners = got_ref.shape[0]
    each = width // owners
    some = owners // wide
    square = lambda value: value.reshape(width, width)
    rows_of = lambda place: pl.ds(pl.multiple_of(place * each, each), each)
    w_output = lambda ref: ref.at[:, rows_of(WO)]
    w_inner = lambda ref, at: ref.at[:, rows_of(WI + at)]
    w_outer = lambda ref, at: ref.at[pl.ds(at * some, some), pl.ds(0, wide * each)]

    def fetch_inner(at):
        return pltpu.make_async_copy(w_inner(got_ref, at), w_inner(w_ref, at), w_sems.at[0, at])

    def fetch_outer(at):
        return pltpu.make_async_copy(w_outer(got_ref, at), w_outer(w_ref, at), w_sems.at[1, at])

    def fetch_output():
        return pltpu.make_async_copy(w_output(got_ref), w_output(w_ref), w_sems.at[0, wide])

    def slot(group, i):
        return group % 2 * 16 + group // 2 * 8 + i % 2 * 4 + i // 2 if mapped else group * 8 + i

    def outer(at):
        turn = (2 * wide - 1 - at) % 2
        return [
            pltpu.make_async_copy(
                out_buf.at[turn, i], grads.at[slot(at, i), pl.ds(0, wide * each)], sems.at[turn, i]
            )
            for i in range(some)
        ]

    def inner(at):
        turn = (2 * wide - 1 - at) % 2
        top = pl.multiple_of((wide + 1 + at) * each, each)
        return [
            pltpu.make_async_copy(
                in_buf.at[turn, e], grads.at[slot(e // 8, e % 8), pl.ds(top, each)], sems.at[2 + turn, e]
            )
            for e in range(owners)
        ]

    def output():
        return [
            pltpu.make_async_copy(
                wo_buf.at[e], grads.at[slot(e // 8, e % 8), pl.ds(wide * each, each)], sems.at[4, e]
            )
            for e in range(owners)
        ]

    def start(copies):
        for copy in copies:
            copy.start()

    def wait(copies):
        for copy in copies:
            copy.wait()

    @pl.when(step == 0)
    def _():
        fetch_output().start()
        for at in range(wide):
            fetch_inner(at).start()
            fetch_outer(at).start()
        fetch_output().wait()
        hidden = own_ref[...].astype(F32) + mm(ctx_ref[...], square(w_output(w_ref)[...])) + vec(0)
        centred = hidden - mean(hidden)
        inverse = lax.rsqrt(mean(centred * centred) + NORM_EPS)
        normed = centred * inverse
        n1_ref[...] = normed
        inv_ref[...] = inverse
        first = normed * vec(1) + vec(2)
        first_ref[...] = first
        low_ref[...] = first.astype(BF)
        lowt_ref[...] = first.astype(BF).T

    @pl.when(step < wide)
    def _():
        chunk = pl.ds(pl.multiple_of(step * width, width), width)
        fetch_inner(step).wait()
        fetch_outer(step).wait()
        pre = mm(low_ref[...], square(w_inner(w_ref, step)[...])) + bin_ref[pl.ds(step, 1), :]
        cdf = 0.5 * (1.0 + lax.erf(pre * SQRT_HALF))
        act = (pre * cdf).astype(BF)
        pre_ref[:, chunk] = pre
        cdf_ref[:, chunk] = cdf
        act_ref[:, chunk] = act
        more = mm(act, square(w_outer(w_ref, step)[...]))

        @pl.when(step == 0)
        def _():
            acc_ref[...] = more

        @pl.when(step > 0)
        def _():
            acc_ref[...] += more

    @pl.when(step == wide - 1)
    def _():
        hidden = first_ref[...] + acc_ref[...] + vec(3)
        centred = hidden - mean(hidden)
        inverse = lax.rsqrt(mean(centred * centred) + NORM_EPS)
        normed = centred * inverse
        out_ref[...] = (normed * vec(4) + vec(5)).astype(BF)
        grad = cot_ref[...].astype(F32)
        sums_ref[0:1, :] = down(grad * normed)
        sums_ref[1:2, :] = down(grad)
        e = grad * vec(4)
        back = inverse * (e - mean(e) - normed * mean(e * normed))
        gffn_ref[...] = back
        low = back.astype(BF)
        glow_ref[...] = low
        sums_ref[2:3, :] = down(low.astype(F32))

    @pl.when(step >= wide)
    def _():
        at = 2 * wide - 1 - step
        chunk = pl.ds(pl.multiple_of(at * width, width), width)
        pre = pre_ref[:, chunk]
        slope = cdf_ref[:, chunk] + pre * jnp.exp(-0.5 * pre * pre) * INV_ROOT_TAU
        low = glow_ref[...]
        grad = (nt(low, square(w_outer(w_ref, at)[...])) * slope).astype(BF)
        sbin_ref[pl.ds(at, 1), :] = down(grad.astype(F32))
        turn = step % 2

        @pl.when(step >= wide + 2)
        def _():
            wait(outer(at + 2) + inner(at + 2))

        out_buf[turn] = tn(act_ref[:, chunk], low).astype(BF).reshape(some, wide * each, width)
        start(outer(at))
        in_buf[turn] = mm(lowt_ref[...], grad).astype(BF).reshape(owners, each, width)
        start(inner(at))
        gffn_ref[...] += nt(grad, square(w_inner(w_ref, at)[...]))

    @pl.when(step == 2 * wide - 1)
    def _():
        grad = gffn_ref[...]
        normed = n1_ref[...]
        sums_ref[3:4, :] = down(grad * normed)
        sums_ref[4:5, :] = down(grad)
        e = grad * vec(1)
        back = inv_ref[...] * (e - mean(e) - normed * mean(e * normed))
        h1_ref[...] = back
        low = back.astype(BF)
        sums_ref[5:6, :] = down(low.astype(F32))
        wo_buf[...] = tn(ctx_ref[...], low).astype(BF).reshape(owners, each, width)
        start(output())
        gctx = nt(low, square(w_output(w_ref)[...])).astype(BF)
        gctx_ref[...] = gctx
        sums_ref[6:7, :] = down(gctx.astype(F32))
        sums_ref[7:8, :] = jnp.zeros((1, width), F32)
        wait(outer(1) + inner(1) + outer(0) + inner(0) + output())


def middle_call(ctx, own, cot, got, vec, b_inner, mapped):
    rows, width = own.shape
    owners = got.shape[0]
    each = width // owners
    wide = WIDE
    whole = lambda shape: pl.BlockSpec(shape, lambda s: (0,) * len(shape))
    shape = jax.ShapeDtypeStruct
    return pl.pallas_call(
        functools.partial(middle_kernel, wide, mapped),
        grid=(2 * wide,),
        in_specs=[
            whole((rows, width)), whole((rows, width)), whole((rows, width)),
            pl.BlockSpec(memory_space=pl.ANY),
            whole((8, width)), whole((8, width)),
        ],
        out_specs=[
            whole((rows, width)), whole((rows, width)), whole((rows, width)),
            pl.BlockSpec(memory_space=pl.ANY),
            whole((8, width)), whole((8, width)),
        ],
        out_shape=[
            shape((rows, width), BF), shape((rows, width), F32), shape((rows, width), BF),
            shape((owners, (2 * wide + 1) * each, width), BF),
            shape((8, width), F32), shape((8, width), F32),
        ],
        scratch_shapes=[
            pltpu.VMEM((rows, width), F32), pltpu.VMEM((rows, width), F32), pltpu.VMEM((rows, 1), F32),
            pltpu.VMEM((rows, width), BF), pltpu.VMEM((rows, wide * width), F32),
            pltpu.VMEM((rows, wide * width), F32), pltpu.VMEM((rows, wide * width), BF),
            pltpu.VMEM((rows, width), F32), pltpu.VMEM((rows, width), F32),
            pltpu.VMEM((rows, width), BF), pltpu.VMEM((width, rows), BF),
            pltpu.VMEM((owners, (2 * wide + 1) * each, width), BF),
            pltpu.VMEM((2, owners // wide, wide * each, width), BF),
            pltpu.VMEM((2, owners, each, width), BF),
            pltpu.VMEM((owners, each, width), BF), pltpu.SemaphoreType.DMA((5, owners)),
            pltpu.SemaphoreType.DMA((2, wide + 1)),
        ],
        compiler_params=pltpu.CompilerParams(vmem_limit_bytes=60 * 2**20),
        cost_estimate=pl.CostEstimate(
            flops=2 * rows * width * width * (6 * wide + 3), bytes_accessed=32 * 2**20,
            transcendentals=2 * rows * width * wide,
        ),
        name="middle",
    )(ctx, own, cot, got, vec, b_inner)


def back_kernel(rows, bound, started, *refs):
    near_ref, gctx_ref, ctx_ref, q_ref, k_ref, v_ref, lse_ref, segq_ref, segk_ref = refs[:9]
    dk_ref, dv_ref, dq_ref, kt_ref, p_ref, ds_ref = refs[-6:]
    q, g = q_ref[...], gctx_ref[...]
    part = q.shape[1]
    heads = part // HDIM
    masks = [heads_mask(q.shape, h) for h in range(heads)]
    q_parts = [jnp.where(m, q, 0) for m in masks]
    g_parts = [jnp.where(m, g, 0) for m in masks]
    product = (g.astype(F32) * ctx_ref[...].astype(F32)).T
    inner = [
        jnp.sum(product[h * HDIM : (h + 1) * HDIM], axis=0, keepdims=True) for h in range(heads)
    ]

    def body():
        k, v = k_ref[...], v_ref[...]
        kt_ref[...] = k.T
        for h in range(heads):
            s = nt(k, q_parts[h])
            if bound is None:
                s = jnp.where(segk_ref[...] == segq_ref[...], s, MASK_FILL)
            p = jnp.exp(s - lse_ref[0, h : h + 1, :])
            across = slice(h * rows, (h + 1) * rows)
            ds = (p * (nt(v, g_parts[h]) - inner[h])).astype(BF)
            p_ref[:, across] = p.astype(BF)
            ds_ref[:, across] = ds
            mine = slice(h * HDIM, (h + 1) * HDIM)
            more = mm(kt_ref[mine, :], ds)
            dq_ref[mine, :] = refs[9][mine, :] + more if started else more
        dk_ref[...] = mm(ds_ref[...], jnp.concatenate(q_parts, 0)).astype(BF)
        dv_ref[...] = mm(p_ref[...], jnp.concatenate(g_parts, 0)).astype(BF)

    if bound is None:

        @pl.when(near_ref[0] == 0)
        def _():
            dq_ref[...] = refs[9][...]

        pl.when(near_ref[0] > 0)(body)
    else:
        body()


def back_call(start, steps, bound, near, gctx, ctx, q, k, v, lse, segq, segk, dq0=None, into=None):
    rows, width = q.shape
    tall = k.shape[0]
    part = 256
    cols = lambda depth: pl.BlockSpec((depth, part), lambda g: (0, start + g))
    whole = lambda shape: pl.BlockSpec(shape, lambda g: (0,) * len(shape))
    down = pl.BlockSpec((part, rows), lambda g: (start + g, 0))
    shape = jax.ShapeDtypeStruct
    extra = ([dq0] if dq0 is not None else []) + list(into or [])
    specs = ([down] if dq0 is not None else []) + [pl.BlockSpec(memory_space=pl.ANY)] * len(into or [])
    return pl.pallas_call(
        functools.partial(back_kernel, rows, bound, dq0 is not None),
        grid=(steps,),
        in_specs=[
            pl.BlockSpec(memory_space=pltpu.SMEM),
            cols(rows), cols(rows), cols(rows), cols(tall), cols(tall),
            pl.BlockSpec((1, 8, rows), lambda g: (start + g, 0, 0)),
            whole((1, rows)), whole(segk.shape),
        ] + specs,
        out_specs=[cols(tall), cols(tall), down],
        out_shape=[shape((tall, width), BF), shape((tall, width), BF), shape((width, rows), F32)],
        input_output_aliases={9 + i: i for i in range(3)} if into else {},
        scratch_shapes=[
            pltpu.VMEM((part, tall), BF),
            pltpu.VMEM((tall, part // HDIM * rows), BF),
            pltpu.VMEM((tall, part // HDIM * rows), BF),
        ],
        compiler_params=pltpu.CompilerParams(vmem_limit_bytes=60 * 2**20),
        cost_estimate=pl.CostEstimate(
            flops=2 * 10 * 2 * tall * rows * part * steps * 2,
            bytes_accessed=8 * tall * part * steps, transcendentals=tall * rows * 4 * steps,
        ),
        name="attention_back",
    )(near, gctx, ctx, q, k, v, lse, segq, segk, *extra)


def product_kernel(rows, bound, near_ref, dk_ref, dv_ref, wk_ref, wv_ref, gx_ref):
    @pl.when((pl.program_id(0) < near_ref[0]) | (bound is not None))
    def _():
        width = dk_ref.shape[1]
        wk, wv = wk_ref[...].reshape(width, width), wv_ref[...].reshape(width, width)
        gx_ref[0] = (nt(dk_ref[...], wk) + nt(dv_ref[...], wv)).astype(BF)


def product_call(bound, near, dk, dv, got, rows):
    tall, width = dk.shape
    owners, each = got.shape[0], width // got.shape[0]
    weight = lambda place: pl.BlockSpec((owners, each, width), lambda b: (0, place, 0))
    return pl.pallas_call(
        functools.partial(product_kernel, rows, bound),
        grid=(tall // rows,),
        in_specs=[
            pl.BlockSpec(memory_space=pltpu.SMEM),
            pl.BlockSpec((rows, width), lambda b: (b, 0)),
            pl.BlockSpec((rows, width), lambda b: (b, 0)),
            weight(WK), weight(WV),
        ],
        out_specs=pl.BlockSpec((1, rows, width), lambda b: (b, 0, 0)),
        out_shape=jax.ShapeDtypeStruct((tall // rows, rows, width), BF),
        compiler_params=pltpu.CompilerParams(vmem_limit_bytes=60 * 2**20),
        cost_estimate=pl.CostEstimate(
            flops=4 * tall * width * width, bytes_accessed=6 * tall * width, transcendentals=0
        ),
        name="token_product",
    )(near, dk, dv, got, got)


def weight_kernel(blocks, first, rows, runs, *refs):
    spots = refs[:blocks]
    (near_ref, core_ref, own_ref, dq_ref, wq_ref, h1_ref, dkp_ref, dvp_ref, dkn_ref, dvn_ref,
     send_ref, keep_ref, gown_ref, sums_ref, x_ref, xt_ref, sems) = refs[blocks:]
    core = core_ref[0]
    step = pl.program_id(0)

    @pl.when(step == 0)
    def _():
        copies = [
            pltpu.make_async_copy(spot, x_ref.at[pl.ds(i * rows, rows)], sems.at[i])
            for i, spot in enumerate(spots)
        ]
        for copy in copies:
            copy.start()
        gown_ref[...] = h1_ref[...]
        for i, copy in enumerate(copies):
            copy.wait()
            xt_ref[:, i * rows : (i + 1) * rows] = x_ref[i * rows : (i + 1) * rows, :].T

    scale = HDIM**-0.5
    dq = dq_ref[...].T.astype(BF)
    part = dq.shape[1]
    width = x_ref.shape[1]
    gown_ref[...] += nt(dq, wq_ref[...].reshape(width, part)) * scale
    half = send_ref.shape[0]
    each = width // (2 * half)

    def put(i, grad):
        away, here = halves(grad.astype(BF), runs, core)
        send_ref[:, i * each : (i + 1) * each, :] = away.reshape(half, each, part)
        keep_ref[:, i * each : (i + 1) * each, :] = here.reshape(half, each, part)

    put(WQ, tn(own_ref[...], dq) * scale)
    sums_ref[0:1, :] = jnp.sum(dq.astype(F32), axis=0, keepdims=True) * scale

    def body(near):
        for i, p_ref, n_ref in ((WK, dkp_ref, dkn_ref), (WV, dvp_ref, dvn_ref)):
            grad = mm(xt_ref[:, :PROMPT], p_ref[...])
            if near:
                grad = grad + mm(xt_ref[:, PROMPT:], n_ref[...])
            put(i, grad)

    pl.when(near_ref[0] == 0)(lambda: body(False))
    pl.when(near_ref[0] > 0)(lambda: body(True))
    sums_ref[1:8, :] = jnp.zeros((7, part), F32)


def weight_call(spots, first, near, own, dq, got, h1, dkp, dvp, dkn, dvn, core, runs):
    rows, width = own.shape
    blocks = len(spots)
    tall = blocks * rows
    part = 256
    steps = width // part
    cols = lambda depth, size=part: pl.BlockSpec((depth, size), lambda g: (0, g))
    whole = lambda shape: pl.BlockSpec(shape, lambda g: (0,) * len(shape))
    shape = jax.ShapeDtypeStruct
    owners, each = got.shape[0], width // got.shape[0]
    half = owners // 2
    slab = pl.BlockSpec((half, 3 * each, part), lambda g: (0, 0, g))
    return pl.pallas_call(
        functools.partial(weight_kernel, blocks, first, rows, runs),
        grid=(steps,),
        in_specs=[pl.BlockSpec(memory_space=pl.ANY)] * blocks
        + [
            pl.BlockSpec(memory_space=pltpu.SMEM),
            pl.BlockSpec(memory_space=pltpu.SMEM),
            whole((rows, width)), pl.BlockSpec((part, rows), lambda g: (g, 0)),
            pl.BlockSpec((owners, each, part), lambda g: (0, WQ, g)),
            whole((rows, width)), cols(PROMPT), cols(PROMPT), cols(tall - PROMPT), cols(tall - PROMPT),
        ],
        out_specs=[
            slab, slab, whole((rows, width)), cols(8),
        ],
        out_shape=[
            shape((half, 3 * each, width), BF), shape((half, 3 * each, width), BF),
            shape((rows, width), F32), shape((8, width), F32),
        ],
        scratch_shapes=[
            pltpu.VMEM((tall, width), BF), pltpu.VMEM((width, tall), BF), pltpu.SemaphoreType.DMA((blocks,)),
        ],
        compiler_params=pltpu.CompilerParams(vmem_limit_bytes=60 * 2**20),
        cost_estimate=pl.CostEstimate(
            flops=4 * tall * width * width, bytes_accessed=12 * tall * width, transcendentals=0
        ),
        name="weight_product",
    )(*spots, near, core, own, dq, got, h1, dkp, dvp, dkn, dvn)


def real_owners(grads, count, step, width):
    split = count // 32
    take = lambda v: v.reshape(32, -1, split, step, width).transpose(0, 2, 1, 3, 4).reshape(count, -1, width)
    outer, rest = grads[:, : 4 * split * step], grads[:, 4 * split * step :]
    return jnp.concatenate([outer.reshape(count, 4 * step, width), take(rest)], 1)


def solution(mesh):
    plan = Plan(mesh.shape["grp"], mesh.shape["row"])
    fine = Mesh(mesh.devices.reshape(plan.grp // 2, 2, 4, plan.row // 4), AXES)

    def per_device(
        tokens, cont_lengths, cotangent, w_query, w_key, w_value, w_output, w_inner, w_outer,
        bias_query, bias_value, bias_output, gain_first, shift_first, bias_inner, bias_outer,
        gain_second, shift_second,
    ):
        count = plan.count
        _, rows, width = tokens.shape
        step = w_query.shape[0]
        wide = w_inner.shape[1] // width
        own = tokens[0]

        early = (bias_query, bias_value)
        late = (bias_output, gain_first, shift_first, bias_outer, gain_second, shift_second, bias_inner)
        small = len(late) - 1

        def in_line(vectors):
            line, place = 0, 0
            for vector in vectors:
                size = vector.shape[0]
                line = line + jnp.pad(vector, (place, width - place - size))
                place += size
            return jnp.pad(line[None], ((0, 7), (0, 0)))

        line = jnp.concatenate([in_line(early), in_line(late)], 0)
        runs = plan.grp
        row = lax.axis_index(ROW)
        core = lax.axis_index("core").astype(jnp.int32).reshape(1)
        exchange = Tokens(plan, own)
        squares = (w_query, w_key, w_value)
        if step % 8 == 0:
            first_pack, pack = pack_call(w_output, w_inner, w_outer, *squares, line)
            got = lax.all_gather(pack, AXES, axis=0, tiled=True).reshape(count, -1, width)
            lines = got[:, (WI + WIDE) * step]

            def swaps(value, bits):
                masks = [0]
                for bit in bits:
                    masks = masks + [m ^ bit for m in masks]
                return [plan.swap(value, m) for m in masks[1:]]

            def stage(held, bit):
                return jnp.concatenate([held, plan.swap(held, bit)], 0)

            away = swaps(first_pack, plan.z)
            *away, same, beside = tie(*away, *exchange.stage_one())
            exchange.same, exchange.beside = same, beside
            cut = step + 16
            one = jnp.stack([v[:cut] for v in (first_pack, *away)])
            two = jnp.stack([v[cut:] for v in (first_pack, *away)])
            one, two = stage(one, plan.x[0]), stage(two, plan.y[0])
            one, two, *seen = tie(one, two, *exchange.stage_two())
            exchange.other, exchange.same_y, exchange.diagonal = seen
            one, two = stage(one, plan.y[0]), stage(two, plan.x[0])
            exchange.stage_three()
            one, exchange.other_y = tie(one, exchange.other_y)
            pieces = [one, plan.swap(one, plan.core[0]), two, plan.swap(two, plan.core[0])]
            order = lambda *bits: ([(bit, 1 << i) for i, bit in enumerate(bits)], plan.core[0])
            places = (
                order(*plan.z, plan.x[0], plan.y[0]),
                order(*plan.z, plan.y[0], plan.x[0]),
            )
            me = plan.me().astype(jnp.int32).reshape(1)
        else:
            inner_rows = [w_inner[:, i * width : (i + 1) * width] for i in range(wide)]
            pack = jnp.concatenate([w_outer, w_output, *inner_rows, *squares, line], 0)
            got = lax.all_gather(pack, AXES, axis=0, tiled=True).reshape(count, -1, width)
            lines = got[:, 12 * step + 8]
            cuts = [wide * step, (wide + 1) * step, (2 * wide + 1) * step, 12 * step]
            outer, output, inner, rest, marks = jnp.split(got, cuts, axis=1)
            apart = lambda v, n: v.reshape(count, n, step, width).transpose(1, 0, 2, 3)
            inner, rest = [
                v.reshape(v.shape[0], 32, width // 32, width).transpose(1, 0, 2, 3)
                for v in (apart(inner, wide), apart(rest, 3))
            ]
            got = jnp.concatenate([v.reshape(32, -1, width) for v in (outer, output, inner)], 1)
            pairs = marks[:, 0, : 2 * step].reshape(32, count // 32, 2, step).transpose(0, 2, 1, 3)
            pairs = jnp.pad(pairs.reshape(32, 1, -1), ((0, 0), (0, 7), (0, width - 2 * width // 32)))
            one = jnp.concatenate([rest[:, 0], pairs, rest[:, 1, :8]], 1)
            two = jnp.concatenate([rest[:, 1, 8:], rest[:, 2]], 1)
            pieces = [one[:16], one[16:], two[:16], two[16:]]
            places = (([(1, 1), (2, 2), (4, 4), (8, 8)], 16),) * 2
            me = jnp.zeros((1,), jnp.int32)
        spots, near = exchange.spots()
        first_near = PROMPT // rows

        table = lines[:, : small * step].reshape(count, small, step).transpose(1, 0, 2)
        table = table.reshape(small, width).astype(F32)
        v_bin = lines[:, small * step : (small + wide) * step].reshape(wide, width).astype(F32)
        v_bin = jnp.pad(v_bin, ((0, 8 - wide), (0, 0)))
        segments = segment_ids(cont_lengths[0], plan.row * rows)
        seg_own = lax.dynamic_slice_in_dim(segments, row * rows, rows, 0)[None, :]
        seg_near = near_segments(plan, segments, rows)[:, None]
        near = near.astype(jnp.int32).reshape(1)

        squares, queries, keys_p, values_p, keys_n, values_n, context, log_total = attention_call(
            spots, first_near, near, me, own, pieces, places, seg_own, seg_near
        )
        vec = jnp.concatenate([table, jnp.zeros((2, width), F32)], 0)
        layer_out, grad_h1, grad_context, grads, sums, sums_bin = middle_call(
            context, own, cotangent[0], got, vec, v_bin, step % 8 == 0
        )
        if step % 8:
            grads = real_owners(grads, count, step, width)
            grads = grads.reshape(plan.grp // 2, 2, 4, plan.row // 4, -1, width)
            grads = grads.transpose(1, 0, 3, 2, 4, 5).reshape(count, -1, width)
        level = lambda value, axes: lax.psum_scatter(value, axes, scatter_dimension=0, tiled=True)
        grads = level(grads, "core")
        core_bit = plan.core[0]
        left = [1 << i for i in reversed(range(plan.bits)) if 1 << i != core_bit]
        parts = width // 256
        dkp, dvp, dqp = back_call(
            0, parts, first_near, near, grad_context, context, queries, keys_p, values_p, log_total,
            seg_own, seg_near,
        )
        shared_p = product_call(first_near, near, dkp, dvp, squares, rows)
        grads, shared_p, dqp = tie(grads, shared_p, dqp)
        grads = level(grads, ("x", "y"))
        returned = Return(plan, rows)
        returned.prompt_one(shared_p)
        dkn, dvn, dq = back_call(
            0, parts, None, near, grad_context, context, queries, keys_n, values_n, log_total,
            seg_own, seg_near, dqp,
        )
        send, keep, grad_own, sums_qkv = weight_call(
            spots, first_near, near, own, dq, squares, grad_h1, dkp, dvp, dkn, dvn, core, runs
        )
        send, keep, returned.same, returned.same_y, dkn, dvn = tie(
            send, keep, returned.same, returned.same_y, dkn, dvn
        )
        returned.prompt_two()
        shared_n = product_call(None, near, dkn, dvn, squares, rows)

        order = (6, 5, 3, 4, 2, 0, 1)
        small = len(early) + len(late) - 1
        d_table = jnp.concatenate([sums_qkv[:1]] + [sums[i : i + 1] for i in order], 0)
        d_lines = jnp.concatenate(
            [
                d_table.reshape(small, count, step).transpose(1, 0, 2).reshape(count, -1),
                sums_bin[:wide].reshape(count, wide * step),
            ],
            1,
        )
        d_lines = jnp.pad(d_lines, ((0, 0), (0, width - d_lines.shape[1])))[:, None].astype(BF)
        d_lines = jnp.pad(d_lines, ((0, 0), (0, 7), (0, 0)))
        place = core[0]
        pick = Reduce(plan, [])
        if step % 8:
            real = lambda v: v.reshape(16, 3, count // 32, step, width).transpose(0, 2, 1, 3, 4)
            send, keep = [real(v).reshape(count // 2, 3 * step, width) for v in (send, keep)]
        send = jnp.concatenate([send, pick.cut(d_lines, core_bit, 1 - place)], 1)
        keep = jnp.concatenate([keep, pick.cut(d_lines, core_bit, place)], 1)
        reduce = Reduce(plan, [keep, plan.swap(send, core_bit)], left)
        for bit in plan.x + plan.y + plan.z[::-1]:
            held = reduce.terms
            if bit == plan.x[0]:
                held = tie(*held)
                returned.prompt_three()
            elif bit == plan.y[0]:
                *held, grads, shared_n, returned.back = tie(*held, grads, shared_n, returned.back)
                grads = level(grads, "z")
            elif bit == plan.z[-1]:
                *held, shared_n = tie(*held, shared_n)
                returned.near(shared_n)
            elif bit == plan.z[0]:
                *held, returned.own = tie(*held, returned.own)
            reduce.terms = list(held)
            reduce.stage(bit)
        o_ab = grads.reshape(-1, width).astype(F32)
        grad_tokens = grad_own + returned.total()
        o_first = reduce.result()
        o_line = o_first[3 * step]
        o_small = [o_line[i * step : (i + 1) * step] for i in range(small)]
        o_bin = o_line[small * step : (small + wide) * step]
        return (
            layer_out[None],
            grad_tokens.astype(BF)[None],
            o_first[:step],
            o_first[step : 2 * step],
            o_first[2 * step : 3 * step],
            o_ab[wide * step : (wide + 1) * step],
            jnp.concatenate([o_ab[i * step : (i + 1) * step] for i in range(wide + 1, 2 * wide + 1)], 1),
            o_ab[: wide * step],
            o_small[0],
            o_small[1],
            o_small[2],
            o_small[3],
            o_small[4],
            o_bin,
            o_small[5],
            o_small[6],
            o_small[7],
        )

    split = P(GRP, ROW, None)
    owned2, owned1 = P(AXES, None), P(AXES)
    in_specs = (split, P(GRP, None), split) + (owned2,) * 6 + (owned1,) * 9
    out_specs = (split, split) + (owned2,) * 6 + (owned1,) * 9
    return jax.shard_map(
        per_device, mesh=fine, in_specs=in_specs, out_specs=out_specs, check_vma=False
    )
```

```python
import functools

import jax
import jax.numpy as jnp
import numpy as np
from jax import lax
from jax.experimental import pallas as pl
from jax.experimental.pallas import tpu as pltpu
from jax.sharding import Mesh
from jax.sharding import PartitionSpec as P

HEADS = 12
HDIM = 64
PROMPT = 1024
CONT_MOST = 256
BF = jnp.bfloat16
F32 = jnp.float32

NORM_EPS = 1e-12
MASK_FILL = -1000000000.0
SQRT_HALF = 0.7071067811865476
INV_ROOT_TAU = 0.3989422804014327
AXES = ("x", "core", "z", "y")
GRP, ROW = AXES[:2], AXES[2:]
WIDE = 4
WO, WI = 4, 5
WQ, WK, WV = 0, 1, 2


def mm(left, right):
    return jnp.dot(left, right, preferred_element_type=F32)


def segment_ids(lengths, group_len):
    ends = jnp.cumsum(lengths)
    places = jnp.arange(group_len, dtype=jnp.int32)
    passed = jnp.sum(((places - PROMPT)[:, None] >= ends[None, :]).astype(jnp.int32), axis=-1)
    return jnp.where(places < PROMPT, 0, 1 + passed)


class Plan:
    def __init__(self, grp, row):
        self.grp, self.row, self.count = grp, row, grp * row
        y = row // 4
        bits = lambda base, size: [base << i for i in range(size.bit_length() - 1)]
        self.y, self.z = bits(1, y), bits(y, 4)
        self.core, self.x = bits(row, 2), bits(2 * row, grp // 2)
        self.bits = self.count.bit_length() - 1

    def swap(self, value, mask):
        return lax.ppermute(value, AXES, [(i, i ^ mask) for i in range(self.count)])

    def send(self, value, moves):
        pairs = [(g * self.row + a, g * self.row + b) for g in range(self.grp) for a, b in moves]
        return lax.ppermute(value, AXES, pairs)

    def me(self):
        return lax.axis_index(AXES)


class Reduce:
    def __init__(self, plan, terms, left=None):
        self.plan, self.terms = plan, list(terms)
        self.left = left or [1 << i for i in reversed(range(plan.bits))]

    def cut(self, term, bit, place):
        at = self.left.index(bit)
        high, low = 1 << at, 1 << (len(self.left) - at - 1)
        _, rows, width = term.shape
        term = term.reshape(high, 2, low * rows, width)
        return lax.dynamic_slice_in_dim(term, place, 1, 1).reshape(high * low, rows, width)

    def total(self, terms):
        return sum([t.astype(F32) for t in terms[1:]], terms[0].astype(F32))

    def stage(self, bit):
        place = (self.plan.me() // bit) & 1
        away = self.total([self.cut(t, bit, 1 - place) for t in self.terms]).astype(BF)
        here = [self.cut(t, bit, place) for t in self.terms]
        self.left = [b for b in self.left if b != bit]
        self.terms = here + [self.plan.swap(away, bit)]

    def result(self):
        return self.total(self.terms)[0]


def tie(*values):
    return lax.optimization_barrier(values)


class Tokens:
    def __init__(self, plan, own):
        self.plan, self.own = plan, own
        self.rows = own.shape[0]
        self.ready = plan.row == 8

    def stage_one(self):
        if self.ready:
            plan, own = self.plan, self.own
            across = plan.send(own, [(0, 4), (1, 5), (2, 6), (3, 7)])
            self.same = jnp.where(lax.axis_index(ROW) < 4, own, across)
            self.beside = plan.swap(own, 1)
            return [self.same, self.beside]
        return []

    def stage_two(self):
        if self.ready:
            plan = self.plan
            self.other = plan.swap(self.same, 2)
            self.same_y = plan.swap(self.same, 1)
            self.diagonal = plan.send(self.own, [(5, 6), (6, 5)])
            return [self.other, self.same_y, self.diagonal]
        return []

    def stage_three(self):
        if self.ready:
            self.other_y = self.plan.swap(self.same_y, 2)

    def spots(self):
        row, rows, own = lax.axis_index(ROW), self.rows, self.own
        if self.ready:
            near = jnp.where(row < 4, 0, jnp.where((row == 5) | (row == 6), 3, 2))
            return [
                self.same, self.other, self.same_y, self.other_y, own, self.beside, self.diagonal,
            ], near
        every = lax.all_gather(own, ROW, axis=0, tiled=True)
        start = jnp.maximum(row * rows - CONT_MOST, 0)
        padded = jnp.concatenate([every, jnp.zeros((CONT_MOST, own.shape[1]), own.dtype)], 0)
        near = lax.dynamic_slice_in_dim(padded, start, rows + 2 * CONT_MOST, 0)
        every = jnp.concatenate([every[:PROMPT], near], 0)
        spots = [every[i : i + rows] for i in range(0, every.shape[0], rows)]
        return spots, jnp.where(row * rows < PROMPT, 0, near.shape[0] // rows)


def near_segments(plan, segments, rows):
    row = lax.axis_index(ROW)
    if plan.row != 8:
        start = jnp.maximum(row * rows - CONT_MOST, 0)
        padded = jnp.concatenate([segments, jnp.full((CONT_MOST,), -1, jnp.int32)], 0)
        near = lax.dynamic_slice_in_dim(padded, start, rows + 2 * CONT_MOST, 0)
        return jnp.where((near == 0) | (row * rows < PROMPT), -1, near)
    pieces = []
    for block, valid in (
        (row, row >= 4),
        (row ^ 1, row >= 4),
        (11 - row, (row == 5) | (row == 6)),
    ):
        block = jnp.clip(block, 0, 7)
        ids = lax.dynamic_slice_in_dim(segments, block * rows, rows, 0)
        pieces.append(jnp.where(valid, ids, -1))
    return jnp.concatenate(pieces, 0)


class Return:
    def __init__(self, plan, rows):
        self.plan, self.rows = plan, rows

    def prompt_one(self, parts):
        self.prompt = self.same = self.same_y = self.own = self.back = parts
        if self.plan.row == 8:
            same, same_y = parts[0].astype(F32), parts[2].astype(F32)
            self.same_y = (same_y + self.plan.swap(parts[3], 2).astype(F32)).astype(BF)
            self.same = same + self.plan.swap(parts[1], 2).astype(F32)

    def prompt_two(self):
        if self.plan.row == 8:
            self.same = self.same + self.plan.swap(self.same_y, 1).astype(F32)

    def prompt_three(self):
        if self.plan.row == 8:
            self.back = self.plan.send(self.same.astype(BF), [(4, 0), (5, 1), (6, 2), (7, 3)])

    def near(self, parts):
        self.around = parts
        if self.plan.row == 8:
            own = parts[0].astype(F32) + self.plan.swap(parts[1], 1).astype(F32)
            self.own = own + self.plan.send(parts[2], [(5, 6), (6, 5)]).astype(F32)

    def total(self):
        row, rows = lax.axis_index(ROW), self.rows
        if self.plan.row == 8:
            return jnp.where(row < 4, self.same + self.back.astype(F32), self.own)
        around = self.around.reshape(-1, self.around.shape[-1]).astype(F32)
        start = jnp.maximum(row * rows - CONT_MOST, 0)
        whole = jnp.zeros((self.plan.row * rows + CONT_MOST, around.shape[1]), F32)
        whole = whole.at[:PROMPT].set(self.prompt.reshape(PROMPT, -1).astype(F32))
        near = jnp.where(row * rows < PROMPT, 0, around)
        near = lax.dynamic_slice_in_dim(whole, start, rows + 2 * CONT_MOST, 0) + near
        whole = lax.dynamic_update_slice_in_dim(whole, near, start, 0)
        return lax.psum_scatter(whole[: self.plan.row * rows], ROW, scatter_dimension=0, tiled=True)


def heads_mask(lanes, head):
    lane = lax.broadcasted_iota(jnp.int32, lanes, 1)
    return (lane >= head * HDIM) & (lane < (head + 1) * HDIM)


def nt(left, right):
    return lax.dot_general(left, right, (((1,), (1,)), ((), ())), preferred_element_type=F32)


def tn(left, right):
    return lax.dot_general(left, right, (((0,), (0,)), ((), ())), preferred_element_type=F32)


def pack_kernel(wo_ref, wi_ref, wu_ref, wq_ref, wk_ref, wv_ref, line_ref, early_ref, late_ref):
    step, width = wo_ref.shape
    early_ref[:step, :] = wq_ref[...]
    early_ref[step : step + 8, :] = line_ref[:8, :]
    early_ref[step + 8 : 2 * step + 8, :] = wk_ref[...]
    early_ref[2 * step + 8 :, :] = wv_ref[...]
    late_ref[: WIDE * step, :] = wu_ref[...]
    late_ref[WO * step : WI * step, :] = wo_ref[...]
    for i in range(WIDE):
        late_ref[(WI + i) * step : (WI + i + 1) * step, :] = wi_ref[:, i * width : (i + 1) * width]
    late_ref[(WI + WIDE) * step :, :] = line_ref[8:, :]


def pack_call(w_output, w_inner, w_outer, w_query, w_key, w_value, line):
    step, width = w_output.shape
    shape = lambda rows: jax.ShapeDtypeStruct((rows, width), BF)
    return pl.pallas_call(
        pack_kernel, out_shape=[shape(3 * step + 8), shape((WI + WIDE) * step + 8)], name="pack"
    )(w_output, w_inner, w_outer, w_query, w_key, w_value, line)


def attention_kernel(blocks, first, rows, places, *refs):
    spots = refs[:blocks]
    (near_ref, me_ref, own_ref, a0_ref, a1_ref, b0_ref, b1_ref, segq_ref, segk_ref,
     w_out, q_ref, kp_ref, vp_ref, kn_ref, vn_ref, ctx_ref, lse_ref,
     x_ref, w_ref, s_ref, vt_ref, out_ref, line_ref, bias_ref, sems, w_sems, o_sem) = refs[blocks:]
    near = near_ref[0]
    depth = own_ref.shape[1]
    owners = w_ref.shape[0]
    each = depth // owners
    part = q_ref.shape[1]

    def weights(act):
        @pl.loop(0, owners)
        def _(e):
            away = e ^ me_ref[0]
            for (bits, half), (zero, one), parts in (
                (places[0], (a0_ref, a1_ref), ((0, each, w_ref, 0), (each, 8, line_ref, 0), (each + 8, 8, w_ref, each))),
                (places[1], (b0_ref, b1_ref), ((0, 2 * each - 8, w_ref, each + 8),)),
            ):
                j = sum([((away // bit) & 1) * weight for bit, weight in bits])
                for which, source in enumerate((zero, one)):

                    @pl.when(((away // half) & 1) == which)
                    def _():
                        for k, (top, size, target, base) in enumerate(parts):
                            act(pltpu.make_async_copy(
                                source.at[j, pl.ds(top, size)], target.at[e, pl.ds(base, size)],
                                w_sems.at[k if zero is a0_ref else 3, e],
                            ))

    @pl.when(pl.program_id(0) == 0)
    def _():
        copies = [
            pltpu.make_async_copy(spot, x_ref.at[pl.ds(i * rows, rows)], sems.at[i])
            for i, spot in enumerate(spots)
        ]
        weights(lambda c: c.start())
        for copy in copies:
            copy.start()
        weights(lambda c: c.wait())
        for copy in copies:
            copy.wait()
        pltpu.make_async_copy(w_ref, w_out, o_sem).start()
        line = line_ref[:, 0, :128]
        place = lax.broadcasted_iota(jnp.int32, (128, depth), 0)
        lane = lax.broadcasted_iota(jnp.int32, (128, depth), 1)
        mine = lax.broadcasted_iota(jnp.int32, (owners, depth), 0)
        mine = mine == lax.broadcasted_iota(jnp.int32, (owners, depth), 1) // each
        for i in range(2):
            spread = mm(line, jnp.where(place == lane % each + i * each, 1.0, 0.0).astype(BF))
            bias_ref[i : i + 1, :] = jnp.sum(jnp.where(mine, spread, 0.0), axis=0, keepdims=True)

    lanes = pl.ds(pl.multiple_of(pl.program_id(0) * part, part), part)
    wq, wk, wv = [
        w_ref[:, i * each : (i + 1) * each, lanes].reshape(depth, part) for i in (WQ, WK, WV)
    ]
    queries = (mm(own_ref[...], wq) + bias_ref[0:1, lanes]) * (HDIM**-0.5)
    q_ref[...] = queries.astype(BF)

    heads = part // HDIM
    q = q_ref[...]
    tall = x_ref.shape[0]

    def body(sets):
        for k_ref, v_ref, base, size, _ in sets:
            x = x_ref[base : base + size, :]
            k_ref[...] = mm(x, wk).astype(BF)
            v = (mm(x, wv) + bias_ref[1:2, lanes]).astype(BF)
            v_ref[...] = v
            vt_ref[:, base : base + size] = v.T
        for h in range(heads):
            q_h = jnp.where(heads_mask(q.shape, h), q, 0)
            peak = jnp.full((1, rows), MASK_FILL, F32)
            for k_ref, _, base, size, masked in sets:
                s = nt(k_ref[...], q_h)
                if masked:
                    s = jnp.where(segk_ref[...] == segq_ref[...], s, MASK_FILL)
                s_ref[h % 2, base : base + size, :] = s
                peak = jnp.maximum(peak, jnp.max(s, axis=0, keepdims=True))
            total, mixed = jnp.zeros((1, rows), F32), jnp.zeros((HDIM, rows), F32)
            for _, _, base, size, _ in sets:
                p = jnp.exp(s_ref[h % 2, base : base + size, :] - peak)
                total = total + jnp.sum(p, axis=0, keepdims=True)
                mixed = mixed + mm(vt_ref[h * HDIM : (h + 1) * HDIM, base : base + size], p.astype(BF))
            out_ref[h * HDIM : (h + 1) * HDIM, :] = mixed / total
            lse_ref[0, h : h + 1, :] = peak + jnp.log(total)

    prompt = (kp_ref, vp_ref, 0, PROMPT, False)

    @pl.when(near == 0)
    def _():
        body([prompt])

    @pl.when(near > 0)
    def _():
        body([prompt, (kn_ref, vn_ref, PROMPT, tall - PROMPT, True)])

    ctx_ref[...] = out_ref[...].T.astype(BF)

    @pl.when(pl.program_id(0) == pl.num_programs(0) - 1)
    def _():
        pltpu.make_async_copy(w_ref, w_out, o_sem).wait()


def attention_call(spots, first, near, me, own, pieces, places, segq, segk):
    rows, width = own.shape
    blocks = len(spots)
    tall = blocks * rows
    part = 256
    steps = width // part
    heads = part // HDIM
    cols = lambda depth: pl.BlockSpec((depth, part), lambda g: (0, g))
    flops = 2 * tall * width * width * 2 + 4 * tall * rows * width * 4
    owners = 2 * pieces[0].shape[0]
    each = width // owners
    return pl.pallas_call(
        functools.partial(attention_kernel, blocks, first, rows, places),
        grid=(steps,),
        in_specs=[pl.BlockSpec(memory_space=pl.ANY)] * blocks
        + [
            pl.BlockSpec(memory_space=pltpu.SMEM),
            pl.BlockSpec(memory_space=pltpu.SMEM),
            pl.BlockSpec((rows, width), lambda g: (0, 0)),
        ] + [pl.BlockSpec(memory_space=pl.ANY)] * 4 + [
            pl.BlockSpec((1, rows), lambda g: (0, 0)),
            pl.BlockSpec(segk.shape, lambda g: (0, 0)),
        ],
        out_specs=[
            pl.BlockSpec(memory_space=pl.ANY),
            cols(rows), cols(PROMPT), cols(PROMPT), cols(tall - PROMPT), cols(tall - PROMPT),
            cols(rows), pl.BlockSpec((1, 8, rows), lambda g: (g, 0, 0)),
        ],
        out_shape=[
            jax.ShapeDtypeStruct((owners, 3 * each, width), BF),
            jax.ShapeDtypeStruct((rows, width), BF),
            jax.ShapeDtypeStruct((PROMPT, width), BF),
            jax.ShapeDtypeStruct((PROMPT, width), BF),
            jax.ShapeDtypeStruct((tall - PROMPT, width), BF),
            jax.ShapeDtypeStruct((tall - PROMPT, width), BF),
            jax.ShapeDtypeStruct((rows, width), BF),
            jax.ShapeDtypeStruct((steps, 8, rows), F32),
        ],
        scratch_shapes=[
            pltpu.VMEM((tall, width), BF),
            pltpu.VMEM((owners, 3 * each, width), BF),
            pltpu.VMEM((2, tall, rows), F32),
            pltpu.VMEM((part, tall), BF),
            pltpu.VMEM((part, rows), F32),
            pltpu.VMEM((owners, 8, width), BF),
            pltpu.VMEM((8, width), F32),
            pltpu.SemaphoreType.DMA((blocks,)),
            pltpu.SemaphoreType.DMA((4, owners)),
            pltpu.SemaphoreType.DMA,
        ],
        compiler_params=pltpu.CompilerParams(vmem_limit_bytes=60 * 2**20),
        cost_estimate=pl.CostEstimate(
            flops=flops, bytes_accessed=12 * 2**20, transcendentals=tall * rows * 12
        ),
        name="attention",
    )(*spots, near, me, own, *pieces, segq, segk)


def halves(value, runs, core):
    depth = value.shape[0] // runs
    pick = lambda first: jnp.concatenate(
        [value[i * depth : (i + 1) * depth] for i in range(first, runs, 2)], 0
    )
    even, odd = pick(0), pick(1)
    return jnp.where(core == 0, odd, even), jnp.where(core == 0, even, odd)


def middle_kernel(wide, mapped, core_ref, ctx_ref, own_ref, cot_ref, got_ref, vec_ref, bin_ref,
                  out_ref, h1_ref, gctx_ref, send, keep, sums_ref, sbin_ref,
                  first_ref, n1_ref, inv_ref, low_ref, pre_ref, cdf_ref, act_ref, acc_ref,
                  gffn_ref, glow_ref, lowt_ref, w_ref, out_buf, in_buf, wo_buf, sems, w_sems):
    step = pl.program_id(0)
    width = ctx_ref.shape[1]
    vec = lambda i: vec_ref[i : i + 1, :]
    mean = lambda v: jnp.sum(v, axis=-1, keepdims=True) * (1.0 / width)
    down = lambda v: jnp.sum(v, axis=0, keepdims=True)
    owners = got_ref.shape[0]
    each = width // owners
    some = owners // wide
    square = lambda value: value.reshape(width, width)
    rows_of = lambda place: pl.ds(pl.multiple_of(place * each, each), each)
    w_output = lambda ref: ref.at[:, rows_of(WO)]
    w_inner = lambda ref, at: ref.at[:, rows_of(WI + at)]
    w_outer = lambda ref, at: ref.at[pl.ds(at * some, some), pl.ds(0, wide * each)]

    def fetch_inner(at):
        return pltpu.make_async_copy(w_inner(got_ref, at), w_inner(w_ref, at), w_sems.at[0, at])

    def fetch_outer(at):
        return pltpu.make_async_copy(w_outer(got_ref, at), w_outer(w_ref, at), w_sems.at[1, at])

    def fetch_output():
        return pltpu.make_async_copy(w_output(got_ref), w_output(w_ref), w_sems.at[0, wide])

    def home(core, group, i):
        half = keep if group % 2 == core else send
        return half.at[group // 2 * 8 + (i % 2 * 4 + i // 2 if mapped else i)]

    def outer(at, core, act):
        turn = (2 * wide - 1 - at) % 2
        for i in range(some):
            for parity in range(2):

                @pl.when(at % 2 == parity)
                def _():
                    half = keep if parity == core else send
                    place = half.at[at // 2 * 8 + (i % 2 * 4 + i // 2 if mapped else i)]
                    act(pltpu.make_async_copy(
                        out_buf.at[turn, i], place.at[pl.ds(0, wide * each)], sems.at[turn, i]
                    ))

    def inner(at, core, act):
        turn = (2 * wide - 1 - at) % 2
        top = pl.multiple_of((wide + 1 + at) * each, each)
        for e in range(owners):
            place = home(core, e // 8, e % 8).at[pl.ds(top, each)]
            act(pltpu.make_async_copy(in_buf.at[turn, e], place, sems.at[2 + turn, e]))

    def output(at, core, act):
        for e in range(owners):
            place = home(core, e // 8, e % 8).at[pl.ds(wide * each, each)]
            act(pltpu.make_async_copy(wo_buf.at[e], place, sems.at[4, e]))

    def on_core(*calls):
        for core in range(2):

            @pl.when(core_ref[0] == core)
            def _():
                for call, at, act in calls:
                    call(at, core, act)

    go, end = lambda copy: copy.start(), lambda copy: copy.wait()

    @pl.when(step == 0)
    def _():
        fetch_output().start()
        for at in range(wide):
            fetch_inner(at).start()
            fetch_outer(at).start()
        fetch_output().wait()
        hidden = own_ref[...].astype(F32) + mm(ctx_ref[...], square(w_output(w_ref)[...])) + vec(0)
        centred = hidden - mean(hidden)
        inverse = lax.rsqrt(mean(centred * centred) + NORM_EPS)
        normed = centred * inverse
        n1_ref[...] = normed
        inv_ref[...] = inverse
        first = normed * vec(1) + vec(2)
        first_ref[...] = first
        low_ref[...] = first.astype(BF)
        lowt_ref[...] = first.astype(BF).T

    @pl.when(step < wide)
    def _():
        chunk = pl.ds(pl.multiple_of(step * width, width), width)
        fetch_inner(step).wait()
        fetch_outer(step).wait()
        pre = mm(low_ref[...], square(w_inner(w_ref, step)[...])) + bin_ref[pl.ds(step, 1), :]
        cdf = 0.5 * (1.0 + lax.erf(pre * SQRT_HALF))
        act = (pre * cdf).astype(BF)
        pre_ref[:, chunk] = pre
        cdf_ref[:, chunk] = cdf
        act_ref[:, chunk] = act
        more = mm(act, square(w_outer(w_ref, step)[...]))

        @pl.when(step == 0)
        def _():
            acc_ref[...] = more

        @pl.when(step > 0)
        def _():
            acc_ref[...] += more

    @pl.when(step == wide - 1)
    def _():
        hidden = first_ref[...] + acc_ref[...] + vec(3)
        centred = hidden - mean(hidden)
        inverse = lax.rsqrt(mean(centred * centred) + NORM_EPS)
        normed = centred * inverse
        out_ref[...] = (normed * vec(4) + vec(5)).astype(BF)
        grad = cot_ref[...].astype(F32)
        sums_ref[0:1, :] = down(grad * normed)
        sums_ref[1:2, :] = down(grad)
        e = grad * vec(4)
        back = inverse * (e - mean(e) - normed * mean(e * normed))
        gffn_ref[...] = back
        low = back.astype(BF)
        glow_ref[...] = low
        sums_ref[2:3, :] = down(low.astype(F32))

    @pl.when(step >= wide)
    def _():
        at = 2 * wide - 1 - step
        chunk = pl.ds(pl.multiple_of(at * width, width), width)
        pre = pre_ref[:, chunk]
        slope = cdf_ref[:, chunk] + pre * jnp.exp(-0.5 * pre * pre) * INV_ROOT_TAU
        low = glow_ref[...]
        grad = (nt(low, square(w_outer(w_ref, at)[...])) * slope).astype(BF)
        sbin_ref[pl.ds(at, 1), :] = down(grad.astype(F32))
        turn = step % 2

        @pl.when(step >= wide + 2)
        def _():
            on_core((outer, at + 2, end), (inner, at + 2, end))

        out_buf[turn] = tn(act_ref[:, chunk], low).astype(BF).reshape(some, wide * each, width)
        on_core((outer, at, go))
        in_buf[turn] = mm(lowt_ref[...], grad).astype(BF).reshape(owners, each, width)
        on_core((inner, at, go))
        gffn_ref[...] += nt(grad, square(w_inner(w_ref, at)[...]))

    @pl.when(step == 2 * wide - 1)
    def _():
        grad = gffn_ref[...]
        normed = n1_ref[...]
        sums_ref[3:4, :] = down(grad * normed)
        sums_ref[4:5, :] = down(grad)
        e = grad * vec(1)
        back = inv_ref[...] * (e - mean(e) - normed * mean(e * normed))
        h1_ref[...] = back
        low = back.astype(BF)
        sums_ref[5:6, :] = down(low.astype(F32))
        wo_buf[...] = tn(ctx_ref[...], low).astype(BF).reshape(owners, each, width)
        on_core((output, 0, go))
        gctx = nt(low, square(w_output(w_ref)[...])).astype(BF)
        gctx_ref[...] = gctx
        sums_ref[6:7, :] = down(gctx.astype(F32))
        sums_ref[7:8, :] = jnp.zeros((1, width), F32)
        on_core(*[(call, at, end) for at in (1, 0) for call in (outer, inner)], (output, 0, end))


def middle_call(core, ctx, own, cot, got, vec, b_inner, mapped):
    rows, width = own.shape
    owners = got.shape[0]
    each = width // owners
    wide = WIDE
    whole = lambda shape: pl.BlockSpec(shape, lambda s: (0,) * len(shape))
    shape = jax.ShapeDtypeStruct
    return pl.pallas_call(
        functools.partial(middle_kernel, wide, mapped),
        grid=(2 * wide,),
        in_specs=[
            pl.BlockSpec(memory_space=pltpu.SMEM),
            whole((rows, width)), whole((rows, width)), whole((rows, width)),
            pl.BlockSpec(memory_space=pl.ANY),
            whole((8, width)), whole((8, width)),
        ],
        out_specs=[
            whole((rows, width)), whole((rows, width)), whole((rows, width)),
            pl.BlockSpec(memory_space=pl.ANY), pl.BlockSpec(memory_space=pl.ANY),
            whole((8, width)), whole((8, width)),
        ],
        out_shape=[
            shape((rows, width), BF), shape((rows, width), F32), shape((rows, width), BF),
            shape((owners // 2, (2 * wide + 1) * each, width), BF),
            shape((owners // 2, (2 * wide + 1) * each, width), BF),
            shape((8, width), F32), shape((8, width), F32),
        ],
        scratch_shapes=[
            pltpu.VMEM((rows, width), F32), pltpu.VMEM((rows, width), F32), pltpu.VMEM((rows, 1), F32),
            pltpu.VMEM((rows, width), BF), pltpu.VMEM((rows, wide * width), F32),
            pltpu.VMEM((rows, wide * width), F32), pltpu.VMEM((rows, wide * width), BF),
            pltpu.VMEM((rows, width), F32), pltpu.VMEM((rows, width), F32),
            pltpu.VMEM((rows, width), BF), pltpu.VMEM((width, rows), BF),
            pltpu.VMEM((owners, (2 * wide + 1) * each, width), BF),
            pltpu.VMEM((2, owners // wide, wide * each, width), BF),
            pltpu.VMEM((2, owners, each, width), BF),
            pltpu.VMEM((owners, each, width), BF), pltpu.SemaphoreType.DMA((5, owners)),
            pltpu.SemaphoreType.DMA((2, wide + 1)),
        ],
        compiler_params=pltpu.CompilerParams(vmem_limit_bytes=60 * 2**20),
        cost_estimate=pl.CostEstimate(
            flops=2 * rows * width * width * (6 * wide + 3), bytes_accessed=32 * 2**20,
            transcendentals=2 * rows * width * wide,
        ),
        name="middle",
    )(core, ctx, own, cot, got, vec, b_inner)


def back_kernel(rows, bound, started, *refs):
    near_ref, gctx_ref, ctx_ref, q_ref, k_ref, v_ref, lse_ref, segq_ref, segk_ref = refs[:9]
    dk_ref, dv_ref, dq_ref, kt_ref, p_ref, ds_ref = refs[-6:]
    q, g = q_ref[...], gctx_ref[...]
    part = q.shape[1]
    heads = part // HDIM
    masks = [heads_mask(q.shape, h) for h in range(heads)]
    q_parts = [jnp.where(m, q, 0) for m in masks]
    g_parts = [jnp.where(m, g, 0) for m in masks]
    product = (g.astype(F32) * ctx_ref[...].astype(F32)).T
    inner = [
        jnp.sum(product[h * HDIM : (h + 1) * HDIM], axis=0, keepdims=True) for h in range(heads)
    ]

    def body():
        k, v = k_ref[...], v_ref[...]
        kt_ref[...] = k.T
        for h in range(heads):
            s = nt(k, q_parts[h])
            if bound is None:
                s = jnp.where(segk_ref[...] == segq_ref[...], s, MASK_FILL)
            p = jnp.exp(s - lse_ref[0, h : h + 1, :])
            across = slice(h * rows, (h + 1) * rows)
            ds = (p * (nt(v, g_parts[h]) - inner[h])).astype(BF)
            p_ref[:, across] = p.astype(BF)
            ds_ref[:, across] = ds
            mine = slice(h * HDIM, (h + 1) * HDIM)
            more = mm(kt_ref[mine, :], ds)
            dq_ref[mine, :] = refs[9][mine, :] + more if started else more
        dk_ref[...] = mm(ds_ref[...], jnp.concatenate(q_parts, 0)).astype(BF)
        dv_ref[...] = mm(p_ref[...], jnp.concatenate(g_parts, 0)).astype(BF)

    if bound is None:

        @pl.when(near_ref[0] == 0)
        def _():
            dq_ref[...] = refs[9][...]

        pl.when(near_ref[0] > 0)(body)
    else:
        body()


def back_call(start, steps, bound, near, gctx, ctx, q, k, v, lse, segq, segk, dq0=None, into=None):
    rows, width = q.shape
    tall = k.shape[0]
    part = 256
    cols = lambda depth: pl.BlockSpec((depth, part), lambda g: (0, start + g))
    whole = lambda shape: pl.BlockSpec(shape, lambda g: (0,) * len(shape))
    down = pl.BlockSpec((part, rows), lambda g: (start + g, 0))
    shape = jax.ShapeDtypeStruct
    extra = ([dq0] if dq0 is not None else []) + list(into or [])
    specs = ([down] if dq0 is not None else []) + [pl.BlockSpec(memory_space=pl.ANY)] * len(into or [])
    return pl.pallas_call(
        functools.partial(back_kernel, rows, bound, dq0 is not None),
        grid=(steps,),
        in_specs=[
            pl.BlockSpec(memory_space=pltpu.SMEM),
            cols(rows), cols(rows), cols(rows), cols(tall), cols(tall),
            pl.BlockSpec((1, 8, rows), lambda g: (start + g, 0, 0)),
            whole((1, rows)), whole(segk.shape),
        ] + specs,
        out_specs=[cols(tall), cols(tall), down],
        out_shape=[shape((tall, width), BF), shape((tall, width), BF), shape((width, rows), F32)],
        input_output_aliases={9 + i: i for i in range(3)} if into else {},
        scratch_shapes=[
            pltpu.VMEM((part, tall), BF),
            pltpu.VMEM((tall, part // HDIM * rows), BF),
            pltpu.VMEM((tall, part // HDIM * rows), BF),
        ],
        compiler_params=pltpu.CompilerParams(vmem_limit_bytes=60 * 2**20),
        cost_estimate=pl.CostEstimate(
            flops=2 * 10 * 2 * tall * rows * part * steps * 2,
            bytes_accessed=8 * tall * part * steps, transcendentals=tall * rows * 4 * steps,
        ),
        name="attention_back",
    )(near, gctx, ctx, q, k, v, lse, segq, segk, *extra)


def product_kernel(rows, bound, near_ref, dk_ref, dv_ref, wk_ref, wv_ref, gx_ref):
    @pl.when((pl.program_id(0) < near_ref[0]) | (bound is not None))
    def _():
        width = dk_ref.shape[1]
        wk, wv = wk_ref[...].reshape(width, width), wv_ref[...].reshape(width, width)
        gx_ref[0] = (nt(dk_ref[...], wk) + nt(dv_ref[...], wv)).astype(BF)


def product_call(bound, near, dk, dv, got, rows):
    tall, width = dk.shape
    owners, each = got.shape[0], width // got.shape[0]
    weight = lambda place: pl.BlockSpec((owners, each, width), lambda b: (0, place, 0))
    return pl.pallas_call(
        functools.partial(product_kernel, rows, bound),
        grid=(tall // rows,),
        in_specs=[
            pl.BlockSpec(memory_space=pltpu.SMEM),
            pl.BlockSpec((rows, width), lambda b: (b, 0)),
            pl.BlockSpec((rows, width), lambda b: (b, 0)),
            weight(WK), weight(WV),
        ],
        out_specs=pl.BlockSpec((1, rows, width), lambda b: (b, 0, 0)),
        out_shape=jax.ShapeDtypeStruct((tall // rows, rows, width), BF),
        compiler_params=pltpu.CompilerParams(vmem_limit_bytes=60 * 2**20),
        cost_estimate=pl.CostEstimate(
            flops=4 * tall * width * width, bytes_accessed=6 * tall * width, transcendentals=0
        ),
        name="token_product",
    )(near, dk, dv, got, got)


def weight_kernel(blocks, first, rows, runs, *refs):
    spots = refs[:blocks]
    (near_ref, core_ref, own_ref, dq_ref, wq_ref, h1_ref, dkp_ref, dvp_ref, dkn_ref, dvn_ref,
     send_ref, keep_ref, gown_ref, sums_ref, x_ref, xt_ref, sems) = refs[blocks:]
    core = core_ref[0]
    step = pl.program_id(0)

    @pl.when(step == 0)
    def _():
        copies = [
            pltpu.make_async_copy(spot, x_ref.at[pl.ds(i * rows, rows)], sems.at[i])
            for i, spot in enumerate(spots)
        ]
        for copy in copies:
            copy.start()
        gown_ref[...] = h1_ref[...]
        for i, copy in enumerate(copies):
            copy.wait()
            xt_ref[:, i * rows : (i + 1) * rows] = x_ref[i * rows : (i + 1) * rows, :].T

    scale = HDIM**-0.5
    dq = dq_ref[...].T.astype(BF)
    part = dq.shape[1]
    width = x_ref.shape[1]
    gown_ref[...] += nt(dq, wq_ref[...].reshape(width, part)) * scale
    half = send_ref.shape[0]
    each = width // (2 * half)

    def put(i, grad):
        away, here = halves(grad.astype(BF), runs, core)
        send_ref[:, i * each : (i + 1) * each, :] = away.reshape(half, each, part)
        keep_ref[:, i * each : (i + 1) * each, :] = here.reshape(half, each, part)

    put(WQ, tn(own_ref[...], dq) * scale)
    sums_ref[0:1, :] = jnp.sum(dq.astype(F32), axis=0, keepdims=True) * scale

    def body(near):
        for i, p_ref, n_ref in ((WK, dkp_ref, dkn_ref), (WV, dvp_ref, dvn_ref)):
            grad = mm(xt_ref[:, :PROMPT], p_ref[...])
            if near:
                grad = grad + mm(xt_ref[:, PROMPT:], n_ref[...])
            put(i, grad)

    pl.when(near_ref[0] == 0)(lambda: body(False))
    pl.when(near_ref[0] > 0)(lambda: body(True))
    sums_ref[1:8, :] = jnp.zeros((7, part), F32)


def weight_call(spots, first, near, own, dq, got, h1, dkp, dvp, dkn, dvn, core, runs):
    rows, width = own.shape
    blocks = len(spots)
    tall = blocks * rows
    part = 256
    steps = width // part
    cols = lambda depth, size=part: pl.BlockSpec((depth, size), lambda g: (0, g))
    whole = lambda shape: pl.BlockSpec(shape, lambda g: (0,) * len(shape))
    shape = jax.ShapeDtypeStruct
    owners, each = got.shape[0], width // got.shape[0]
    half = owners // 2
    slab = pl.BlockSpec((half, 3 * each, part), lambda g: (0, 0, g))
    return pl.pallas_call(
        functools.partial(weight_kernel, blocks, first, rows, runs),
        grid=(steps,),
        in_specs=[pl.BlockSpec(memory_space=pl.ANY)] * blocks
        + [
            pl.BlockSpec(memory_space=pltpu.SMEM),
            pl.BlockSpec(memory_space=pltpu.SMEM),
            whole((rows, width)), pl.BlockSpec((part, rows), lambda g: (g, 0)),
            pl.BlockSpec((owners, each, part), lambda g: (0, WQ, g)),
            whole((rows, width)), cols(PROMPT), cols(PROMPT), cols(tall - PROMPT), cols(tall - PROMPT),
        ],
        out_specs=[
            slab, slab, whole((rows, width)), cols(8),
        ],
        out_shape=[
            shape((half, 3 * each, width), BF), shape((half, 3 * each, width), BF),
            shape((rows, width), F32), shape((8, width), F32),
        ],
        scratch_shapes=[
            pltpu.VMEM((tall, width), BF), pltpu.VMEM((width, tall), BF), pltpu.SemaphoreType.DMA((blocks,)),
        ],
        compiler_params=pltpu.CompilerParams(vmem_limit_bytes=60 * 2**20),
        cost_estimate=pl.CostEstimate(
            flops=4 * tall * width * width, bytes_accessed=12 * tall * width, transcendentals=0
        ),
        name="weight_product",
    )(*spots, near, core, own, dq, got, h1, dkp, dvp, dkn, dvn)


def real_owners(grads, count, step, width):
    split = count // 32
    take = lambda v: v.reshape(32, -1, split, step, width).transpose(0, 2, 1, 3, 4).reshape(count, -1, width)
    outer, rest = grads[:, : 4 * split * step], grads[:, 4 * split * step :]
    return jnp.concatenate([outer.reshape(count, 4 * step, width), take(rest)], 1)


def solution(mesh):
    plan = Plan(mesh.shape["grp"], mesh.shape["row"])
    fine = Mesh(mesh.devices.reshape(plan.grp // 2, 2, 4, plan.row // 4), AXES)

    def per_device(
        tokens, cont_lengths, cotangent, w_query, w_key, w_value, w_output, w_inner, w_outer,
        bias_query, bias_value, bias_output, gain_first, shift_first, bias_inner, bias_outer,
        gain_second, shift_second,
    ):
        count = plan.count
        _, rows, width = tokens.shape
        step = w_query.shape[0]
        wide = w_inner.shape[1] // width
        own = tokens[0]

        early = (bias_query, bias_value)
        late = (bias_output, gain_first, shift_first, bias_outer, gain_second, shift_second, bias_inner)
        small = len(late) - 1

        def in_line(vectors):
            line, place = 0, 0
            for vector in vectors:
                size = vector.shape[0]
                line = line + jnp.pad(vector, (place, width - place - size))
                place += size
            return jnp.pad(line[None], ((0, 7), (0, 0)))

        line = jnp.concatenate([in_line(early), in_line(late)], 0)
        runs = plan.grp
        row = lax.axis_index(ROW)
        core = lax.axis_index("core").astype(jnp.int32).reshape(1)
        exchange = Tokens(plan, own)
        squares = (w_query, w_key, w_value)
        if step % 8 == 0:
            first_pack, pack = pack_call(w_output, w_inner, w_outer, *squares, line)
            got = lax.all_gather(pack, AXES, axis=0, tiled=True).reshape(count, -1, width)
            lines = got[:, (WI + WIDE) * step]

            def swaps(value, bits):
                masks = [0]
                for bit in bits:
                    masks = masks + [m ^ bit for m in masks]
                return [plan.swap(value, m) for m in masks[1:]]

            def stage(held, bit):
                return jnp.concatenate([held, plan.swap(held, bit)], 0)

            away = swaps(first_pack, plan.z)
            *away, same, beside = tie(*away, *exchange.stage_one())
            exchange.same, exchange.beside = same, beside
            cut = step + 16
            one = jnp.stack([v[:cut] for v in (first_pack, *away)])
            two = jnp.stack([v[cut:] for v in (first_pack, *away)])
            one, two = stage(one, plan.x[0]), stage(two, plan.y[0])
            one, two, *seen = tie(one, two, *exchange.stage_two())
            exchange.other, exchange.same_y, exchange.diagonal = seen
            one, two = stage(one, plan.y[0]), stage(two, plan.x[0])
            exchange.stage_three()
            one, exchange.other_y = tie(one, exchange.other_y)
            pieces = [one, plan.swap(one, plan.core[0]), two, plan.swap(two, plan.core[0])]
            order = lambda *bits: ([(bit, 1 << i) for i, bit in enumerate(bits)], plan.core[0])
            places = (
                order(*plan.z, plan.x[0], plan.y[0]),
                order(*plan.z, plan.y[0], plan.x[0]),
            )
            me = plan.me().astype(jnp.int32).reshape(1)
        else:
            inner_rows = [w_inner[:, i * width : (i + 1) * width] for i in range(wide)]
            pack = jnp.concatenate([w_outer, w_output, *inner_rows, *squares, line], 0)
            got = lax.all_gather(pack, AXES, axis=0, tiled=True).reshape(count, -1, width)
            lines = got[:, 12 * step + 8]
            cuts = [wide * step, (wide + 1) * step, (2 * wide + 1) * step, 12 * step]
            outer, output, inner, rest, marks = jnp.split(got, cuts, axis=1)
            apart = lambda v, n: v.reshape(count, n, step, width).transpose(1, 0, 2, 3)
            inner, rest = [
                v.reshape(v.shape[0], 32, width // 32, width).transpose(1, 0, 2, 3)
                for v in (apart(inner, wide), apart(rest, 3))
            ]
            got = jnp.concatenate([v.reshape(32, -1, width) for v in (outer, output, inner)], 1)
            pairs = marks[:, 0, : 2 * step].reshape(32, count // 32, 2, step).transpose(0, 2, 1, 3)
            pairs = jnp.pad(pairs.reshape(32, 1, -1), ((0, 0), (0, 7), (0, width - 2 * width // 32)))
            one = jnp.concatenate([rest[:, 0], pairs, rest[:, 1, :8]], 1)
            two = jnp.concatenate([rest[:, 1, 8:], rest[:, 2]], 1)
            pieces = [one[:16], one[16:], two[:16], two[16:]]
            places = (([(1, 1), (2, 2), (4, 4), (8, 8)], 16),) * 2
            me = jnp.zeros((1,), jnp.int32)
        spots, near = exchange.spots()
        first_near = PROMPT // rows

        table = lines[:, : small * step].reshape(count, small, step).transpose(1, 0, 2)
        table = table.reshape(small, width).astype(F32)
        v_bin = lines[:, small * step : (small + wide) * step].reshape(wide, width).astype(F32)
        v_bin = jnp.pad(v_bin, ((0, 8 - wide), (0, 0)))
        segments = segment_ids(cont_lengths[0], plan.row * rows)
        seg_own = lax.dynamic_slice_in_dim(segments, row * rows, rows, 0)[None, :]
        seg_near = near_segments(plan, segments, rows)[:, None]
        near = near.astype(jnp.int32).reshape(1)

        squares, queries, keys_p, values_p, keys_n, values_n, context, log_total = attention_call(
            spots, first_near, near, me, own, pieces, places, seg_own, seg_near
        )
        vec = jnp.concatenate([table, jnp.zeros((2, width), F32)], 0)
        layer_out, grad_h1, grad_context, g_send, g_keep, sums, sums_bin = middle_call(
            core if step % 8 == 0 else jnp.zeros_like(core), context, own, cotangent[0], got, vec, v_bin, step % 8 == 0
        )
        level = lambda value, axes: lax.psum_scatter(value, axes, scatter_dimension=0, tiled=True)
        if step % 8:
            pair = [v.reshape(2, 8, -1, width) for v in (g_keep, g_send)]
            grads = real_owners(jnp.stack(pair, 1).reshape(32, -1, width), count, step, width)
            grads = grads.reshape(plan.grp // 2, 2, 4, plan.row // 4, -1, width)
            grads = grads.transpose(1, 0, 3, 2, 4, 5).reshape(count, -1, width)
            g_got = level(grads, "core")
            g_keep = jnp.zeros_like(g_got)
        else:
            g_got = plan.swap(g_send, plan.core[0])
        core_bit = plan.core[0]
        left = [1 << i for i in reversed(range(plan.bits)) if 1 << i != core_bit]
        parts = width // 256
        dkp, dvp, dqp = back_call(
            0, parts, first_near, near, grad_context, context, queries, keys_p, values_p, log_total,
            seg_own, seg_near,
        )
        g_keep, g_got, dkp, dvp, dqp = tie(g_keep, g_got, dkp, dvp, dqp)
        grads = level((g_keep.astype(F32) + g_got.astype(F32)).astype(BF), ("x", "y"))
        shared_p = product_call(first_near, near, dkp, dvp, squares, rows)
        returned = Return(plan, rows)
        returned.prompt_one(shared_p)
        dkn, dvn, dq = back_call(
            0, parts, None, near, grad_context, context, queries, keys_n, values_n, log_total,
            seg_own, seg_near, dqp,
        )
        send, keep, grad_own, sums_qkv = weight_call(
            spots, first_near, near, own, dq, squares, grad_h1, dkp, dvp, dkn, dvn, core, runs
        )
        send, keep, returned.same, returned.same_y, dkn, dvn = tie(
            send, keep, returned.same, returned.same_y, dkn, dvn
        )
        returned.prompt_two()
        shared_n = product_call(None, near, dkn, dvn, squares, rows)

        order = (6, 5, 3, 4, 2, 0, 1)
        small = len(early) + len(late) - 1
        d_table = jnp.concatenate([sums_qkv[:1]] + [sums[i : i + 1] for i in order], 0)
        d_lines = jnp.concatenate(
            [
                d_table.reshape(small, count, step).transpose(1, 0, 2).reshape(count, -1),
                sums_bin[:wide].reshape(count, wide * step),
            ],
            1,
        )
        d_lines = jnp.pad(d_lines, ((0, 0), (0, width - d_lines.shape[1])))[:, None].astype(BF)
        d_lines = jnp.pad(d_lines, ((0, 0), (0, 7), (0, 0)))
        place = core[0]
        pick = Reduce(plan, [])
        if step % 8:
            real = lambda v: v.reshape(16, 3, count // 32, step, width).transpose(0, 2, 1, 3, 4)
            send, keep = [real(v).reshape(count // 2, 3 * step, width) for v in (send, keep)]
        send = jnp.concatenate([send, pick.cut(d_lines, core_bit, 1 - place)], 1)
        keep = jnp.concatenate([keep, pick.cut(d_lines, core_bit, place)], 1)
        reduce = Reduce(plan, [keep, plan.swap(send, core_bit)], left)
        for bit in plan.x + plan.y + plan.z[::-1]:
            held = reduce.terms
            if bit == plan.x[0]:
                held = tie(*held)
                returned.prompt_three()
            elif bit == plan.y[0]:
                *held, grads, shared_n, returned.back = tie(*held, grads, shared_n, returned.back)
                grads = level(grads, "z")
            elif bit == plan.z[-1]:
                *held, shared_n = tie(*held, shared_n)
                returned.near(shared_n)
            elif bit == plan.z[0]:
                *held, returned.own = tie(*held, returned.own)
            reduce.terms = list(held)
            reduce.stage(bit)
        o_ab = grads.reshape(-1, width).astype(F32)
        grad_tokens = grad_own + returned.total()
        o_first = reduce.result()
        o_line = o_first[3 * step]
        o_small = [o_line[i * step : (i + 1) * step] for i in range(small)]
        o_bin = o_line[small * step : (small + wide) * step]
        return (
            layer_out[None],
            grad_tokens.astype(BF)[None],
            o_first[:step],
            o_first[step : 2 * step],
            o_first[2 * step : 3 * step],
            o_ab[wide * step : (wide + 1) * step],
            jnp.concatenate([o_ab[i * step : (i + 1) * step] for i in range(wide + 1, 2 * wide + 1)], 1),
            o_ab[: wide * step],
            o_small[0],
            o_small[1],
            o_small[2],
            o_small[3],
            o_small[4],
            o_bin,
            o_small[5],
            o_small[6],
            o_small[7],
        )

    split = P(GRP, ROW, None)
    owned2, owned1 = P(AXES, None), P(AXES)
    in_specs = (split, P(GRP, None), split) + (owned2,) * 6 + (owned1,) * 9
    out_specs = (split, split) + (owned2,) * 6 + (owned1,) * 9
    return jax.shard_map(
        per_device, mesh=fine, in_specs=in_specs, out_specs=out_specs, check_vma=False
    )
```

```python
import functools

import jax
import jax.numpy as jnp
import numpy as np
from jax import lax
from jax.experimental import pallas as pl
from jax.experimental.pallas import tpu as pltpu
from jax.sharding import Mesh
from jax.sharding import PartitionSpec as P

HEADS = 12
HDIM = 64
PROMPT = 1024
CONT_MOST = 256
BF = jnp.bfloat16
F32 = jnp.float32

NORM_EPS = 1e-12
MASK_FILL = -1000000000.0
SQRT_HALF = 0.7071067811865476
INV_ROOT_TAU = 0.3989422804014327
AXES = ("x", "core", "z", "y")
GRP, ROW = AXES[:2], AXES[2:]
WIDE = 4
WO, WI = 4, 5
WQ, WK, WV = 0, 1, 2


def mm(left, right):
    return jnp.dot(left, right, preferred_element_type=F32)


def segment_ids(lengths, group_len):
    ends = jnp.cumsum(lengths)
    places = jnp.arange(group_len, dtype=jnp.int32)
    passed = jnp.sum(((places - PROMPT)[:, None] >= ends[None, :]).astype(jnp.int32), axis=-1)
    return jnp.where(places < PROMPT, 0, 1 + passed)


class Plan:
    def __init__(self, grp, row):
        self.grp, self.row, self.count = grp, row, grp * row
        y = row // 4
        bits = lambda base, size: [base << i for i in range(size.bit_length() - 1)]
        self.y, self.z = bits(1, y), bits(y, 4)
        self.core, self.x = bits(row, 2), bits(2 * row, grp // 2)
        self.bits = self.count.bit_length() - 1

    def swap(self, value, mask):
        return lax.ppermute(value, AXES, [(i, i ^ mask) for i in range(self.count)])

    def send(self, value, moves):
        pairs = [(g * self.row + a, g * self.row + b) for g in range(self.grp) for a, b in moves]
        return lax.ppermute(value, AXES, pairs)

    def me(self):
        return lax.axis_index(AXES)


class Reduce:
    def __init__(self, plan, terms, left=None):
        self.plan, self.terms = plan, list(terms)
        self.left = left or [1 << i for i in reversed(range(plan.bits))]

    def cut(self, term, bit, place):
        at = self.left.index(bit)
        high, low = 1 << at, 1 << (len(self.left) - at - 1)
        _, rows, width = term.shape
        term = term.reshape(high, 2, low * rows, width)
        return lax.dynamic_slice_in_dim(term, place, 1, 1).reshape(high * low, rows, width)

    def total(self, terms):
        return sum([t.astype(F32) for t in terms[1:]], terms[0].astype(F32))

    def stage(self, bit):
        place = (self.plan.me() // bit) & 1
        away = self.total([self.cut(t, bit, 1 - place) for t in self.terms]).astype(BF)
        here = [self.cut(t, bit, place) for t in self.terms]
        self.left = [b for b in self.left if b != bit]
        self.terms = here + [self.plan.swap(away, bit)]

    def stage_direct(self, bits):
        masks = [0]
        for bit in bits:
            masks = masks + [m ^ bit for m in masks]
        me, left = self.plan.me(), self.left
        parts = []
        for mask in masks:
            terms, self.left = self.terms, left
            for bit in bits:
                place = ((me ^ mask) // bit) & 1
                terms = [self.cut(t, bit, place) for t in terms]
                self.left = [b for b in self.left if b != bit]
            parts.append(terms)
        away = [self.total(p).astype(BF) for p in parts[1:]]
        self.terms = parts[0] + [self.plan.swap(v, m) for v, m in zip(away, masks[1:])]

    def result(self):
        return self.total(self.terms)[0]


def tie(*values):
    return lax.optimization_barrier(values)


class Tokens:
    def __init__(self, plan, own):
        self.plan, self.own = plan, own
        self.rows = own.shape[0]
        self.ready = plan.row == 8

    def stage_one(self):
        if self.ready:
            plan, own = self.plan, self.own
            across = plan.send(own, [(0, 4), (1, 5), (2, 6), (3, 7)])
            self.same = jnp.where(lax.axis_index(ROW) < 4, own, across)
            self.beside = plan.swap(own, 1)
            return [self.same, self.beside]
        return []

    def stage_two(self):
        if self.ready:
            plan = self.plan
            self.other = plan.swap(self.same, 2)
            self.same_y = plan.swap(self.same, 1)
            self.diagonal = plan.send(self.own, [(5, 6), (6, 5)])
            return [self.other, self.same_y, self.diagonal]
        return []

    def stage_three(self):
        if self.ready:
            self.other_y = self.plan.swap(self.same_y, 2)

    def spots(self):
        row, rows, own = lax.axis_index(ROW), self.rows, self.own
        if self.ready:
            near = jnp.where(row < 4, 0, jnp.where((row == 5) | (row == 6), 3, 2))
            return [
                self.same, self.other, self.same_y, self.other_y, own, self.beside, self.diagonal,
            ], near
        every = lax.all_gather(own, ROW, axis=0, tiled=True)
        start = jnp.maximum(row * rows - CONT_MOST, 0)
        padded = jnp.concatenate([every, jnp.zeros((CONT_MOST, own.shape[1]), own.dtype)], 0)
        near = lax.dynamic_slice_in_dim(padded, start, rows + 2 * CONT_MOST, 0)
        every = jnp.concatenate([every[:PROMPT], near], 0)
        spots = [every[i : i + rows] for i in range(0, every.shape[0], rows)]
        return spots, jnp.where(row * rows < PROMPT, 0, near.shape[0] // rows)


def near_segments(plan, segments, rows):
    row = lax.axis_index(ROW)
    if plan.row != 8:
        start = jnp.maximum(row * rows - CONT_MOST, 0)
        padded = jnp.concatenate([segments, jnp.full((CONT_MOST,), -1, jnp.int32)], 0)
        near = lax.dynamic_slice_in_dim(padded, start, rows + 2 * CONT_MOST, 0)
        return jnp.where((near == 0) | (row * rows < PROMPT), -1, near)
    pieces = []
    for block, valid in (
        (row, row >= 4),
        (row ^ 1, row >= 4),
        (11 - row, (row == 5) | (row == 6)),
    ):
        block = jnp.clip(block, 0, 7)
        ids = lax.dynamic_slice_in_dim(segments, block * rows, rows, 0)
        pieces.append(jnp.where(valid, ids, -1))
    return jnp.concatenate(pieces, 0)


class Return:
    def __init__(self, plan, rows):
        self.plan, self.rows = plan, rows

    def prompt_one(self, parts):
        self.prompt = self.same = self.same_y = self.own = self.back = parts
        if self.plan.row == 8:
            same, same_y = parts[0].astype(F32), parts[2].astype(F32)
            self.same_y = (same_y + self.plan.swap(parts[3], 2).astype(F32)).astype(BF)
            self.same = same + self.plan.swap(parts[1], 2).astype(F32)

    def prompt_two(self):
        if self.plan.row == 8:
            self.same = self.same + self.plan.swap(self.same_y, 1).astype(F32)

    def prompt_three(self):
        if self.plan.row == 8:
            self.back = self.plan.send(self.same.astype(BF), [(4, 0), (5, 1), (6, 2), (7, 3)])

    def near(self, parts):
        self.around = parts
        if self.plan.row == 8:
            own = parts[0].astype(F32) + self.plan.swap(parts[1], 1).astype(F32)
            self.own = own + self.plan.send(parts[2], [(5, 6), (6, 5)]).astype(F32)

    def total(self):
        row, rows = lax.axis_index(ROW), self.rows
        if self.plan.row == 8:
            return jnp.where(row < 4, self.same + self.back.astype(F32), self.own)
        around = self.around.reshape(-1, self.around.shape[-1]).astype(F32)
        start = jnp.maximum(row * rows - CONT_MOST, 0)
        whole = jnp.zeros((self.plan.row * rows + CONT_MOST, around.shape[1]), F32)
        whole = whole.at[:PROMPT].set(self.prompt.reshape(PROMPT, -1).astype(F32))
        near = jnp.where(row * rows < PROMPT, 0, around)
        near = lax.dynamic_slice_in_dim(whole, start, rows + 2 * CONT_MOST, 0) + near
        whole = lax.dynamic_update_slice_in_dim(whole, near, start, 0)
        return lax.psum_scatter(whole[: self.plan.row * rows], ROW, scatter_dimension=0, tiled=True)


def heads_mask(lanes, head):
    lane = lax.broadcasted_iota(jnp.int32, lanes, 1)
    return (lane >= head * HDIM) & (lane < (head + 1) * HDIM)


def nt(left, right):
    return lax.dot_general(left, right, (((1,), (1,)), ((), ())), preferred_element_type=F32)


def tn(left, right):
    return lax.dot_general(left, right, (((0,), (0,)), ((), ())), preferred_element_type=F32)


def pack_kernel(wo_ref, wi_ref, wu_ref, wq_ref, wk_ref, wv_ref, line_ref, early_ref, late_ref):
    step, width = wo_ref.shape
    early_ref[:step, :] = wq_ref[...]
    early_ref[step : step + 8, :] = line_ref[:8, :]
    early_ref[step + 8 : 2 * step + 8, :] = wk_ref[...]
    early_ref[2 * step + 8 :, :] = wv_ref[...]
    late_ref[: WIDE * step, :] = wu_ref[...]
    late_ref[WO * step : WI * step, :] = wo_ref[...]
    for i in range(WIDE):
        late_ref[(WI + i) * step : (WI + i + 1) * step, :] = wi_ref[:, i * width : (i + 1) * width]
    late_ref[(WI + WIDE) * step :, :] = line_ref[8:, :]


def pack_call(w_output, w_inner, w_outer, w_query, w_key, w_value, line):
    step, width = w_output.shape
    shape = lambda rows: jax.ShapeDtypeStruct((rows, width), BF)
    return pl.pallas_call(
        pack_kernel, out_shape=[shape(3 * step + 8), shape((WI + WIDE) * step + 8)], name="pack"
    )(w_output, w_inner, w_outer, w_query, w_key, w_value, line)


def attention_kernel(blocks, first, rows, places, *refs):
    spots = refs[:blocks]
    (near_ref, me_ref, own_ref, a0_ref, a1_ref, b0_ref, b1_ref, segq_ref, segk_ref,
     w_out, q_ref, kp_ref, vp_ref, kn_ref, vn_ref, ctx_ref, lse_ref,
     x_ref, w_ref, s_ref, vt_ref, out_ref, line_ref, bias_ref, sems, w_sems, o_sem) = refs[blocks:]
    near = near_ref[0]
    depth = own_ref.shape[1]
    owners = w_ref.shape[0]
    each = depth // owners
    part = q_ref.shape[1]

    def weights(act):
        @pl.loop(0, owners)
        def _(e):
            away = e ^ me_ref[0]
            for (bits, half), (zero, one), parts in (
                (places[0], (a0_ref, a1_ref), ((0, each, w_ref, 0), (each, 8, line_ref, 0), (each + 8, 8, w_ref, each))),
                (places[1], (b0_ref, b1_ref), ((0, 2 * each - 8, w_ref, each + 8),)),
            ):
                j = sum([((away // bit) & 1) * weight for bit, weight in bits])
                for which, source in enumerate((zero, one)):

                    @pl.when(((away // half) & 1) == which)
                    def _():
                        for k, (top, size, target, base) in enumerate(parts):
                            act(pltpu.make_async_copy(
                                source.at[j, pl.ds(top, size)], target.at[e, pl.ds(base, size)],
                                w_sems.at[k if zero is a0_ref else 3, e],
                            ))

    @pl.when(pl.program_id(0) == 0)
    def _():
        copies = [
            pltpu.make_async_copy(spot, x_ref.at[pl.ds(i * rows, rows)], sems.at[i])
            for i, spot in enumerate(spots)
        ]
        weights(lambda c: c.start())
        for copy in copies:
            copy.start()
        weights(lambda c: c.wait())
        for copy in copies:
            copy.wait()
        pltpu.make_async_copy(w_ref, w_out, o_sem).start()
        line = line_ref[:, 0, :128]
        place = lax.broadcasted_iota(jnp.int32, (128, depth), 0)
        lane = lax.broadcasted_iota(jnp.int32, (128, depth), 1)
        mine = lax.broadcasted_iota(jnp.int32, (owners, depth), 0)
        mine = mine == lax.broadcasted_iota(jnp.int32, (owners, depth), 1) // each
        for i in range(2):
            spread = mm(line, jnp.where(place == lane % each + i * each, 1.0, 0.0).astype(BF))
            bias_ref[i : i + 1, :] = jnp.sum(jnp.where(mine, spread, 0.0), axis=0, keepdims=True)

    lanes = pl.ds(pl.multiple_of(pl.program_id(0) * part, part), part)
    wq, wk, wv = [
        w_ref[:, i * each : (i + 1) * each, lanes].reshape(depth, part) for i in (WQ, WK, WV)
    ]
    queries = (mm(own_ref[...], wq) + bias_ref[0:1, lanes]) * (HDIM**-0.5)
    q_ref[...] = queries.astype(BF)

    heads = part // HDIM
    q = q_ref[...]
    tall = x_ref.shape[0]

    def body(sets):
        for k_ref, v_ref, base, size, _ in sets:
            x = x_ref[base : base + size, :]
            k_ref[...] = mm(x, wk).astype(BF)
            v = (mm(x, wv) + bias_ref[1:2, lanes]).astype(BF)
            v_ref[...] = v
            vt_ref[:, base : base + size] = v.T
        for h in range(heads):
            q_h = jnp.where(heads_mask(q.shape, h), q, 0)
            peak = jnp.full((1, rows), MASK_FILL, F32)
            for k_ref, _, base, size, masked in sets:
                s = nt(k_ref[...], q_h)
                if masked:
                    s = jnp.where(segk_ref[...] == segq_ref[...], s, MASK_FILL)
                s_ref[h % 2, base : base + size, :] = s
                peak = jnp.maximum(peak, jnp.max(s, axis=0, keepdims=True))
            total, mixed = jnp.zeros((1, rows), F32), jnp.zeros((HDIM, rows), F32)
            for _, _, base, size, _ in sets:
                p = jnp.exp(s_ref[h % 2, base : base + size, :] - peak)
                total = total + jnp.sum(p, axis=0, keepdims=True)
                mixed = mixed + mm(vt_ref[h * HDIM : (h + 1) * HDIM, base : base + size], p.astype(BF))
            out_ref[h * HDIM : (h + 1) * HDIM, :] = mixed / total
            lse_ref[0, h : h + 1, :] = peak + jnp.log(total)

    prompt = (kp_ref, vp_ref, 0, PROMPT, False)

    @pl.when(near == 0)
    def _():
        body([prompt])

    @pl.when(near > 0)
    def _():
        body([prompt, (kn_ref, vn_ref, PROMPT, tall - PROMPT, True)])

    ctx_ref[...] = out_ref[...].T.astype(BF)

    @pl.when(pl.program_id(0) == pl.num_programs(0) - 1)
    def _():
        pltpu.make_async_copy(w_ref, w_out, o_sem).wait()


def attention_call(spots, first, near, me, own, pieces, places, segq, segk):
    rows, width = own.shape
    blocks = len(spots)
    tall = blocks * rows
    part = 256
    steps = width // part
    heads = part // HDIM
    cols = lambda depth: pl.BlockSpec((depth, part), lambda g: (0, g))
    flops = 2 * tall * width * width * 2 + 4 * tall * rows * width * 4
    owners = 2 * pieces[0].shape[0]
    each = width // owners
    return pl.pallas_call(
        functools.partial(attention_kernel, blocks, first, rows, places),
        grid=(steps,),
        in_specs=[pl.BlockSpec(memory_space=pl.ANY)] * blocks
        + [
            pl.BlockSpec(memory_space=pltpu.SMEM),
            pl.BlockSpec(memory_space=pltpu.SMEM),
            pl.BlockSpec((rows, width), lambda g: (0, 0)),
        ] + [pl.BlockSpec(memory_space=pl.ANY)] * 4 + [
            pl.BlockSpec((1, rows), lambda g: (0, 0)),
            pl.BlockSpec(segk.shape, lambda g: (0, 0)),
        ],
        out_specs=[
            pl.BlockSpec(memory_space=pl.ANY),
            cols(rows), cols(PROMPT), cols(PROMPT), cols(tall - PROMPT), cols(tall - PROMPT),
            cols(rows), pl.BlockSpec((1, 8, rows), lambda g: (g, 0, 0)),
        ],
        out_shape=[
            jax.ShapeDtypeStruct((owners, 3 * each, width), BF),
            jax.ShapeDtypeStruct((rows, width), BF),
            jax.ShapeDtypeStruct((PROMPT, width), BF),
            jax.ShapeDtypeStruct((PROMPT, width), BF),
            jax.ShapeDtypeStruct((tall - PROMPT, width), BF),
            jax.ShapeDtypeStruct((tall - PROMPT, width), BF),
            jax.ShapeDtypeStruct((rows, width), BF),
            jax.ShapeDtypeStruct((steps, 8, rows), F32),
        ],
        scratch_shapes=[
            pltpu.VMEM((tall, width), BF),
            pltpu.VMEM((owners, 3 * each, width), BF),
            pltpu.VMEM((2, tall, rows), F32),
            pltpu.VMEM((part, tall), BF),
            pltpu.VMEM((part, rows), F32),
            pltpu.VMEM((owners, 8, width), BF),
            pltpu.VMEM((8, width), F32),
            pltpu.SemaphoreType.DMA((blocks,)),
            pltpu.SemaphoreType.DMA((4, owners)),
            pltpu.SemaphoreType.DMA,
        ],
        compiler_params=pltpu.CompilerParams(vmem_limit_bytes=60 * 2**20),
        cost_estimate=pl.CostEstimate(
            flops=flops, bytes_accessed=12 * 2**20, transcendentals=tall * rows * 12
        ),
        name="attention",
    )(*spots, near, me, own, *pieces, segq, segk)


def halves(value, runs, core):
    depth = value.shape[0] // runs
    pick = lambda first: jnp.concatenate(
        [value[i * depth : (i + 1) * depth] for i in range(first, runs, 2)], 0
    )
    even, odd = pick(0), pick(1)
    return jnp.where(core == 0, odd, even), jnp.where(core == 0, even, odd)


def middle_kernel(wide, mapped, ctx_ref, own_ref, cot_ref, got_ref, vec_ref, bin_ref,
                  out_ref, h1_ref, gctx_ref, grads, sums_ref, sbin_ref,
                  first_ref, n1_ref, inv_ref, low_ref, pre_ref, cdf_ref, act_ref, acc_ref,
                  gffn_ref, glow_ref, lowt_ref, w_ref, out_buf, in_buf, wo_buf, sems, w_sems):
    step = pl.program_id(0)
    width = ctx_ref.shape[1]
    vec = lambda i: vec_ref[i : i + 1, :]
    mean = lambda v: jnp.sum(v, axis=-1, keepdims=True) * (1.0 / width)
    down = lambda v: jnp.sum(v, axis=0, keepdims=True)
    owners = got_ref.shape[0]
    each = width // owners
    some = owners // wide
    square = lambda value: value.reshape(width, width)
    rows_of = lambda place: pl.ds(pl.multiple_of(place * each, each), each)
    w_output = lambda ref: ref.at[:, rows_of(WO)]
    w_inner = lambda ref, at: ref.at[:, rows_of(WI + at)]
    w_outer = lambda ref, at: ref.at[pl.ds(at * some, some), pl.ds(0, wide * each)]

    def fetch_inner(at):
        return pltpu.make_async_copy(w_inner(got_ref, at), w_inner(w_ref, at), w_sems.at[0, at])

    def fetch_outer(at):
        return pltpu.make_async_copy(w_outer(got_ref, at), w_outer(w_ref, at), w_sems.at[1, at])

    def fetch_output():
        return pltpu.make_async_copy(w_output(got_ref), w_output(w_ref), w_sems.at[0, wide])

    def slot(group, i):
        return group % 2 * 16 + group // 2 * 8 + i % 2 * 4 + i // 2 if mapped else group * 8 + i

    def outer(at):
        turn = (2 * wide - 1 - at) % 2
        return [
            pltpu.make_async_copy(
                out_buf.at[turn, i], grads.at[slot(at, i), pl.ds(0, wide * each)], sems.at[turn, i]
            )
            for i in range(some)
        ]

    def inner(at):
        turn = (2 * wide - 1 - at) % 2
        top = pl.multiple_of((wide + 1 + at) * each, each)
        return [
            pltpu.make_async_copy(
                in_buf.at[turn, e], grads.at[slot(e // 8, e % 8), pl.ds(top, each)], sems.at[2 + turn, e]
            )
            for e in range(owners)
        ]

    def output():
        return [
            pltpu.make_async_copy(
                wo_buf.at[e], grads.at[slot(e // 8, e % 8), pl.ds(wide * each, each)], sems.at[4, e]
            )
            for e in range(owners)
        ]

    def start(copies):
        for copy in copies:
            copy.start()

    def wait(copies):
        for copy in copies:
            copy.wait()

    @pl.when(step == 0)
    def _():
        fetch_output().start()
        for at in range(wide):
            fetch_inner(at).start()
            fetch_outer(at).start()
        fetch_output().wait()
        hidden = own_ref[...].astype(F32) + mm(ctx_ref[...], square(w_output(w_ref)[...])) + vec(0)
        centred = hidden - mean(hidden)
        inverse = lax.rsqrt(mean(centred * centred) + NORM_EPS)
        normed = centred * inverse
        n1_ref[...] = normed
        inv_ref[...] = inverse
        first = normed * vec(1) + vec(2)
        first_ref[...] = first
        low_ref[...] = first.astype(BF)
        lowt_ref[...] = first.astype(BF).T

    @pl.when(step < wide)
    def _():
        chunk = pl.ds(pl.multiple_of(step * width, width), width)
        fetch_inner(step).wait()
        fetch_outer(step).wait()
        pre = mm(low_ref[...], square(w_inner(w_ref, step)[...])) + bin_ref[pl.ds(step, 1), :]
        cdf = 0.5 * (1.0 + lax.erf(pre * SQRT_HALF))
        act = (pre * cdf).astype(BF)
        pre_ref[:, chunk] = pre
        cdf_ref[:, chunk] = cdf
        act_ref[:, chunk] = act
        more = mm(act, square(w_outer(w_ref, step)[...]))

        @pl.when(step == 0)
        def _():
            acc_ref[...] = more

        @pl.when(step > 0)
        def _():
            acc_ref[...] += more

    @pl.when(step == wide - 1)
    def _():
        hidden = first_ref[...] + acc_ref[...] + vec(3)
        centred = hidden - mean(hidden)
        inverse = lax.rsqrt(mean(centred * centred) + NORM_EPS)
        normed = centred * inverse
        out_ref[...] = (normed * vec(4) + vec(5)).astype(BF)
        grad = cot_ref[...].astype(F32)
        sums_ref[0:1, :] = down(grad * normed)
        sums_ref[1:2, :] = down(grad)
        e = grad * vec(4)
        back = inverse * (e - mean(e) - normed * mean(e * normed))
        gffn_ref[...] = back
        low = back.astype(BF)
        glow_ref[...] = low
        sums_ref[2:3, :] = down(low.astype(F32))

    @pl.when(step >= wide)
    def _():
        at = 2 * wide - 1 - step
        chunk = pl.ds(pl.multiple_of(at * width, width), width)
        pre = pre_ref[:, chunk]
        slope = cdf_ref[:, chunk] + pre * jnp.exp(-0.5 * pre * pre) * INV_ROOT_TAU
        low = glow_ref[...]
        grad = (nt(low, square(w_outer(w_ref, at)[...])) * slope).astype(BF)
        sbin_ref[pl.ds(at, 1), :] = down(grad.astype(F32))
        turn = step % 2

        @pl.when(step >= wide + 2)
        def _():
            wait(outer(at + 2) + inner(at + 2))

        out_buf[turn] = tn(act_ref[:, chunk], low).astype(BF).reshape(some, wide * each, width)
        start(outer(at))
        in_buf[turn] = mm(lowt_ref[...], grad).astype(BF).reshape(owners, each, width)
        start(inner(at))
        gffn_ref[...] += nt(grad, square(w_inner(w_ref, at)[...]))

    @pl.when(step == 2 * wide - 1)
    def _():
        grad = gffn_ref[...]
        normed = n1_ref[...]
        sums_ref[3:4, :] = down(grad * normed)
        sums_ref[4:5, :] = down(grad)
        e = grad * vec(1)
        back = inv_ref[...] * (e - mean(e) - normed * mean(e * normed))
        h1_ref[...] = back
        low = back.astype(BF)
        sums_ref[5:6, :] = down(low.astype(F32))
        wo_buf[...] = tn(ctx_ref[...], low).astype(BF).reshape(owners, each, width)
        start(output())
        gctx = nt(low, square(w_output(w_ref)[...])).astype(BF)
        gctx_ref[...] = gctx
        sums_ref[6:7, :] = down(gctx.astype(F32))
        sums_ref[7:8, :] = jnp.zeros((1, width), F32)
        wait(outer(1) + inner(1) + outer(0) + inner(0) + output())


def middle_call(ctx, own, cot, got, vec, b_inner, mapped):
    rows, width = own.shape
    owners = got.shape[0]
    each = width // owners
    wide = WIDE
    whole = lambda shape: pl.BlockSpec(shape, lambda s: (0,) * len(shape))
    shape = jax.ShapeDtypeStruct
    return pl.pallas_call(
        functools.partial(middle_kernel, wide, mapped),
        grid=(2 * wide,),
        in_specs=[
            whole((rows, width)), whole((rows, width)), whole((rows, width)),
            pl.BlockSpec(memory_space=pl.ANY),
            whole((8, width)), whole((8, width)),
        ],
        out_specs=[
            whole((rows, width)), whole((rows, width)), whole((rows, width)),
            pl.BlockSpec(memory_space=pl.ANY),
            whole((8, width)), whole((8, width)),
        ],
        out_shape=[
            shape((rows, width), BF), shape((rows, width), F32), shape((rows, width), BF),
            shape((owners, (2 * wide + 1) * each, width), BF),
            shape((8, width), F32), shape((8, width), F32),
        ],
        scratch_shapes=[
            pltpu.VMEM((rows, width), F32), pltpu.VMEM((rows, width), F32), pltpu.VMEM((rows, 1), F32),
            pltpu.VMEM((rows, width), BF), pltpu.VMEM((rows, wide * width), F32),
            pltpu.VMEM((rows, wide * width), F32), pltpu.VMEM((rows, wide * width), BF),
            pltpu.VMEM((rows, width), F32), pltpu.VMEM((rows, width), F32),
            pltpu.VMEM((rows, width), BF), pltpu.VMEM((width, rows), BF),
            pltpu.VMEM((owners, (2 * wide + 1) * each, width), BF),
            pltpu.VMEM((2, owners // wide, wide * each, width), BF),
            pltpu.VMEM((2, owners, each, width), BF),
            pltpu.VMEM((owners, each, width), BF), pltpu.SemaphoreType.DMA((5, owners)),
            pltpu.SemaphoreType.DMA((2, wide + 1)),
        ],
        compiler_params=pltpu.CompilerParams(vmem_limit_bytes=60 * 2**20),
        cost_estimate=pl.CostEstimate(
            flops=2 * rows * width * width * (6 * wide + 3), bytes_accessed=32 * 2**20,
            transcendentals=2 * rows * width * wide,
        ),
        name="middle",
    )(ctx, own, cot, got, vec, b_inner)


def back_kernel(rows, bound, started, *refs):
    near_ref, gctx_ref, ctx_ref, q_ref, k_ref, v_ref, lse_ref, segq_ref, segk_ref = refs[:9]
    dk_ref, dv_ref, dq_ref, kt_ref, p_ref, ds_ref = refs[-6:]
    q, g = q_ref[...], gctx_ref[...]
    part = q.shape[1]
    heads = part // HDIM
    masks = [heads_mask(q.shape, h) for h in range(heads)]
    q_parts = [jnp.where(m, q, 0) for m in masks]
    g_parts = [jnp.where(m, g, 0) for m in masks]
    product = (g.astype(F32) * ctx_ref[...].astype(F32)).T
    inner = [
        jnp.sum(product[h * HDIM : (h + 1) * HDIM], axis=0, keepdims=True) for h in range(heads)
    ]

    def body():
        k, v = k_ref[...], v_ref[...]
        kt_ref[...] = k.T
        for h in range(heads):
            s = nt(k, q_parts[h])
            if bound is None:
                s = jnp.where(segk_ref[...] == segq_ref[...], s, MASK_FILL)
            p = jnp.exp(s - lse_ref[0, h : h + 1, :])
            across = slice(h * rows, (h + 1) * rows)
            ds = (p * (nt(v, g_parts[h]) - inner[h])).astype(BF)
            p_ref[:, across] = p.astype(BF)
            ds_ref[:, across] = ds
            mine = slice(h * HDIM, (h + 1) * HDIM)
            more = mm(kt_ref[mine, :], ds)
            dq_ref[mine, :] = refs[9][mine, :] + more if started else more
        dk_ref[...] = mm(ds_ref[...], jnp.concatenate(q_parts, 0)).astype(BF)
        dv_ref[...] = mm(p_ref[...], jnp.concatenate(g_parts, 0)).astype(BF)

    if bound is None:

        @pl.when(near_ref[0] == 0)
        def _():
            dq_ref[...] = refs[9][...]

        pl.when(near_ref[0] > 0)(body)
    else:
        body()


def back_call(start, steps, bound, near, gctx, ctx, q, k, v, lse, segq, segk, dq0=None, into=None):
    rows, width = q.shape
    tall = k.shape[0]
    part = 256
    cols = lambda depth: pl.BlockSpec((depth, part), lambda g: (0, start + g))
    whole = lambda shape: pl.BlockSpec(shape, lambda g: (0,) * len(shape))
    down = pl.BlockSpec((part, rows), lambda g: (start + g, 0))
    shape = jax.ShapeDtypeStruct
    extra = ([dq0] if dq0 is not None else []) + list(into or [])
    specs = ([down] if dq0 is not None else []) + [pl.BlockSpec(memory_space=pl.ANY)] * len(into or [])
    return pl.pallas_call(
        functools.partial(back_kernel, rows, bound, dq0 is not None),
        grid=(steps,),
        in_specs=[
            pl.BlockSpec(memory_space=pltpu.SMEM),
            cols(rows), cols(rows), cols(rows), cols(tall), cols(tall),
            pl.BlockSpec((1, 8, rows), lambda g: (start + g, 0, 0)),
            whole((1, rows)), whole(segk.shape),
        ] + specs,
        out_specs=[cols(tall), cols(tall), down],
        out_shape=[shape((tall, width), BF), shape((tall, width), BF), shape((width, rows), F32)],
        input_output_aliases={9 + i: i for i in range(3)} if into else {},
        scratch_shapes=[
            pltpu.VMEM((part, tall), BF),
            pltpu.VMEM((tall, part // HDIM * rows), BF),
            pltpu.VMEM((tall, part // HDIM * rows), BF),
        ],
        compiler_params=pltpu.CompilerParams(vmem_limit_bytes=60 * 2**20),
        cost_estimate=pl.CostEstimate(
            flops=2 * 10 * 2 * tall * rows * part * steps * 2,
            bytes_accessed=8 * tall * part * steps, transcendentals=tall * rows * 4 * steps,
        ),
        name="attention_back",
    )(near, gctx, ctx, q, k, v, lse, segq, segk, *extra)


def product_kernel(rows, bound, near_ref, dk_ref, dv_ref, wk_ref, wv_ref, gx_ref):
    @pl.when((pl.program_id(0) < near_ref[0]) | (bound is not None))
    def _():
        width = dk_ref.shape[1]
        wk, wv = wk_ref[...].reshape(width, width), wv_ref[...].reshape(width, width)
        gx_ref[0] = (nt(dk_ref[...], wk) + nt(dv_ref[...], wv)).astype(BF)


def product_call(bound, near, dk, dv, got, rows):
    tall, width = dk.shape
    owners, each = got.shape[0], width // got.shape[0]
    weight = lambda place: pl.BlockSpec((owners, each, width), lambda b: (0, place, 0))
    return pl.pallas_call(
        functools.partial(product_kernel, rows, bound),
        grid=(tall // rows,),
        in_specs=[
            pl.BlockSpec(memory_space=pltpu.SMEM),
            pl.BlockSpec((rows, width), lambda b: (b, 0)),
            pl.BlockSpec((rows, width), lambda b: (b, 0)),
            weight(WK), weight(WV),
        ],
        out_specs=pl.BlockSpec((1, rows, width), lambda b: (b, 0, 0)),
        out_shape=jax.ShapeDtypeStruct((tall // rows, rows, width), BF),
        compiler_params=pltpu.CompilerParams(vmem_limit_bytes=60 * 2**20),
        cost_estimate=pl.CostEstimate(
            flops=4 * tall * width * width, bytes_accessed=6 * tall * width, transcendentals=0
        ),
        name="token_product",
    )(near, dk, dv, got, got)


def weight_kernel(blocks, first, rows, runs, *refs):
    spots = refs[:blocks]
    (near_ref, core_ref, own_ref, dq_ref, wq_ref, h1_ref, dkp_ref, dvp_ref, dkn_ref, dvn_ref,
     send_ref, keep_ref, gown_ref, sums_ref, x_ref, xt_ref, sems) = refs[blocks:]
    core = core_ref[0]
    step = pl.program_id(0)

    @pl.when(step == 0)
    def _():
        copies = [
            pltpu.make_async_copy(spot, x_ref.at[pl.ds(i * rows, rows)], sems.at[i])
            for i, spot in enumerate(spots)
        ]
        for copy in copies:
            copy.start()
        gown_ref[...] = h1_ref[...]
        for i, copy in enumerate(copies):
            copy.wait()
            xt_ref[:, i * rows : (i + 1) * rows] = x_ref[i * rows : (i + 1) * rows, :].T

    scale = HDIM**-0.5
    dq = dq_ref[...].T.astype(BF)
    part = dq.shape[1]
    width = x_ref.shape[1]
    gown_ref[...] += nt(dq, wq_ref[...].reshape(width, part)) * scale
    half = send_ref.shape[0]
    each = width // (2 * half)

    def put(i, grad):
        away, here = halves(grad.astype(BF), runs, core)
        send_ref[:, i * each : (i + 1) * each, :] = away.reshape(half, each, part)
        keep_ref[:, i * each : (i + 1) * each, :] = here.reshape(half, each, part)

    put(WQ, tn(own_ref[...], dq) * scale)
    sums_ref[0:1, :] = jnp.sum(dq.astype(F32), axis=0, keepdims=True) * scale

    def body(near):
        for i, p_ref, n_ref in ((WK, dkp_ref, dkn_ref), (WV, dvp_ref, dvn_ref)):
            grad = mm(xt_ref[:, :PROMPT], p_ref[...])
            if near:
                grad = grad + mm(xt_ref[:, PROMPT:], n_ref[...])
            put(i, grad)

    pl.when(near_ref[0] == 0)(lambda: body(False))
    pl.when(near_ref[0] > 0)(lambda: body(True))
    sums_ref[1:8, :] = jnp.zeros((7, part), F32)


def weight_call(spots, first, near, own, dq, got, h1, dkp, dvp, dkn, dvn, core, runs):
    rows, width = own.shape
    blocks = len(spots)
    tall = blocks * rows
    part = 256
    steps = width // part
    cols = lambda depth, size=part: pl.BlockSpec((depth, size), lambda g: (0, g))
    whole = lambda shape: pl.BlockSpec(shape, lambda g: (0,) * len(shape))
    shape = jax.ShapeDtypeStruct
    owners, each = got.shape[0], width // got.shape[0]
    half = owners // 2
    slab = pl.BlockSpec((half, 3 * each, part), lambda g: (0, 0, g))
    return pl.pallas_call(
        functools.partial(weight_kernel, blocks, first, rows, runs),
        grid=(steps,),
        in_specs=[pl.BlockSpec(memory_space=pl.ANY)] * blocks
        + [
            pl.BlockSpec(memory_space=pltpu.SMEM),
            pl.BlockSpec(memory_space=pltpu.SMEM),
            whole((rows, width)), pl.BlockSpec((part, rows), lambda g: (g, 0)),
            pl.BlockSpec((owners, each, part), lambda g: (0, WQ, g)),
            whole((rows, width)), cols(PROMPT), cols(PROMPT), cols(tall - PROMPT), cols(tall - PROMPT),
        ],
        out_specs=[
            slab, slab, whole((rows, width)), cols(8),
        ],
        out_shape=[
            shape((half, 3 * each, width), BF), shape((half, 3 * each, width), BF),
            shape((rows, width), F32), shape((8, width), F32),
        ],
        scratch_shapes=[
            pltpu.VMEM((tall, width), BF), pltpu.VMEM((width, tall), BF), pltpu.SemaphoreType.DMA((blocks,)),
        ],
        compiler_params=pltpu.CompilerParams(vmem_limit_bytes=60 * 2**20),
        cost_estimate=pl.CostEstimate(
            flops=4 * tall * width * width, bytes_accessed=12 * tall * width, transcendentals=0
        ),
        name="weight_product",
    )(*spots, near, core, own, dq, got, h1, dkp, dvp, dkn, dvn)


def real_owners(grads, count, step, width):
    split = count // 32
    take = lambda v: v.reshape(32, -1, split, step, width).transpose(0, 2, 1, 3, 4).reshape(count, -1, width)
    outer, rest = grads[:, : 4 * split * step], grads[:, 4 * split * step :]
    return jnp.concatenate([outer.reshape(count, 4 * step, width), take(rest)], 1)


def solution(mesh):
    plan = Plan(mesh.shape["grp"], mesh.shape["row"])
    fine = Mesh(mesh.devices.reshape(plan.grp // 2, 2, 4, plan.row // 4), AXES)

    def per_device(
        tokens, cont_lengths, cotangent, w_query, w_key, w_value, w_output, w_inner, w_outer,
        bias_query, bias_value, bias_output, gain_first, shift_first, bias_inner, bias_outer,
        gain_second, shift_second,
    ):
        count = plan.count
        _, rows, width = tokens.shape
        step = w_query.shape[0]
        wide = w_inner.shape[1] // width
        own = tokens[0]

        early = (bias_query, bias_value)
        late = (bias_output, gain_first, shift_first, bias_outer, gain_second, shift_second, bias_inner)
        small = len(late) - 1

        def in_line(vectors):
            line, place = 0, 0
            for vector in vectors:
                size = vector.shape[0]
                line = line + jnp.pad(vector, (place, width - place - size))
                place += size
            return jnp.pad(line[None], ((0, 7), (0, 0)))

        line = jnp.concatenate([in_line(early), in_line(late)], 0)
        runs = plan.grp
        row = lax.axis_index(ROW)
        core = lax.axis_index("core").astype(jnp.int32).reshape(1)
        exchange = Tokens(plan, own)
        squares = (w_query, w_key, w_value)
        if step % 8 == 0:
            first_pack, pack = pack_call(w_output, w_inner, w_outer, *squares, line)
            got = lax.all_gather(pack, AXES, axis=0, tiled=True).reshape(count, -1, width)
            lines = got[:, (WI + WIDE) * step]

            def swaps(value, bits):
                masks = [0]
                for bit in bits:
                    masks = masks + [m ^ bit for m in masks]
                return [plan.swap(value, m) for m in masks[1:]]

            def stage(held, bit):
                return jnp.concatenate([held, plan.swap(held, bit)], 0)

            away = swaps(first_pack, plan.z)
            *away, same, beside = tie(*away, *exchange.stage_one())
            exchange.same, exchange.beside = same, beside
            cut = step + 16
            one = jnp.stack([v[:cut] for v in (first_pack, *away)])
            two = jnp.stack([v[cut:] for v in (first_pack, *away)])
            one, two = stage(one, plan.x[0]), stage(two, plan.y[0])
            one, two, *seen = tie(one, two, *exchange.stage_two())
            exchange.other, exchange.same_y, exchange.diagonal = seen
            one, two = stage(one, plan.y[0]), stage(two, plan.x[0])
            exchange.stage_three()
            one, exchange.other_y = tie(one, exchange.other_y)
            pieces = [one, plan.swap(one, plan.core[0]), two, plan.swap(two, plan.core[0])]
            order = lambda *bits: ([(bit, 1 << i) for i, bit in enumerate(bits)], plan.core[0])
            places = (
                order(*plan.z, plan.x[0], plan.y[0]),
                order(*plan.z, plan.y[0], plan.x[0]),
            )
            me = plan.me().astype(jnp.int32).reshape(1)
        else:
            inner_rows = [w_inner[:, i * width : (i + 1) * width] for i in range(wide)]
            pack = jnp.concatenate([w_outer, w_output, *inner_rows, *squares, line], 0)
            got = lax.all_gather(pack, AXES, axis=0, tiled=True).reshape(count, -1, width)
            lines = got[:, 12 * step + 8]
            cuts = [wide * step, (wide + 1) * step, (2 * wide + 1) * step, 12 * step]
            outer, output, inner, rest, marks = jnp.split(got, cuts, axis=1)
            apart = lambda v, n: v.reshape(count, n, step, width).transpose(1, 0, 2, 3)
            inner, rest = [
                v.reshape(v.shape[0], 32, width // 32, width).transpose(1, 0, 2, 3)
                for v in (apart(inner, wide), apart(rest, 3))
            ]
            got = jnp.concatenate([v.reshape(32, -1, width) for v in (outer, output, inner)], 1)
            pairs = marks[:, 0, : 2 * step].reshape(32, count // 32, 2, step).transpose(0, 2, 1, 3)
            pairs = jnp.pad(pairs.reshape(32, 1, -1), ((0, 0), (0, 7), (0, width - 2 * width // 32)))
            one = jnp.concatenate([rest[:, 0], pairs, rest[:, 1, :8]], 1)
            two = jnp.concatenate([rest[:, 1, 8:], rest[:, 2]], 1)
            pieces = [one[:16], one[16:], two[:16], two[16:]]
            places = (([(1, 1), (2, 2), (4, 4), (8, 8)], 16),) * 2
            me = jnp.zeros((1,), jnp.int32)
        spots, near = exchange.spots()
        first_near = PROMPT // rows

        table = lines[:, : small * step].reshape(count, small, step).transpose(1, 0, 2)
        table = table.reshape(small, width).astype(F32)
        v_bin = lines[:, small * step : (small + wide) * step].reshape(wide, width).astype(F32)
        v_bin = jnp.pad(v_bin, ((0, 8 - wide), (0, 0)))
        segments = segment_ids(cont_lengths[0], plan.row * rows)
        seg_own = lax.dynamic_slice_in_dim(segments, row * rows, rows, 0)[None, :]
        seg_near = near_segments(plan, segments, rows)[:, None]
        near = near.astype(jnp.int32).reshape(1)

        squares, queries, keys_p, values_p, keys_n, values_n, context, log_total = attention_call(
            spots, first_near, near, me, own, pieces, places, seg_own, seg_near
        )
        vec = jnp.concatenate([table, jnp.zeros((2, width), F32)], 0)
        layer_out, grad_h1, grad_context, grads, sums, sums_bin = middle_call(
            context, own, cotangent[0], got, vec, v_bin, step % 8 == 0
        )
        if step % 8:
            grads = real_owners(grads, count, step, width)
            grads = grads.reshape(plan.grp // 2, 2, 4, plan.row // 4, -1, width)
            grads = grads.transpose(1, 0, 3, 2, 4, 5).reshape(count, -1, width)
        level = lambda value, axes: lax.psum_scatter(value, axes, scatter_dimension=0, tiled=True)
        grads = level(grads, "core")
        core_bit = plan.core[0]
        left = [1 << i for i in reversed(range(plan.bits)) if 1 << i != core_bit]
        parts = width // 256
        dkp, dvp, dqp = back_call(
            0, parts, first_near, near, grad_context, context, queries, keys_p, values_p, log_total,
            seg_own, seg_near,
        )
        shared_p = product_call(first_near, near, dkp, dvp, squares, rows)
        grads, shared_p, dqp = tie(grads, shared_p, dqp)
        grads = level(grads, ("x", "y"))
        returned = Return(plan, rows)
        returned.prompt_one(shared_p)
        dkn, dvn, dq = back_call(
            0, parts, None, near, grad_context, context, queries, keys_n, values_n, log_total,
            seg_own, seg_near, dqp,
        )
        send, keep, grad_own, sums_qkv = weight_call(
            spots, first_near, near, own, dq, squares, grad_h1, dkp, dvp, dkn, dvn, core, runs
        )
        send, keep, returned.same, returned.same_y, dkn, dvn = tie(
            send, keep, returned.same, returned.same_y, dkn, dvn
        )
        returned.prompt_two()
        shared_n = product_call(None, near, dkn, dvn, squares, rows)

        order = (6, 5, 3, 4, 2, 0, 1)
        small = len(early) + len(late) - 1
        d_table = jnp.concatenate([sums_qkv[:1]] + [sums[i : i + 1] for i in order], 0)
        d_lines = jnp.concatenate(
            [
                d_table.reshape(small, count, step).transpose(1, 0, 2).reshape(count, -1),
                sums_bin[:wide].reshape(count, wide * step),
            ],
            1,
        )
        d_lines = jnp.pad(d_lines, ((0, 0), (0, width - d_lines.shape[1])))[:, None].astype(BF)
        d_lines = jnp.pad(d_lines, ((0, 0), (0, 7), (0, 0)))
        place = core[0]
        pick = Reduce(plan, [])
        if step % 8:
            real = lambda v: v.reshape(16, 3, count // 32, step, width).transpose(0, 2, 1, 3, 4)
            send, keep = [real(v).reshape(count // 2, 3 * step, width) for v in (send, keep)]
        send = jnp.concatenate([send, pick.cut(d_lines, core_bit, 1 - place)], 1)
        keep = jnp.concatenate([keep, pick.cut(d_lines, core_bit, place)], 1)
        reduce = Reduce(plan, [keep, plan.swap(send, core_bit)], left)
        for bit in plan.x + plan.y:
            held = reduce.terms
            if bit == plan.x[0]:
                held = tie(*held)
                returned.prompt_three()
            elif bit == plan.y[0]:
                *held, grads, shared_n, returned.back = tie(*held, grads, shared_n, returned.back)
                grads = level(grads, "z")
            reduce.terms = list(held)
            reduce.stage(bit)
        *held, shared_n = tie(*reduce.terms, shared_n)
        reduce.terms = list(held)
        returned.near(shared_n)
        reduce.stage_direct(plan.z)
        o_ab = grads.reshape(-1, width).astype(F32)
        grad_tokens = grad_own + returned.total()
        o_first = reduce.result()
        o_line = o_first[3 * step]
        o_small = [o_line[i * step : (i + 1) * step] for i in range(small)]
        o_bin = o_line[small * step : (small + wide) * step]
        return (
            layer_out[None],
            grad_tokens.astype(BF)[None],
            o_first[:step],
            o_first[step : 2 * step],
            o_first[2 * step : 3 * step],
            o_ab[wide * step : (wide + 1) * step],
            jnp.concatenate([o_ab[i * step : (i + 1) * step] for i in range(wide + 1, 2 * wide + 1)], 1),
            o_ab[: wide * step],
            o_small[0],
            o_small[1],
            o_small[2],
            o_small[3],
            o_small[4],
            o_bin,
            o_small[5],
            o_small[6],
            o_small[7],
        )

    split = P(GRP, ROW, None)
    owned2, owned1 = P(AXES, None), P(AXES)
    in_specs = (split, P(GRP, None), split) + (owned2,) * 6 + (owned1,) * 9
    out_specs = (split, split) + (owned2,) * 6 + (owned1,) * 9
    return jax.shard_map(
        per_device, mesh=fine, in_specs=in_specs, out_specs=out_specs, check_vma=False
    )
```

```python
import functools

import jax
import jax.numpy as jnp
import numpy as np
from jax import lax
from jax.experimental import pallas as pl
from jax.experimental.pallas import tpu as pltpu
from jax.sharding import Mesh
from jax.sharding import PartitionSpec as P

HEADS = 12
HDIM = 64
PROMPT = 1024
CONT_MOST = 256
BF = jnp.bfloat16
F32 = jnp.float32

NORM_EPS = 1e-12
MASK_FILL = -1000000000.0
SQRT_HALF = 0.7071067811865476
INV_ROOT_TAU = 0.3989422804014327
AXES = ("x", "core", "z", "y")
GRP, ROW = AXES[:2], AXES[2:]
WIDE = 4
WO, WI = 4, 5
WQ, WK, WV = 0, 1, 2


def mm(left, right):
    return jnp.dot(left, right, preferred_element_type=F32)


def segment_ids(lengths, group_len):
    ends = jnp.cumsum(lengths)
    places = jnp.arange(group_len, dtype=jnp.int32)
    passed = jnp.sum(((places - PROMPT)[:, None] >= ends[None, :]).astype(jnp.int32), axis=-1)
    return jnp.where(places < PROMPT, 0, 1 + passed)


class Plan:
    def __init__(self, grp, row):
        self.grp, self.row, self.count = grp, row, grp * row
        y = row // 4
        bits = lambda base, size: [base << i for i in range(size.bit_length() - 1)]
        self.y, self.z = bits(1, y), bits(y, 4)
        self.core, self.x = bits(row, 2), bits(2 * row, grp // 2)
        self.bits = self.count.bit_length() - 1

    def swap(self, value, mask):
        return lax.ppermute(value, AXES, [(i, i ^ mask) for i in range(self.count)])

    def send(self, value, moves):
        pairs = [(g * self.row + a, g * self.row + b) for g in range(self.grp) for a, b in moves]
        return lax.ppermute(value, AXES, pairs)

    def me(self):
        return lax.axis_index(AXES)


class Reduce:
    def __init__(self, plan, terms, left=None):
        self.plan, self.terms = plan, list(terms)
        self.left = left or [1 << i for i in reversed(range(plan.bits))]

    def cut(self, term, bit, place):
        at = self.left.index(bit)
        high, low = 1 << at, 1 << (len(self.left) - at - 1)
        _, rows, width = term.shape
        term = term.reshape(high, 2, low * rows, width)
        return lax.dynamic_slice_in_dim(term, place, 1, 1).reshape(high * low, rows, width)

    def total(self, terms):
        return sum([t.astype(F32) for t in terms[1:]], terms[0].astype(F32))

    def stage(self, bit):
        place = (self.plan.me() // bit) & 1
        away = self.total([self.cut(t, bit, 1 - place) for t in self.terms]).astype(BF)
        here = [self.cut(t, bit, place) for t in self.terms]
        self.left = [b for b in self.left if b != bit]
        self.terms = here + [self.plan.swap(away, bit)]

    def stage_direct(self, bits):
        masks = [0]
        for bit in bits:
            masks = masks + [m ^ bit for m in masks]
        me, left = self.plan.me(), self.left
        parts = []
        for mask in masks:
            terms, self.left = self.terms, left
            for bit in bits:
                place = ((me ^ mask) // bit) & 1
                terms = [self.cut(t, bit, place) for t in terms]
                self.left = [b for b in self.left if b != bit]
            parts.append(terms)
        away = [self.total(p).astype(BF) for p in parts[1:]]
        self.terms = parts[0] + [self.plan.swap(v, m) for v, m in zip(away, masks[1:])]

    def result(self):
        return self.total(self.terms)[0]


def tie(*values):
    return lax.optimization_barrier(values)


class Tokens:
    def __init__(self, plan, own):
        self.plan, self.own = plan, own
        self.rows = own.shape[0]
        self.ready = plan.row == 8

    def stage_one(self):
        if self.ready:
            plan, own = self.plan, self.own
            across = plan.send(own, [(0, 4), (1, 5), (2, 6), (3, 7)])
            self.same = jnp.where(lax.axis_index(ROW) < 4, own, across)
            self.beside = plan.swap(own, 1)
            return [self.same, self.beside]
        return []

    def stage_two(self):
        if self.ready:
            plan = self.plan
            self.other = plan.swap(self.same, 2)
            self.same_y = plan.swap(self.same, 1)
            self.diagonal = plan.send(self.own, [(5, 6), (6, 5)])
            return [self.other, self.same_y, self.diagonal]
        return []

    def stage_three(self):
        if self.ready:
            self.other_y = self.plan.swap(self.same_y, 2)

    def spots(self):
        row, rows, own = lax.axis_index(ROW), self.rows, self.own
        if self.ready:
            near = jnp.where(row < 4, 0, jnp.where((row == 5) | (row == 6), 3, 2))
            return [
                self.same, self.other, self.same_y, self.other_y, own, self.beside, self.diagonal,
            ], near
        every = lax.all_gather(own, ROW, axis=0, tiled=True)
        start = jnp.maximum(row * rows - CONT_MOST, 0)
        padded = jnp.concatenate([every, jnp.zeros((CONT_MOST, own.shape[1]), own.dtype)], 0)
        near = lax.dynamic_slice_in_dim(padded, start, rows + 2 * CONT_MOST, 0)
        every = jnp.concatenate([every[:PROMPT], near], 0)
        spots = [every[i : i + rows] for i in range(0, every.shape[0], rows)]
        return spots, jnp.where(row * rows < PROMPT, 0, near.shape[0] // rows)


def near_segments(plan, segments, rows):
    row = lax.axis_index(ROW)
    if plan.row != 8:
        start = jnp.maximum(row * rows - CONT_MOST, 0)
        padded = jnp.concatenate([segments, jnp.full((CONT_MOST,), -1, jnp.int32)], 0)
        near = lax.dynamic_slice_in_dim(padded, start, rows + 2 * CONT_MOST, 0)
        return jnp.where((near == 0) | (row * rows < PROMPT), -1, near)
    pieces = []
    for block, valid in (
        (row, row >= 4),
        (row ^ 1, row >= 4),
        (11 - row, (row == 5) | (row == 6)),
    ):
        block = jnp.clip(block, 0, 7)
        ids = lax.dynamic_slice_in_dim(segments, block * rows, rows, 0)
        pieces.append(jnp.where(valid, ids, -1))
    return jnp.concatenate(pieces, 0)


class Return:
    def __init__(self, plan, rows):
        self.plan, self.rows = plan, rows

    def prompt_one(self, parts):
        self.prompt = self.same = self.same_y = self.own = self.back = parts
        if self.plan.row == 8:
            same, same_y = parts[0].astype(F32), parts[2].astype(F32)
            self.same_y = (same_y + self.plan.swap(parts[3], 2).astype(F32)).astype(BF)
            self.same = same + self.plan.swap(parts[1], 2).astype(F32)

    def prompt_two(self):
        if self.plan.row == 8:
            self.same = self.same + self.plan.swap(self.same_y, 1).astype(F32)

    def prompt_three(self):
        if self.plan.row == 8:
            self.back = self.plan.send(self.same.astype(BF), [(4, 0), (5, 1), (6, 2), (7, 3)])

    def near(self, parts):
        self.around = parts
        if self.plan.row == 8:
            own = parts[0].astype(F32) + self.plan.swap(parts[1], 1).astype(F32)
            self.own = own + self.plan.send(parts[2], [(5, 6), (6, 5)]).astype(F32)

    def total(self):
        row, rows = lax.axis_index(ROW), self.rows
        if self.plan.row == 8:
            return jnp.where(row < 4, self.same + self.back.astype(F32), self.own)
        around = self.around.reshape(-1, self.around.shape[-1]).astype(F32)
        start = jnp.maximum(row * rows - CONT_MOST, 0)
        whole = jnp.zeros((self.plan.row * rows + CONT_MOST, around.shape[1]), F32)
        whole = whole.at[:PROMPT].set(self.prompt.reshape(PROMPT, -1).astype(F32))
        near = jnp.where(row * rows < PROMPT, 0, around)
        near = lax.dynamic_slice_in_dim(whole, start, rows + 2 * CONT_MOST, 0) + near
        whole = lax.dynamic_update_slice_in_dim(whole, near, start, 0)
        return lax.psum_scatter(whole[: self.plan.row * rows], ROW, scatter_dimension=0, tiled=True)


def heads_mask(lanes, head):
    lane = lax.broadcasted_iota(jnp.int32, lanes, 1)
    return (lane >= head * HDIM) & (lane < (head + 1) * HDIM)


def nt(left, right):
    return lax.dot_general(left, right, (((1,), (1,)), ((), ())), preferred_element_type=F32)


def tn(left, right):
    return lax.dot_general(left, right, (((0,), (0,)), ((), ())), preferred_element_type=F32)


def pack_kernel(wo_ref, wi_ref, wu_ref, wq_ref, wk_ref, wv_ref, line_ref, early_ref, late_ref):
    step, width = wo_ref.shape
    early_ref[:step, :] = wq_ref[...]
    early_ref[step : step + 8, :] = line_ref[:8, :]
    early_ref[step + 8 : 2 * step + 8, :] = wk_ref[...]
    early_ref[2 * step + 8 :, :] = wv_ref[...]
    late_ref[: WIDE * step, :] = wu_ref[...]
    late_ref[WO * step : WI * step, :] = wo_ref[...]
    for i in range(WIDE):
        late_ref[(WI + i) * step : (WI + i + 1) * step, :] = wi_ref[:, i * width : (i + 1) * width]
    late_ref[(WI + WIDE) * step :, :] = line_ref[8:, :]


def pack_call(w_output, w_inner, w_outer, w_query, w_key, w_value, line):
    step, width = w_output.shape
    shape = lambda rows: jax.ShapeDtypeStruct((rows, width), BF)
    return pl.pallas_call(
        pack_kernel, out_shape=[shape(3 * step + 8), shape((WI + WIDE) * step + 8)], name="pack"
    )(w_output, w_inner, w_outer, w_query, w_key, w_value, line)


def attention_kernel(blocks, first, rows, places, *refs):
    spots = refs[:blocks]
    (near_ref, me_ref, own_ref, a0_ref, a1_ref, b0_ref, b1_ref, segq_ref, segk_ref,
     w_out, q_ref, kp_ref, vp_ref, kn_ref, vn_ref, ctx_ref, lse_ref,
     x_ref, w_ref, s_ref, vt_ref, out_ref, line_ref, bias_ref, sems, w_sems, o_sem) = refs[blocks:]
    near = near_ref[0]
    depth = own_ref.shape[1]
    owners = w_ref.shape[0]
    each = depth // owners
    part = q_ref.shape[1]

    def weights(act):
        @pl.loop(0, owners)
        def _(e):
            away = e ^ me_ref[0]
            for (bits, half), (zero, one), parts in (
                (places[0], (a0_ref, a1_ref), ((0, each, w_ref, 0), (each, 8, line_ref, 0), (each + 8, 8, w_ref, each))),
                (places[1], (b0_ref, b1_ref), ((0, 2 * each - 8, w_ref, each + 8),)),
            ):
                j = sum([((away // bit) & 1) * weight for bit, weight in bits])
                for which, source in enumerate((zero, one)):

                    @pl.when(((away // half) & 1) == which)
                    def _():
                        for k, (top, size, target, base) in enumerate(parts):
                            act(pltpu.make_async_copy(
                                source.at[j, pl.ds(top, size)], target.at[e, pl.ds(base, size)],
                                w_sems.at[k if zero is a0_ref else 3, e],
                            ))

    @pl.when(pl.program_id(0) == 0)
    def _():
        copies = [
            pltpu.make_async_copy(spot, x_ref.at[pl.ds(i * rows, rows)], sems.at[i])
            for i, spot in enumerate(spots)
        ]
        weights(lambda c: c.start())
        for copy in copies:
            copy.start()
        weights(lambda c: c.wait())
        for copy in copies:
            copy.wait()
        pltpu.make_async_copy(w_ref, w_out, o_sem).start()
        line = line_ref[:, 0, :128]
        place = lax.broadcasted_iota(jnp.int32, (128, depth), 0)
        lane = lax.broadcasted_iota(jnp.int32, (128, depth), 1)
        mine = lax.broadcasted_iota(jnp.int32, (owners, depth), 0)
        mine = mine == lax.broadcasted_iota(jnp.int32, (owners, depth), 1) // each
        for i in range(2):
            spread = mm(line, jnp.where(place == lane % each + i * each, 1.0, 0.0).astype(BF))
            bias_ref[i : i + 1, :] = jnp.sum(jnp.where(mine, spread, 0.0), axis=0, keepdims=True)

    lanes = pl.ds(pl.multiple_of(pl.program_id(0) * part, part), part)
    wq, wk, wv = [
        w_ref[:, i * each : (i + 1) * each, lanes].reshape(depth, part) for i in (WQ, WK, WV)
    ]
    queries = (mm(own_ref[...], wq) + bias_ref[0:1, lanes]) * (HDIM**-0.5)
    q_ref[...] = queries.astype(BF)

    heads = part // HDIM
    q = q_ref[...]
    tall = x_ref.shape[0]

    def body(sets):
        for k_ref, v_ref, base, size, _ in sets:
            x = x_ref[base : base + size, :]
            k_ref[...] = mm(x, wk).astype(BF)
            v = (mm(x, wv) + bias_ref[1:2, lanes]).astype(BF)
            v_ref[...] = v
            vt_ref[:, base : base + size] = v.T
        for h in range(heads):
            q_h = jnp.where(heads_mask(q.shape, h), q, 0)
            peak = jnp.full((1, rows), MASK_FILL, F32)
            for k_ref, _, base, size, masked in sets:
                s = nt(k_ref[...], q_h)
                if masked:
                    s = jnp.where(segk_ref[...] == segq_ref[...], s, MASK_FILL)
                s_ref[h % 2, base : base + size, :] = s
                peak = jnp.maximum(peak, jnp.max(s, axis=0, keepdims=True))
            total, mixed = jnp.zeros((1, rows), F32), jnp.zeros((HDIM, rows), F32)
            for _, _, base, size, _ in sets:
                p = jnp.exp(s_ref[h % 2, base : base + size, :] - peak)
                total = total + jnp.sum(p, axis=0, keepdims=True)
                mixed = mixed + mm(vt_ref[h * HDIM : (h + 1) * HDIM, base : base + size], p.astype(BF))
            out_ref[h * HDIM : (h + 1) * HDIM, :] = mixed / total
            lse_ref[0, h : h + 1, :] = peak + jnp.log(total)

    prompt = (kp_ref, vp_ref, 0, PROMPT, False)

    @pl.when(near == 0)
    def _():
        body([prompt])

    @pl.when(near > 0)
    def _():
        body([prompt, (kn_ref, vn_ref, PROMPT, tall - PROMPT, True)])

    ctx_ref[...] = out_ref[...].T.astype(BF)

    @pl.when(pl.program_id(0) == pl.num_programs(0) - 1)
    def _():
        pltpu.make_async_copy(w_ref, w_out, o_sem).wait()


def attention_call(spots, first, near, me, own, pieces, places, segq, segk):
    rows, width = own.shape
    blocks = len(spots)
    tall = blocks * rows
    part = 256
    steps = width // part
    heads = part // HDIM
    cols = lambda depth: pl.BlockSpec((depth, part), lambda g: (0, g))
    flops = 2 * tall * width * width * 2 + 4 * tall * rows * width * 4
    owners = 2 * pieces[0].shape[0]
    each = width // owners
    return pl.pallas_call(
        functools.partial(attention_kernel, blocks, first, rows, places),
        grid=(steps,),
        in_specs=[pl.BlockSpec(memory_space=pl.ANY)] * blocks
        + [
            pl.BlockSpec(memory_space=pltpu.SMEM),
            pl.BlockSpec(memory_space=pltpu.SMEM),
            pl.BlockSpec((rows, width), lambda g: (0, 0)),
        ] + [pl.BlockSpec(memory_space=pl.ANY)] * 4 + [
            pl.BlockSpec((1, rows), lambda g: (0, 0)),
            pl.BlockSpec(segk.shape, lambda g: (0, 0)),
        ],
        out_specs=[
            pl.BlockSpec(memory_space=pl.ANY),
            cols(rows), cols(PROMPT), cols(PROMPT), cols(tall - PROMPT), cols(tall - PROMPT),
            cols(rows), pl.BlockSpec((1, 8, rows), lambda g: (g, 0, 0)),
        ],
        out_shape=[
            jax.ShapeDtypeStruct((owners, 3 * each, width), BF),
            jax.ShapeDtypeStruct((rows, width), BF),
            jax.ShapeDtypeStruct((PROMPT, width), BF),
            jax.ShapeDtypeStruct((PROMPT, width), BF),
            jax.ShapeDtypeStruct((tall - PROMPT, width), BF),
            jax.ShapeDtypeStruct((tall - PROMPT, width), BF),
            jax.ShapeDtypeStruct((rows, width), BF),
            jax.ShapeDtypeStruct((steps, 8, rows), F32),
        ],
        scratch_shapes=[
            pltpu.VMEM((tall, width), BF),
            pltpu.VMEM((owners, 3 * each, width), BF),
            pltpu.VMEM((2, tall, rows), F32),
            pltpu.VMEM((part, tall), BF),
            pltpu.VMEM((part, rows), F32),
            pltpu.VMEM((owners, 8, width), BF),
            pltpu.VMEM((8, width), F32),
            pltpu.SemaphoreType.DMA((blocks,)),
            pltpu.SemaphoreType.DMA((4, owners)),
            pltpu.SemaphoreType.DMA,
        ],
        compiler_params=pltpu.CompilerParams(vmem_limit_bytes=60 * 2**20),
        cost_estimate=pl.CostEstimate(
            flops=flops, bytes_accessed=12 * 2**20, transcendentals=tall * rows * 12
        ),
        name="attention",
    )(*spots, near, me, own, *pieces, segq, segk)


def halves(value, runs, core):
    depth = value.shape[0] // runs
    pick = lambda first: jnp.concatenate(
        [value[i * depth : (i + 1) * depth] for i in range(first, runs, 2)], 0
    )
    even, odd = pick(0), pick(1)
    return jnp.where(core == 0, odd, even), jnp.where(core == 0, even, odd)


def middle_kernel(wide, mapped, ctx_ref, own_ref, cot_ref, got_ref, vec_ref, bin_ref,
                  out_ref, h1_ref, gctx_ref, grads, sums_ref, sbin_ref,
                  first_ref, n1_ref, inv_ref, low_ref, pre_ref, cdf_ref, act_ref, acc_ref,
                  gffn_ref, glow_ref, lowt_ref, w_ref, out_buf, in_buf, wo_buf, sems, w_sems):
    step = pl.program_id(0)
    width = ctx_ref.shape[1]
    vec = lambda i: vec_ref[i : i + 1, :]
    mean = lambda v: jnp.sum(v, axis=-1, keepdims=True) * (1.0 / width)
    down = lambda v: jnp.sum(v, axis=0, keepdims=True)
    owners = got_ref.shape[0]
    each = width // owners
    some = owners // wide
    square = lambda value: value.reshape(width, width)
    rows_of = lambda place: pl.ds(pl.multiple_of(place * each, each), each)
    w_output = lambda ref: ref.at[:, rows_of(WO)]
    w_inner = lambda ref, at: ref.at[:, rows_of(WI + at)]
    w_outer = lambda ref, at: ref.at[pl.ds(at * some, some), pl.ds(0, wide * each)]

    def fetch_inner(at):
        return pltpu.make_async_copy(w_inner(got_ref, at), w_inner(w_ref, at), w_sems.at[0, at])

    def fetch_outer(at):
        return pltpu.make_async_copy(w_outer(got_ref, at), w_outer(w_ref, at), w_sems.at[1, at])

    def fetch_output():
        return pltpu.make_async_copy(w_output(got_ref), w_output(w_ref), w_sems.at[0, wide])

    def slot(group, i):
        return group % 2 * 16 + group // 2 * 8 + i % 2 * 4 + i // 2 if mapped else group * 8 + i

    def outer(at):
        turn = (2 * wide - 1 - at) % 2
        return [
            pltpu.make_async_copy(
                out_buf.at[turn, i], grads.at[slot(at, i), pl.ds(0, wide * each)], sems.at[turn, i]
            )
            for i in range(some)
        ]

    def inner(at):
        turn = (2 * wide - 1 - at) % 2
        top = pl.multiple_of((wide + 1 + at) * each, each)
        return [
            pltpu.make_async_copy(
                in_buf.at[turn, e], grads.at[slot(e // 8, e % 8), pl.ds(top, each)], sems.at[2 + turn, e]
            )
            for e in range(owners)
        ]

    def output():
        return [
            pltpu.make_async_copy(
                wo_buf.at[e], grads.at[slot(e // 8, e % 8), pl.ds(wide * each, each)], sems.at[4, e]
            )
            for e in range(owners)
        ]

    def start(copies):
        for copy in copies:
            copy.start()

    def wait(copies):
        for copy in copies:
            copy.wait()

    @pl.when(step == 0)
    def _():
        fetch_output().start()
        for at in range(wide):
            fetch_inner(at).start()
            fetch_outer(at).start()
        fetch_output().wait()
        hidden = own_ref[...].astype(F32) + mm(ctx_ref[...], square(w_output(w_ref)[...])) + vec(0)
        centred = hidden - mean(hidden)
        inverse = lax.rsqrt(mean(centred * centred) + NORM_EPS)
        normed = centred * inverse
        n1_ref[...] = normed
        inv_ref[...] = inverse
        first = normed * vec(1) + vec(2)
        first_ref[...] = first
        low_ref[...] = first.astype(BF)
        lowt_ref[...] = first.astype(BF).T

    @pl.when(step < wide)
    def _():
        chunk = pl.ds(pl.multiple_of(step * width, width), width)
        fetch_inner(step).wait()
        fetch_outer(step).wait()
        pre = mm(low_ref[...], square(w_inner(w_ref, step)[...])) + bin_ref[pl.ds(step, 1), :]
        cdf = 0.5 * (1.0 + lax.erf(pre * SQRT_HALF))
        act = (pre * cdf).astype(BF)
        pre_ref[:, chunk] = pre
        cdf_ref[:, chunk] = cdf
        act_ref[:, chunk] = act
        more = mm(act, square(w_outer(w_ref, step)[...]))

        @pl.when(step == 0)
        def _():
            acc_ref[...] = more

        @pl.when(step > 0)
        def _():
            acc_ref[...] += more

    @pl.when(step == wide - 1)
    def _():
        hidden = first_ref[...] + acc_ref[...] + vec(3)
        centred = hidden - mean(hidden)
        inverse = lax.rsqrt(mean(centred * centred) + NORM_EPS)
        normed = centred * inverse
        out_ref[...] = (normed * vec(4) + vec(5)).astype(BF)
        grad = cot_ref[...].astype(F32)
        sums_ref[0:1, :] = down(grad * normed)
        sums_ref[1:2, :] = down(grad)
        e = grad * vec(4)
        back = inverse * (e - mean(e) - normed * mean(e * normed))
        gffn_ref[...] = back
        low = back.astype(BF)
        glow_ref[...] = low
        sums_ref[2:3, :] = down(low.astype(F32))

    @pl.when(step >= wide)
    def _():
        at = 2 * wide - 1 - step
        chunk = pl.ds(pl.multiple_of(at * width, width), width)
        pre = pre_ref[:, chunk]
        slope = cdf_ref[:, chunk] + pre * jnp.exp(-0.5 * pre * pre) * INV_ROOT_TAU
        low = glow_ref[...]
        grad = (nt(low, square(w_outer(w_ref, at)[...])) * slope).astype(BF)
        sbin_ref[pl.ds(at, 1), :] = down(grad.astype(F32))
        turn = step % 2

        @pl.when(step >= wide + 2)
        def _():
            wait(outer(at + 2) + inner(at + 2))

        out_buf[turn] = tn(act_ref[:, chunk], low).astype(BF).reshape(some, wide * each, width)
        start(outer(at))
        in_buf[turn] = mm(lowt_ref[...], grad).astype(BF).reshape(owners, each, width)
        start(inner(at))
        gffn_ref[...] += nt(grad, square(w_inner(w_ref, at)[...]))

    @pl.when(step == 2 * wide - 1)
    def _():
        grad = gffn_ref[...]
        normed = n1_ref[...]
        sums_ref[3:4, :] = down(grad * normed)
        sums_ref[4:5, :] = down(grad)
        e = grad * vec(1)
        back = inv_ref[...] * (e - mean(e) - normed * mean(e * normed))
        h1_ref[...] = back
        low = back.astype(BF)
        sums_ref[5:6, :] = down(low.astype(F32))
        wo_buf[...] = tn(ctx_ref[...], low).astype(BF).reshape(owners, each, width)
        start(output())
        gctx = nt(low, square(w_output(w_ref)[...])).astype(BF)
        gctx_ref[...] = gctx
        sums_ref[6:7, :] = down(gctx.astype(F32))
        sums_ref[7:8, :] = jnp.zeros((1, width), F32)
        wait(outer(1) + inner(1) + outer(0) + inner(0) + output())


def middle_call(ctx, own, cot, got, vec, b_inner, mapped):
    rows, width = own.shape
    owners = got.shape[0]
    each = width // owners
    wide = WIDE
    whole = lambda shape: pl.BlockSpec(shape, lambda s: (0,) * len(shape))
    shape = jax.ShapeDtypeStruct
    return pl.pallas_call(
        functools.partial(middle_kernel, wide, mapped),
        grid=(2 * wide,),
        in_specs=[
            whole((rows, width)), whole((rows, width)), whole((rows, width)),
            pl.BlockSpec(memory_space=pl.ANY),
            whole((8, width)), whole((8, width)),
        ],
        out_specs=[
            whole((rows, width)), whole((rows, width)), whole((rows, width)),
            pl.BlockSpec(memory_space=pl.ANY),
            whole((8, width)), whole((8, width)),
        ],
        out_shape=[
            shape((rows, width), BF), shape((rows, width), F32), shape((rows, width), BF),
            shape((owners, (2 * wide + 1) * each, width), BF),
            shape((8, width), F32), shape((8, width), F32),
        ],
        scratch_shapes=[
            pltpu.VMEM((rows, width), F32), pltpu.VMEM((rows, width), F32), pltpu.VMEM((rows, 1), F32),
            pltpu.VMEM((rows, width), BF), pltpu.VMEM((rows, wide * width), F32),
            pltpu.VMEM((rows, wide * width), F32), pltpu.VMEM((rows, wide * width), BF),
            pltpu.VMEM((rows, width), F32), pltpu.VMEM((rows, width), F32),
            pltpu.VMEM((rows, width), BF), pltpu.VMEM((width, rows), BF),
            pltpu.VMEM((owners, (2 * wide + 1) * each, width), BF),
            pltpu.VMEM((2, owners // wide, wide * each, width), BF),
            pltpu.VMEM((2, owners, each, width), BF),
            pltpu.VMEM((owners, each, width), BF), pltpu.SemaphoreType.DMA((5, owners)),
            pltpu.SemaphoreType.DMA((2, wide + 1)),
        ],
        compiler_params=pltpu.CompilerParams(vmem_limit_bytes=60 * 2**20),
        cost_estimate=pl.CostEstimate(
            flops=2 * rows * width * width * (6 * wide + 3), bytes_accessed=32 * 2**20,
            transcendentals=2 * rows * width * wide,
        ),
        name="middle",
    )(ctx, own, cot, got, vec, b_inner)


def back_kernel(rows, bound, started, *refs):
    near_ref, gctx_ref, ctx_ref, q_ref, k_ref, v_ref, lse_ref, segq_ref, segk_ref = refs[:9]
    dk_ref, dv_ref, dq_ref, kt_ref, p_ref, ds_ref = refs[-6:]
    q, g = q_ref[...], gctx_ref[...]
    part = q.shape[1]
    heads = part // HDIM
    masks = [heads_mask(q.shape, h) for h in range(heads)]
    q_parts = [jnp.where(m, q, 0) for m in masks]
    g_parts = [jnp.where(m, g, 0) for m in masks]
    product = (g.astype(F32) * ctx_ref[...].astype(F32)).T
    inner = [
        jnp.sum(product[h * HDIM : (h + 1) * HDIM], axis=0, keepdims=True) for h in range(heads)
    ]

    def body():
        k, v = k_ref[...], v_ref[...]
        kt_ref[...] = k.T
        for h in range(heads):
            s = nt(k, q_parts[h])
            if bound is None:
                s = jnp.where(segk_ref[...] == segq_ref[...], s, MASK_FILL)
            p = jnp.exp(s - lse_ref[0, h : h + 1, :])
            across = slice(h * rows, (h + 1) * rows)
            ds = (p * (nt(v, g_parts[h]) - inner[h])).astype(BF)
            p_ref[:, across] = p.astype(BF)
            ds_ref[:, across] = ds
            mine = slice(h * HDIM, (h + 1) * HDIM)
            more = mm(kt_ref[mine, :], ds)
            dq_ref[mine, :] = refs[9][mine, :] + more if started else more
        dk_ref[...] = mm(ds_ref[...], jnp.concatenate(q_parts, 0)).astype(BF)
        dv_ref[...] = mm(p_ref[...], jnp.concatenate(g_parts, 0)).astype(BF)

    if bound is None:

        @pl.when(near_ref[0] == 0)
        def _():
            dq_ref[...] = refs[9][...]

        pl.when(near_ref[0] > 0)(body)
    else:
        body()


def back_call(start, steps, bound, near, gctx, ctx, q, k, v, lse, segq, segk, dq0=None, into=None):
    rows, width = q.shape
    tall = k.shape[0]
    part = 256
    cols = lambda depth: pl.BlockSpec((depth, part), lambda g: (0, start + g))
    whole = lambda shape: pl.BlockSpec(shape, lambda g: (0,) * len(shape))
    down = pl.BlockSpec((part, rows), lambda g: (start + g, 0))
    shape = jax.ShapeDtypeStruct
    extra = ([dq0] if dq0 is not None else []) + list(into or [])
    specs = ([down] if dq0 is not None else []) + [pl.BlockSpec(memory_space=pl.ANY)] * len(into or [])
    return pl.pallas_call(
        functools.partial(back_kernel, rows, bound, dq0 is not None),
        grid=(steps,),
        in_specs=[
            pl.BlockSpec(memory_space=pltpu.SMEM),
            cols(rows), cols(rows), cols(rows), cols(tall), cols(tall),
            pl.BlockSpec((1, 8, rows), lambda g: (start + g, 0, 0)),
            whole((1, rows)), whole(segk.shape),
        ] + specs,
        out_specs=[cols(tall), cols(tall), down],
        out_shape=[shape((tall, width), BF), shape((tall, width), BF), shape((width, rows), F32)],
        input_output_aliases={9 + i: i for i in range(3)} if into else {},
        scratch_shapes=[
            pltpu.VMEM((part, tall), BF),
            pltpu.VMEM((tall, part // HDIM * rows), BF),
            pltpu.VMEM((tall, part // HDIM * rows), BF),
        ],
        compiler_params=pltpu.CompilerParams(vmem_limit_bytes=60 * 2**20),
        cost_estimate=pl.CostEstimate(
            flops=2 * 10 * 2 * tall * rows * part * steps * 2,
            bytes_accessed=8 * tall * part * steps, transcendentals=tall * rows * 4 * steps,
        ),
        name="attention_back",
    )(near, gctx, ctx, q, k, v, lse, segq, segk, *extra)


def product_kernel(rows, bound, near_ref, dk_ref, dv_ref, wk_ref, wv_ref, gx_ref):
    @pl.when((pl.program_id(0) < near_ref[0]) | (bound is not None))
    def _():
        width = dk_ref.shape[1]
        wk, wv = wk_ref[...].reshape(width, width), wv_ref[...].reshape(width, width)
        gx_ref[0] = (nt(dk_ref[...], wk) + nt(dv_ref[...], wv)).astype(BF)


def product_call(bound, near, dk, dv, got, rows):
    tall, width = dk.shape
    owners, each = got.shape[0], width // got.shape[0]
    weight = lambda place: pl.BlockSpec((owners, each, width), lambda b: (0, place, 0))
    return pl.pallas_call(
        functools.partial(product_kernel, rows, bound),
        grid=(tall // rows,),
        in_specs=[
            pl.BlockSpec(memory_space=pltpu.SMEM),
            pl.BlockSpec((rows, width), lambda b: (b, 0)),
            pl.BlockSpec((rows, width), lambda b: (b, 0)),
            weight(WK), weight(WV),
        ],
        out_specs=pl.BlockSpec((1, rows, width), lambda b: (b, 0, 0)),
        out_shape=jax.ShapeDtypeStruct((tall // rows, rows, width), BF),
        compiler_params=pltpu.CompilerParams(vmem_limit_bytes=60 * 2**20),
        cost_estimate=pl.CostEstimate(
            flops=4 * tall * width * width, bytes_accessed=6 * tall * width, transcendentals=0
        ),
        name="token_product",
    )(near, dk, dv, got, got)


def weight_kernel(blocks, first, rows, runs, *refs):
    spots = refs[:blocks]
    (near_ref, core_ref, own_ref, dq_ref, wq_ref, h1_ref, dkp_ref, dvp_ref, dkn_ref, dvn_ref,
     send_ref, keep_ref, gown_ref, sums_ref, x_ref, xt_ref, sems) = refs[blocks:]
    core = core_ref[0]
    step = pl.program_id(0)

    @pl.when(step == 0)
    def _():
        copies = [
            pltpu.make_async_copy(spot, x_ref.at[pl.ds(i * rows, rows)], sems.at[i])
            for i, spot in enumerate(spots)
        ]
        for copy in copies:
            copy.start()
        gown_ref[...] = h1_ref[...]
        for i, copy in enumerate(copies):
            copy.wait()
            xt_ref[:, i * rows : (i + 1) * rows] = x_ref[i * rows : (i + 1) * rows, :].T

    scale = HDIM**-0.5
    dq = dq_ref[...].T.astype(BF)
    part = dq.shape[1]
    width = x_ref.shape[1]
    gown_ref[...] += nt(dq, wq_ref[...].reshape(width, part)) * scale
    half = send_ref.shape[0]
    each = width // (2 * half)

    def put(i, grad):
        away, here = halves(grad.astype(BF), runs, core)
        send_ref[:, i * each : (i + 1) * each, :] = away.reshape(half, each, part)
        keep_ref[:, i * each : (i + 1) * each, :] = here.reshape(half, each, part)

    put(WQ, tn(own_ref[...], dq) * scale)
    sums_ref[0:1, :] = jnp.sum(dq.astype(F32), axis=0, keepdims=True) * scale

    def body(near):
        for i, p_ref, n_ref in ((WK, dkp_ref, dkn_ref), (WV, dvp_ref, dvn_ref)):
            grad = mm(xt_ref[:, :PROMPT], p_ref[...])
            if near:
                grad = grad + mm(xt_ref[:, PROMPT:], n_ref[...])
            put(i, grad)

    pl.when(near_ref[0] == 0)(lambda: body(False))
    pl.when(near_ref[0] > 0)(lambda: body(True))
    sums_ref[1:8, :] = jnp.zeros((7, part), F32)


def weight_call(spots, first, near, own, dq, got, h1, dkp, dvp, dkn, dvn, core, runs):
    rows, width = own.shape
    blocks = len(spots)
    tall = blocks * rows
    part = 256
    steps = width // part
    cols = lambda depth, size=part: pl.BlockSpec((depth, size), lambda g: (0, g))
    whole = lambda shape: pl.BlockSpec(shape, lambda g: (0,) * len(shape))
    shape = jax.ShapeDtypeStruct
    owners, each = got.shape[0], width // got.shape[0]
    half = owners // 2
    slab = pl.BlockSpec((half, 3 * each, part), lambda g: (0, 0, g))
    return pl.pallas_call(
        functools.partial(weight_kernel, blocks, first, rows, runs),
        grid=(steps,),
        in_specs=[pl.BlockSpec(memory_space=pl.ANY)] * blocks
        + [
            pl.BlockSpec(memory_space=pltpu.SMEM),
            pl.BlockSpec(memory_space=pltpu.SMEM),
            whole((rows, width)), pl.BlockSpec((part, rows), lambda g: (g, 0)),
            pl.BlockSpec((owners, each, part), lambda g: (0, WQ, g)),
            whole((rows, width)), cols(PROMPT), cols(PROMPT), cols(tall - PROMPT), cols(tall - PROMPT),
        ],
        out_specs=[
            slab, slab, whole((rows, width)), cols(8),
        ],
        out_shape=[
            shape((half, 3 * each, width), BF), shape((half, 3 * each, width), BF),
            shape((rows, width), F32), shape((8, width), F32),
        ],
        scratch_shapes=[
            pltpu.VMEM((tall, width), BF), pltpu.VMEM((width, tall), BF), pltpu.SemaphoreType.DMA((blocks,)),
        ],
        compiler_params=pltpu.CompilerParams(vmem_limit_bytes=60 * 2**20),
        cost_estimate=pl.CostEstimate(
            flops=4 * tall * width * width, bytes_accessed=12 * tall * width, transcendentals=0
        ),
        name="weight_product",
    )(*spots, near, core, own, dq, got, h1, dkp, dvp, dkn, dvn)


def real_owners(grads, count, step, width):
    split = count // 32
    take = lambda v: v.reshape(32, -1, split, step, width).transpose(0, 2, 1, 3, 4).reshape(count, -1, width)
    outer, rest = grads[:, : 4 * split * step], grads[:, 4 * split * step :]
    return jnp.concatenate([outer.reshape(count, 4 * step, width), take(rest)], 1)


def solution(mesh):
    plan = Plan(mesh.shape["grp"], mesh.shape["row"])
    fine = Mesh(mesh.devices.reshape(plan.grp // 2, 2, 4, plan.row // 4), AXES)

    def per_device(
        tokens, cont_lengths, cotangent, w_query, w_key, w_value, w_output, w_inner, w_outer,
        bias_query, bias_value, bias_output, gain_first, shift_first, bias_inner, bias_outer,
        gain_second, shift_second,
    ):
        count = plan.count
        _, rows, width = tokens.shape
        step = w_query.shape[0]
        wide = w_inner.shape[1] // width
        own = tokens[0]

        early = (bias_query, bias_value)
        late = (bias_output, gain_first, shift_first, bias_outer, gain_second, shift_second, bias_inner)
        small = len(late) - 1

        def in_line(vectors):
            line, place = 0, 0
            for vector in vectors:
                size = vector.shape[0]
                line = line + jnp.pad(vector, (place, width - place - size))
                place += size
            return jnp.pad(line[None], ((0, 7), (0, 0)))

        line = jnp.concatenate([in_line(early), in_line(late)], 0)
        runs = plan.grp
        row = lax.axis_index(ROW)
        core = lax.axis_index("core").astype(jnp.int32).reshape(1)
        exchange = Tokens(plan, own)
        squares = (w_query, w_key, w_value)
        if step % 8 == 0:
            first_pack, pack = pack_call(w_output, w_inner, w_outer, *squares, line)
            got = lax.all_gather(pack, AXES, axis=0, tiled=True).reshape(count, -1, width)
            lines = got[:, (WI + WIDE) * step]

            def swaps(value, bits):
                masks = [0]
                for bit in bits:
                    masks = masks + [m ^ bit for m in masks]
                return [plan.swap(value, m) for m in masks[1:]]

            def stage(held, bit):
                return jnp.concatenate([held, plan.swap(held, bit)], 0)

            away = swaps(first_pack, plan.z)
            *away, same, beside = tie(*away, *exchange.stage_one())
            exchange.same, exchange.beside = same, beside
            cut = step + 16
            one = jnp.stack([v[:cut] for v in (first_pack, *away)])
            two = jnp.stack([v[cut:] for v in (first_pack, *away)])
            one, two = stage(one, plan.x[0]), stage(two, plan.y[0])
            one, two, *seen = tie(one, two, *exchange.stage_two())
            exchange.other, exchange.same_y, exchange.diagonal = seen
            one, two = stage(one, plan.y[0]), stage(two, plan.x[0])
            exchange.stage_three()
            one, exchange.other_y = tie(one, exchange.other_y)
            pieces = [one, plan.swap(one, plan.core[0]), two, plan.swap(two, plan.core[0])]
            order = lambda *bits: ([(bit, 1 << i) for i, bit in enumerate(bits)], plan.core[0])
            places = (
                order(*plan.z, plan.x[0], plan.y[0]),
                order(*plan.z, plan.y[0], plan.x[0]),
            )
            me = plan.me().astype(jnp.int32).reshape(1)
        else:
            inner_rows = [w_inner[:, i * width : (i + 1) * width] for i in range(wide)]
            pack = jnp.concatenate([w_outer, w_output, *inner_rows, *squares, line], 0)
            got = lax.all_gather(pack, AXES, axis=0, tiled=True).reshape(count, -1, width)
            lines = got[:, 12 * step + 8]
            cuts = [wide * step, (wide + 1) * step, (2 * wide + 1) * step, 12 * step]
            outer, output, inner, rest, marks = jnp.split(got, cuts, axis=1)
            apart = lambda v, n: v.reshape(count, n, step, width).transpose(1, 0, 2, 3)
            inner, rest = [
                v.reshape(v.shape[0], 32, width // 32, width).transpose(1, 0, 2, 3)
                for v in (apart(inner, wide), apart(rest, 3))
            ]
            got = jnp.concatenate([v.reshape(32, -1, width) for v in (outer, output, inner)], 1)
            pairs = marks[:, 0, : 2 * step].reshape(32, count // 32, 2, step).transpose(0, 2, 1, 3)
            pairs = jnp.pad(pairs.reshape(32, 1, -1), ((0, 0), (0, 7), (0, width - 2 * width // 32)))
            one = jnp.concatenate([rest[:, 0], pairs, rest[:, 1, :8]], 1)
            two = jnp.concatenate([rest[:, 1, 8:], rest[:, 2]], 1)
            pieces = [one[:16], one[16:], two[:16], two[16:]]
            places = (([(1, 1), (2, 2), (4, 4), (8, 8)], 16),) * 2
            me = jnp.zeros((1,), jnp.int32)
        spots, near = exchange.spots()
        first_near = PROMPT // rows

        table = lines[:, : small * step].reshape(count, small, step).transpose(1, 0, 2)
        table = table.reshape(small, width).astype(F32)
        v_bin = lines[:, small * step : (small + wide) * step].reshape(wide, width).astype(F32)
        v_bin = jnp.pad(v_bin, ((0, 8 - wide), (0, 0)))
        segments = segment_ids(cont_lengths[0], plan.row * rows)
        seg_own = lax.dynamic_slice_in_dim(segments, row * rows, rows, 0)[None, :]
        seg_near = near_segments(plan, segments, rows)[:, None]
        near = near.astype(jnp.int32).reshape(1)

        squares, queries, keys_p, values_p, keys_n, values_n, context, log_total = attention_call(
            spots, first_near, near, me, own, pieces, places, seg_own, seg_near
        )
        vec = jnp.concatenate([table, jnp.zeros((2, width), F32)], 0)
        layer_out, grad_h1, grad_context, grads, sums, sums_bin = middle_call(
            context, own, cotangent[0], got, vec, v_bin, step % 8 == 0
        )
        if step % 8:
            grads = real_owners(grads, count, step, width)
            grads = grads.reshape(plan.grp // 2, 2, 4, plan.row // 4, -1, width)
            grads = grads.transpose(1, 0, 3, 2, 4, 5).reshape(count, -1, width)
        level = lambda value, axes: lax.psum_scatter(value, axes, scatter_dimension=0, tiled=True)
        grads = level(grads, "core")
        core_bit = plan.core[0]
        left = [1 << i for i in reversed(range(plan.bits)) if 1 << i != core_bit]
        parts = width // 256
        dkp, dvp, dqp = back_call(
            0, parts, first_near, near, grad_context, context, queries, keys_p, values_p, log_total,
            seg_own, seg_near,
        )
        shared_p = product_call(first_near, near, dkp, dvp, squares, rows)
        grads, shared_p, dqp = tie(grads, shared_p, dqp)
        grads = level(grads, ("x", "y"))
        returned = Return(plan, rows)
        returned.prompt_one(shared_p)
        dkn, dvn, dq = back_call(
            0, parts, None, near, grad_context, context, queries, keys_n, values_n, log_total,
            seg_own, seg_near, dqp,
        )
        send, keep, grad_own, sums_qkv = weight_call(
            spots, first_near, near, own, dq, squares, grad_h1, dkp, dvp, dkn, dvn, core, runs
        )
        send, keep, returned.same, returned.same_y, dkn, dvn = tie(
            send, keep, returned.same, returned.same_y, dkn, dvn
        )
        returned.prompt_two()
        shared_n = product_call(None, near, dkn, dvn, squares, rows)

        order = (6, 5, 3, 4, 2, 0, 1)
        small = len(early) + len(late) - 1
        d_table = jnp.concatenate([sums_qkv[:1]] + [sums[i : i + 1] for i in order], 0)
        d_lines = jnp.concatenate(
            [
                d_table.reshape(small, count, step).transpose(1, 0, 2).reshape(count, -1),
                sums_bin[:wide].reshape(count, wide * step),
            ],
            1,
        )
        d_lines = jnp.pad(d_lines, ((0, 0), (0, width - d_lines.shape[1])))[:, None].astype(BF)
        d_lines = jnp.pad(d_lines, ((0, 0), (0, 7), (0, 0)))
        place = core[0]
        pick = Reduce(plan, [])
        if step % 8:
            real = lambda v: v.reshape(16, 3, count // 32, step, width).transpose(0, 2, 1, 3, 4)
            send, keep = [real(v).reshape(count // 2, 3 * step, width) for v in (send, keep)]
        send = jnp.concatenate([send, pick.cut(d_lines, core_bit, 1 - place)], 1)
        keep = jnp.concatenate([keep, pick.cut(d_lines, core_bit, place)], 1)
        reduce = Reduce(plan, [keep, plan.swap(send, core_bit)], left)
        returned.prompt_three()
        reduce.stage_direct(plan.x + plan.y)
        *held, grads, shared_n, returned.back = tie(
            *reduce.terms, grads, shared_n, returned.back
        )
        reduce.terms = list(held)
        grads = level(grads, "z")
        *held, shared_n = tie(*reduce.terms, shared_n)
        reduce.terms = list(held)
        returned.near(shared_n)
        reduce.stage_direct(plan.z)
        o_ab = grads.reshape(-1, width).astype(F32)
        grad_tokens = grad_own + returned.total()
        o_first = reduce.result()
        o_line = o_first[3 * step]
        o_small = [o_line[i * step : (i + 1) * step] for i in range(small)]
        o_bin = o_line[small * step : (small + wide) * step]
        return (
            layer_out[None],
            grad_tokens.astype(BF)[None],
            o_first[:step],
            o_first[step : 2 * step],
            o_first[2 * step : 3 * step],
            o_ab[wide * step : (wide + 1) * step],
            jnp.concatenate([o_ab[i * step : (i + 1) * step] for i in range(wide + 1, 2 * wide + 1)], 1),
            o_ab[: wide * step],
            o_small[0],
            o_small[1],
            o_small[2],
            o_small[3],
            o_small[4],
            o_bin,
            o_small[5],
            o_small[6],
            o_small[7],
        )

    split = P(GRP, ROW, None)
    owned2, owned1 = P(AXES, None), P(AXES)
    in_specs = (split, P(GRP, None), split) + (owned2,) * 6 + (owned1,) * 9
    out_specs = (split, split) + (owned2,) * 6 + (owned1,) * 9
    return jax.shard_map(
        per_device, mesh=fine, in_specs=in_specs, out_specs=out_specs, check_vma=False
    )
```
